32 devices in a mesh: dp: 8 (over z, y), ctx: 2 (over x), tp: 2 (over core).
Axes of the slice: x: 2, y: 2, z: 4, core: 2. Of those that a mesh axis runs over, the one named last changes fastest.
Arguments:
- hidden_in: bfloat16 [2, 8, 1024, 1152], P(None, 'dp', 'ctx'), may hold values from -6 to 6
- out_grad: bfloat16 [2, 8, 1024, 1152], P(None, 'dp', 'ctx'), may hold values from -6 to 6
- norm1_gain: bfloat16 [1152], P('dp'), may hold values from 0.5 to 1.5
- in_weight: bfloat16 [1152, 2, 2304], P('dp', None, 'tp'), may hold values from -0.1875 to 0.1875
- conv_weight: bfloat16 [4, 2304], P(None, ('tp', 'dp')), may hold values from -3 to 3
- conv_bias: bfloat16 [2304], P(('tp', 'dp')), may hold values from -0.5 to 0.5
- xproj_weight: bfloat16 [2304, 104], P(('tp', 'dp')), may hold values from -0.359375 to 0.359375
- dt_weight: bfloat16 [72, 2304], P(None, ('tp', 'dp')), may hold values from -0.75 to 0.75
- dt_bias: bfloat16 [2304], P(('tp', 'dp')), may hold values from -7 to -3
- decay_log: bfloat16 [16, 2304], P(None, ('tp', 'dp')), may hold values from 0 to 2.796875
- skip_weight: bfloat16 [2304], P(('tp', 'dp')), may hold values from 0.5 to 1.5
- out_weight: bfloat16 [2304, 1152], P('tp', 'dp'), may hold values from -0.375 to 0.375
- norm2_gain: bfloat16 [1152], P('dp'), may hold values from 0.5 to 1.5
- router_weight: bfloat16 [1152, 8], P('dp'), may hold values from -0.119628906 to 0.119628906
- fc1_weight: bfloat16 [8, 1152, 3072], P(None, 'dp', 'tp'), may hold values from -0.1875 to 0.1875
- fc2_weight: bfloat16 [8, 3072, 1152], P(None, 'tp', 'dp'), may hold values from -0.75 to 0.75
- expert_ids: int32 [16384, 1], P(('dp', 'ctx')), may hold values from 0 to 7; in each aligned block of 512 rows (0 to 511, 512 to 1023, ...) at most 128 rows name the same one
- keep_mask: int32 [16384], P(('dp', 'ctx')), may hold values 0 or 1
Outputs:
- output: bfloat16 [2, 8, 1024, 1152], P(None, 'dp', 'ctx')
- input_grad: bfloat16 [2, 8, 1024, 1152], P(None, 'dp', 'ctx')
- norm1_gain_grad: float32 [1152], P('dp')
- in_weight_grad: float32 [1152, 2, 2304], P('dp', None, 'tp')
- conv_weight_grad: float32 [4, 2304], P(None, ('tp', 'dp'))
- conv_bias_grad: float32 [2304], P(('tp', 'dp'))
- xproj_weight_grad: float32 [2304, 104], P(('tp', 'dp'))
- dt_weight_grad: float32 [72, 2304], P(None, ('tp', 'dp'))
- dt_bias_grad: float32 [2304], P(('tp', 'dp'))
- decay_log_grad: float32 [16, 2304], P(None, ('tp', 'dp'))
- skip_weight_grad: float32 [2304], P(('tp', 'dp'))
- out_weight_grad: float32 [2304, 1152], P('tp', 'dp')
- norm2_gain_grad: float32 [1152], P('dp')
- router_weight_grad: float32 [1152, 8], P('dp')
- fc1_weight_grad: float32 [8, 1152, 3072], P(None, 'dp', 'tp')
- fc2_weight_grad: float32 [8, 3072, 1152], P(None, 'tp', 'dp')
The draws below stay inside these ranges and needn't reach their ends.
Inputs may be any that keep to these rules, and one draw needn't show every extreme that they name: `expert_ids`: in each aligned block of 512 rows (one device's tokens of one micro-batch) no expert is named by more than 128 rows, a bound that some block reaches.
All inputs are finite; a program needn't handle non-finite values. No bound on the sum of `keep_mask` on one device may be relied on, other than what follows from the above.
Results may differ from the reference program's by a relative error of at most 0.014.
The reference program's roundings to bfloat16 on the way count: a program that leaves them out, or rounds other values in their place, can miss the bound.
Values may be sent and summed in bfloat16 or wider, within the bound.
A program may use at most 512 MiB of HBM per device.

```python
import math
import jax
import jax.numpy as jnp
import numpy as np
from jax import lax

D = 1152
DI = 2304
NS = 16
DTR = 72
KC = 4
FFE = 3072
E = 8
MB = 2
SEQ_LEN = 1024
TOK_MB = 512
SEQS = 8
CAP = 128
ROWS = 16384
N_DP = 8
N_CTX = 2


def with_ends(array, own_key, low, largest):
    dims = array.shape
    index_at = [jax.random.randint(jax.random.fold_in(own_key, axis), (), 0, dims[axis]) for axis in range(len(dims))]
    array = array.at[tuple(index_at)].set(low)
    longest = dims.index(max(dims))
    index_at[longest] = (index_at[longest] + 1) % dims[longest]
    return array.at[tuple(index_at)].set(largest)


def level_of(key, extent, shards, low, largest):
    factor_of = 1.0
    for axis_at, blocks in shards:
        draws = jax.random.uniform(jax.random.fold_in(jax.random.fold_in(key, 6), axis_at), (blocks,), jnp.float32, low / len(shards), largest / len(shards))
        factor_of = factor_of * jnp.repeat(jnp.exp(draws), extent[axis_at] // blocks).reshape((-1,) + (1,) * (len(extent) - 1 - axis_at))
    return factor_of


def shared_out(rng, own, number, rows, number_of, top, reach, lean):
    sequence = jax.random.permutation(rng, number_of)
    crowded, ordinary = portions_of(number_of, rows * top, reach, lean, True), portions_of(number_of, rows * top, reach, lean, False)
    places = jnp.arange(number_of)

    def named(sizes, rotation):
        used = int((sizes > 0).sum())
        fixed = max(1, used // 4)
        moved = fixed + (places - fixed + rotation * (used - fixed)) % max(1, number_of - fixed)
        return jnp.zeros((number_of,), jnp.int32).at[sequence[jnp.where(places < fixed, places, moved)]].set(jnp.asarray(sizes, jnp.int32))

    sizes = jnp.where(number % 4 == 0, named(crowded, number // 4), named(ordinary, number - number // 4 - 1))
    mixed = jax.random.permutation(jax.random.fold_in(own, 3), number_of)
    source_of, taker = mixed[0:number_of // 2 * 2:2], mixed[1:number_of // 2 * 2:2]
    room = jnp.minimum(sizes[source_of] - 1, reach - sizes[taker]) // 2
    room = jnp.where((source_of == sequence[0]) | (taker == sequence[0]) | (sizes[taker] == 0), 0, jnp.maximum(room, 0))
    moved = jax.random.randint(jax.random.fold_in(own, 4), (number_of // 2,), 0, 1 << 20) % (room + 1)
    sizes = sizes.at[source_of].add(-moved).at[taker].add(moved)
    items = jnp.searchsorted(jnp.cumsum(sizes), jnp.arange(rows * top), side="right").astype(jnp.int32)
    table = items.reshape(top, rows).T
    table = table[jax.random.permutation(jax.random.fold_in(own, 1), rows)]
    rotation = jax.random.randint(jax.random.fold_in(own, 2), (rows, 1), 0, top)
    return jnp.take_along_axis(table, (jnp.arange(top)[None, :] + rotation) % top, axis=1)


def portions_of(count, total, bound, lean, full):
    weights = [(1 << 20) // math.isqrt(standing ** lean) + 1 for standing in range(1, count + 1)]
    largest = bound if full else min(bound, max(-(-total // count), total * weights[0] // sum(weights)))
    least = 1 if total - largest >= count - 1 else 0
    given, rest = [largest] + [least] * (count - 1), total - largest - least * (count - 1)
    while rest > 0:
        free = [i for i in range(1, count) if given[i] < largest] or [i for i in range(1, count) if given[i] < bound]
        pool, budget = sum([weights[i] for i in free]), rest
        for i in free:
            more = min(bound - given[i], max(1, budget * weights[i] // pool), rest)
            given[i] = given[i] + more
            rest = rest - more
    return np.array(given)


def centred(own_key, shape, width, most, pieces=(), kind=jnp.bfloat16):
    values = width * jax.random.normal(own_key, shape, jnp.float32)
    if pieces:
        values = values * level_of(own_key, shape, pieces, -0.22, 0.18)
    return jnp.clip(values, -most, most).astype(kind)


def setup_inputs(seed: int = 0) -> dict:
    splits = jax.random.split(jax.random.key(seed), 19)
    hidden_in = centred(splits[0], (MB, SEQS, SEQ_LEN, D), 1.0, 6.0, ((1, 8), (2, 2)))
    out_grad = centred(splits[1], (MB, SEQS, SEQ_LEN, D), 1.0, 6.0, ((1, 8), (2, 2)))
    norm1_gain = jnp.clip(1.0 + 0.1 * jax.random.normal(splits[2], (D,), jnp.float32), 0.5, 1.5).astype(jnp.bfloat16)
    in_weight = centred(splits[3], (D, 2, DI), D ** -0.5, 0.1875, ((0, 8), (2, 2)))
    conv_weight = centred(splits[4], (KC, DI), KC ** -0.5, 3.0, ((1, 16),))
    conv_bias = jnp.clip(jax.random.uniform(splits[5], (DI,), jnp.float32, -0.5, 0.5) * level_of(splits[5], (DI,), ((0, 16),), -0.4, 0.0), -0.5, 0.5).astype(jnp.bfloat16)
    xproj_weight = centred(splits[6], (DI, DTR + 2 * NS), 0.06, 0.359375, ((0, 16),))
    dt_weight = centred(splits[7], (DTR, DI), DTR ** -0.5, 0.75, ((1, 16),))
    dt_bias = jnp.clip(-7.0 + 4.0 * jax.random.uniform(splits[8], (DI,), jnp.float32) ** level_of(splits[8], (DI,), ((0, 16),), -0.2, 0.2), -7.0, -3.0).astype(jnp.bfloat16)
    decay_log = jnp.clip(2.796875 * jax.random.uniform(splits[9], (NS, DI), jnp.float32) ** level_of(splits[9], (NS, DI), ((1, 16),), -0.2, 0.2), 0.0, 2.796875).astype(jnp.bfloat16)
    skip_weight = jnp.clip(0.5 + 1.0 * jax.random.uniform(splits[10], (DI,), jnp.float32) ** level_of(splits[10], (DI,), ((0, 16),), -0.2, 0.2), 0.5, 1.5).astype(jnp.bfloat16)
    out_weight = centred(splits[11], (DI, D), (DI // 8) ** -0.5, 0.375, ((0, 2), (1, 8)))
    norm2_gain = jnp.clip(1.0 + 0.1 * jax.random.normal(splits[12], (D,), jnp.float32), 0.5, 1.5).astype(jnp.bfloat16)
    router_weight = centred(splits[13], (D, E), 0.02, 0.119628906, ((0, 8),))
    fc1_weight = centred(splits[14], (E, D, FFE), D ** -0.5, 0.1875, ((1, 8), (2, 2)))
    fc2_weight = centred(splits[15], (E, FFE, D), 64 ** -0.5, 0.75, ((1, 2), (2, 8)))
    expert_ids_keys = jax.random.split(jax.random.fold_in(splits[16], 1), ROWS // TOK_MB)
    expert_ids_turns = jax.random.permutation(jax.random.fold_in(splits[16], 3), ROWS // TOK_MB)
    expert_ids = jax.vmap(lambda own, number: shared_out(jax.random.fold_in(splits[16], 2), own, number, TOK_MB, E, 1, CAP, 2))(expert_ids_keys, expert_ids_turns).reshape((ROWS, 1))
    keep_mask = with_ends((jax.random.randint(splits[17], (ROWS,), 0, 8) < 7).astype(jnp.int32), jax.random.fold_in(splits[17], 1), 0, 1)
    return {"hidden_in": hidden_in, "out_grad": out_grad, "norm1_gain": norm1_gain, "in_weight": in_weight, "conv_weight": conv_weight, "conv_bias": conv_bias, "xproj_weight": xproj_weight, "dt_weight": dt_weight, "dt_bias": dt_bias, "decay_log": decay_log, "skip_weight": skip_weight, "out_weight": out_weight, "norm2_gain": norm2_gain, "router_weight": router_weight, "fc1_weight": fc1_weight, "fc2_weight": fc2_weight, "expert_ids": expert_ids, "keep_mask": keep_mask}


EPSILON = 1e-05

@jax.custom_vjp
def low(v):
    return lax.optimization_barrier(v.astype(jnp.bfloat16)).astype(jnp.float32)

@jax.custom_vjp
def low_back(v):
    return v

def low_keep(v):
    return (low(v), None)

def low_pass(kept, grad):
    return (grad,)

def back_keep(v):
    return (v, None)

def back_low(kept, grad):
    return (low(grad),)
low.defvjp(low_keep, low_pass)
low_back.defvjp(back_keep, back_low)

def matrix_product_highest(pattern, left_side, right_side):
    return jnp.einsum(pattern, left_side, right_side, precision=lax.Precision.HIGHEST, preferred_element_type=jnp.float32)

def rms_norm(values, gain_vec):
    inverse = lax.rsqrt(lax.optimization_barrier(jnp.mean(values * values, axis=-1, keepdims=True)) + EPSILON)
    return values * inverse * gain_vec

def selective_scan(step_size, xconv, state_in, state_out, rate_mat):
    seq_count, length, channels = step_size.shape
    block_len = math.gcd(length, 32)

    def time_step(carried, step_in):
        delta_now, input_now, mix_in, mix_out = step_in
        carried = jnp.exp(delta_now[:, None, :] * rate_mat) * carried + (delta_now * input_now)[:, None, :] * mix_in[:, :, None]
        return (carried, lax.optimization_barrier(jnp.sum(mix_out[:, :, None] * carried, axis=1)))

    @jax.checkpoint
    def block_step(carried, block_in):
        return lax.scan(time_step, carried, block_in)
    stacked = tuple((array_in.reshape(seq_count, length // block_len, block_len, array_in.shape[2]).transpose(1, 2, 0, 3) for array_in in (step_size, xconv, state_in, state_out)))
    start_state = jnp.zeros((seq_count, rate_mat.shape[0], channels), jnp.float32)
    _, outputs = lax.scan(block_step, start_state, stacked)
    return outputs.reshape(length, seq_count, channels).transpose(1, 0, 2)

def slot_tables(ids_flat, experts, capacity):
    onehot = (ids_flat[:, None] == jnp.arange(experts, dtype=jnp.int32)[None, :]).astype(jnp.int32)
    slot_rank = lax.optimization_barrier(jnp.sum((jnp.cumsum(onehot, axis=0) - 1) * onehot, axis=1)).astype(jnp.int32)
    token_slot = (ids_flat * capacity + slot_rank).astype(jnp.int32)
    matches = token_slot[None, :] == jnp.arange(experts * capacity, dtype=jnp.int32)[:, None]
    positions = jnp.arange(ids_flat.shape[0], dtype=jnp.int32)[None, :]
    slot_ids = lax.optimization_barrier(jnp.sum(jnp.where(matches, positions, 0), axis=1)).astype(jnp.int32)
    return (token_slot, slot_ids)

def expert_block(inputs, slot_ids, token_slot, first_layer, second_layer):
    experts = first_layer.shape[0]
    model_width = inputs.shape[1]
    picked = jnp.take(inputs, slot_ids, axis=0).reshape(experts, -1, model_width)
    hidden = low_back(matrix_product_highest('ecd,edf->ecf', picked, first_layer))
    active = low(jax.nn.gelu(hidden, approximate=False))
    result = low_back(matrix_product_highest('ecf,efd->ecd', active, second_layer))
    return jnp.take(result.reshape(-1, model_width), token_slot, axis=0)

def layer_forward(weights, values, ids_flat, keep_flat, token_slot, slot_ids):
    gain_one, input_projection, conv_taps, conv_shift, x_proj, dt_proj, dt_shift, decay_log, skip_gain, output_projection, gain_two, router, first_layer, second_layer = weights
    seq_count, length, model_width = values.shape
    tap_count = conv_taps.shape[0]
    low_rank = dt_proj.shape[0]
    state_count = decay_log.shape[0]
    normalized_rows = low(rms_norm(values, gain_one))
    mixer_input_rows = matrix_product_highest('ueh,hzp->uezp', normalized_rows, input_projection)
    x_pre = low_back(low(mixer_input_rows[:, :, 0]))
    z_gate = low_back(mixer_input_rows[:, :, 1])
    padded = jnp.pad(x_pre, ((0, 0), (tap_count - 1, 0), (0, 0)))
    conv_pre = conv_shift + jnp.zeros_like(x_pre)
    for tap_index in range(tap_count):
        conv_pre = conv_pre + conv_taps[tap_index] * padded[:, tap_index:tap_index + length]
    xconv = low(jax.nn.silu(conv_pre))
    projected = low_back(matrix_product_highest('slc,cr->slr', xconv, x_proj))
    dt_low = low(projected[:, :, :low_rank])
    state_in = projected[:, :, low_rank:low_rank + state_count]
    state_out = projected[:, :, low_rank + state_count:]
    step_size = jax.nn.softplus(matrix_product_highest('slr,rc->slc', dt_low, dt_proj) + dt_shift)
    rate_mat = -jnp.exp(decay_log)
    scanned = selective_scan(step_size, xconv, state_in, state_out, rate_mat) + skip_gain * xconv
    gated_output = low(scanned * jax.nn.silu(z_gate))
    mixer_output_rows = low_back(matrix_product_highest('zhi,ip->zhp', gated_output, output_projection))
    middle = values + mixer_output_rows
    normed_two = low(rms_norm(middle, gain_two))
    flat = normed_two.reshape(-1, model_width)
    logits = matrix_product_highest('td,de->te', flat, router)
    router_prob = jax.nn.softmax(logits, axis=-1)
    onehot = (ids_flat[:, None] == jnp.arange(router.shape[1], dtype=jnp.int32)[None, :]).astype(jnp.float32)
    gate_prob = lax.optimization_barrier(jnp.sum(router_prob * onehot, axis=1)) * keep_flat
    expert_out = expert_block(flat, slot_ids, token_slot, first_layer, second_layer)
    return middle + (gate_prob[:, None] * expert_out).reshape(seq_count, length, model_width)

def reference(hidden_in, out_grad, norm1_gain, in_weight, conv_weight, conv_bias, xproj_weight, dt_weight, dt_bias, decay_log, skip_weight, out_weight, norm2_gain, router_weight, fc1_weight, fc2_weight, expert_ids, keep_mask):
    weights = tuple((weight.astype(jnp.float32) for weight in (norm1_gain, in_weight, conv_weight, conv_bias, xproj_weight, dt_weight, dt_bias, decay_log, skip_weight, out_weight, norm2_gain, router_weight, fc1_weight, fc2_weight)))
    model_width = hidden_in.shape[-1]
    piece_len = SEQ_LEN // N_CTX
    seqs_group = TOK_MB // piece_len
    experts = router_weight.shape[1]
    group_cap = N_CTX * CAP

    def to_tokens(array_in):
        shaped = array_in.reshape(N_DP, N_CTX, MB, seqs_group, piece_len).transpose(2, 0, 3, 1, 4)
        return shaped.reshape(MB * N_DP, seqs_group * SEQ_LEN)
    ids_all = to_tokens(expert_ids[:, 0]).astype(jnp.int32)
    keep_all = to_tokens(keep_mask).astype(jnp.float32)
    acts = hidden_in.astype(jnp.float32).reshape(MB * N_DP, seqs_group, SEQ_LEN, model_width)
    cotans = out_grad.astype(jnp.float32).reshape(MB * N_DP, seqs_group, SEQ_LEN, model_width)

    def one_group(totals, group_in):
        values, cotan, ids_flat, keep_flat = group_in
        token_slot, slot_ids = slot_tables(ids_flat, experts, group_cap)

        def forward_fn(weight_set, acts_in):
            return layer_forward(weight_set, acts_in, ids_flat, keep_flat, token_slot, slot_ids)
        outputs, pullback = jax.vjp(forward_fn, weights, values)
        weight_grads, input_grad = pullback(cotan)
        return (jax.tree.map(jnp.add, totals, weight_grads), (outputs, input_grad))
    zero_set = tuple((jnp.zeros_like(weight) for weight in weights))
    totals, (outputs, input_grads) = lax.scan(one_group, zero_set, (acts, cotans, ids_all, keep_all))
    output = outputs.reshape(hidden_in.shape).astype(jnp.bfloat16)
    input_grad = input_grads.reshape(hidden_in.shape).astype(jnp.bfloat16)
    return (output, input_grad, totals[0], totals[1], totals[2], totals[3], totals[4], totals[5], totals[6], totals[7], totals[8], totals[9], totals[10], totals[11], totals[12], totals[13])
```

```python
from functools import partial
import math

import jax
import jax.numpy as jnp
from jax import lax
from jax.experimental import pallas as pl
from jax.experimental.pallas import tpu as pltpu
from jax.sharding import PartitionSpec as P

EPSILON = 1e-05
HIGHEST = lax.Precision.HIGHEST
SEGMENTS = 8
LANES = 128
VMEM_LIMIT = 56 * 1024 * 1024
LOG2E = math.log2(math.e)
BF16 = jnp.bfloat16
F32 = jnp.float32


def swapped(value, axis):
    return lax.ppermute(value, axis, [(0, 1), (1, 0)])


def passed_along(value, axis, steps):
    count = lax.axis_size(axis)
    leading, last = (max(0, -steps), min(count, count - steps))
    return lax.ppermute(value, axis, [(source, source + steps) for source in range(leading, last)])


def axis_sum(value, axis):
    if lax.axis_size(axis) == 2:
        return value + swapped(value, axis)
    return lax.psum(value, axis)


def entering_pieces(decay, value, axis, backward):
    count = lax.axis_size(axis)
    if count == 2:
        return passed_along(value, axis, -1 if backward else 1)
    mine = lax.axis_index(axis)
    decays = lax.all_gather(decay, axis)
    values = lax.all_gather(value, axis)
    running = jnp.zeros_like(value)
    for position in range(count - 1):
        at = count - 1 - position if backward else position
        longer = values[at] + decays[at] * running
        ahead = at > mine if backward else at < mine
        running = jnp.where(ahead, longer, running)
    return running


def contract_rows(left_side, right_side, precision=None):
    return lax.dot_general(
        left_side,
        right_side,
        (((0,), (0,)), ((), ())),
        precision=precision,
        preferred_element_type=F32,
    )


def contract_cols(left_side, right_side, precision=None):
    return lax.dot_general(
        left_side,
        right_side,
        (((1,), (1,)), ((), ())),
        precision=precision,
        preferred_element_type=F32,
    )


def rms_forward(values, gain_vec):
    inverse = lax.rsqrt(jnp.mean(values * values, axis=-1, keepdims=True) + EPSILON)
    return (values * inverse * gain_vec, inverse)


def rms_backward(values, inverse, gain_vec, grad_out):
    weighted = grad_out * gain_vec
    inner_mean = jnp.mean(values * weighted, axis=-1, keepdims=True)
    grad_values = inverse * weighted - values * inverse * inverse * inverse * inner_mean
    grad_gain = jnp.sum(grad_out * values * inverse, axis=0)
    return (grad_values, grad_gain)


def sublane_rows():
    return lax.broadcasted_iota(jnp.int32, (SEGMENTS, LANES), 0)


def joined_forward(decay, value, row):
    for reach in (1, 2, 4):
        inside = row >= reach
        value = value + jnp.where(inside, decay * pltpu.roll(value, reach, 0), 0.0)
        decay = jnp.where(inside, decay * pltpu.roll(decay, reach, 0), decay)
    return decay, value


def joined_backward(decay, value, row):
    for reach in (1, 2, 4):
        inside = row < SEGMENTS - reach
        value = value + jnp.where(inside, decay * pltpu.roll(value, SEGMENTS - reach, 0), 0.0)
        decay = jnp.where(inside, decay * pltpu.roll(decay, SEGMENTS - reach, 0), decay)
    return decay, value


def ends_kernel(step_ref, input_ref, mix_in_ref, rate_ref, decay_ref, state_ref, last_ref):
    steps, states = step_ref.shape[0], mix_in_ref.shape[1]
    zero = jnp.zeros((SEGMENTS, LANES), F32)

    def body(at, carry):
        held, total = carry
        step = step_ref[at]
        driven = step * input_ref[at]
        held = tuple(
            jnp.exp2(step * rate_ref[n]) * held[n] + mix_in_ref[at, n] * driven
            for n in range(states)
        )
        return held, total + step

    held, total = lax.fori_loop(0, steps, body, ((zero,) * states, zero))
    row = sublane_rows()
    for n in range(states):
        decay, value = joined_forward(jnp.exp2(total * rate_ref[n]), held[n], row)
        decay_ref[n] = decay
        state_ref[n] = value
        last_ref[n : n + 1] = value[SEGMENTS - 1 :]


def states_kernel(
    step_ref, input_ref, mix_in_ref, mix_out_ref, rate_ref, decay_ref, state_ref, enter_ref,
    out_ref, start_ref,
):
    steps, states = step_ref.shape[0], mix_in_ref.shape[1]
    row = sublane_rows()
    held = []
    for n in range(states):
        first = jnp.broadcast_to(enter_ref[n : n + 1], (SEGMENTS, LANES))
        inner = pltpu.roll(state_ref[n], 1, 0) + pltpu.roll(decay_ref[n], 1, 0) * first
        start = jnp.where(row >= 1, inner, first)
        start_ref[n] = start
        held.append(start)

    def body(at, held):
        step = step_ref[at]
        driven = step * input_ref[at]
        held = tuple(
            jnp.exp2(step * rate_ref[n]) * held[n] + mix_in_ref[at, n] * driven
            for n in range(states)
        )
        parts = [mix_out_ref[at, n] * held[n] for n in range(states)]
        while len(parts) > 1:
            parts = [parts[i] + parts[i + 1] for i in range(0, len(parts), 2)]
        out_ref[at] = parts[0]
        return held

    lax.fori_loop(0, steps, body, tuple(held))


def adjoint_ends_kernel(step_ref, mix_out_ref, grad_ref, rate_ref, decay_ref, adjoint_ref, first_ref):
    steps, states = step_ref.shape[0], mix_out_ref.shape[1]
    zero = jnp.zeros((SEGMENTS, LANES), F32)

    def body(back, carry):
        at = steps - 1 - back
        incoming, total = carry
        step = step_ref[at]
        grad = grad_ref[at]
        incoming = tuple(
            jnp.exp2(step * rate_ref[n]) * (mix_out_ref[at, n] * grad + incoming[n])
            for n in range(states)
        )
        return incoming, total + step

    incoming, total = lax.fori_loop(0, steps, body, ((zero,) * states, zero))
    row = sublane_rows()
    for n in range(states):
        decay, value = joined_backward(jnp.exp2(total * rate_ref[n]), incoming[n], row)
        decay_ref[n] = decay
        adjoint_ref[n] = value
        first_ref[n : n + 1] = value[:1]


def adjoint_kernel(
    step_ref, input_ref, mix_in_ref, mix_out_ref, grad_ref, rate_ref, start_ref, decay_ref, adjoint_ref,
    enter_ref,
    in_sum_ref, rate_sum_ref, decay_sum_ref, in_grad_ref, out_grad_ref, states_ref,
):
    steps, states = step_ref.shape[0], mix_in_ref.shape[1]
    row = sublane_rows()
    zero = jnp.zeros((SEGMENTS, LANES), F32)

    @pl.when(pl.program_id(1) == 0)
    def clear():
        in_grad_ref[...] = jnp.zeros_like(in_grad_ref)
        out_grad_ref[...] = jnp.zeros_like(out_grad_ref)

    for n in range(states):
        states_ref[0, n] = start_ref[n]

    def ahead(at, held):
        step = step_ref[at]
        driven = step * input_ref[at]
        held = tuple(
            jnp.exp2(step * rate_ref[n]) * held[n] + mix_in_ref[at, n] * driven
            for n in range(states)
        )
        for n in range(states):
            states_ref[at + 1, n] = held[n]
        return held

    lax.fori_loop(0, steps, ahead, tuple(start_ref[n] for n in range(states)))

    incoming = []
    for n in range(states):
        final = jnp.broadcast_to(enter_ref[n : n + 1], (SEGMENTS, LANES))
        inner = (
            pltpu.roll(adjoint_ref[n], SEGMENTS - 1, 0)
            + pltpu.roll(decay_ref[n], SEGMENTS - 1, 0) * final
        )
        incoming.append(jnp.where(row < SEGMENTS - 1, inner, final))

    def body(back, carry):
        at = steps - 1 - back
        incoming, decay_sums = carry
        step = step_ref[at]
        grad = grad_ref[at]
        driven = step * input_ref[at]
        in_sum, rate_sum = zero, zero
        following, sums = [], []
        for n in range(states):
            rate = rate_ref[n]
            adjoint = mix_out_ref[at, n] * grad + incoming[n]
            onward = jnp.exp2(step * rate) * adjoint
            decay_grad = onward * states_ref[at, n]
            in_sum = in_sum + adjoint * mix_in_ref[at, n]
            rate_sum = rate_sum + decay_grad * rate
            sums.append(decay_sums[n] + decay_grad * step)
            in_grad_ref[at, n] += adjoint * driven
            out_grad_ref[at, n] += grad * states_ref[at + 1, n]
            following.append(onward)
        in_sum_ref[at] = in_sum
        rate_sum_ref[at] = rate_sum
        return tuple(following), tuple(sums)

    _, sums = lax.fori_loop(0, steps, body, (tuple(incoming), (zero,) * states))
    for n in range(states):
        decay_sum_ref[n : n + 1] = jnp.sum(sums[n], axis=0, keepdims=True)


class Scan:
    def __init__(self, steps, chains, states, width):
        self.grid = (chains, width // LANES)
        self.rows_spec = pl.BlockSpec(
            (steps, None, SEGMENTS, LANES), lambda chain, block: (0, chain, 0, block)
        )
        self.mix_spec = pl.BlockSpec(
            (None, steps, states, SEGMENTS, LANES), lambda chain, block: (chain, 0, 0, 0, 0)
        )
        self.rate_spec = pl.BlockSpec((states, SEGMENTS, LANES), lambda chain, block: (0, 0, block))
        self.state_spec = pl.BlockSpec(
            (None, states, SEGMENTS, LANES), lambda chain, block: (chain, 0, 0, block)
        )
        self.edge_spec = pl.BlockSpec((None, states, LANES), lambda chain, block: (chain, 0, block))
        self.rows = jax.ShapeDtypeStruct((steps, chains, SEGMENTS, width), F32)
        self.mix = jax.ShapeDtypeStruct((chains, steps, states, SEGMENTS, LANES), F32)
        self.state = jax.ShapeDtypeStruct((chains, states, SEGMENTS, width), F32)
        self.edge = jax.ShapeDtypeStruct((chains, states, width), F32)
        self.scratch = pltpu.VMEM((steps + 1, states, SEGMENTS, LANES), F32)
        self.work = steps * chains * SEGMENTS * width * states

    def call(self, kernel, ops, args, in_specs, outs, out_specs, scratch=()):
        size = sum(math.prod(a.shape) * a.dtype.itemsize for a in (*args, *outs))
        return pl.pallas_call(
            kernel,
            grid=self.grid,
            in_specs=in_specs,
            out_specs=out_specs,
            out_shape=outs,
            scratch_shapes=list(scratch),
            compiler_params=pltpu.CompilerParams(vmem_limit_bytes=VMEM_LIMIT),
            cost_estimate=pl.CostEstimate(
                flops=ops * self.work, transcendentals=self.work, bytes_accessed=size
            ),
        )(*args)

    def ends(self, step, inputs, mix_in, rate):
        return self.call(
            ends_kernel, 5, (step, inputs, mix_in, rate),
            [self.rows_spec, self.rows_spec, self.mix_spec, self.rate_spec],
            [self.state, self.state, self.edge],
            [self.state_spec, self.state_spec, self.edge_spec],
        )

    def run(self, step, inputs, mix_in, mix_out, rate, decay, state, enter):
        return self.call(
            states_kernel, 7, (step, inputs, mix_in, mix_out, rate, decay, state, enter),
            [self.rows_spec, self.rows_spec, self.mix_spec, self.mix_spec, self.rate_spec,
             self.state_spec, self.state_spec, self.edge_spec],
            [self.rows, self.state],
            [self.rows_spec, self.state_spec],
        )

    def adjoint_ends(self, step, mix_out, grad, rate):
        return self.call(
            adjoint_ends_kernel, 5, (step, mix_out, grad, rate),
            [self.rows_spec, self.mix_spec, self.rows_spec, self.rate_spec],
            [self.state, self.state, self.edge],
            [self.state_spec, self.state_spec, self.edge_spec],
        )

    def adjoint(self, step, inputs, mix_in, mix_out, grad, rate, start, decay, adjoint, enter):
        return self.call(
            adjoint_kernel, 20,
            (step, inputs, mix_in, mix_out, grad, rate, start, decay, adjoint, enter),
            [self.rows_spec, self.rows_spec, self.mix_spec, self.mix_spec, self.rows_spec,
             self.rate_spec, self.state_spec, self.state_spec, self.state_spec, self.edge_spec],
            [self.rows, self.rows, self.edge, self.mix, self.mix],
            [self.rows_spec, self.rows_spec, self.edge_spec, self.mix_spec, self.mix_spec],
            [self.scratch],
        )


def expert_exchange(value, experts):
    count = lax.axis_size("dp")
    groups = None
    if count != experts:
        groups = [
            [base + e for e in range(experts)] for base in range(0, count, experts)
        ]
    return lax.all_to_all(value, "dp", 0, 0, axis_index_groups=groups, tiled=True)


def own_expert(shards):
    experts, rows, columns = shards.shape
    count = lax.axis_size("dp")
    if count != experts:
        shards = jnp.concatenate([shards] * (count // experts), axis=0)
    return lax.all_to_all(shards, "dp", 0, 0, tiled=True).reshape(count * rows, columns)


def halves_sum(value, axis):
    count = lax.axis_size("ctx")
    if count != 2:
        return lax.psum_scatter(value, "ctx", scatter_dimension=axis, tiled=True)
    mine = lax.axis_index("ctx")
    part = value.shape[axis] // 2
    own = lax.dynamic_slice_in_dim(value, mine * part, part, axis)
    other = lax.dynamic_slice_in_dim(value, (1 - mine) * part, part, axis)
    return own + swapped(other.astype(BF16), "ctx").astype(F32)


def halves_joined(value, axis):
    count = lax.axis_size("ctx")
    if count != 2:
        return lax.all_gather(value, "ctx", axis=axis, tiled=True)
    other = swapped(value, "ctx")
    first = lax.axis_index("ctx") == 0
    return jnp.concatenate(
        [jnp.where(first, value, other), jnp.where(first, other, value)], axis=axis
    )


def expert_weight_grad(grad, experts):
    count = lax.axis_size("dp")
    part = halves_sum(grad, 1)
    blocks = part.astype(BF16).reshape(count, part.shape[0] // count, part.shape[1])
    blocks = lax.all_to_all(blocks, "dp", 0, 0, tiled=True)
    if count != experts:
        blocks = jnp.sum(
            blocks.reshape(count // experts, experts, *blocks.shape[1:]).astype(F32), axis=0
        ).astype(BF16)
    return halves_joined(blocks, 2).astype(F32)


def weight_grad(grad, axis):
    count = lax.axis_size("dp")
    blocks = grad.reshape(count, grad.shape[0] // count, grad.shape[1])
    part = halves_sum(blocks, axis)
    part = lax.all_to_all(part.astype(BF16), "dp", 0, 0, tiled=True)
    return halves_joined(jnp.sum(part.astype(F32), axis=0), axis - 1)


def local(
    hidden_in,
    out_grad,
    norm1_gain,
    in_weight,
    conv_weight,
    conv_bias,
    xproj_weight,
    dt_weight,
    dt_bias,
    decay_log,
    skip_weight,
    out_weight,
    norm2_gain,
    router_weight,
    fc1_weight,
    fc2_weight,
    expert_ids,
    keep_mask,
):
    batches, seqs, length, model_width = hidden_in.shape
    chains = batches * seqs
    tokens = chains * length
    steps = length // SEGMENTS
    shard, _, inner = in_weight.shape
    taps = conv_weight.shape[0]
    low_rank = dt_weight.shape[0]
    states = decay_log.shape[0]
    experts = fc1_weight.shape[0]
    dp_count = lax.axis_size("dp")
    tp_count = lax.axis_size("tp")
    capacity = tokens // 4
    part_cap = capacity // tp_count
    slots = experts * part_cap
    tp_index = lax.axis_index("tp")
    scan = Scan(steps, chains, states, inner)

    def to_rows(value):
        value = value.reshape(chains, SEGMENTS, steps, -1).transpose(2, 0, 1, 3)
        return value.reshape(tokens, -1)

    def from_rows(value):
        value = value.reshape(steps, chains, SEGMENTS, -1).transpose(1, 2, 0, 3)
        return value.reshape(batches, seqs, length, -1)

    small = jnp.concatenate(
        [
            norm1_gain[None],
            conv_weight,
            conv_bias[None],
            dt_weight,
            dt_bias[None],
            decay_log,
            skip_weight[None],
            norm2_gain[None],
            router_weight.T,
            xproj_weight.T,
        ],
        axis=0,
    )
    small_all = lax.all_gather(small, "dp", axis=0)
    small_all = small_all.transpose(1, 0, 2).reshape(small.shape[0], dp_count * shard)
    in_flat = lax.all_gather(
        in_weight.reshape(shard, 2 * inner), "dp", axis=0, tiled=True
    )
    bounds = [0]
    for count in (1, taps, 1, low_rank, 1, states, 1, 1, experts, low_rank + 2 * states):
        bounds.append(bounds[-1] + count)
    pieces = [small_all[bounds[i] : bounds[i + 1]] for i in range(len(bounds) - 1)]
    gain_one_f = pieces[0].astype(F32)
    tap_weights = pieces[1].astype(F32)
    conv_shift = pieces[2].astype(F32)
    dt_proj = pieces[3]
    dt_shift = pieces[4].astype(F32)
    decay_rate = -jnp.exp(pieces[5].astype(F32))
    skip_row = pieces[6].astype(F32)
    gain_two_f = pieces[7].astype(F32)
    router_t = pieces[8]
    x_proj_t = pieces[9]
    rate_rows = jnp.broadcast_to((decay_rate * LOG2E)[:, None, :], (states, SEGMENTS, inner))
    out_proj_t = lax.all_gather(out_weight.T, "dp", axis=0, tiled=True)
    first_layer = own_expert(fc1_weight)
    second_layer_t = own_expert(fc2_weight.transpose(0, 2, 1))

    route = to_rows(expert_ids)[:, 0]
    keep = to_rows(keep_mask)[:, 0].astype(F32)
    onehot_int = (route[:, None] == jnp.arange(experts, dtype=jnp.int32)[None, :]).astype(jnp.int32)
    rank = jnp.sum((jnp.cumsum(onehot_int, axis=0) - 1) * onehot_int, axis=1) - tp_index * part_cap
    here = (rank >= 0) & (rank < part_cap)
    token_slot = jnp.where(here, route * part_cap + rank, -1)
    place = (
        token_slot[None, :] == jnp.arange(slots, dtype=jnp.int32)[:, None]
    ).astype(BF16)

    def dispatched(value):
        sent = jnp.dot(place, value, preferred_element_type=F32).astype(BF16)
        got = expert_exchange(sent.reshape(experts, part_cap, -1), experts)
        return got.reshape(slots, -1)

    def returned(value):
        got = expert_exchange(value.reshape(experts, part_cap, -1), experts)
        return axis_sum(contract_rows(place, got.reshape(slots, -1)).astype(BF16), "tp")

    cotan_bf = to_rows(out_grad)
    cotan = cotan_bf.astype(F32)
    slot_cotan = dispatched((cotan * keep[:, None]).astype(BF16))

    values = to_rows(hidden_in).astype(F32)
    normalized_rows, inverse_one = rms_forward(values, gain_one_f)
    normed_bf = normalized_rows.astype(BF16)
    mixed = jnp.dot(normed_bf, in_flat, preferred_element_type=F32)
    x_pre = mixed[:, :inner].astype(BF16).reshape(steps, chains, SEGMENTS, inner)
    z_gate = mixed[:, inner:].reshape(steps, chains, SEGMENTS, inner)
    tail = x_pre[steps - taps + 1 :]
    edge_in = passed_along(tail[:, :, SEGMENTS - 1 :], "ctx", 1)
    halo = jnp.concatenate([edge_in, tail[:, :, : SEGMENTS - 1]], axis=2)
    extended = jnp.concatenate([halo, x_pre], axis=0).astype(F32)
    conv_pre = jnp.broadcast_to(conv_shift[0], x_pre.shape)
    for tap in range(taps):
        conv_pre = conv_pre + tap_weights[tap] * extended[tap : tap + steps]
    xconv_bf = jax.nn.silu(conv_pre).astype(BF16)
    xconv = xconv_bf.astype(F32)
    xconv_rows = xconv_bf.reshape(tokens, inner)
    projected = axis_sum(contract_cols(xconv_rows, x_proj_t), "tp")
    dt_low = projected[:, :low_rank].astype(BF16)

    def mixes(value):
        value = value.reshape(steps, chains, SEGMENTS, states).transpose(1, 0, 3, 2)
        return jnp.broadcast_to(value[..., None], (*value.shape, LANES))

    mix_in = mixes(projected[:, low_rank : low_rank + states])
    mix_out = mixes(projected[:, low_rank + states :])
    dt_pre = (jnp.dot(dt_low, dt_proj, preferred_element_type=F32) + dt_shift).reshape(x_pre.shape)
    step_size = jax.nn.softplus(dt_pre)
    seg_decay, seg_state, last_state = scan.ends(step_size, xconv, mix_in, rate_rows)
    entering = entering_pieces(seg_decay[:, :, SEGMENTS - 1], last_state, "ctx", False)
    scan_out, seg_start = scan.run(
        step_size, xconv, mix_in, mix_out, rate_rows, seg_decay, seg_state, entering
    )
    scanned = scan_out + skip_row[0] * xconv
    z_silu = jax.nn.silu(z_gate)
    gated_bf = (scanned * z_silu).astype(BF16).reshape(tokens, inner)
    middle = values + axis_sum(contract_cols(gated_bf, out_proj_t), "tp")

    normed_two, inverse_two = rms_forward(middle, gain_two_f)
    normed_two_bf = normed_two.astype(BF16)
    own_rows = dispatched(normed_two_bf)
    slot_rows = jnp.concatenate([own_rows, swapped(own_rows, "tp")], axis=0)
    slot_cotan_all = jnp.concatenate([slot_cotan, swapped(slot_cotan, "tp")], axis=0)
    expert_mask = (
        jnp.arange(experts, dtype=jnp.int32) == lax.rem(lax.axis_index("dp"), experts)
    ).astype(F32)[None, :]
    slot_prob = jax.nn.softmax(contract_cols(slot_rows, router_t), axis=-1)
    slot_gate = jnp.sum(slot_prob * expert_mask, axis=1, keepdims=True)
    slot_grad = (slot_gate * slot_cotan_all.astype(F32)).astype(BF16)
    hidden = jnp.dot(slot_rows, first_layer, preferred_element_type=F32)
    active_bf = jax.nn.gelu(hidden, approximate=False).astype(BF16)
    active_grad = jnp.dot(slot_grad, second_layer_t, preferred_element_type=F32)
    hidden_grad_bf = jax.vjp(partial(jax.nn.gelu, approximate=False), hidden)[1](active_grad)[
        0
    ].astype(BF16)

    def own_half(value):
        return value[:slots] + swapped(value[slots:], "tp")

    slot_out = own_half(contract_cols(active_bf, second_layer_t))
    picked_grad = own_half(contract_cols(hidden_grad_bf, first_layer))
    gate_grad = jnp.sum(slot_out * slot_cotan.astype(F32), axis=1, keepdims=True)
    logit_grad = gate_grad * slot_gate[:slots] * (expert_mask - slot_prob[:slots])
    router_grad_t = axis_sum(contract_rows(logit_grad, own_rows.astype(F32), HIGHEST), "tp")
    picked_grad = picked_grad + jnp.dot(
        logit_grad, router_t.astype(F32), precision=HIGHEST, preferred_element_type=F32
    )
    normed_two_grad = returned(picked_grad.astype(BF16)).astype(F32)
    expert_out = returned(slot_out.astype(BF16)).astype(F32)
    first_grad = expert_weight_grad(contract_rows(slot_rows, hidden_grad_bf), experts)
    second_grad = expert_weight_grad(contract_rows(slot_grad, active_bf), experts)
    router_prob = jax.nn.softmax(contract_cols(normed_two_bf, router_t), axis=-1)
    gate_prob = jnp.sum(router_prob * onehot_int.astype(F32), axis=1) * keep
    result = from_rows((middle + gate_prob[:, None] * expert_out).astype(BF16))

    middle_norm_grad, gain_two_grad = rms_backward(middle, inverse_two, gain_two_f, normed_two_grad)
    middle_grad = cotan + middle_norm_grad
    mixer_grad_bf = middle_grad.astype(BF16)
    out_proj_grad = weight_grad(contract_rows(mixer_grad_bf, gated_bf), 1)
    gated_grad = jnp.dot(mixer_grad_bf, out_proj_t, preferred_element_type=F32).reshape(x_pre.shape)
    scan_grad = gated_grad * z_silu
    z_grad = jax.vjp(jax.nn.silu, z_gate)[1](gated_grad * scanned)[0]
    back_decay, back_adjoint, first_adjoint = scan.adjoint_ends(
        step_size, mix_out, scan_grad, rate_rows
    )
    leaving = entering_pieces(back_decay[:, :, 0], first_adjoint, "ctx", True)
    in_sum, rate_sum, decay_sum, in_lanes, out_lanes = scan.adjoint(
        step_size, xconv, mix_in, mix_out, scan_grad, rate_rows, seg_start, back_decay, back_adjoint,
        leaving,
    )
    step_grad = rate_sum * (1.0 / LOG2E) + in_sum * xconv
    decay_log_grad = jnp.sum(decay_sum, axis=0) * decay_rate
    xconv_grad = in_sum * step_size + skip_row[0] * scan_grad

    def unmixed(value):
        return jnp.sum(value, axis=-1).transpose(1, 0, 3, 2).reshape(tokens, states)

    skip_grad = jnp.sum(scan_grad * xconv, axis=(0, 1, 2))
    pre_grad = (step_grad * jax.nn.sigmoid(dt_pre)).reshape(tokens, inner)
    dt_shift_grad = jnp.sum(pre_grad, axis=0)
    dt_proj_grad = contract_rows(dt_low.astype(F32), pre_grad, HIGHEST)
    dt_low_grad = contract_cols(pre_grad, dt_proj.astype(F32), HIGHEST)
    proj_part = jnp.concatenate([dt_low_grad, unmixed(in_lanes), unmixed(out_lanes)], axis=1)
    proj_grad_bf = axis_sum(proj_part, "tp").astype(BF16)
    x_proj_grad_t = contract_rows(proj_grad_bf, xconv_rows)
    xconv_grad = xconv_grad + jnp.dot(
        proj_grad_bf, x_proj_t, preferred_element_type=F32
    ).reshape(x_pre.shape)
    conv_grad = jax.vjp(jax.nn.silu, conv_pre)[1](xconv_grad)[0]
    taps_grad = jnp.stack(
        [
            jnp.sum(conv_grad * extended[tap : tap + steps], axis=(0, 1, 2))
            for tap in range(taps)
        ]
    )
    shift_grad = jnp.sum(conv_grad, axis=(0, 1, 2))
    head = conv_grad[: taps - 1]
    edge_back = passed_along(head[:, :, :1], "ctx", -1)
    later = jnp.concatenate([head[:, :, 1:], edge_back], axis=2)
    reaching = jnp.concatenate([conv_grad, later], axis=0)
    x_pre_grad = tap_weights[taps - 1] * conv_grad
    for tap in range(taps - 1):
        ahead = taps - 1 - tap
        x_pre_grad = x_pre_grad + tap_weights[tap] * reaching[ahead : ahead + steps]
    mixed_grad_bf = jnp.concatenate(
        [
            x_pre_grad.astype(BF16).reshape(tokens, inner),
            z_grad.astype(BF16).reshape(tokens, inner),
        ],
        axis=1,
    )
    in_proj_grad = weight_grad(contract_rows(normed_bf, mixed_grad_bf), 2)
    normed_grad = axis_sum(contract_cols(mixed_grad_bf, in_flat), "tp")
    values_norm_grad, gain_one_grad = rms_backward(values, inverse_one, gain_one_f, normed_grad)
    input_grad = from_rows((middle_grad + values_norm_grad).astype(BF16))

    small_grads = jnp.concatenate(
        [
            gain_one_grad[None],
            taps_grad,
            shift_grad[None],
            dt_proj_grad,
            dt_shift_grad[None],
            decay_log_grad,
            skip_grad[None],
            gain_two_grad[None],
            router_grad_t,
            x_proj_grad_t,
        ],
        axis=0,
    )
    small_grads = small_grads.reshape(small.shape[0], dp_count, shard).transpose(1, 0, 2)
    small_grads = lax.psum_scatter(small_grads, "dp", scatter_dimension=0, tiled=True)[0]
    small_grads = axis_sum(small_grads, "ctx")
    sums = [small_grads[bounds[i] : bounds[i + 1]] for i in range(len(bounds) - 1)]
    return (
        result,
        input_grad,
        sums[0][0],
        in_proj_grad.reshape(shard, 2, inner),
        sums[1],
        sums[2][0],
        sums[9].T,
        sums[3],
        sums[4][0],
        sums[5],
        sums[6][0],
        out_proj_grad.T,
        sums[7][0],
        sums[8].T,
        first_grad,
        second_grad.transpose(0, 2, 1),
    )


def solution(mesh):
    weights = (
        P("dp"),
        P("dp", None, "tp"),
        P(None, ("tp", "dp")),
        P(("tp", "dp")),
        P(("tp", "dp"), None),
        P(None, ("tp", "dp")),
        P(("tp", "dp")),
        P(None, ("tp", "dp")),
        P(("tp", "dp")),
        P("tp", "dp"),
        P("dp"),
        P("dp", None),
        P(None, "dp", "tp"),
        P(None, "tp", "dp"),
    )
    rows = P(None, "dp", "ctx", None)
    return jax.shard_map(
        local,
        mesh=mesh,
        in_specs=(rows, rows, *weights, P(("dp", "ctx"), None), P(("dp", "ctx"))),
        out_specs=(rows, rows, *weights),
        check_vma=False,
    )
```

```python
from functools import partial
import math

import jax
import jax.numpy as jnp
from jax import lax
from jax.experimental import pallas as pl
from jax.experimental.pallas import tpu as pltpu
from jax.sharding import PartitionSpec as P

EPSILON = 1e-05
HIGHEST = lax.Precision.HIGHEST
SEGMENTS = 8
LANES = 128
VMEM_LIMIT = 56 * 1024 * 1024
LOG2E = math.log2(math.e)
BF16 = jnp.bfloat16
F32 = jnp.float32


def swapped(value, axis):
    return lax.ppermute(value, axis, [(0, 1), (1, 0)])


def passed_along(value, axis, steps):
    count = lax.axis_size(axis)
    leading, last = (max(0, -steps), min(count, count - steps))
    return lax.ppermute(value, axis, [(source, source + steps) for source in range(leading, last)])


def axis_sum(value, axis):
    if lax.axis_size(axis) == 2:
        return value + swapped(value, axis)
    return lax.psum(value, axis)


def together(*values):
    return lax.optimization_barrier(values)


def entering_pieces(decay, value, axis, backward):
    count = lax.axis_size(axis)
    if count == 2:
        return passed_along(value, axis, -1 if backward else 1)
    mine = lax.axis_index(axis)
    decays = lax.all_gather(decay, axis)
    values = lax.all_gather(value, axis)
    running = jnp.zeros_like(value)
    for position in range(count - 1):
        at = count - 1 - position if backward else position
        longer = values[at] + decays[at] * running
        ahead = at > mine if backward else at < mine
        running = jnp.where(ahead, longer, running)
    return running


def contract_rows(left_side, right_side, precision=None):
    return lax.dot_general(
        left_side,
        right_side,
        (((0,), (0,)), ((), ())),
        precision=precision,
        preferred_element_type=F32,
    )


def contract_cols(left_side, right_side, precision=None):
    return lax.dot_general(
        left_side,
        right_side,
        (((1,), (1,)), ((), ())),
        precision=precision,
        preferred_element_type=F32,
    )


def rms_forward(values, gain_vec):
    inverse = lax.rsqrt(jnp.mean(values * values, axis=-1, keepdims=True) + EPSILON)
    return (values * inverse * gain_vec, inverse)


def rms_backward(values, inverse, gain_vec, grad_out):
    weighted = grad_out * gain_vec
    inner_mean = jnp.mean(values * weighted, axis=-1, keepdims=True)
    grad_values = inverse * weighted - values * inverse * inverse * inverse * inner_mean
    grad_gain = jnp.sum(grad_out * values * inverse, axis=0)
    return (grad_values, grad_gain)


def sublane_rows():
    return lax.broadcasted_iota(jnp.int32, (SEGMENTS, LANES), 0)


def joined_forward(decay, value, row):
    for reach in (1, 2, 4):
        inside = row >= reach
        value = value + jnp.where(inside, decay * pltpu.roll(value, reach, 0), 0.0)
        decay = jnp.where(inside, decay * pltpu.roll(decay, reach, 0), decay)
    return decay, value


def joined_backward(decay, value, row):
    for reach in (1, 2, 4):
        inside = row < SEGMENTS - reach
        value = value + jnp.where(inside, decay * pltpu.roll(value, SEGMENTS - reach, 0), 0.0)
        decay = jnp.where(inside, decay * pltpu.roll(decay, SEGMENTS - reach, 0), decay)
    return decay, value


def ends_kernel(step_ref, input_ref, mix_in_ref, rate_ref, decay_ref, state_ref, last_ref):
    steps, states = step_ref.shape[0], mix_in_ref.shape[1]
    zero = jnp.zeros((SEGMENTS, LANES), F32)

    def body(at, carry):
        held, total = carry
        step = step_ref[at]
        driven = step * input_ref[at]
        held = tuple(
            jnp.exp2(step * rate_ref[n]) * held[n] + mix_in_ref[at, n] * driven
            for n in range(states)
        )
        return held, total + step

    held, total = lax.fori_loop(0, steps, body, ((zero,) * states, zero))
    row = sublane_rows()
    for n in range(states):
        decay, value = joined_forward(jnp.exp2(total * rate_ref[n]), held[n], row)
        decay_ref[n] = decay
        state_ref[n] = value
        last_ref[n : n + 1] = value[SEGMENTS - 1 :]


def states_kernel(
    step_ref, input_ref, mix_in_ref, mix_out_ref, rate_ref, decay_ref, state_ref, enter_ref,
    out_ref, start_ref,
):
    steps, states = step_ref.shape[0], mix_in_ref.shape[1]
    row = sublane_rows()
    held = []
    for n in range(states):
        first = jnp.broadcast_to(enter_ref[n : n + 1], (SEGMENTS, LANES))
        inner = pltpu.roll(state_ref[n], 1, 0) + pltpu.roll(decay_ref[n], 1, 0) * first
        start = jnp.where(row >= 1, inner, first)
        start_ref[n] = start
        held.append(start)

    def body(at, held):
        step = step_ref[at]
        driven = step * input_ref[at]
        held = tuple(
            jnp.exp2(step * rate_ref[n]) * held[n] + mix_in_ref[at, n] * driven
            for n in range(states)
        )
        parts = [mix_out_ref[at, n] * held[n] for n in range(states)]
        while len(parts) > 1:
            parts = [parts[i] + parts[i + 1] for i in range(0, len(parts), 2)]
        out_ref[at] = parts[0]
        return held

    lax.fori_loop(0, steps, body, tuple(held))


def adjoint_ends_kernel(step_ref, mix_out_ref, grad_ref, rate_ref, decay_ref, adjoint_ref, first_ref):
    steps, states = step_ref.shape[0], mix_out_ref.shape[1]
    zero = jnp.zeros((SEGMENTS, LANES), F32)

    def body(back, carry):
        at = steps - 1 - back
        incoming, total = carry
        step = step_ref[at]
        grad = grad_ref[at]
        incoming = tuple(
            jnp.exp2(step * rate_ref[n]) * (mix_out_ref[at, n] * grad + incoming[n])
            for n in range(states)
        )
        return incoming, total + step

    incoming, total = lax.fori_loop(0, steps, body, ((zero,) * states, zero))
    row = sublane_rows()
    for n in range(states):
        decay, value = joined_backward(jnp.exp2(total * rate_ref[n]), incoming[n], row)
        decay_ref[n] = decay
        adjoint_ref[n] = value
        first_ref[n : n + 1] = value[:1]


def adjoint_kernel(
    step_ref, input_ref, mix_in_ref, mix_out_ref, grad_ref, rate_ref, start_ref, decay_ref, adjoint_ref,
    enter_ref,
    in_sum_ref, rate_sum_ref, decay_sum_ref, in_grad_ref, out_grad_ref, states_ref,
):
    steps, states = step_ref.shape[0], mix_in_ref.shape[1]
    row = sublane_rows()
    zero = jnp.zeros((SEGMENTS, LANES), F32)

    @pl.when(pl.program_id(1) == 0)
    def clear():
        in_grad_ref[...] = jnp.zeros_like(in_grad_ref)
        out_grad_ref[...] = jnp.zeros_like(out_grad_ref)

    for n in range(states):
        states_ref[0, n] = start_ref[n]

    def ahead(at, held):
        step = step_ref[at]
        driven = step * input_ref[at]
        held = tuple(
            jnp.exp2(step * rate_ref[n]) * held[n] + mix_in_ref[at, n] * driven
            for n in range(states)
        )
        for n in range(states):
            states_ref[at + 1, n] = held[n]
        return held

    lax.fori_loop(0, steps, ahead, tuple(start_ref[n] for n in range(states)))

    incoming = []
    for n in range(states):
        final = jnp.broadcast_to(enter_ref[n : n + 1], (SEGMENTS, LANES))
        inner = (
            pltpu.roll(adjoint_ref[n], SEGMENTS - 1, 0)
            + pltpu.roll(decay_ref[n], SEGMENTS - 1, 0) * final
        )
        incoming.append(jnp.where(row < SEGMENTS - 1, inner, final))

    def body(back, carry):
        at = steps - 1 - back
        incoming, decay_sums = carry
        step = step_ref[at]
        grad = grad_ref[at]
        driven = step * input_ref[at]
        in_sum, rate_sum = zero, zero
        following, sums = [], []
        for n in range(states):
            rate = rate_ref[n]
            adjoint = mix_out_ref[at, n] * grad + incoming[n]
            onward = jnp.exp2(step * rate) * adjoint
            decay_grad = onward * states_ref[at, n]
            in_sum = in_sum + adjoint * mix_in_ref[at, n]
            rate_sum = rate_sum + decay_grad * rate
            sums.append(decay_sums[n] + decay_grad * step)
            in_grad_ref[at, n] += adjoint * driven
            out_grad_ref[at, n] += grad * states_ref[at + 1, n]
            following.append(onward)
        in_sum_ref[at] = in_sum
        rate_sum_ref[at] = rate_sum
        return tuple(following), tuple(sums)

    _, sums = lax.fori_loop(0, steps, body, (tuple(incoming), (zero,) * states))
    for n in range(states):
        decay_sum_ref[n : n + 1] = jnp.sum(sums[n], axis=0, keepdims=True)


class Scan:
    def __init__(self, steps, chains, states, width):
        self.grid = (chains, width // LANES)
        self.rows_spec = pl.BlockSpec(
            (steps, None, SEGMENTS, LANES), lambda chain, block: (0, chain, 0, block)
        )
        self.mix_spec = pl.BlockSpec(
            (None, steps, states, SEGMENTS, LANES), lambda chain, block: (chain, 0, 0, 0, 0)
        )
        self.rate_spec = pl.BlockSpec((states, SEGMENTS, LANES), lambda chain, block: (0, 0, block))
        self.state_spec = pl.BlockSpec(
            (None, states, SEGMENTS, LANES), lambda chain, block: (chain, 0, 0, block)
        )
        self.edge_spec = pl.BlockSpec((None, states, LANES), lambda chain, block: (chain, 0, block))
        self.rows = jax.ShapeDtypeStruct((steps, chains, SEGMENTS, width), F32)
        self.mix = jax.ShapeDtypeStruct((chains, steps, states, SEGMENTS, LANES), F32)
        self.state = jax.ShapeDtypeStruct((chains, states, SEGMENTS, width), F32)
        self.edge = jax.ShapeDtypeStruct((chains, states, width), F32)
        self.scratch = pltpu.VMEM((steps + 1, states, SEGMENTS, LANES), F32)
        self.work = steps * chains * SEGMENTS * width * states

    def call(self, kernel, ops, args, in_specs, outs, out_specs, scratch=()):
        size = sum(math.prod(a.shape) * a.dtype.itemsize for a in (*args, *outs))
        return pl.pallas_call(
            kernel,
            grid=self.grid,
            in_specs=in_specs,
            out_specs=out_specs,
            out_shape=outs,
            scratch_shapes=list(scratch),
            compiler_params=pltpu.CompilerParams(vmem_limit_bytes=VMEM_LIMIT),
            cost_estimate=pl.CostEstimate(
                flops=ops * self.work, transcendentals=self.work, bytes_accessed=size
            ),
        )(*args)

    def ends(self, step, inputs, mix_in, rate):
        return self.call(
            ends_kernel, 5, (step, inputs, mix_in, rate),
            [self.rows_spec, self.rows_spec, self.mix_spec, self.rate_spec],
            [self.state, self.state, self.edge],
            [self.state_spec, self.state_spec, self.edge_spec],
        )

    def run(self, step, inputs, mix_in, mix_out, rate, decay, state, enter):
        return self.call(
            states_kernel, 7, (step, inputs, mix_in, mix_out, rate, decay, state, enter),
            [self.rows_spec, self.rows_spec, self.mix_spec, self.mix_spec, self.rate_spec,
             self.state_spec, self.state_spec, self.edge_spec],
            [self.rows, self.state],
            [self.rows_spec, self.state_spec],
        )

    def adjoint_ends(self, step, mix_out, grad, rate):
        return self.call(
            adjoint_ends_kernel, 5, (step, mix_out, grad, rate),
            [self.rows_spec, self.mix_spec, self.rows_spec, self.rate_spec],
            [self.state, self.state, self.edge],
            [self.state_spec, self.state_spec, self.edge_spec],
        )

    def adjoint(self, step, inputs, mix_in, mix_out, grad, rate, start, decay, adjoint, enter):
        return self.call(
            adjoint_kernel, 20,
            (step, inputs, mix_in, mix_out, grad, rate, start, decay, adjoint, enter),
            [self.rows_spec, self.rows_spec, self.mix_spec, self.mix_spec, self.rows_spec,
             self.rate_spec, self.state_spec, self.state_spec, self.state_spec, self.edge_spec],
            [self.rows, self.rows, self.edge, self.mix, self.mix],
            [self.rows_spec, self.rows_spec, self.edge_spec, self.mix_spec, self.mix_spec],
            [self.scratch],
        )


def expert_kernel(
    rows_ref, cotan_ref, router_ref, mask_ref, up_a, up_b, down_a, down_b,
    out_ref, picked_ref, prob_ref, grad_ref, active_a, active_b, hidden_a, hidden_b,
):
    rows = rows_ref[...]
    logits = contract_cols(rows, router_ref[...])
    shifted = jnp.exp(logits - jnp.max(logits, axis=1, keepdims=True))
    prob = shifted / jnp.sum(shifted, axis=1, keepdims=True)
    gate = jnp.sum(prob * mask_ref[...], axis=1, keepdims=True)
    grad = (gate * cotan_ref[...].astype(F32)).astype(BF16)
    prob_ref[...] = prob
    grad_ref[...] = grad
    out, picked = None, None
    for up, down, active_ref, hidden_ref in (
        (up_a, down_a, active_a, hidden_a),
        (up_b, down_b, active_b, hidden_b),
    ):
        hidden = jnp.dot(rows, up[...], preferred_element_type=F32)
        share = 0.5 + 0.5 * lax.erf(hidden * math.sqrt(0.5))
        slope = share + hidden * (jnp.exp(-0.5 * hidden * hidden) * (1.0 / math.sqrt(2 * math.pi)))
        active = (hidden * share).astype(BF16)
        active_ref[...] = active
        hidden_grad = (jnp.dot(grad, down[...], preferred_element_type=F32) * slope).astype(BF16)
        hidden_ref[...] = hidden_grad
        out_part = contract_cols(active, down[...])
        picked_part = contract_cols(hidden_grad, up[...])
        out = out_part if out is None else out + out_part
        picked = picked_part if picked is None else picked + picked_part
    out_ref[...] = out
    picked_ref[...] = picked


def expert_call(rows, cotan, router_t, mask, ups, downs):
    count, width = rows.shape
    hidden = ups[0].shape[1]
    block = math.gcd(count, 512)
    row_spec = pl.BlockSpec((block, width), lambda at: (at, 0))
    hidden_spec = pl.BlockSpec((block, hidden), lambda at: (at, 0))
    prob_spec = pl.BlockSpec((block, router_t.shape[0]), lambda at: (at, 0))

    def whole(array):
        return pl.BlockSpec(array.shape, lambda at: (0, 0), pipeline_mode=pl.Buffered(1))

    fixed = (router_t, mask, *ups, *downs)
    wide, narrow = jax.ShapeDtypeStruct((count, width), F32), jax.ShapeDtypeStruct((count, width), BF16)
    inner = jax.ShapeDtypeStruct((count, hidden), BF16)
    return pl.pallas_call(
        expert_kernel,
        grid=(count // block,),
        in_specs=[row_spec, row_spec, *(whole(array) for array in fixed)],
        out_specs=[row_spec, row_spec, prob_spec, row_spec, *(hidden_spec,) * 4],
        out_shape=[
            wide, wide, jax.ShapeDtypeStruct((count, router_t.shape[0]), F32), narrow, *(inner,) * 4
        ],
        compiler_params=pltpu.CompilerParams(vmem_limit_bytes=VMEM_LIMIT),
        cost_estimate=pl.CostEstimate(
            flops=16 * count * width * hidden,
            transcendentals=4 * count * hidden,
            bytes_accessed=count * (14 * width + 8 * hidden) + 8 * width * hidden,
        ),
    )(rows, cotan, *fixed)


def expert_exchange(value, experts):
    count = lax.axis_size("dp")
    groups = None
    if count != experts:
        groups = [
            [base + e for e in range(experts)] for base in range(0, count, experts)
        ]
    return lax.all_to_all(value, "dp", 0, 0, axis_index_groups=groups, tiled=True)


def by_ctx(first, second):
    lead = lax.axis_index("ctx") == 0
    return jnp.where(lead, first, second), jnp.where(lead, second, first)


def own_expert_blocks(up_shards, down_shards):
    experts, _, hidden = up_shards.shape
    count = lax.axis_size("dp")
    half = hidden // 2
    both = jnp.concatenate([up_shards, down_shards], axis=1)
    if lax.axis_size("ctx") == 2:
        both = by_ctx(both[:, :, :half], both[:, :, half:])[0]
    if count != experts:
        both = jnp.concatenate([both] * (count // experts), axis=0)
    return lax.all_to_all(both, "dp", 0, 0, tiled=True)


def own_expert(both):
    count, rows = both.shape[0], both.shape[1] // 2

    def layers(value):
        return tuple(
            value[:, at : at + rows].reshape(count * rows, value.shape[2]) for at in (0, rows)
        )

    if lax.axis_size("ctx") == 2:
        own, other = layers(both), layers(swapped(both, "ctx"))
    else:
        half = both.shape[2] // 2
        own, other = layers(both[:, :, :half]), layers(both[:, :, half:])
    return (own[0], other[0]), (own[1], other[1])


def gathered(*values):
    bounds = [0]
    for value in values:
        bounds.append(bounds[-1] + value.shape[1])
    got = lax.all_gather(jnp.concatenate(values, axis=1), "dp")
    return [got[:, :, bounds[i] : bounds[i + 1]] for i in range(len(values))]


def half_gathered(*values):
    if lax.axis_size("ctx") == 2:
        half = values[0].shape[0] // 2
        values = [by_ctx(value[:half], value[half:])[0] for value in values]
    return gathered(*values)


def half_joined(*values):
    joined = []
    for value in values:
        if lax.axis_size("ctx") == 2:
            value = jnp.concatenate(by_ctx(value, swapped(value, "ctx")), axis=1)
        joined.append(value.reshape(value.shape[0] * value.shape[1], value.shape[2]))
    return joined


def halves_sent(blocks):
    if lax.axis_size("ctx") != 2:
        return lax.psum_scatter(blocks, "ctx", scatter_dimension=1, tiled=True), None
    half = blocks.shape[1] // 2
    own, other = by_ctx(blocks[:, :half], blocks[:, half:])
    return own, swapped(other.astype(BF16), "ctx")


def halves_added(own, other):
    return (own if other is None else own + other.astype(F32)).astype(BF16)


def halves_joined(value, axis):
    count = lax.axis_size("ctx")
    if count != 2:
        return lax.all_gather(value, "ctx", axis=axis, tiled=True)
    other = swapped(value, "ctx")
    first = lax.axis_index("ctx") == 0
    return jnp.concatenate(
        [jnp.where(first, value, other), jnp.where(first, other, value)], axis=axis
    )


def expert_weight_products(rows, hidden_grads, grads, actives):
    pairs = ((rows, hidden_grads), (grads, actives))
    far = [contract_rows(left, rights[1]) for left, rights in pairs]
    if lax.axis_size("ctx") == 2:
        far = [swapped(value.astype(BF16), "ctx") for value in far]
    return [contract_rows(left, rights[0]) for left, rights in pairs], far


def expert_weight_parts(near, far):
    count = lax.axis_size("dp")
    parts = []
    for own, other in zip(near, far):
        if lax.axis_size("ctx") == 2:
            part = own + other.astype(F32)
        else:
            part = lax.psum_scatter(
                jnp.concatenate([own, other], axis=1), "ctx", scatter_dimension=1, tiled=True
            )
        parts.append(part.astype(BF16).reshape(count, part.shape[0] // count, part.shape[1]))
    return jnp.concatenate(parts, axis=1)


def expert_weight_grads(blocks, experts):
    count = lax.axis_size("dp")
    if count != experts:
        blocks = jnp.sum(
            blocks.reshape(count // experts, experts, *blocks.shape[1:]).astype(F32), axis=0
        ).astype(BF16)
    if lax.axis_size("ctx") == 2:
        first, second = by_ctx(blocks, swapped(blocks, "ctx"))
        joined = jnp.concatenate([first, second], axis=2)
    else:
        joined = lax.all_gather(blocks, "ctx", axis=2, tiled=True)
    shard = joined.shape[1] // 2
    return joined[:, :shard].astype(F32), joined[:, shard:].astype(F32)


def weight_part(grad):
    count = lax.axis_size("dp")
    return halves_sent(grad.reshape(count, grad.shape[0] // count, grad.shape[1]))


def weight_shards(blocks, number):
    sums = jnp.sum(blocks.astype(F32), axis=0)
    rows = sums.shape[0] // number
    joined = halves_joined(sums.reshape(number, rows, sums.shape[1]), 1)
    return [joined[at] for at in range(number)]


def local(
    hidden_in,
    out_grad,
    norm1_gain,
    in_weight,
    conv_weight,
    conv_bias,
    xproj_weight,
    dt_weight,
    dt_bias,
    decay_log,
    skip_weight,
    out_weight,
    norm2_gain,
    router_weight,
    fc1_weight,
    fc2_weight,
    expert_ids,
    keep_mask,
):
    batches, seqs, length, model_width = hidden_in.shape
    chains = batches * seqs
    tokens = chains * length
    steps = length // SEGMENTS
    shard, _, inner = in_weight.shape
    taps = conv_weight.shape[0]
    low_rank = dt_weight.shape[0]
    states = decay_log.shape[0]
    experts = fc1_weight.shape[0]
    dp_count = lax.axis_size("dp")
    tp_count = lax.axis_size("tp")
    capacity = tokens // 4
    part_cap = capacity // tp_count
    slots = experts * part_cap
    tp_index = lax.axis_index("tp")
    scan = Scan(steps, chains, states, inner)

    def to_rows(value):
        value = value.reshape(chains, SEGMENTS, steps, -1).transpose(2, 0, 1, 3)
        return value.reshape(tokens, -1)

    def from_rows(value):
        value = value.reshape(steps, chains, SEGMENTS, -1).transpose(1, 2, 0, 3)
        return value.reshape(batches, seqs, length, -1)

    small = jnp.concatenate(
        [
            norm1_gain[None],
            conv_weight,
            conv_bias[None],
            dt_weight,
            dt_bias[None],
            decay_log,
            skip_weight[None],
            norm2_gain[None],
            router_weight.T,
            xproj_weight.T,
        ],
        axis=0,
    )
    kinds = small.shape[0]
    small_wide = jnp.pad(small.T, ((0, 0), (0, -kinds % LANES)))
    in_x, small_all = gathered(in_weight[:, 0], small_wide)
    in_x = in_x.reshape(dp_count * shard, inner)
    small_all = small_all.reshape(dp_count * shard, -1)[:, :kinds].T
    small_all, out_shard, in_z_shard, up_shards, down_shards = together(
        small_all, out_weight.T, in_weight[:, 1], fc1_weight, fc2_weight.transpose(0, 2, 1)
    )
    bounds = [0]
    for count in (1, taps, 1, low_rank, 1, states, 1, 1, experts, low_rank + 2 * states):
        bounds.append(bounds[-1] + count)
    pieces = [small_all[bounds[i] : bounds[i + 1]] for i in range(len(bounds) - 1)]
    gain_one_f = pieces[0].astype(F32)
    tap_weights = pieces[1].astype(F32)
    conv_shift = pieces[2].astype(F32)
    dt_proj = pieces[3]
    dt_shift = pieces[4].astype(F32)
    decay_rate = -jnp.exp(pieces[5].astype(F32))
    skip_row = pieces[6].astype(F32)
    gain_two_f = pieces[7].astype(F32)
    router_t = pieces[8]
    x_proj_t = pieces[9]
    rate_rows = jnp.broadcast_to((decay_rate * LOG2E)[:, None, :], (states, SEGMENTS, inner))
    later_halves = half_gathered(out_shard, in_z_shard)
    expert_blocks = own_expert_blocks(up_shards, down_shards)

    route = to_rows(expert_ids)[:, 0]
    keep = to_rows(keep_mask)[:, 0].astype(F32)
    onehot_int = (route[:, None] == jnp.arange(experts, dtype=jnp.int32)[None, :]).astype(jnp.int32)
    rank = jnp.sum((jnp.cumsum(onehot_int, axis=0) - 1) * onehot_int, axis=1) - tp_index * part_cap
    here = (rank >= 0) & (rank < part_cap)
    token_slot = jnp.where(here, route * part_cap + rank, -1)
    place = (
        token_slot[None, :] == jnp.arange(slots, dtype=jnp.int32)[:, None]
    ).astype(BF16)

    def slotted(value):
        sent = jnp.dot(place, value, preferred_element_type=F32).astype(BF16)
        return sent.reshape(experts, part_cap, -1)

    def exchanged(value):
        return expert_exchange(value, experts).reshape(slots, -1)

    def landed(value):
        return axis_sum(contract_rows(place, value).astype(BF16), "tp").astype(F32)

    cotan_bf = to_rows(out_grad)
    cotan = cotan_bf.astype(F32)
    sent_cotan = slotted((cotan * keep[:, None]).astype(BF16))

    values = to_rows(hidden_in).astype(F32)
    normalized_rows, inverse_one = rms_forward(values, gain_one_f)
    normed_bf = normalized_rows.astype(BF16)
    x_pre = jnp.dot(normed_bf, in_x, preferred_element_type=F32).astype(BF16)
    x_pre = x_pre.reshape(steps, chains, SEGMENTS, inner)
    tail = x_pre[steps - taps + 1 :]
    edge_in = passed_along(tail[:, :, SEGMENTS - 1 :], "ctx", 1)
    halo = jnp.concatenate([edge_in, tail[:, :, : SEGMENTS - 1]], axis=2)
    extended = jnp.concatenate([halo, x_pre], axis=0).astype(F32)
    conv_pre = jnp.broadcast_to(conv_shift[0], x_pre.shape)
    for tap in range(taps):
        conv_pre = conv_pre + tap_weights[tap] * extended[tap : tap + steps]
    xconv_bf = jax.nn.silu(conv_pre).astype(BF16)
    xconv = xconv_bf.astype(F32)
    xconv_rows = xconv_bf.reshape(tokens, inner)
    projected = axis_sum(contract_cols(xconv_rows, x_proj_t), "tp")
    dt_low = projected[:, :low_rank].astype(BF16)

    def mixes(value):
        value = value.reshape(steps, chains, SEGMENTS, states).transpose(1, 0, 3, 2)
        return jnp.broadcast_to(value[..., None], (*value.shape, LANES))

    mix_in = mixes(projected[:, low_rank : low_rank + states])
    mix_out = mixes(projected[:, low_rank + states :])
    dt_pre = (jnp.dot(dt_low, dt_proj, preferred_element_type=F32) + dt_shift).reshape(x_pre.shape)
    step_size = jax.nn.softplus(dt_pre)
    seg_decay, seg_state, last_state = scan.ends(step_size, xconv, mix_in, rate_rows)
    seg_state, sent_cotan, expert_blocks = together(seg_state, sent_cotan, expert_blocks)
    ups, downs = own_expert(expert_blocks)
    slot_cotan = exchanged(sent_cotan)
    entering = entering_pieces(seg_decay[:, :, SEGMENTS - 1], last_state, "ctx", False)
    entering, later_halves = together(entering, later_halves)
    out_proj_t, in_z = half_joined(*later_halves)
    scan_out, seg_start = scan.run(
        step_size, xconv, mix_in, mix_out, rate_rows, seg_decay, seg_state, entering
    )
    z_gate = jnp.dot(normed_bf, in_z, preferred_element_type=F32).reshape(x_pre.shape)
    scanned = scan_out + skip_row[0] * xconv
    z_silu = jax.nn.silu(z_gate)
    gated_bf = (scanned * z_silu).astype(BF16).reshape(tokens, inner)
    gated_bf, slot_cotan, ups, downs = together(gated_bf, slot_cotan, ups, downs)
    middle = values + axis_sum(contract_cols(gated_bf, out_proj_t), "tp")

    normed_two, inverse_two = rms_forward(middle, gain_two_f)
    normed_two_bf = normed_two.astype(BF16)
    own_rows = exchanged(slotted(normed_two_bf))
    expert_mask = (
        jnp.arange(experts, dtype=jnp.int32) == lax.rem(lax.axis_index("dp"), experts)
    ).astype(F32)[None, :]
    far_rows, far_cotan = swapped(own_rows, "tp"), swapped(slot_cotan, "tp")
    far = expert_call(far_rows, far_cotan, router_t, expert_mask, ups, downs)
    near = expert_call(own_rows, slot_cotan, router_t, expert_mask, ups, downs)
    slot_out = near[0] + swapped(far[0], "tp")
    picked_grad = near[1] + swapped(far[1], "tp")
    slot_prob = near[2]
    slot_gate = jnp.sum(slot_prob * expert_mask, axis=1, keepdims=True)
    gate_grad = jnp.sum(slot_out * slot_cotan.astype(F32), axis=1, keepdims=True)
    logit_grad = gate_grad * slot_gate * (expert_mask - slot_prob)
    router_grad_t = axis_sum(contract_rows(logit_grad, own_rows.astype(F32), HIGHEST), "tp")
    picked_grad = picked_grad + jnp.dot(
        logit_grad, router_t.astype(F32), precision=HIGHEST, preferred_element_type=F32
    )
    got_grad = exchanged(picked_grad.astype(BF16).reshape(experts, part_cap, -1))

    def both_rows(at):
        return jnp.concatenate([far[at], near[at]], axis=0)

    near_parts, far_parts = expert_weight_products(
        jnp.concatenate([far_rows, own_rows], axis=0),
        (both_rows(6), both_rows(7)),
        both_rows(3),
        (both_rows(4), both_rows(5)),
    )
    got_grad, slot_out, near_parts = together(got_grad, slot_out, near_parts)
    normed_two_grad = landed(got_grad)
    got_out = exchanged(slot_out.astype(BF16).reshape(experts, part_cap, -1))
    middle_norm_grad, gain_two_grad = rms_backward(middle, inverse_two, gain_two_f, normed_two_grad)
    middle_grad = cotan + middle_norm_grad
    mixer_grad_bf = middle_grad.astype(BF16)
    out_part = weight_part(contract_rows(mixer_grad_bf, gated_bf))
    gated_grad = jnp.dot(mixer_grad_bf, out_proj_t, preferred_element_type=F32).reshape(x_pre.shape)
    scan_grad = gated_grad * z_silu
    z_grad = jax.vjp(jax.nn.silu, z_gate)[1](gated_grad * scanned)[0]
    z_grad_bf = z_grad.astype(BF16).reshape(tokens, inner)
    in_z_part = weight_part(contract_rows(normed_bf, z_grad_bf))
    back_decay, back_adjoint, first_adjoint = scan.adjoint_ends(
        step_size, mix_out, scan_grad, rate_rows
    )
    first_adjoint, got_out, far_parts = together(first_adjoint, got_out, far_parts)
    weight_blocks = lax.all_to_all(
        expert_weight_parts(near_parts, far_parts), "dp", 0, 0, tiled=True
    )
    leaving = entering_pieces(back_decay[:, :, 0], first_adjoint, "ctx", True)
    in_sum, rate_sum, decay_sum, in_lanes, out_lanes = scan.adjoint(
        step_size, xconv, mix_in, mix_out, scan_grad, rate_rows, seg_start, back_decay, back_adjoint,
        leaving,
    )
    in_sum, weight_blocks, out_part, in_z_part = together(in_sum, weight_blocks, out_part, in_z_part)
    out_blocks = lax.all_to_all(
        jnp.concatenate([halves_added(*out_part), halves_added(*in_z_part)], axis=1),
        "dp", 0, 0, tiled=True,
    )
    router_prob = jax.nn.softmax(contract_cols(normed_two_bf, router_t), axis=-1)
    gate_prob = jnp.sum(router_prob * onehot_int.astype(F32), axis=1) * keep
    result = from_rows((middle + gate_prob[:, None] * landed(got_out)).astype(BF16))
    step_grad = rate_sum * (1.0 / LOG2E) + in_sum * xconv
    decay_log_grad = jnp.sum(decay_sum, axis=0) * decay_rate
    xconv_grad = in_sum * step_size + skip_row[0] * scan_grad

    def unmixed(value):
        return jnp.sum(value, axis=-1).transpose(1, 0, 3, 2).reshape(tokens, states)

    skip_grad = jnp.sum(scan_grad * xconv, axis=(0, 1, 2))
    pre_grad = (step_grad * jax.nn.sigmoid(dt_pre)).reshape(tokens, inner)
    dt_shift_grad = jnp.sum(pre_grad, axis=0)
    dt_proj_grad = contract_rows(dt_low.astype(F32), pre_grad, HIGHEST)
    dt_low_grad = contract_cols(pre_grad, dt_proj.astype(F32), HIGHEST)
    proj_part = jnp.concatenate([dt_low_grad, unmixed(in_lanes), unmixed(out_lanes)], axis=1)
    proj_grad_bf = axis_sum(proj_part, "tp").astype(BF16)
    x_proj_grad_t = contract_rows(proj_grad_bf, xconv_rows)
    xconv_grad = xconv_grad + jnp.dot(
        proj_grad_bf, x_proj_t, preferred_element_type=F32
    ).reshape(x_pre.shape)
    conv_grad = jax.vjp(jax.nn.silu, conv_pre)[1](xconv_grad)[0]
    taps_grad = jnp.stack(
        [
            jnp.sum(conv_grad * extended[tap : tap + steps], axis=(0, 1, 2))
            for tap in range(taps)
        ]
    )
    shift_grad = jnp.sum(conv_grad, axis=(0, 1, 2))
    head = conv_grad[: taps - 1]
    edge_back = passed_along(head[:, :, :1], "ctx", -1)
    later = jnp.concatenate([head[:, :, 1:], edge_back], axis=2)
    reaching = jnp.concatenate([conv_grad, later], axis=0)
    x_pre_grad = tap_weights[taps - 1] * conv_grad
    for tap in range(taps - 1):
        ahead = taps - 1 - tap
        x_pre_grad = x_pre_grad + tap_weights[tap] * reaching[ahead : ahead + steps]
    x_grad_bf = x_pre_grad.astype(BF16).reshape(tokens, inner)
    in_x_part = weight_part(contract_rows(normed_bf, x_grad_bf))
    in_x_part, out_blocks, weight_blocks = together(in_x_part, out_blocks, weight_blocks)
    first_grad, second_grad = expert_weight_grads(weight_blocks, experts)
    in_x_blocks = lax.all_to_all(halves_added(*in_x_part), "dp", 0, 0, tiled=True)
    out_proj_grad, in_z_grad = weight_shards(out_blocks, 2)
    normed_grad = axis_sum(
        contract_cols(x_grad_bf, in_x) + contract_cols(z_grad_bf, in_z), "tp"
    )
    values_norm_grad, gain_one_grad = rms_backward(values, inverse_one, gain_one_f, normed_grad)
    input_grad = from_rows((middle_grad + values_norm_grad).astype(BF16))

    in_x_grad = weight_shards(in_x_blocks, 1)[0]

    def scattered(value):
        value = value.reshape(value.shape[0], dp_count, shard).transpose(1, 0, 2)
        return lax.psum_scatter(value, "dp", scatter_dimension=0, tiled=True)[0]

    small_grads = scattered(
        jnp.concatenate(
            [
                taps_grad,
                shift_grad[None],
                dt_proj_grad,
                dt_shift_grad[None],
                decay_log_grad,
                skip_grad[None],
                gain_two_grad[None],
                router_grad_t,
                x_proj_grad_t,
            ],
            axis=0,
        )
    )
    small_grads, gain_one_part = together(small_grads, scattered(gain_one_grad[None]))
    small_grads = axis_sum(jnp.concatenate([gain_one_part, small_grads], axis=0), "ctx")
    sums = [small_grads[bounds[i] : bounds[i + 1]] for i in range(len(bounds) - 1)]
    return (
        result,
        input_grad,
        sums[0][0],
        jnp.stack([in_x_grad, in_z_grad], axis=1),
        sums[1],
        sums[2][0],
        sums[9].T,
        sums[3],
        sums[4][0],
        sums[5],
        sums[6][0],
        out_proj_grad.T,
        sums[7][0],
        sums[8].T,
        first_grad,
        second_grad.transpose(0, 2, 1),
    )


def solution(mesh):
    weights = (
        P("dp"),
        P("dp", None, "tp"),
        P(None, ("tp", "dp")),
        P(("tp", "dp")),
        P(("tp", "dp"), None),
        P(None, ("tp", "dp")),
        P(("tp", "dp")),
        P(None, ("tp", "dp")),
        P(("tp", "dp")),
        P("tp", "dp"),
        P("dp"),
        P("dp", None),
        P(None, "dp", "tp"),
        P(None, "tp", "dp"),
    )
    rows = P(None, "dp", "ctx", None)
    return jax.shard_map(
        local,
        mesh=mesh,
        in_specs=(rows, rows, *weights, P(("dp", "ctx"), None), P(("dp", "ctx"))),
        out_specs=(rows, rows, *weights),
        check_vma=False,
    )
```

```python
from functools import partial
import math

import jax
import jax.numpy as jnp
from jax import lax
from jax.experimental import pallas as pl
from jax.experimental.pallas import tpu as pltpu
from jax.sharding import PartitionSpec as P

EPSILON = 1e-05
HIGHEST = lax.Precision.HIGHEST
SEGMENTS = 8
LANES = 128
VMEM_LIMIT = 56 * 1024 * 1024
LOG2E = math.log2(math.e)
BF16 = jnp.bfloat16
F32 = jnp.float32


def swapped(value, axis):
    return lax.ppermute(value, axis, [(0, 1), (1, 0)])


def passed_along(value, axis, steps):
    count = lax.axis_size(axis)
    leading, last = (max(0, -steps), min(count, count - steps))
    return lax.ppermute(value, axis, [(source, source + steps) for source in range(leading, last)])


def axis_sum(value, axis):
    if lax.axis_size(axis) == 2:
        return value + swapped(value, axis)
    return lax.psum(value, axis)


def together(*values):
    return lax.optimization_barrier(values)


def entering_pieces(decay, value, axis, backward):
    count = lax.axis_size(axis)
    if count == 2:
        return passed_along(value, axis, -1 if backward else 1)
    mine = lax.axis_index(axis)
    decays = lax.all_gather(decay, axis)
    values = lax.all_gather(value, axis)
    running = jnp.zeros_like(value)
    for position in range(count - 1):
        at = count - 1 - position if backward else position
        longer = values[at] + decays[at] * running
        ahead = at > mine if backward else at < mine
        running = jnp.where(ahead, longer, running)
    return running


def contract_rows(left_side, right_side, precision=None):
    return lax.dot_general(
        left_side,
        right_side,
        (((0,), (0,)), ((), ())),
        precision=precision,
        preferred_element_type=F32,
    )


def contract_cols(left_side, right_side, precision=None):
    return lax.dot_general(
        left_side,
        right_side,
        (((1,), (1,)), ((), ())),
        precision=precision,
        preferred_element_type=F32,
    )


def rms_forward(values, gain_vec):
    inverse = lax.rsqrt(jnp.mean(values * values, axis=-1, keepdims=True) + EPSILON)
    return (values * inverse * gain_vec, inverse)


def rms_backward(values, inverse, gain_vec, grad_out):
    weighted = grad_out * gain_vec
    inner_mean = jnp.mean(values * weighted, axis=-1, keepdims=True)
    grad_values = inverse * weighted - values * inverse * inverse * inverse * inner_mean
    grad_gain = jnp.sum(grad_out * values * inverse, axis=0)
    return (grad_values, grad_gain)


def sublane_rows():
    return lax.broadcasted_iota(jnp.int32, (SEGMENTS, LANES), 0)


def joined_forward(decay, value, row):
    for reach in (1, 2, 4):
        inside = row >= reach
        value = value + jnp.where(inside, decay * pltpu.roll(value, reach, 0), 0.0)
        decay = jnp.where(inside, decay * pltpu.roll(decay, reach, 0), decay)
    return decay, value


def joined_backward(decay, value, row):
    for reach in (1, 2, 4):
        inside = row < SEGMENTS - reach
        value = value + jnp.where(inside, decay * pltpu.roll(value, SEGMENTS - reach, 0), 0.0)
        decay = jnp.where(inside, decay * pltpu.roll(decay, SEGMENTS - reach, 0), decay)
    return decay, value


def ends_kernel(step_ref, input_ref, mix_in_ref, rate_ref, decay_ref, state_ref, last_ref):
    steps, states = step_ref.shape[0], mix_in_ref.shape[1]
    zero = jnp.zeros((SEGMENTS, LANES), F32)

    def body(at, carry):
        held, total = carry
        step = step_ref[at]
        driven = step * input_ref[at]
        held = tuple(
            jnp.exp2(step * rate_ref[n]) * held[n] + mix_in_ref[at, n] * driven
            for n in range(states)
        )
        return held, total + step

    held, total = lax.fori_loop(0, steps, body, ((zero,) * states, zero))
    row = sublane_rows()
    for n in range(states):
        decay, value = joined_forward(jnp.exp2(total * rate_ref[n]), held[n], row)
        decay_ref[n] = decay
        state_ref[n] = value
        last_ref[n : n + 1] = value[SEGMENTS - 1 :]


def states_kernel(
    step_ref, input_ref, mix_in_ref, mix_out_ref, rate_ref, decay_ref, state_ref, enter_ref,
    out_ref, start_ref,
):
    steps, states = step_ref.shape[0], mix_in_ref.shape[1]
    row = sublane_rows()
    held = []
    for n in range(states):
        first = jnp.broadcast_to(enter_ref[n : n + 1], (SEGMENTS, LANES))
        inner = pltpu.roll(state_ref[n], 1, 0) + pltpu.roll(decay_ref[n], 1, 0) * first
        start = jnp.where(row >= 1, inner, first)
        start_ref[n] = start
        held.append(start)

    def body(at, held):
        step = step_ref[at]
        driven = step * input_ref[at]
        held = tuple(
            jnp.exp2(step * rate_ref[n]) * held[n] + mix_in_ref[at, n] * driven
            for n in range(states)
        )
        parts = [mix_out_ref[at, n] * held[n] for n in range(states)]
        while len(parts) > 1:
            parts = [parts[i] + parts[i + 1] for i in range(0, len(parts), 2)]
        out_ref[at] = parts[0]
        return held

    lax.fori_loop(0, steps, body, tuple(held))


def adjoint_ends_kernel(step_ref, mix_out_ref, grad_ref, rate_ref, decay_ref, adjoint_ref, first_ref):
    steps, states = step_ref.shape[0], mix_out_ref.shape[1]
    zero = jnp.zeros((SEGMENTS, LANES), F32)

    def body(back, carry):
        at = steps - 1 - back
        incoming, total = carry
        step = step_ref[at]
        grad = grad_ref[at]
        incoming = tuple(
            jnp.exp2(step * rate_ref[n]) * (mix_out_ref[at, n] * grad + incoming[n])
            for n in range(states)
        )
        return incoming, total + step

    incoming, total = lax.fori_loop(0, steps, body, ((zero,) * states, zero))
    row = sublane_rows()
    for n in range(states):
        decay, value = joined_backward(jnp.exp2(total * rate_ref[n]), incoming[n], row)
        decay_ref[n] = decay
        adjoint_ref[n] = value
        first_ref[n : n + 1] = value[:1]


def adjoint_kernel(
    step_ref, input_ref, mix_in_ref, mix_out_ref, grad_ref, rate_ref, start_ref, decay_ref, adjoint_ref,
    enter_ref,
    in_sum_ref, rate_sum_ref, decay_sum_ref, in_grad_ref, out_grad_ref, states_ref,
):
    steps, states = step_ref.shape[0], mix_in_ref.shape[1]
    row = sublane_rows()
    zero = jnp.zeros((SEGMENTS, LANES), F32)

    @pl.when(pl.program_id(1) == 0)
    def clear():
        in_grad_ref[...] = jnp.zeros_like(in_grad_ref)
        out_grad_ref[...] = jnp.zeros_like(out_grad_ref)

    for n in range(states):
        states_ref[0, n] = start_ref[n]

    def ahead(at, held):
        step = step_ref[at]
        driven = step * input_ref[at]
        held = tuple(
            jnp.exp2(step * rate_ref[n]) * held[n] + mix_in_ref[at, n] * driven
            for n in range(states)
        )
        for n in range(states):
            states_ref[at + 1, n] = held[n]
        return held

    lax.fori_loop(0, steps, ahead, tuple(start_ref[n] for n in range(states)))

    incoming = []
    for n in range(states):
        final = jnp.broadcast_to(enter_ref[n : n + 1], (SEGMENTS, LANES))
        inner = (
            pltpu.roll(adjoint_ref[n], SEGMENTS - 1, 0)
            + pltpu.roll(decay_ref[n], SEGMENTS - 1, 0) * final
        )
        incoming.append(jnp.where(row < SEGMENTS - 1, inner, final))

    def body(back, carry):
        at = steps - 1 - back
        incoming, decay_sums = carry
        step = step_ref[at]
        grad = grad_ref[at]
        driven = step * input_ref[at]
        in_sum, rate_sum = zero, zero
        following, sums = [], []
        for n in range(states):
            rate = rate_ref[n]
            adjoint = mix_out_ref[at, n] * grad + incoming[n]
            onward = jnp.exp2(step * rate) * adjoint
            decay_grad = onward * states_ref[at, n]
            in_sum = in_sum + adjoint * mix_in_ref[at, n]
            rate_sum = rate_sum + decay_grad * rate
            sums.append(decay_sums[n] + decay_grad * step)
            in_grad_ref[at, n] += adjoint * driven
            out_grad_ref[at, n] += grad * states_ref[at + 1, n]
            following.append(onward)
        in_sum_ref[at] = in_sum
        rate_sum_ref[at] = rate_sum
        return tuple(following), tuple(sums)

    _, sums = lax.fori_loop(0, steps, body, (tuple(incoming), (zero,) * states))
    for n in range(states):
        decay_sum_ref[n : n + 1] = jnp.sum(sums[n], axis=0, keepdims=True)


class Scan:
    def __init__(self, steps, chains, states, width):
        self.grid = (chains, width // LANES)
        self.rows_spec = pl.BlockSpec(
            (steps, None, SEGMENTS, LANES), lambda chain, block: (0, chain, 0, block)
        )
        self.mix_spec = pl.BlockSpec(
            (None, steps, states, SEGMENTS, LANES), lambda chain, block: (chain, 0, 0, 0, 0)
        )
        self.rate_spec = pl.BlockSpec((states, SEGMENTS, LANES), lambda chain, block: (0, 0, block))
        self.state_spec = pl.BlockSpec(
            (None, states, SEGMENTS, LANES), lambda chain, block: (chain, 0, 0, block)
        )
        self.edge_spec = pl.BlockSpec((None, states, LANES), lambda chain, block: (chain, 0, block))
        self.rows = jax.ShapeDtypeStruct((steps, chains, SEGMENTS, width), F32)
        self.mix = jax.ShapeDtypeStruct((chains, steps, states, SEGMENTS, LANES), F32)
        self.state = jax.ShapeDtypeStruct((chains, states, SEGMENTS, width), F32)
        self.edge = jax.ShapeDtypeStruct((chains, states, width), F32)
        self.scratch = pltpu.VMEM((steps + 1, states, SEGMENTS, LANES), F32)
        self.work = steps * chains * SEGMENTS * width * states

    def call(self, kernel, ops, args, in_specs, outs, out_specs, scratch=()):
        size = sum(math.prod(a.shape) * a.dtype.itemsize for a in (*args, *outs))
        return pl.pallas_call(
            kernel,
            grid=self.grid,
            in_specs=in_specs,
            out_specs=out_specs,
            out_shape=outs,
            scratch_shapes=list(scratch),
            compiler_params=pltpu.CompilerParams(vmem_limit_bytes=VMEM_LIMIT),
            cost_estimate=pl.CostEstimate(
                flops=ops * self.work, transcendentals=self.work, bytes_accessed=size
            ),
        )(*args)

    def ends(self, step, inputs, mix_in, rate):
        return self.call(
            ends_kernel, 5, (step, inputs, mix_in, rate),
            [self.rows_spec, self.rows_spec, self.mix_spec, self.rate_spec],
            [self.state, self.state, self.edge],
            [self.state_spec, self.state_spec, self.edge_spec],
        )

    def run(self, step, inputs, mix_in, mix_out, rate, decay, state, enter):
        return self.call(
            states_kernel, 7, (step, inputs, mix_in, mix_out, rate, decay, state, enter),
            [self.rows_spec, self.rows_spec, self.mix_spec, self.mix_spec, self.rate_spec,
             self.state_spec, self.state_spec, self.edge_spec],
            [self.rows, self.state],
            [self.rows_spec, self.state_spec],
        )

    def adjoint_ends(self, step, mix_out, grad, rate):
        return self.call(
            adjoint_ends_kernel, 5, (step, mix_out, grad, rate),
            [self.rows_spec, self.mix_spec, self.rows_spec, self.rate_spec],
            [self.state, self.state, self.edge],
            [self.state_spec, self.state_spec, self.edge_spec],
        )

    def adjoint(self, step, inputs, mix_in, mix_out, grad, rate, start, decay, adjoint, enter):
        return self.call(
            adjoint_kernel, 20,
            (step, inputs, mix_in, mix_out, grad, rate, start, decay, adjoint, enter),
            [self.rows_spec, self.rows_spec, self.mix_spec, self.mix_spec, self.rows_spec,
             self.rate_spec, self.state_spec, self.state_spec, self.state_spec, self.edge_spec],
            [self.rows, self.rows, self.edge, self.mix, self.mix],
            [self.rows_spec, self.rows_spec, self.edge_spec, self.mix_spec, self.mix_spec],
            [self.scratch],
        )


def expert_kernel(
    rows_ref, cotan_ref, router_ref, mask_ref, up_a, down_a, up_b, down_b,
    out_ref, picked_ref, prob_ref, grad_ref, active_a, active_b, hidden_a, hidden_b,
):
    rows = rows_ref[...]
    logits = contract_cols(rows, router_ref[...])
    shifted = jnp.exp(logits - jnp.max(logits, axis=1, keepdims=True))
    prob = shifted / jnp.sum(shifted, axis=1, keepdims=True)
    gate = jnp.sum(prob * mask_ref[...], axis=1, keepdims=True)
    grad = (gate * cotan_ref[...].astype(F32)).astype(BF16)
    prob_ref[...] = prob
    grad_ref[...] = grad
    out, picked = None, None
    for up, down, active_ref, hidden_ref in (
        (up_a, down_a, active_a, hidden_a),
        (up_b, down_b, active_b, hidden_b),
    ):
        up, down = (value[...].reshape(-1, value.shape[2]) for value in (up, down))
        hidden = jnp.dot(rows, up, preferred_element_type=F32)
        share = 0.5 + 0.5 * lax.erf(hidden * math.sqrt(0.5))
        slope = share + hidden * (jnp.exp(-0.5 * hidden * hidden) * (1.0 / math.sqrt(2 * math.pi)))
        active = (hidden * share).astype(BF16)
        active_ref[...] = active
        hidden_grad = (jnp.dot(grad, down, preferred_element_type=F32) * slope).astype(BF16)
        hidden_ref[...] = hidden_grad
        out_part = contract_cols(active, down)
        picked_part = contract_cols(hidden_grad, up)
        out = out_part if out is None else out + out_part
        picked = picked_part if picked is None else picked + picked_part
    out_ref[...] = out
    picked_ref[...] = picked


def expert_call(rows, cotan, router_t, mask, halves):
    count, width = rows.shape
    hidden = halves[0].shape[2]
    block = math.gcd(count, 512)
    row_spec = pl.BlockSpec((block, width), lambda at: (at, 0))
    hidden_spec = pl.BlockSpec((block, hidden), lambda at: (at, 0))
    prob_spec = pl.BlockSpec((block, router_t.shape[0]), lambda at: (at, 0))

    def whole(array):
        return pl.BlockSpec(array.shape, lambda at: (0, 0), pipeline_mode=pl.Buffered(1))

    def layer(both, at):
        devices, rows, columns = both.shape
        return pl.BlockSpec(
            (devices, rows // 2, columns), lambda step: (0, at, 0), pipeline_mode=pl.Buffered(1)
        )

    fixed = (router_t, mask, halves[0], halves[0], halves[1], halves[1])
    fixed_specs = [whole(router_t), whole(mask), *(layer(both, at) for both in halves for at in (0, 1))]
    wide, narrow = jax.ShapeDtypeStruct((count, width), F32), jax.ShapeDtypeStruct((count, width), BF16)
    inner = jax.ShapeDtypeStruct((count, hidden), BF16)
    return pl.pallas_call(
        expert_kernel,
        grid=(count // block,),
        in_specs=[row_spec, row_spec, *fixed_specs],
        out_specs=[row_spec, row_spec, prob_spec, row_spec, *(hidden_spec,) * 4],
        out_shape=[
            wide, wide, jax.ShapeDtypeStruct((count, router_t.shape[0]), F32), narrow, *(inner,) * 4
        ],
        compiler_params=pltpu.CompilerParams(vmem_limit_bytes=VMEM_LIMIT),
        cost_estimate=pl.CostEstimate(
            flops=16 * count * width * hidden,
            transcendentals=4 * count * hidden,
            bytes_accessed=count * (14 * width + 8 * hidden) + 8 * width * hidden,
        ),
    )(rows, cotan, *fixed)


def expert_exchange(value, experts):
    count = lax.axis_size("dp")
    groups = None
    if count != experts:
        groups = [
            [base + e for e in range(experts)] for base in range(0, count, experts)
        ]
    return lax.all_to_all(value, "dp", 0, 0, axis_index_groups=groups, tiled=True)


def by_ctx(first, second):
    lead = lax.axis_index("ctx") == 0
    return jnp.where(lead, first, second), jnp.where(lead, second, first)


def own_expert_blocks(up_shards, down_shards):
    experts, _, hidden = up_shards.shape
    count = lax.axis_size("dp")
    half = hidden // 2
    both = jnp.concatenate([up_shards, down_shards], axis=1)
    if lax.axis_size("ctx") == 2:
        both = by_ctx(both[:, :, :half], both[:, :, half:])[0]
    if count != experts:
        both = jnp.concatenate([both] * (count // experts), axis=0)
    return lax.all_to_all(both, "dp", 0, 0, tiled=True)


def own_expert(both):
    if lax.axis_size("ctx") == 2:
        return both, swapped(both, "ctx")
    half = both.shape[2] // 2
    return both[:, :, :half], both[:, :, half:]


def gather_kernel(count, parts, *refs):
    ins, outs = refs[:parts], refs[parts : 2 * parts]
    send_sem, recv_sem, own_sem = refs[2 * parts :]
    places = count // 2
    me = lax.axis_index("dp")
    place, side = lax.div(me, 2), lax.rem(me, 2)
    across = me + 1 - 2 * side
    barrier = pltpu.get_barrier_semaphore()

    def greet(device):
        pl.semaphore_signal(
            barrier, inc=1, device_id={"dp": device}, device_id_type=pl.DeviceIdType.MESH
        )

    greet(across)
    for step in (-1, 1):
        there = place + step

        @pl.when((there >= 0) & (there < places))
        def greet_place(step=step):
            greet(me + 2 * step)

    neighbours = 1 + (place > 0).astype(jnp.int32) + (place < places - 1).astype(jnp.int32)
    pl.semaphore_wait(barrier, neighbours)

    def copy(part, slot, kind, device, own):
        return pltpu.make_async_remote_copy(
            src_ref=ins[part] if own else outs[part].at[slot],
            dst_ref=outs[part].at[slot],
            send_sem=send_sem.at[kind, part, slot],
            recv_sem=recv_sem.at[part, slot],
            device_id={"dp": device},
            device_id_type=pl.DeviceIdType.MESH,
        )

    def passed_on(slot, steps, own, act):
        for step in steps:
            there = place + step

            @pl.when((there >= 0) & (there < places))
            def along(step=step):
                for part in range(parts):
                    act(copy(part, slot, step + 1, me + 2 * step, own))

        for part in range(parts):
            act(copy(part, slot, 1, across, own))

    def start(one):
        one.start()

    def sent(one):
        one.wait_send()

    mine = [
        pltpu.make_async_copy(ins[part], outs[part].at[me], own_sem.at[part])
        for part in range(parts)
    ]
    for one in mine:
        one.start()
    passed_on(me, (-1, 1), True, start)
    for far in range(1, places):
        for step in (-1, 1):
            origin = place - step * far

            @pl.when((origin >= 0) & (origin < places))
            def forward(step=step, far=far):
                slot = me - 2 * step * far
                for part in range(parts):
                    copy(part, slot, 1, across, False).wait_recv()
                passed_on(slot, (step,), False, start)

    for at in range(places):
        for part in range(parts):
            copy(part, 2 * at + 1 - side, 1, across, False).wait_recv()
    for one in mine:
        one.wait()
    passed_on(me, (-1, 1), True, sent)
    for far in range(1, places):
        for step in (-1, 1):
            origin = place - step * far

            @pl.when((origin >= 0) & (origin < places))
            def forwarded(step=step, far=far):
                passed_on(me - 2 * step * far, (step,), False, sent)


def gathered(*values):
    count = lax.axis_size("dp")
    parts = len(values)
    anywhere = pl.BlockSpec(memory_space=pl.ANY)
    size = sum(math.prod(value.shape) * 2 for value in values)
    return pl.pallas_call(
        partial(gather_kernel, count, parts),
        in_specs=[anywhere] * parts,
        out_specs=[anywhere] * parts,
        out_shape=[jax.ShapeDtypeStruct((count, *value.shape), value.dtype) for value in values],
        scratch_shapes=[
            pltpu.SemaphoreType.DMA((3, parts, count)),
            pltpu.SemaphoreType.DMA((parts, count)),
            pltpu.SemaphoreType.DMA((parts,)),
        ],
        compiler_params=pltpu.CompilerParams(collective_id=0, has_side_effects=True),
        cost_estimate=pl.CostEstimate(
            flops=0, transcendentals=0, bytes_accessed=2 * count * size
        ),
    )(*values)


def other_joined(own, first_shard, second_shard):
    count = lax.axis_size("ctx")
    if count == 2:
        return by_ctx(own, swapped(own, "ctx"))
    del first_shard, second_shard
    every = lax.all_gather(own, "ctx")
    return every[0], every[1]


def halves_sent(blocks):
    if lax.axis_size("ctx") != 2:
        return lax.psum_scatter(blocks, "ctx", scatter_dimension=1, tiled=True), None
    half = blocks.shape[1] // 2
    own, other = by_ctx(blocks[:, :half], blocks[:, half:])
    return own, swapped(other.astype(BF16), "ctx")


def halves_added(own, other):
    return (own if other is None else own + other.astype(F32)).astype(BF16)


def halves_joined(value, axis):
    count = lax.axis_size("ctx")
    if count != 2:
        return lax.all_gather(value, "ctx", axis=axis, tiled=True)
    other = swapped(value, "ctx")
    first = lax.axis_index("ctx") == 0
    return jnp.concatenate(
        [jnp.where(first, value, other), jnp.where(first, other, value)], axis=axis
    )


def expert_weight_products(rows, hidden_grads, grads, actives):
    pairs = ((rows, hidden_grads), (grads, actives))
    far = [contract_rows(left, rights[1]) for left, rights in pairs]
    if lax.axis_size("ctx") == 2:
        far = [swapped(value.astype(BF16), "ctx") for value in far]
    return [contract_rows(left, rights[0]) for left, rights in pairs], far


def expert_weight_parts(near, far):
    count = lax.axis_size("dp")
    parts = []
    for own, other in zip(near, far):
        if lax.axis_size("ctx") == 2:
            part = own + other.astype(F32)
        else:
            part = lax.psum_scatter(
                jnp.concatenate([own, other], axis=1), "ctx", scatter_dimension=1, tiled=True
            )
        parts.append(part.astype(BF16).reshape(count, part.shape[0] // count, part.shape[1]))
    return jnp.concatenate(parts, axis=1)


def expert_weight_halves(blocks, experts):
    count = lax.axis_size("dp")
    if count != experts:
        blocks = jnp.sum(
            blocks.reshape(count // experts, experts, *blocks.shape[1:]).astype(F32), axis=0
        ).astype(BF16)
    if lax.axis_size("ctx") == 2:
        return blocks, swapped(blocks, "ctx")
    return blocks, lax.all_gather(blocks, "ctx", axis=2, tiled=True)


def expert_weight_grads(blocks, far_blocks):
    joined = far_blocks
    if lax.axis_size("ctx") == 2:
        joined = jnp.concatenate(by_ctx(blocks, far_blocks), axis=2)
    shard = joined.shape[1] // 2
    return joined[:, :shard].astype(F32), joined[:, shard:].astype(F32)


def weight_part(grad):
    count = lax.axis_size("dp")
    return halves_sent(grad.reshape(count, grad.shape[0] // count, grad.shape[1]))


def weight_shards(blocks, number):
    sums = jnp.sum(blocks.astype(F32), axis=0)
    rows = sums.shape[0] // number
    joined = halves_joined(sums.reshape(number, rows, sums.shape[1]), 1)
    return [joined[at] for at in range(number)]


def local(
    hidden_in,
    out_grad,
    norm1_gain,
    in_weight,
    conv_weight,
    conv_bias,
    xproj_weight,
    dt_weight,
    dt_bias,
    decay_log,
    skip_weight,
    out_weight,
    norm2_gain,
    router_weight,
    fc1_weight,
    fc2_weight,
    expert_ids,
    keep_mask,
):
    batches, seqs, length, model_width = hidden_in.shape
    chains = batches * seqs
    tokens = chains * length
    steps = length // SEGMENTS
    shard, _, inner = in_weight.shape
    taps = conv_weight.shape[0]
    low_rank = dt_weight.shape[0]
    states = decay_log.shape[0]
    experts = fc1_weight.shape[0]
    dp_count = lax.axis_size("dp")
    tp_count = lax.axis_size("tp")
    capacity = tokens // 4
    part_cap = capacity // tp_count
    slots = experts * part_cap
    tp_index = lax.axis_index("tp")
    scan = Scan(steps, chains, states, inner)

    def to_rows(value):
        value = value.reshape(chains, SEGMENTS, steps, -1).transpose(2, 0, 1, 3)
        return value.reshape(tokens, -1)

    def from_rows(value):
        value = value.reshape(steps, chains, SEGMENTS, -1).transpose(1, 2, 0, 3)
        return value.reshape(batches, seqs, length, -1)

    pieces = [
        norm1_gain[None],
        conv_weight,
        conv_bias[None],
        dt_weight,
        dt_bias[None],
        decay_log,
        skip_weight[None],
        norm2_gain[None],
        router_weight.T,
        xproj_weight.T,
    ]
    bounds = [0]
    for piece in pieces:
        bounds.append(bounds[-1] + piece.shape[0])
    small = sum(
        jnp.pad(piece, ((low, bounds[-1] - high), (0, 0)))
        for piece, low, high in zip(pieces, bounds, bounds[1:])
    )
    kinds = small.shape[0]
    small_wide = jnp.pad(small.T, ((0, 0), (0, -kinds % LANES)))
    in_x, small_all, later = gathered(
        in_weight[:, 0], small_wide, by_ctx(out_weight.T, in_weight[:, 1])[0]
    )
    in_x = in_x.reshape(dp_count * shard, inner)
    later = later.reshape(dp_count * shard, inner)
    small_all = small_all.reshape(dp_count * shard, -1)[:, :kinds].T
    small_all, up_shards, down_shards = together(
        small_all, fc1_weight, fc2_weight.transpose(0, 2, 1)
    )
    pieces = [small_all[bounds[i] : bounds[i + 1]] for i in range(len(bounds) - 1)]
    gain_one_f = pieces[0].astype(F32)
    tap_weights = pieces[1].astype(F32)
    conv_shift = pieces[2].astype(F32)
    dt_proj = pieces[3]
    dt_shift = pieces[4].astype(F32)
    decay_rate = -jnp.exp(pieces[5].astype(F32))
    skip_row = pieces[6].astype(F32)
    gain_two_f = pieces[7].astype(F32)
    router_t = pieces[8]
    x_proj_t = pieces[9]
    rate_rows = jnp.broadcast_to((decay_rate * LOG2E)[:, None, :], (states, SEGMENTS, inner))
    expert_blocks = own_expert_blocks(up_shards, down_shards)

    route = to_rows(expert_ids)[:, 0]
    keep = to_rows(keep_mask)[:, 0].astype(F32)
    onehot_int = (route[:, None] == jnp.arange(experts, dtype=jnp.int32)[None, :]).astype(jnp.int32)
    rank = jnp.sum((jnp.cumsum(onehot_int, axis=0) - 1) * onehot_int, axis=1) - tp_index * part_cap
    here = (rank >= 0) & (rank < part_cap)
    token_slot = jnp.where(here, route * part_cap + rank, -1)
    place = (
        token_slot[None, :] == jnp.arange(slots, dtype=jnp.int32)[:, None]
    ).astype(BF16)

    def slotted(value):
        sent = jnp.dot(place, value, preferred_element_type=F32).astype(BF16)
        return sent.reshape(experts, part_cap, -1)

    def exchanged(value):
        return expert_exchange(value, experts).reshape(slots, -1)

    def landed(value):
        return axis_sum(contract_rows(place, value).astype(BF16), "tp").astype(F32)

    cotan_bf = to_rows(out_grad)
    cotan = cotan_bf.astype(F32)
    sent_cotan = slotted((cotan * keep[:, None]).astype(BF16))

    values = to_rows(hidden_in).astype(F32)
    normalized_rows, inverse_one = rms_forward(values, gain_one_f)
    normed_bf = normalized_rows.astype(BF16)
    x_pre = jnp.dot(normed_bf, in_x, preferred_element_type=F32).astype(BF16)
    x_pre = x_pre.reshape(steps, chains, SEGMENTS, inner)
    tail = x_pre[steps - taps + 1 :]
    edge_in = passed_along(tail[:, :, SEGMENTS - 1 :], "ctx", 1)
    edge_in, later = together(edge_in, later)
    out_proj_t, in_z = other_joined(later, out_weight.T, in_weight[:, 1])
    halo = jnp.concatenate([edge_in, tail[:, :, : SEGMENTS - 1]], axis=2)
    extended = jnp.concatenate([halo, x_pre], axis=0).astype(F32)
    conv_pre = jnp.broadcast_to(conv_shift[0], x_pre.shape)
    for tap in range(taps):
        conv_pre = conv_pre + tap_weights[tap] * extended[tap : tap + steps]
    xconv_bf = jax.nn.silu(conv_pre).astype(BF16)
    xconv = xconv_bf.astype(F32)
    xconv_rows = xconv_bf.reshape(tokens, inner)
    projected = axis_sum(contract_cols(xconv_rows, x_proj_t), "tp")
    dt_low = projected[:, :low_rank].astype(BF16)

    def mixes(value):
        value = value.reshape(steps, chains, SEGMENTS, states).transpose(1, 0, 3, 2)
        return jnp.broadcast_to(value[..., None], (*value.shape, LANES))

    mix_in = mixes(projected[:, low_rank : low_rank + states])
    mix_out = mixes(projected[:, low_rank + states :])
    dt_pre = (jnp.dot(dt_low, dt_proj, preferred_element_type=F32) + dt_shift).reshape(x_pre.shape)
    step_size = jax.nn.softplus(dt_pre)
    seg_decay, seg_state, last_state = scan.ends(step_size, xconv, mix_in, rate_rows)
    seg_state, sent_cotan, expert_blocks = together(seg_state, sent_cotan, expert_blocks)
    slot_cotan = exchanged(sent_cotan)
    entering = entering_pieces(seg_decay[:, :, SEGMENTS - 1], last_state, "ctx", False)
    entering, expert_blocks = together(entering, expert_blocks)
    halves = own_expert(expert_blocks)
    scan_out, seg_start = scan.run(
        step_size, xconv, mix_in, mix_out, rate_rows, seg_decay, seg_state, entering
    )
    z_gate = jnp.dot(normed_bf, in_z, preferred_element_type=F32).reshape(x_pre.shape)
    scanned = scan_out + skip_row[0] * xconv
    z_silu = jax.nn.silu(z_gate)
    gated_bf = (scanned * z_silu).astype(BF16).reshape(tokens, inner)
    gated_bf, slot_cotan = together(gated_bf, slot_cotan)
    middle = values + axis_sum(contract_cols(gated_bf, out_proj_t), "tp")

    normed_two, inverse_two = rms_forward(middle, gain_two_f)
    normed_two_bf = normed_two.astype(BF16)
    own_rows = exchanged(slotted(normed_two_bf))
    expert_mask = (
        jnp.arange(experts, dtype=jnp.int32) == lax.rem(lax.axis_index("dp"), experts)
    ).astype(F32)[None, :]
    far_rows, far_cotan = swapped(own_rows, "tp"), swapped(slot_cotan, "tp")
    far = expert_call(far_rows, far_cotan, router_t, expert_mask, halves)
    near = expert_call(own_rows, slot_cotan, router_t, expert_mask, halves)
    slot_out = near[0] + swapped(far[0], "tp")
    picked_grad = near[1] + swapped(far[1], "tp")
    slot_prob = near[2]
    slot_gate = jnp.sum(slot_prob * expert_mask, axis=1, keepdims=True)
    gate_grad = jnp.sum(slot_out * slot_cotan.astype(F32), axis=1, keepdims=True)
    logit_grad = gate_grad * slot_gate * (expert_mask - slot_prob)
    router_grad_t = axis_sum(contract_rows(logit_grad, own_rows.astype(F32), HIGHEST), "tp")
    picked_grad = picked_grad + jnp.dot(
        logit_grad, router_t.astype(F32), precision=HIGHEST, preferred_element_type=F32
    )
    got_grad = exchanged(picked_grad.astype(BF16).reshape(experts, part_cap, -1))

    def both_rows(at):
        return jnp.concatenate([far[at], near[at]], axis=0)

    near_parts, far_parts = expert_weight_products(
        jnp.concatenate([far_rows, own_rows], axis=0),
        (both_rows(6), both_rows(7)),
        both_rows(3),
        (both_rows(4), both_rows(5)),
    )
    got_grad, slot_out, near_parts = together(got_grad, slot_out, near_parts)
    normed_two_grad = landed(got_grad)
    got_out = exchanged(slot_out.astype(BF16).reshape(experts, part_cap, -1))
    middle_norm_grad, gain_two_grad = rms_backward(middle, inverse_two, gain_two_f, normed_two_grad)
    middle_grad = cotan + middle_norm_grad
    mixer_grad_bf = middle_grad.astype(BF16)
    out_grad_product = contract_rows(mixer_grad_bf, gated_bf)
    gated_grad = jnp.dot(mixer_grad_bf, out_proj_t, preferred_element_type=F32).reshape(x_pre.shape)
    scan_grad = gated_grad * z_silu
    z_grad = jax.vjp(jax.nn.silu, z_gate)[1](gated_grad * scanned)[0]
    z_grad_bf = z_grad.astype(BF16).reshape(tokens, inner)
    in_z_product = contract_rows(normed_bf, z_grad_bf)
    back_decay, back_adjoint, first_adjoint = scan.adjoint_ends(
        step_size, mix_out, scan_grad, rate_rows
    )
    first_adjoint, got_out, far_parts = together(first_adjoint, got_out, far_parts)
    weight_blocks = lax.all_to_all(
        expert_weight_parts(near_parts, far_parts), "dp", 0, 0, tiled=True
    )
    leaving = entering_pieces(back_decay[:, :, 0], first_adjoint, "ctx", True)
    leaving, out_grad_product, in_z_product = together(leaving, out_grad_product, in_z_product)
    out_part, in_z_part = weight_part(out_grad_product), weight_part(in_z_product)
    in_sum, rate_sum, decay_sum, in_lanes, out_lanes = scan.adjoint(
        step_size, xconv, mix_in, mix_out, scan_grad, rate_rows, seg_start, back_decay, back_adjoint,
        leaving,
    )
    in_sum, weight_blocks, out_part, in_z_part = together(in_sum, weight_blocks, out_part, in_z_part)
    out_blocks = lax.all_to_all(
        jnp.concatenate([halves_added(*out_part), halves_added(*in_z_part)], axis=1),
        "dp", 0, 0, tiled=True,
    )
    router_prob = jax.nn.softmax(contract_cols(normed_two_bf, router_t), axis=-1)
    gate_prob = jnp.sum(router_prob * onehot_int.astype(F32), axis=1) * keep
    result = from_rows((middle + gate_prob[:, None] * landed(got_out)).astype(BF16))
    step_grad = rate_sum * (1.0 / LOG2E) + in_sum * xconv
    decay_log_grad = jnp.sum(decay_sum, axis=0) * decay_rate
    xconv_grad = in_sum * step_size + skip_row[0] * scan_grad

    def unmixed(value):
        return jnp.sum(value, axis=-1).transpose(1, 0, 3, 2).reshape(tokens, states)

    skip_grad = jnp.sum(scan_grad * xconv, axis=(0, 1, 2))
    pre_grad = (step_grad * jax.nn.sigmoid(dt_pre)).reshape(tokens, inner)
    dt_shift_grad = jnp.sum(pre_grad, axis=0)
    dt_proj_grad = contract_rows(dt_low.astype(F32), pre_grad, HIGHEST)
    dt_low_grad = contract_cols(pre_grad, dt_proj.astype(F32), HIGHEST)
    proj_part = jnp.concatenate([dt_low_grad, unmixed(in_lanes), unmixed(out_lanes)], axis=1)
    proj_grad_bf = axis_sum(proj_part, "tp").astype(BF16)
    x_proj_grad_t = contract_rows(proj_grad_bf, xconv_rows)
    xconv_grad = xconv_grad + jnp.dot(
        proj_grad_bf, x_proj_t, preferred_element_type=F32
    ).reshape(x_pre.shape)
    conv_grad = jax.vjp(jax.nn.silu, conv_pre)[1](xconv_grad)[0]
    taps_grad = jnp.stack(
        [
            jnp.sum(conv_grad * extended[tap : tap + steps], axis=(0, 1, 2))
            for tap in range(taps)
        ]
    )
    shift_grad = jnp.sum(conv_grad, axis=(0, 1, 2))
    head = conv_grad[: taps - 1]
    edge_back = passed_along(head[:, :, :1], "ctx", -1)
    edge_back, weight_blocks = together(edge_back, weight_blocks)
    weight_blocks, far_blocks = expert_weight_halves(weight_blocks, experts)
    later = jnp.concatenate([head[:, :, 1:], edge_back], axis=2)
    reaching = jnp.concatenate([conv_grad, later], axis=0)
    x_pre_grad = tap_weights[taps - 1] * conv_grad
    for tap in range(taps - 1):
        ahead = taps - 1 - tap
        x_pre_grad = x_pre_grad + tap_weights[tap] * reaching[ahead : ahead + steps]
    x_grad_bf = x_pre_grad.astype(BF16).reshape(tokens, inner)
    small_grads = jnp.concatenate(
        [
            taps_grad,
            shift_grad[None],
            dt_proj_grad,
            dt_shift_grad[None],
            decay_log_grad,
            skip_grad[None],
            gain_two_grad[None],
            router_grad_t,
            x_proj_grad_t,
        ],
        axis=0,
    )
    small_grads = small_grads.reshape(-1, dp_count, shard).transpose(1, 0, 2)
    x_grad_bf, out_blocks, small_grads = together(x_grad_bf, out_blocks, small_grads)
    small_grads = lax.psum_scatter(small_grads, "dp", scatter_dimension=0, tiled=True)[0]
    out_proj_grad, in_z_grad = weight_shards(out_blocks, 2)
    normed_grad = axis_sum(
        contract_cols(x_grad_bf, in_x) + contract_cols(z_grad_bf, in_z), "tp"
    )
    values_norm_grad, gain_one_grad = rms_backward(values, inverse_one, gain_one_f, normed_grad)
    input_grad = from_rows((middle_grad + values_norm_grad).astype(BF16))

    in_x_part = contract_rows(normed_bf, x_grad_bf).astype(BF16).reshape(dp_count, shard, inner)
    gain_row = gain_one_grad.reshape(dp_count, 1, shard)
    gain_high = gain_row.astype(BF16)
    gain_low = (gain_row - gain_high.astype(F32)).astype(BF16)
    gain_rows = jnp.concatenate([gain_high, gain_low], axis=1)
    gain_rows = jnp.pad(gain_rows, ((0, 0), (0, 6), (0, inner - shard)))
    in_x_blocks = lax.all_to_all(
        jnp.concatenate([in_x_part, gain_rows], axis=1), "dp", 0, 0, tiled=True
    )
    far_blocks, in_x_blocks = together(far_blocks, in_x_blocks)
    first_grad, second_grad = expert_weight_grads(weight_blocks, far_blocks)
    in_x_sums = axis_sum(jnp.sum(in_x_blocks.astype(F32), axis=0), "ctx")
    in_x_grad = in_x_sums[:shard]
    gain_one_grad = in_x_sums[shard : shard + 1, :shard] + in_x_sums[shard + 1 : shard + 2, :shard]
    small_grads, in_x_blocks = together(small_grads, in_x_blocks)
    small_grads = jnp.concatenate([gain_one_grad, axis_sum(small_grads, "ctx")], axis=0)
    sums = [small_grads[bounds[i] : bounds[i + 1]] for i in range(len(bounds) - 1)]
    return (
        result,
        input_grad,
        sums[0][0],
        jnp.stack([in_x_grad, in_z_grad], axis=1),
        sums[1],
        sums[2][0],
        sums[9].T,
        sums[3],
        sums[4][0],
        sums[5],
        sums[6][0],
        out_proj_grad.T,
        sums[7][0],
        sums[8].T,
        first_grad,
        second_grad.transpose(0, 2, 1),
    )


def solution(mesh):
    weights = (
        P("dp"),
        P("dp", None, "tp"),
        P(None, ("tp", "dp")),
        P(("tp", "dp")),
        P(("tp", "dp"), None),
        P(None, ("tp", "dp")),
        P(("tp", "dp")),
        P(None, ("tp", "dp")),
        P(("tp", "dp")),
        P("tp", "dp"),
        P("dp"),
        P("dp", None),
        P(None, "dp", "tp"),
        P(None, "tp", "dp"),
    )
    rows = P(None, "dp", "ctx", None)
    return jax.shard_map(
        local,
        mesh=mesh,
        in_specs=(rows, rows, *weights, P(("dp", "ctx"), None), P(("dp", "ctx"))),
        out_specs=(rows, rows, *weights),
        check_vma=False,
    )
```

```python
from functools import partial
import math

import jax
import jax.numpy as jnp
from jax import lax
from jax.experimental import pallas as pl
from jax.experimental.pallas import tpu as pltpu
from jax.sharding import PartitionSpec as P

EPSILON = 1e-05
HIGHEST = lax.Precision.HIGHEST
SEGMENTS = 8
LANES = 128
VMEM_LIMIT = 56 * 1024 * 1024
LOG2E = math.log2(math.e)
GROUP_A = 4
GROUP_B = 4
GROUP_C = 8
UNROLL_A = 8
UNROLL_B = 8
UNROLL_C = 8
UNROLL_D = 4
UNROLL_E = 8
BLOCKS = 3
COVER = 1
BF16 = jnp.bfloat16
F32 = jnp.float32


def swapped(value, axis):
    return lax.ppermute(value, axis, [(0, 1), (1, 0)])


def passed_along(value, axis, steps):
    count = lax.axis_size(axis)
    leading, last = (max(0, -steps), min(count, count - steps))
    return lax.ppermute(value, axis, [(source, source + steps) for source in range(leading, last)])


def axis_sum(value, axis):
    if lax.axis_size(axis) == 2:
        return value + swapped(value, axis)
    return lax.psum(value, axis)


def together(*values):
    return lax.optimization_barrier(values)


def entering_pieces(decay, value, axis, backward):
    count = lax.axis_size(axis)
    if count == 2:
        return passed_along(value, axis, -1 if backward else 1)
    mine = lax.axis_index(axis)
    decays = lax.all_gather(decay, axis)
    values = lax.all_gather(value, axis)
    running = jnp.zeros_like(value)
    for position in range(count - 1):
        at = count - 1 - position if backward else position
        longer = values[at] + decays[at] * running
        ahead = at > mine if backward else at < mine
        running = jnp.where(ahead, longer, running)
    return running


def contract_rows(left_side, right_side, precision=None):
    return lax.dot_general(
        left_side,
        right_side,
        (((0,), (0,)), ((), ())),
        precision=precision,
        preferred_element_type=F32,
    )


def contract_cols(left_side, right_side, precision=None):
    return lax.dot_general(
        left_side,
        right_side,
        (((1,), (1,)), ((), ())),
        precision=precision,
        preferred_element_type=F32,
    )


def rms_forward(values, gain_vec):
    inverse = lax.rsqrt(jnp.mean(values * values, axis=-1, keepdims=True) + EPSILON)
    return (values * inverse * gain_vec, inverse)


def rms_backward(values, inverse, gain_vec, grad_out):
    weighted = grad_out * gain_vec
    inner_mean = jnp.mean(values * weighted, axis=-1, keepdims=True)
    grad_values = inverse * weighted - values * inverse * inverse * inverse * inner_mean
    grad_gain = jnp.sum(grad_out * values * inverse, axis=0)
    return (grad_values, grad_gain)


def zeros_of(ref):
    return jnp.zeros(ref.shape[1:], F32)


def sublane_rows(lanes):
    return lax.broadcasted_iota(jnp.int32, (SEGMENTS, lanes), 0)


def widened(value, lanes):
    return jnp.concatenate([value] * (lanes // LANES), axis=1) if lanes > LANES else value


def narrowed(value):
    parts = [value[:, at : at + LANES] for at in range(0, value.shape[1], LANES)]
    return sum(parts[1:], parts[0])


def groups_of(states, size):
    size = math.gcd(states, size)
    return [range(first, first + size) for first in range(0, states, size)]


def joined_forward(decay, value, row):
    for reach in (1, 2, 4):
        inside = row >= reach
        value = value + jnp.where(inside, decay * pltpu.roll(value, reach, 0), 0.0)
        decay = jnp.where(inside, decay * pltpu.roll(decay, reach, 0), decay)
    return decay, value


def joined_backward(decay, value, row):
    for reach in (1, 2, 4):
        inside = row < SEGMENTS - reach
        value = value + jnp.where(inside, decay * pltpu.roll(value, SEGMENTS - reach, 0), 0.0)
        decay = jnp.where(inside, decay * pltpu.roll(decay, SEGMENTS - reach, 0), decay)
    return decay, value


def ends_kernel(step_ref, input_ref, mix_in_ref, rate_ref, decay_ref, state_ref, last_ref):
    steps, states, lanes = step_ref.shape[0], mix_in_ref.shape[1], step_ref.shape[2]
    zero = zeros_of(step_ref)
    row = sublane_rows(lanes)
    total = lax.fori_loop(0, steps, lambda at, total: total + step_ref[at], zero, unroll=UNROLL_E)
    for members in groups_of(states, GROUP_A):
        rates = [rate_ref[n] for n in members]

        def body(at, held):
            step = step_ref[at]
            driven = step * input_ref[at]
            return tuple(
                jnp.exp2(step * rate) * before + widened(mix_in_ref[at, n], lanes) * driven
                for n, rate, before in zip(members, rates, held)
            )

        held = lax.fori_loop(0, steps, body, (zero,) * len(members), unroll=UNROLL_A)
        for n, rate, end in zip(members, rates, held):
            decay, value = joined_forward(jnp.exp2(total * rate), end, row)
            decay_ref[n] = decay
            state_ref[n] = value
            last_ref[n : n + 1] = value[SEGMENTS - 1 :]


def states_kernel(
    step_ref, input_ref, mix_in_ref, mix_out_ref, rate_ref, decay_ref, state_ref, enter_ref,
    out_ref, start_ref,
):
    steps, states, lanes = step_ref.shape[0], mix_in_ref.shape[1], step_ref.shape[2]
    row = sublane_rows(lanes)
    for members in groups_of(states, GROUP_B):
        rates = [rate_ref[n] for n in members]
        held = []
        for n in members:
            first = jnp.broadcast_to(enter_ref[n : n + 1], (SEGMENTS, lanes))
            inner = pltpu.roll(state_ref[n], 1, 0) + pltpu.roll(decay_ref[n], 1, 0) * first
            start = jnp.where(row >= 1, inner, first)
            start_ref[n] = start
            held.append(start)

        def body(at, held):
            step = step_ref[at]
            driven = step * input_ref[at]
            held = tuple(
                jnp.exp2(step * rate) * before + widened(mix_in_ref[at, n], lanes) * driven
                for n, rate, before in zip(members, rates, held)
            )
            parts = [widened(mix_out_ref[at, n], lanes) * now for n, now in zip(members, held)]
            if members[0]:
                parts.append(out_ref[at])
            while len(parts) > 1:
                parts = [sum(parts[i + 1 : i + 2], parts[i]) for i in range(0, len(parts), 2)]
            out_ref[at] = parts[0]
            return held

        lax.fori_loop(0, steps, body, tuple(held), unroll=UNROLL_B)


def adjoint_ends_kernel(step_ref, mix_out_ref, grad_ref, rate_ref, decay_ref, adjoint_ref, first_ref):
    steps, states, lanes = step_ref.shape[0], mix_out_ref.shape[1], step_ref.shape[2]
    zero = zeros_of(step_ref)
    row = sublane_rows(lanes)
    total = lax.fori_loop(0, steps, lambda at, total: total + step_ref[at], zero, unroll=UNROLL_E)
    for members in groups_of(states, GROUP_A):
        rates = [rate_ref[n] for n in members]

        def body(back, incoming):
            at = steps - 1 - back
            step = step_ref[at]
            grad = grad_ref[at]
            return tuple(
                jnp.exp2(step * rate) * (widened(mix_out_ref[at, n], lanes) * grad + after)
                for n, rate, after in zip(members, rates, incoming)
            )

        incoming = lax.fori_loop(0, steps, body, (zero,) * len(members), unroll=UNROLL_A)
        for n, rate, end in zip(members, rates, incoming):
            decay, value = joined_backward(jnp.exp2(total * rate), end, row)
            decay_ref[n] = decay
            adjoint_ref[n] = value
            first_ref[n : n + 1] = value[:1]


def adjoint_kernel(
    step_ref, input_ref, mix_in_ref, mix_out_ref, grad_ref, rate_ref, start_ref, decay_ref, adjoint_ref,
    enter_ref, skip_ref,
    pre_ref, conv_ref, decay_sum_ref, sums_ref, mix_ref, states_ref, decays_ref, in_grad_ref, out_grad_ref,
):
    steps, states, lanes = step_ref.shape[0], mix_in_ref.shape[1], step_ref.shape[2]
    row = sublane_rows(lanes)
    zero = zeros_of(step_ref)

    @pl.when(pl.program_id(1) == 0)
    def clear():
        in_grad_ref[...] = jnp.zeros_like(in_grad_ref)
        out_grad_ref[...] = jnp.zeros_like(out_grad_ref)

    for members in groups_of(states, GROUP_C):
        first, group = members[0], len(members)
        rates = [rate_ref[n] for n in members]

        def ahead(at, held):
            step = step_ref[at]
            driven = step * input_ref[at]
            grad = grad_ref[at]
            after = []
            for i, n in enumerate(members):
                states_ref[at, i] = held[i]
                decay = jnp.exp2(step * rates[i])
                decays_ref[at, i] = decay
                now = decay * held[i] + widened(mix_in_ref[at, n], lanes) * driven
                out_grad_ref[at, n] += narrowed(grad * now)
                after.append(now)
            return tuple(after)

        lax.fori_loop(0, steps, ahead, tuple(start_ref[n] for n in members), unroll=UNROLL_C)

        incoming = []
        for n in members:
            final = jnp.broadcast_to(enter_ref[n : n + 1], (SEGMENTS, lanes))
            inner = (
                pltpu.roll(adjoint_ref[n], SEGMENTS - 1, 0)
                + pltpu.roll(decay_ref[n], SEGMENTS - 1, 0) * final
            )
            incoming.append(jnp.where(row < SEGMENTS - 1, inner, final))

        def body(back, carry):
            at = steps - 1 - back
            incoming, decay_sums = carry
            step = step_ref[at]
            grad = grad_ref[at]
            driven = step * input_ref[at]
            in_sum = conv_ref[at] if first else zero
            rate_sum = pre_ref[at] if first else zero
            following, sums = [], []
            for i, n in enumerate(members):
                adjoint = widened(mix_out_ref[at, n], lanes) * grad + incoming[i]
                onward = decays_ref[at, i] * adjoint
                decay_grad = onward * states_ref[at, i]
                in_sum = in_sum + adjoint * widened(mix_in_ref[at, n], lanes)
                rate_sum = rate_sum + decay_grad * rates[i]
                sums.append(decay_sums[i] + decay_grad * step)
                in_grad_ref[at, n] += narrowed(adjoint * driven)
                following.append(onward)
            conv_ref[at] = in_sum
            pre_ref[at] = rate_sum
            return tuple(following), tuple(sums)

        _, sums = lax.fori_loop(
            0, steps, body, (tuple(incoming), (zero,) * group), unroll=UNROLL_D
        )
        for i, n in enumerate(members):
            decay_sum_ref[n : n + 1] = jnp.sum(sums[i], axis=0, keepdims=True)

    skip = skip_ref[...]

    def close(at, carry):
        pre_sum, skip_sum = carry
        step, inputs, grad, in_sum = step_ref[at], input_ref[at], grad_ref[at], conv_ref[at]
        step_grad = pre_ref[at] * (1.0 / LOG2E) + in_sum * inputs
        pre = step_grad * (1.0 - jnp.exp2(step * -LOG2E))
        pre_ref[at] = pre
        conv_ref[at] = in_sum * step + skip * grad
        return pre_sum + pre, skip_sum + grad * inputs

    pre_sum, skip_sum = lax.fori_loop(0, steps, close, (zero, zero), unroll=UNROLL_E)
    sums_ref[0:1] = jnp.sum(pre_sum, axis=0, keepdims=True)
    sums_ref[1:2] = jnp.sum(skip_sum, axis=0, keepdims=True)
    sums_ref[2:] = jnp.zeros((SEGMENTS - 2, lanes), F32)

    @pl.when(pl.program_id(1) == pl.num_programs(1) - 1)
    def across_lanes():
        lane = lax.broadcasted_iota(jnp.int32, (SEGMENTS, LANES), 1)

        def one(at, carry):
            total = jnp.zeros((SEGMENTS, LANES), F32)
            for n in range(states):
                for base, ref in ((0, in_grad_ref), (states, out_grad_ref)):
                    value = jnp.sum(ref[at, n], axis=1, keepdims=True)
                    total = jnp.where(lane == base + n, value, total)
            mix_ref[at] = total
            return carry

        lax.fori_loop(0, steps, one, 0, unroll=UNROLL_E)


class Scan:
    def __init__(self, steps, chains, states, width):
        lanes = LANES * math.gcd(width // LANES, BLOCKS)
        self.grid = (chains, width // lanes)
        self.rows_spec = pl.BlockSpec(
            (steps, None, SEGMENTS, lanes), lambda chain, block: (0, chain, 0, block)
        )
        self.mix_spec = pl.BlockSpec(
            (None, steps, states, SEGMENTS, LANES), lambda chain, block: (chain, 0, 0, 0, 0)
        )
        self.rate_spec = pl.BlockSpec((states, SEGMENTS, lanes), lambda chain, block: (0, 0, block))
        self.state_spec = pl.BlockSpec(
            (None, states, SEGMENTS, lanes), lambda chain, block: (chain, 0, 0, block)
        )
        self.edge_spec = pl.BlockSpec((None, states, lanes), lambda chain, block: (chain, 0, block))
        self.rows = jax.ShapeDtypeStruct((steps, chains, SEGMENTS, width), F32)
        self.mix = jax.ShapeDtypeStruct((chains, steps, states, SEGMENTS, LANES), F32)
        self.state = jax.ShapeDtypeStruct((chains, states, SEGMENTS, width), F32)
        self.edge = jax.ShapeDtypeStruct((chains, states, width), F32)
        self.sums = jax.ShapeDtypeStruct((chains, SEGMENTS, width), F32)
        self.sums_spec = pl.BlockSpec((None, SEGMENTS, lanes), lambda chain, block: (chain, 0, block))
        self.lane_sums = jax.ShapeDtypeStruct((steps, chains, SEGMENTS, LANES), F32)
        self.lane_spec = pl.BlockSpec(
            (steps, None, SEGMENTS, LANES), lambda chain, block: (0, chain, 0, 0)
        )
        self.skip_spec = pl.BlockSpec((1, lanes), lambda chain, block: (0, block))
        self.scratch = [
            pltpu.VMEM((steps, math.gcd(states, GROUP_C), SEGMENTS, lanes), F32),
            pltpu.VMEM((steps, math.gcd(states, GROUP_C), SEGMENTS, lanes), F32),
            pltpu.VMEM((steps, states, SEGMENTS, LANES), F32),
            pltpu.VMEM((steps, states, SEGMENTS, LANES), F32),
        ]
        self.work = steps * chains * SEGMENTS * width * states

    def call(self, kernel, ops, args, in_specs, outs, out_specs, scratch=()):
        size = sum(math.prod(a.shape) * a.dtype.itemsize for a in (*args, *outs))
        return pl.pallas_call(
            kernel,
            grid=self.grid,
            in_specs=in_specs,
            out_specs=out_specs,
            out_shape=outs,
            scratch_shapes=list(scratch),
            compiler_params=pltpu.CompilerParams(vmem_limit_bytes=VMEM_LIMIT),
            cost_estimate=pl.CostEstimate(
                flops=ops * self.work, transcendentals=self.work, bytes_accessed=size // COVER
            ),
        )(*args)

    def ends(self, step, inputs, mix_in, rate):
        return self.call(
            ends_kernel, 5, (step, inputs, mix_in, rate),
            [self.rows_spec, self.rows_spec, self.mix_spec, self.rate_spec],
            [self.state, self.state, self.edge],
            [self.state_spec, self.state_spec, self.edge_spec],
        )

    def run(self, step, inputs, mix_in, mix_out, rate, decay, state, enter):
        return self.call(
            states_kernel, 7, (step, inputs, mix_in, mix_out, rate, decay, state, enter),
            [self.rows_spec, self.rows_spec, self.mix_spec, self.mix_spec, self.rate_spec,
             self.state_spec, self.state_spec, self.edge_spec],
            [self.rows, self.state],
            [self.rows_spec, self.state_spec],
        )

    def adjoint_ends(self, step, mix_out, grad, rate):
        return self.call(
            adjoint_ends_kernel, 5, (step, mix_out, grad, rate),
            [self.rows_spec, self.mix_spec, self.rows_spec, self.rate_spec],
            [self.state, self.state, self.edge],
            [self.state_spec, self.state_spec, self.edge_spec],
        )

    def adjoint(self, step, inputs, mix_in, mix_out, grad, rate, start, decay, adjoint, enter, skip):
        return self.call(
            adjoint_kernel, 20,
            (step, inputs, mix_in, mix_out, grad, rate, start, decay, adjoint, enter, skip),
            [self.rows_spec, self.rows_spec, self.mix_spec, self.mix_spec, self.rows_spec,
             self.rate_spec, self.state_spec, self.state_spec, self.state_spec, self.edge_spec,
             self.skip_spec],
            [self.rows, self.rows, self.edge, self.sums, self.lane_sums],
            [self.rows_spec, self.rows_spec, self.edge_spec, self.sums_spec, self.lane_spec],
            self.scratch,
        )


def conv_back_kernel(
    proj_ref, weight_ref, grad_ref, input_ref, taps_ref, shift_ref,
    out_ref, sums_ref, head_ref, tail_ref, product_ref, conv_ref,
):
    steps, rows, lanes = grad_ref.shape
    count = taps_ref.shape[0]
    reach = count - 1
    taps = [taps_ref[at : at + 1] for at in range(count)]
    shift = shift_ref[...]
    product_ref[...] = jnp.dot(
        proj_ref[...], weight_ref[...], preferred_element_type=F32
    ).reshape(steps, rows, lanes)

    def slopes(at, sums):
        inputs = [input_ref[at + tap].astype(F32) for tap in range(count)]
        pre = shift + sum(tap * value for tap, value in zip(taps, inputs))
        share = 1.0 / (1.0 + jnp.exp(-pre))
        conv = (grad_ref[at] + product_ref[at]) * (share * (1.0 + pre * (1.0 - share)))
        conv_ref[at] = conv
        return (*(total + conv * value for total, value in zip(sums, inputs)), sums[-1] + conv)

    zero = jnp.zeros((rows, lanes), F32)
    sums = lax.fori_loop(0, steps, slopes, (zero,) * (count + 1), unroll=2)
    for at, total in enumerate(sums):
        sums_ref[at : at + 1] = jnp.sum(total, axis=0, keepdims=True)
    sums_ref[count + 1 :] = jnp.zeros((sums_ref.shape[0] - count - 1, lanes), F32)
    row = sublane_rows(lanes)
    for at in range(reach):
        head_ref[at] = conv_ref[at]
        for low in range(0, rows, SEGMENTS):
            rolled = pltpu.roll(conv_ref[at, low : low + SEGMENTS], SEGMENTS - 1, 0)
            conv_ref[steps + at, low : low + SEGMENTS] = jnp.where(
                row < SEGMENTS - 1, rolled, 0.0
            )

    def back(at):
        return sum(taps[tap] * conv_ref[at + reach - tap] for tap in range(count))

    def store(at, carry):
        out_ref[at] = back(at).astype(BF16)
        return carry

    lax.fori_loop(0, steps, store, 0, unroll=2)
    for at in range(reach):
        tail_ref[at] = back(steps - reach + at)


def conv_back(proj, weight, grad, inputs, taps, shift):
    steps, rows, width = grad.shape
    reach = taps.shape[0] - 1
    lanes = LANES * math.gcd(width // LANES, BLOCKS)

    def block(count, dtype=F32):
        spec = pl.BlockSpec((count, rows, lanes), lambda at: (0, 0, at))
        return spec, jax.ShapeDtypeStruct((count, rows, width), dtype)

    def columns(count):
        return pl.BlockSpec((count, lanes), lambda at: (0, at))

    outs = [
        block(steps, BF16),
        (columns(SEGMENTS), jax.ShapeDtypeStruct((SEGMENTS, width), F32)),
        block(reach),
        block(reach),
    ]
    return pl.pallas_call(
        conv_back_kernel,
        grid=(width // lanes,),
        in_specs=[
            pl.BlockSpec(proj.shape, lambda at: (0, 0)),
            columns(weight.shape[0]),
            block(steps)[0],
            block(steps + reach)[0],
            columns(reach + 1),
            columns(1),
        ],
        out_specs=[spec for spec, _ in outs],
        out_shape=[shape for _, shape in outs],
        scratch_shapes=[
            pltpu.VMEM((steps, rows, lanes), F32),
            pltpu.VMEM((steps + reach, rows, lanes), F32),
        ],
        compiler_params=pltpu.CompilerParams(vmem_limit_bytes=VMEM_LIMIT),
        cost_estimate=pl.CostEstimate(flops=1, transcendentals=0, bytes_accessed=1),
    )(proj, weight, grad, inputs, taps, shift)


def expert_kernel(
    rows_ref, cotan_ref, router_ref, mask_ref, up_a, down_a, up_b, down_b,
    out_ref, picked_ref, prob_ref, grad_ref, active_a, active_b, hidden_a, hidden_b,
):
    rows = rows_ref[...]
    logits = contract_cols(rows, router_ref[...])
    shifted = jnp.exp(logits - jnp.max(logits, axis=1, keepdims=True))
    prob = shifted / jnp.sum(shifted, axis=1, keepdims=True)
    gate = jnp.sum(prob * mask_ref[...], axis=1, keepdims=True)
    grad = (gate * cotan_ref[...].astype(F32)).astype(BF16)
    prob_ref[...] = prob
    grad_ref[...] = grad
    out, picked = None, None
    for up, down, active_ref, hidden_ref in (
        (up_a, down_a, active_a, hidden_a),
        (up_b, down_b, active_b, hidden_b),
    ):
        up, down = (value[...].reshape(-1, value.shape[2]) for value in (up, down))
        hidden = jnp.dot(rows, up, preferred_element_type=F32)
        share = 0.5 + 0.5 * lax.erf(hidden * math.sqrt(0.5))
        slope = share + hidden * (jnp.exp(-0.5 * hidden * hidden) * (1.0 / math.sqrt(2 * math.pi)))
        active = (hidden * share).astype(BF16)
        active_ref[...] = active
        hidden_grad = (jnp.dot(grad, down, preferred_element_type=F32) * slope).astype(BF16)
        hidden_ref[...] = hidden_grad
        out_part = contract_cols(active, down)
        picked_part = contract_cols(hidden_grad, up)
        out = out_part if out is None else out + out_part
        picked = picked_part if picked is None else picked + picked_part
    out_ref[...] = out
    picked_ref[...] = picked


def expert_call(rows, cotan, router_t, mask, blocks, far_up, far_down):
    count, width = rows.shape
    shard, hidden = far_up.shape[1:]
    block = math.gcd(count, 512)
    row_spec = pl.BlockSpec((block, width), lambda at: (at, 0))
    hidden_spec = pl.BlockSpec((block, hidden), lambda at: (at, 0))
    prob_spec = pl.BlockSpec((block, router_t.shape[0]), lambda at: (at, 0))

    def whole(array):
        return pl.BlockSpec(array.shape, lambda at: (0, 0), pipeline_mode=pl.Buffered(1))

    def layer(array, at):
        return pl.BlockSpec(
            (array.shape[0], shard, hidden), lambda step: (0, at, 0), pipeline_mode=pl.Buffered(1)
        )

    fixed = (router_t, mask, blocks, blocks, far_up, far_down)
    fixed_specs = [
        whole(router_t), whole(mask),
        layer(blocks, 0), layer(blocks, 1), layer(far_up, 0), layer(far_down, 0),
    ]
    wide, narrow = jax.ShapeDtypeStruct((count, width), F32), jax.ShapeDtypeStruct((count, width), BF16)
    inner = jax.ShapeDtypeStruct((count, hidden), BF16)
    return pl.pallas_call(
        expert_kernel,
        grid=(count // block,),
        in_specs=[row_spec, row_spec, *fixed_specs],
        out_specs=[row_spec, row_spec, prob_spec, row_spec, *(hidden_spec,) * 4],
        out_shape=[
            wide, wide, jax.ShapeDtypeStruct((count, router_t.shape[0]), F32), narrow, *(inner,) * 4
        ],
        compiler_params=pltpu.CompilerParams(vmem_limit_bytes=VMEM_LIMIT),
        cost_estimate=pl.CostEstimate(
            flops=16 * count * width * hidden,
            transcendentals=4 * count * hidden,
            bytes_accessed=count * (14 * width + 8 * hidden) + 8 * width * hidden,
        ),
    )(rows, cotan, *fixed)


def expert_exchange(value, experts):
    count = lax.axis_size("dp")
    groups = None
    if count != experts:
        groups = [
            [base + e for e in range(experts)] for base in range(0, count, experts)
        ]
    return lax.all_to_all(value, "dp", 0, 0, axis_index_groups=groups, tiled=True)


def by_ctx(first, second):
    lead = lax.axis_index("ctx") == 0
    return jnp.where(lead, first, second), jnp.where(lead, second, first)


def own_expert_blocks(up_shards, down_shards):
    experts, _, hidden = up_shards.shape
    count = lax.axis_size("dp")
    half = hidden // 2
    both = jnp.concatenate([up_shards, down_shards], axis=1)
    if lax.axis_size("ctx") == 2:
        both = by_ctx(both[:, :, :half], both[:, :, half:])[0]
    if count != experts:
        both = jnp.concatenate([both] * (count // experts), axis=0)
    return lax.all_to_all(both, "dp", 0, 0, tiled=True)


def other_hidden(both):
    rows = both.shape[1] // 2
    if lax.axis_size("ctx") == 2:
        return swapped(both[:, :rows], "ctx"), swapped(both[:, rows:], "ctx")
    half = both.shape[2] // 2
    return both[:, :rows, half:], both[:, rows:, half:]


def gather_kernel(count, parts, *refs):
    ins, outs = refs[:parts], refs[parts : 2 * parts]
    send_sem, recv_sem, own_sem = refs[2 * parts :]
    places = count // 2
    me = lax.axis_index("dp")
    place, side = lax.div(me, 2), lax.rem(me, 2)
    across = me + 1 - 2 * side
    barrier = pltpu.get_barrier_semaphore()

    def greet(device):
        pl.semaphore_signal(
            barrier, inc=1, device_id={"dp": device}, device_id_type=pl.DeviceIdType.MESH
        )

    greet(across)
    for step in (-1, 1):
        there = place + step

        @pl.when((there >= 0) & (there < places))
        def greet_place(step=step):
            greet(me + 2 * step)

    neighbours = 1 + (place > 0).astype(jnp.int32) + (place < places - 1).astype(jnp.int32)
    pl.semaphore_wait(barrier, neighbours)

    def copy(part, slot, kind, device, own):
        return pltpu.make_async_remote_copy(
            src_ref=ins[part] if own else outs[part].at[slot],
            dst_ref=outs[part].at[slot],
            send_sem=send_sem.at[kind, part, slot],
            recv_sem=recv_sem.at[part, slot],
            device_id={"dp": device},
            device_id_type=pl.DeviceIdType.MESH,
        )

    def passed_on(slot, steps, own, act):
        for step in steps:
            there = place + step

            @pl.when((there >= 0) & (there < places))
            def along(step=step):
                for part in range(parts):
                    act(copy(part, slot, step + 1, me + 2 * step, own))

        for part in range(parts):
            act(copy(part, slot, 1, across, own))

    def start(one):
        one.start()

    def sent(one):
        one.wait_send()

    mine = [
        pltpu.make_async_copy(ins[part], outs[part].at[me], own_sem.at[part])
        for part in range(parts)
    ]
    for one in mine:
        one.start()
    passed_on(me, (-1, 1), True, start)
    for far in range(1, places):
        for step in (-1, 1):
            origin = place - step * far

            @pl.when((origin >= 0) & (origin < places))
            def forward(step=step, far=far):
                slot = me - 2 * step * far
                for part in range(parts):
                    copy(part, slot, 1, across, False).wait_recv()
                passed_on(slot, (step,), False, start)

    for at in range(places):
        for part in range(parts):
            copy(part, 2 * at + 1 - side, 1, across, False).wait_recv()
    for one in mine:
        one.wait()
    passed_on(me, (-1, 1), True, sent)
    for far in range(1, places):
        for step in (-1, 1):
            origin = place - step * far

            @pl.when((origin >= 0) & (origin < places))
            def forwarded(step=step, far=far):
                passed_on(me - 2 * step * far, (step,), False, sent)


def gathered(*values):
    count = lax.axis_size("dp")
    parts = len(values)
    anywhere = pl.BlockSpec(memory_space=pl.ANY)
    size = sum(math.prod(value.shape) * 2 for value in values)
    return pl.pallas_call(
        partial(gather_kernel, count, parts),
        in_specs=[anywhere] * parts,
        out_specs=[anywhere] * parts,
        out_shape=[jax.ShapeDtypeStruct((count, *value.shape), value.dtype) for value in values],
        scratch_shapes=[
            pltpu.SemaphoreType.DMA((3, parts, count)),
            pltpu.SemaphoreType.DMA((parts, count)),
            pltpu.SemaphoreType.DMA((parts,)),
        ],
        compiler_params=pltpu.CompilerParams(collective_id=0, has_side_effects=True),
        cost_estimate=pl.CostEstimate(
            flops=0, transcendentals=0, bytes_accessed=2 * count * size
        ),
    )(*values)


def other_joined(own, first_shard, second_shard):
    count = lax.axis_size("ctx")
    if count == 2:
        return by_ctx(own, swapped(own, "ctx"))
    del first_shard, second_shard
    every = lax.all_gather(own, "ctx")
    return every[0], every[1]


def expert_weight_products(rows, hidden_grads, grads, actives):
    pairs = ((rows, hidden_grads), (grads, actives))
    far = [contract_rows(left, rights[1]) for left, rights in pairs]
    if lax.axis_size("ctx") == 2:
        far = [value.astype(BF16) for value in far]
    return [contract_rows(left, rights[0]) for left, rights in pairs], far


def sent_far(value):
    return swapped(value, "ctx") if lax.axis_size("ctx") == 2 else value


def expert_weight_parts(near, far):
    count = lax.axis_size("dp")
    parts = []
    for own, other in zip(near, far):
        if lax.axis_size("ctx") == 2:
            part = own + other.astype(F32)
        else:
            part = lax.psum_scatter(
                jnp.concatenate([own, other], axis=1), "ctx", scatter_dimension=1, tiled=True
            )
        parts.append(part.astype(BF16).reshape(count, part.shape[0] // count, part.shape[1]))
    return jnp.concatenate(parts, axis=1)


def expert_weight_halves(blocks, experts):
    count = lax.axis_size("dp")
    if count != experts:
        blocks = jnp.sum(
            blocks.reshape(count // experts, experts, *blocks.shape[1:]).astype(F32), axis=0
        ).astype(BF16)
    if lax.axis_size("ctx") == 2:
        return blocks, swapped(blocks, "ctx")
    return blocks, lax.all_gather(blocks, "ctx", axis=2, tiled=True)


def expert_weight_grads(blocks, far_blocks):
    joined = far_blocks
    if lax.axis_size("ctx") == 2:
        joined = jnp.concatenate(by_ctx(blocks, far_blocks), axis=2)
    shard = joined.shape[1] // 2
    return joined[:, :shard].astype(F32), joined[:, shard:].astype(F32)


def pair_products(first, second):
    if lax.axis_size("ctx") != 2:
        return contract_rows(*first), contract_rows(*second).astype(BF16)
    lefts, rights = by_ctx(first[0], second[0]), by_ctx(first[1], second[1])
    return contract_rows(lefts[0], rights[0]), contract_rows(lefts[1], rights[1]).astype(BF16)


def product_part(near, far):
    count = lax.axis_size("dp")

    def blocks(value):
        return value.astype(BF16).reshape(count, value.shape[0] // count, value.shape[1])

    if lax.axis_size("ctx") != 2:
        return jnp.concatenate([blocks(near), blocks(far)], axis=1)
    return blocks(near + far.astype(F32))


def product_shards(blocks):
    sums = jnp.sum(blocks.astype(F32), axis=0)
    if lax.axis_size("ctx") == 2:
        return by_ctx(sums, swapped(sums, "ctx"))
    sums = lax.psum(sums, "ctx")
    rows = sums.shape[0] // 2
    return sums[:rows], sums[rows:]


def local(
    hidden_in,
    out_grad,
    norm1_gain,
    in_weight,
    conv_weight,
    conv_bias,
    xproj_weight,
    dt_weight,
    dt_bias,
    decay_log,
    skip_weight,
    out_weight,
    norm2_gain,
    router_weight,
    fc1_weight,
    fc2_weight,
    expert_ids,
    keep_mask,
):
    batches, seqs, length, model_width = hidden_in.shape
    chains = batches * seqs
    tokens = chains * length
    steps = length // SEGMENTS
    shard, _, inner = in_weight.shape
    taps = conv_weight.shape[0]
    low_rank = dt_weight.shape[0]
    states = decay_log.shape[0]
    experts = fc1_weight.shape[0]
    dp_count = lax.axis_size("dp")
    tp_count = lax.axis_size("tp")
    capacity = tokens // 4
    part_cap = capacity // tp_count
    slots = experts * part_cap
    tp_index = lax.axis_index("tp")
    scan = Scan(steps, chains, states, inner)

    def to_rows(value):
        value = value.reshape(chains, SEGMENTS, steps, -1).transpose(2, 0, 1, 3)
        return value.reshape(tokens, -1)

    def from_rows(value):
        value = value.reshape(steps, chains, SEGMENTS, -1).transpose(1, 2, 0, 3)
        return value.reshape(batches, seqs, length, -1)

    pieces = [
        norm1_gain[None],
        conv_weight,
        conv_bias[None],
        dt_weight,
        dt_bias[None],
        decay_log,
        skip_weight[None],
        norm2_gain[None],
        router_weight.T,
        xproj_weight.T,
    ]
    bounds = [0]
    for piece in pieces:
        bounds.append(bounds[-1] + piece.shape[0])
    small = sum(
        jnp.pad(piece, ((low, bounds[-1] - high), (0, 0)))
        for piece, low, high in zip(pieces, bounds, bounds[1:])
    )
    kinds = small.shape[0]
    small_wide = jnp.pad(small.T, ((0, 0), (0, -kinds % LANES)))
    in_x, small_all, later = gathered(
        in_weight[:, 0], small_wide, by_ctx(out_weight.T, in_weight[:, 1])[0]
    )
    in_x = in_x.reshape(dp_count * shard, inner)
    later = later.reshape(dp_count * shard, inner)
    small_all = small_all.reshape(dp_count * shard, -1)[:, :kinds].T
    small_all, up_shards, down_shards = together(
        small_all, fc1_weight, fc2_weight.transpose(0, 2, 1)
    )
    pieces = [small_all[bounds[i] : bounds[i + 1]] for i in range(len(bounds) - 1)]
    gain_one_f = pieces[0].astype(F32)
    tap_weights = pieces[1].astype(F32)
    conv_shift = pieces[2].astype(F32)
    dt_proj = pieces[3]
    dt_shift = pieces[4].astype(F32)
    decay_rate = -jnp.exp(pieces[5].astype(F32))
    skip_row = pieces[6].astype(F32)
    gain_two_f = pieces[7].astype(F32)
    router_t = pieces[8]
    x_proj_t = pieces[9]
    rate_rows = jnp.broadcast_to((decay_rate * LOG2E)[:, None, :], (states, SEGMENTS, inner))
    expert_blocks = own_expert_blocks(up_shards, down_shards)

    route = to_rows(expert_ids)[:, 0]
    keep = to_rows(keep_mask)[:, 0].astype(F32)
    onehot_int = (route[:, None] == jnp.arange(experts, dtype=jnp.int32)[None, :]).astype(jnp.int32)
    rank = jnp.sum((jnp.cumsum(onehot_int, axis=0) - 1) * onehot_int, axis=1) - tp_index * part_cap
    here = (rank >= 0) & (rank < part_cap)
    token_slot = jnp.where(here, route * part_cap + rank, -1)
    place = (
        token_slot[None, :] == jnp.arange(slots, dtype=jnp.int32)[:, None]
    ).astype(BF16)

    def slotted(value):
        sent = jnp.dot(place, value, preferred_element_type=F32).astype(BF16)
        return sent.reshape(experts, part_cap, -1)

    def exchanged(value):
        return expert_exchange(value, experts).reshape(slots, -1)

    def landed(value):
        return axis_sum(contract_rows(place, value).astype(BF16), "tp").astype(F32)

    cotan_bf = to_rows(out_grad)
    cotan = cotan_bf.astype(F32)
    sent_cotan = slotted((cotan * keep[:, None]).astype(BF16))

    values = to_rows(hidden_in).astype(F32)
    normalized_rows, inverse_one = rms_forward(values, gain_one_f)
    normed_bf = normalized_rows.astype(BF16)
    x_pre = jnp.dot(normed_bf, in_x, preferred_element_type=F32).astype(BF16)
    x_pre = x_pre.reshape(steps, chains, SEGMENTS, inner)
    tail = x_pre[steps - taps + 1 :]
    edge_in = passed_along(tail[:, :, SEGMENTS - 1 :], "ctx", 1)
    edge_in, later = together(edge_in, later)
    out_proj_t, in_z = other_joined(later, out_weight.T, in_weight[:, 1])
    halo = jnp.concatenate([edge_in, tail[:, :, : SEGMENTS - 1]], axis=2)
    extended_bf = jnp.concatenate([halo, x_pre], axis=0)
    extended = extended_bf.astype(F32)
    conv_pre = jnp.broadcast_to(conv_shift[0], x_pre.shape)
    for tap in range(taps):
        conv_pre = conv_pre + tap_weights[tap] * extended[tap : tap + steps]
    xconv_bf = jax.nn.silu(conv_pre).astype(BF16)
    xconv = xconv_bf.astype(F32)
    xconv_rows = xconv_bf.reshape(tokens, inner)
    projected = axis_sum(contract_cols(xconv_rows, x_proj_t), "tp")
    dt_low = projected[:, :low_rank].astype(BF16)

    def mixes(value):
        value = value.reshape(steps, chains, SEGMENTS, states).transpose(1, 0, 3, 2)
        return jnp.broadcast_to(value[..., None], (*value.shape, LANES))

    mix_in = mixes(projected[:, low_rank : low_rank + states])
    mix_out = mixes(projected[:, low_rank + states :])
    dt_pre = (jnp.dot(dt_low, dt_proj, preferred_element_type=F32) + dt_shift).reshape(x_pre.shape)
    step_size = jax.nn.softplus(dt_pre)
    seg_decay, seg_state, last_state = scan.ends(step_size, xconv, mix_in, rate_rows)
    sent_cotan, expert_blocks, _ = together(sent_cotan, expert_blocks, seg_state)
    slot_cotan = exchanged(sent_cotan)
    entering = entering_pieces(seg_decay[:, :, SEGMENTS - 1], last_state, "ctx", False)
    entering, expert_blocks = together(entering, expert_blocks)
    far_up, far_down = other_hidden(expert_blocks)
    scan_out, seg_start = scan.run(
        step_size, xconv, mix_in, mix_out, rate_rows, seg_decay, seg_state, entering
    )
    z_gate = jnp.dot(normed_bf, in_z, preferred_element_type=F32).reshape(x_pre.shape)
    scanned = scan_out + skip_row[0] * xconv
    z_silu = jax.nn.silu(z_gate)
    gated_bf = (scanned * z_silu).astype(BF16).reshape(tokens, inner)
    gated_bf, slot_cotan, far_up = together(gated_bf, slot_cotan, far_up)
    middle = values + axis_sum(contract_cols(gated_bf, out_proj_t), "tp")

    normed_two, inverse_two = rms_forward(middle, gain_two_f)
    normed_two_bf = normed_two.astype(BF16)
    own_rows = exchanged(slotted(normed_two_bf))
    own_rows, far_down = together(own_rows, far_down)
    expert_mask = (
        jnp.arange(experts, dtype=jnp.int32) == lax.rem(lax.axis_index("dp"), experts)
    ).astype(F32)[None, :]
    far_rows, far_cotan = swapped(own_rows, "tp"), swapped(slot_cotan, "tp")
    far = expert_call(far_rows, far_cotan, router_t, expert_mask, expert_blocks, far_up, far_down)
    near = expert_call(own_rows, slot_cotan, router_t, expert_mask, expert_blocks, far_up, far_down)
    slot_out = near[0] + swapped(far[0], "tp")
    picked_grad = near[1] + swapped(far[1], "tp")
    slot_prob = near[2]
    slot_gate = jnp.sum(slot_prob * expert_mask, axis=1, keepdims=True)
    gate_grad = jnp.sum(slot_out * slot_cotan.astype(F32), axis=1, keepdims=True)
    logit_grad = gate_grad * slot_gate * (expert_mask - slot_prob)
    router_grad_t = axis_sum(contract_rows(logit_grad, own_rows.astype(F32), HIGHEST), "tp")
    picked_grad = picked_grad + jnp.dot(
        logit_grad, router_t.astype(F32), precision=HIGHEST, preferred_element_type=F32
    )
    got_grad = exchanged(picked_grad.astype(BF16).reshape(experts, part_cap, -1))

    def both_rows(at):
        return jnp.concatenate([far[at], near[at]], axis=0)

    near_parts, far_parts = expert_weight_products(
        jnp.concatenate([far_rows, own_rows], axis=0),
        (both_rows(6), both_rows(7)),
        both_rows(3),
        (both_rows(4), both_rows(5)),
    )
    far_first = sent_far(far_parts[0])
    got_grad, near_parts, far_second, far_first, slot_out = together(
        got_grad, near_parts, far_parts[1], far_first, slot_out
    )
    far_parts = far_first, sent_far(far_second)
    normed_two_grad = landed(got_grad)
    got_out = exchanged(slot_out.astype(BF16).reshape(experts, part_cap, -1))
    middle_norm_grad, gain_two_grad = rms_backward(middle, inverse_two, gain_two_f, normed_two_grad)
    middle_grad = cotan + middle_norm_grad
    mixer_grad_bf = middle_grad.astype(BF16)
    gated_grad = jnp.dot(mixer_grad_bf, out_proj_t, preferred_element_type=F32).reshape(x_pre.shape)
    scan_grad = gated_grad * z_silu
    z_grad = jax.vjp(jax.nn.silu, z_gate)[1](gated_grad * scanned)[0]
    z_grad_bf = z_grad.astype(BF16).reshape(tokens, inner)
    near_product, far_product = pair_products((mixer_grad_bf, gated_bf), (normed_bf, z_grad_bf))
    weight_parts = expert_weight_parts(near_parts, far_parts)
    scan_grad, weight_parts, got_out = together(scan_grad, weight_parts, got_out)
    weight_blocks = lax.all_to_all(weight_parts, "dp", 0, 0, tiled=True)
    back_decay, back_adjoint, first_adjoint = scan.adjoint_ends(
        step_size, mix_out, scan_grad, rate_rows
    )
    leaving = entering_pieces(back_decay[:, :, 0], first_adjoint, "ctx", True)
    leaving, near_product, far_product = together(leaving, near_product, far_product)
    far_product = sent_far(far_product)
    pre_grad, xconv_grad, decay_sum, scan_sums, mix_grad = scan.adjoint(
        step_size, xconv, mix_in, mix_out, scan_grad, rate_rows, seg_start, back_decay, back_adjoint,
        leaving, skip_row,
    )
    pre_grad, weight_blocks, far_product = together(pre_grad, weight_blocks, far_product)
    out_blocks = lax.all_to_all(product_part(near_product, far_product), "dp", 0, 0, tiled=True)
    decay_log_grad = jnp.sum(decay_sum, axis=0) * decay_rate
    dt_shift_grad, skip_grad = jnp.sum(scan_sums, axis=0)[:2]
    pre_grad = pre_grad.reshape(tokens, inner)
    dt_proj_grad = contract_rows(dt_low.astype(F32), pre_grad, HIGHEST)
    dt_low_grad = contract_cols(pre_grad, dt_proj.astype(F32), HIGHEST)
    mix_grad = mix_grad.reshape(tokens, LANES)[:, : 2 * states]
    proj_part = jnp.concatenate([dt_low_grad, mix_grad], axis=1)
    proj_grad_bf = axis_sum(proj_part, "tp").astype(BF16)
    x_proj_grad_t = contract_rows(proj_grad_bf, xconv_rows)
    flat = (chains * SEGMENTS, inner)
    x_grad_bf, conv_sums, head, last = conv_back(
        proj_grad_bf,
        x_proj_t,
        xconv_grad.reshape(steps, *flat),
        extended_bf.reshape(steps + taps - 1, *flat),
        tap_weights,
        conv_shift,
    )
    taps_grad, shift_grad = conv_sums[:taps], conv_sums[taps]
    edge_back = passed_along(
        head.reshape(taps - 1, chains, SEGMENTS, inner)[:, :, :1], "ctx", -1
    )
    edge_back, weight_blocks, out_blocks = together(edge_back, weight_blocks, out_blocks)
    weight_blocks, far_blocks = expert_weight_halves(weight_blocks, experts)
    reaching = jnp.stack(
        [
            sum(tap_weights[tap] * edge_back[at - tap] for tap in range(at + 1))
            for at in range(taps - 1)
        ]
    )
    reaching = jnp.pad(reaching, ((0, 0), (0, 0), (SEGMENTS - 1, 0), (0, 0)))
    last = (last + reaching.reshape(taps - 1, *flat)).astype(BF16)
    x_grad_bf = lax.dynamic_update_slice(x_grad_bf, last, (steps - taps + 1, 0, 0))
    x_grad_bf = x_grad_bf.reshape(tokens, inner)
    small_grads = jnp.concatenate(
        [
            taps_grad,
            shift_grad[None],
            dt_proj_grad,
            dt_shift_grad[None],
            decay_log_grad,
            skip_grad[None],
            gain_two_grad[None],
            router_grad_t,
            x_proj_grad_t,
        ],
        axis=0,
    )
    small_grads = small_grads.reshape(-1, dp_count, shard).transpose(1, 0, 2)
    x_grad_bf, small_grads, out_blocks = together(x_grad_bf, small_grads, out_blocks)
    small_blocks = lax.all_to_all(small_grads, "dp", 0, 0, tiled=True)
    normed_grad = axis_sum(
        contract_cols(x_grad_bf, in_x) + contract_cols(z_grad_bf, in_z), "tp"
    )
    values_norm_grad, gain_one_grad = rms_backward(values, inverse_one, gain_one_f, normed_grad)
    input_grad = from_rows((middle_grad + values_norm_grad).astype(BF16))

    in_x_part = contract_rows(normed_bf, x_grad_bf).astype(BF16).reshape(dp_count, shard, inner)
    gain_row = gain_one_grad.reshape(dp_count, 1, shard)
    gain_high = gain_row.astype(BF16)
    gain_low = (gain_row - gain_high.astype(F32)).astype(BF16)
    gain_rows = jnp.concatenate([gain_high, gain_low], axis=1)
    gain_rows = jnp.pad(gain_rows, ((0, 0), (0, 6), (0, inner - shard)))
    in_x_part, out_blocks, small_blocks = together(in_x_part, out_blocks, small_blocks)
    out_proj_grad, in_z_grad = product_shards(out_blocks)
    in_x_blocks = lax.all_to_all(
        jnp.concatenate([in_x_part, gain_rows], axis=1), "dp", 0, 0, tiled=True
    )
    in_x_blocks, far_blocks = together(in_x_blocks, far_blocks)
    first_grad, second_grad = expert_weight_grads(weight_blocks, far_blocks)
    router_prob = jax.nn.softmax(contract_cols(normed_two_bf, router_t), axis=-1)
    gate_prob = jnp.sum(router_prob * onehot_int.astype(F32), axis=1) * keep
    result = from_rows((middle + gate_prob[:, None] * landed(got_out)).astype(BF16))
    in_x_sums = axis_sum(jnp.sum(in_x_blocks.astype(F32), axis=0), "ctx")
    in_x_grad = in_x_sums[:shard]
    gain_one_grad = in_x_sums[shard : shard + 1, :shard] + in_x_sums[shard + 1 : shard + 2, :shard]
    small_grads = axis_sum(jnp.sum(small_blocks, axis=0), "ctx")
    small_grads = jnp.concatenate([gain_one_grad, small_grads], axis=0)
    sums = [small_grads[bounds[i] : bounds[i + 1]] for i in range(len(bounds) - 1)]
    return (
        result,
        input_grad,
        sums[0][0],
        jnp.stack([in_x_grad, in_z_grad], axis=1),
        sums[1],
        sums[2][0],
        sums[9].T,
        sums[3],
        sums[4][0],
        sums[5],
        sums[6][0],
        out_proj_grad.T,
        sums[7][0],
        sums[8].T,
        first_grad,
        second_grad.transpose(0, 2, 1),
    )


def solution(mesh):
    weights = (
        P("dp"),
        P("dp", None, "tp"),
        P(None, ("tp", "dp")),
        P(("tp", "dp")),
        P(("tp", "dp"), None),
        P(None, ("tp", "dp")),
        P(("tp", "dp")),
        P(None, ("tp", "dp")),
        P(("tp", "dp")),
        P("tp", "dp"),
        P("dp"),
        P("dp", None),
        P(None, "dp", "tp"),
        P(None, "tp", "dp"),
    )
    rows = P(None, "dp", "ctx", None)
    return jax.shard_map(
        local,
        mesh=mesh,
        in_specs=(rows, rows, *weights, P(("dp", "ctx"), None), P(("dp", "ctx"))),
        out_specs=(rows, rows, *weights),
        check_vma=False,
    )
```

```python
from functools import partial
import math

import jax
import jax.numpy as jnp
from jax import lax
from jax.experimental import pallas as pl
from jax.experimental.pallas import tpu as pltpu
from jax.sharding import PartitionSpec as P

EPSILON = 1e-05
HIGHEST = lax.Precision.HIGHEST
SEGMENTS = 8
LANES = 128
VMEM_LIMIT = 56 * 1024 * 1024
LOG2E = math.log2(math.e)
GROUP_A = 4
GROUP_B = 4
GROUP_C = 8
UNROLL_A = 8
UNROLL_B = 8
UNROLL_C = 8
UNROLL_D = 4
UNROLL_E = 8
BLOCKS = 3
COVER = 100
HALVES = 1
BF16 = jnp.bfloat16
F32 = jnp.float32


def swapped(value, axis):
    return lax.ppermute(value, axis, [(0, 1), (1, 0)])


def passed_along(value, axis, steps):
    count = lax.axis_size(axis)
    leading, last = (max(0, -steps), min(count, count - steps))
    return lax.ppermute(value, axis, [(source, source + steps) for source in range(leading, last)])


def axis_sum(value, axis):
    if lax.axis_size(axis) == 2:
        return value + swapped(value, axis)
    return lax.psum(value, axis)


def together(*values):
    return lax.optimization_barrier(values)


def entering_pieces(decay, value, axis, backward):
    count = lax.axis_size(axis)
    if count == 2:
        return passed_along(value, axis, -1 if backward else 1)
    mine = lax.axis_index(axis)
    decays = lax.all_gather(decay, axis)
    values = lax.all_gather(value, axis)
    running = jnp.zeros_like(value)
    for position in range(count - 1):
        at = count - 1 - position if backward else position
        longer = values[at] + decays[at] * running
        ahead = at > mine if backward else at < mine
        running = jnp.where(ahead, longer, running)
    return running


def contract_rows(left_side, right_side, precision=None):
    return lax.dot_general(
        left_side,
        right_side,
        (((0,), (0,)), ((), ())),
        precision=precision,
        preferred_element_type=F32,
    )


def contract_cols(left_side, right_side, precision=None):
    return lax.dot_general(
        left_side,
        right_side,
        (((1,), (1,)), ((), ())),
        precision=precision,
        preferred_element_type=F32,
    )


def rms_forward(values, gain_vec):
    inverse = lax.rsqrt(jnp.mean(values * values, axis=-1, keepdims=True) + EPSILON)
    return (values * inverse * gain_vec, inverse)


def rms_backward(values, inverse, gain_vec, grad_out):
    weighted = grad_out * gain_vec
    inner_mean = jnp.mean(values * weighted, axis=-1, keepdims=True)
    grad_values = inverse * weighted - values * inverse * inverse * inverse * inner_mean
    grad_gain = jnp.sum(grad_out * values * inverse, axis=0)
    return (grad_values, grad_gain)


def zeros_of(ref):
    return jnp.zeros(ref.shape[1:], F32)


def sublane_rows(lanes):
    return lax.broadcasted_iota(jnp.int32, (SEGMENTS, lanes), 0)


def widened(value, lanes):
    return jnp.concatenate([value] * (lanes // LANES), axis=1) if lanes > LANES else value


def narrowed(value):
    parts = [value[:, at : at + LANES] for at in range(0, value.shape[1], LANES)]
    return sum(parts[1:], parts[0])


def groups_of(states, size):
    size = math.gcd(states, size)
    return [range(first, first + size) for first in range(0, states, size)]


def joined_forward(decay, value, row):
    for reach in (1, 2, 4):
        inside = row >= reach
        value = value + jnp.where(inside, decay * pltpu.roll(value, reach, 0), 0.0)
        decay = jnp.where(inside, decay * pltpu.roll(decay, reach, 0), decay)
    return decay, value


def joined_backward(decay, value, row):
    for reach in (1, 2, 4):
        inside = row < SEGMENTS - reach
        value = value + jnp.where(inside, decay * pltpu.roll(value, SEGMENTS - reach, 0), 0.0)
        decay = jnp.where(inside, decay * pltpu.roll(decay, SEGMENTS - reach, 0), decay)
    return decay, value


def ends_kernel(step_ref, input_ref, mix_in_ref, rate_ref, decay_ref, state_ref, last_ref):
    steps, states, lanes = step_ref.shape[0], mix_in_ref.shape[1], step_ref.shape[2]
    zero = zeros_of(step_ref)
    row = sublane_rows(lanes)
    total = lax.fori_loop(0, steps, lambda at, total: total + step_ref[at], zero, unroll=UNROLL_E)
    for members in groups_of(states, GROUP_A):
        rates = [rate_ref[n] for n in members]

        def body(at, held):
            step = step_ref[at]
            driven = step * input_ref[at]
            return tuple(
                jnp.exp2(step * rate) * before + widened(mix_in_ref[at, n], lanes) * driven
                for n, rate, before in zip(members, rates, held)
            )

        held = lax.fori_loop(0, steps, body, (zero,) * len(members), unroll=UNROLL_A)
        for n, rate, end in zip(members, rates, held):
            decay, value = joined_forward(jnp.exp2(total * rate), end, row)
            decay_ref[n] = decay
            state_ref[n] = value
            last_ref[n : n + 1] = value[SEGMENTS - 1 :]


def states_kernel(
    step_ref, input_ref, mix_in_ref, mix_out_ref, rate_ref, decay_ref, state_ref, enter_ref,
    out_ref, start_ref,
):
    steps, states, lanes = step_ref.shape[0], mix_in_ref.shape[1], step_ref.shape[2]
    row = sublane_rows(lanes)
    for members in groups_of(states, GROUP_B):
        rates = [rate_ref[n] for n in members]
        held = []
        for n in members:
            first = jnp.broadcast_to(enter_ref[n : n + 1], (SEGMENTS, lanes))
            inner = pltpu.roll(state_ref[n], 1, 0) + pltpu.roll(decay_ref[n], 1, 0) * first
            start = jnp.where(row >= 1, inner, first)
            start_ref[n] = start
            held.append(start)

        def body(at, held):
            step = step_ref[at]
            driven = step * input_ref[at]
            held = tuple(
                jnp.exp2(step * rate) * before + widened(mix_in_ref[at, n], lanes) * driven
                for n, rate, before in zip(members, rates, held)
            )
            parts = [widened(mix_out_ref[at, n], lanes) * now for n, now in zip(members, held)]
            if members[0]:
                parts.append(out_ref[at])
            while len(parts) > 1:
                parts = [sum(parts[i + 1 : i + 2], parts[i]) for i in range(0, len(parts), 2)]
            out_ref[at] = parts[0]
            return held

        lax.fori_loop(0, steps, body, tuple(held), unroll=UNROLL_B)


def adjoint_ends_kernel(step_ref, mix_out_ref, grad_ref, rate_ref, decay_ref, adjoint_ref, first_ref):
    steps, states, lanes = step_ref.shape[0], mix_out_ref.shape[1], step_ref.shape[2]
    zero = zeros_of(step_ref)
    row = sublane_rows(lanes)
    total = lax.fori_loop(0, steps, lambda at, total: total + step_ref[at], zero, unroll=UNROLL_E)
    for members in groups_of(states, GROUP_A):
        rates = [rate_ref[n] for n in members]

        def body(back, incoming):
            at = steps - 1 - back
            step = step_ref[at]
            grad = grad_ref[at]
            return tuple(
                jnp.exp2(step * rate) * (widened(mix_out_ref[at, n], lanes) * grad + after)
                for n, rate, after in zip(members, rates, incoming)
            )

        incoming = lax.fori_loop(0, steps, body, (zero,) * len(members), unroll=UNROLL_A)
        for n, rate, end in zip(members, rates, incoming):
            decay, value = joined_backward(jnp.exp2(total * rate), end, row)
            decay_ref[n] = decay
            adjoint_ref[n] = value
            first_ref[n : n + 1] = value[:1]


def adjoint_kernel(
    step_ref, input_ref, mix_in_ref, mix_out_ref, grad_ref, rate_ref, start_ref, decay_ref, adjoint_ref,
    enter_ref, skip_ref,
    pre_ref, conv_ref, decay_sum_ref, sums_ref, mix_ref, states_ref, decays_ref, in_grad_ref, out_grad_ref,
):
    steps, states, lanes = step_ref.shape[0], mix_in_ref.shape[1], step_ref.shape[2]
    row = sublane_rows(lanes)
    zero = zeros_of(step_ref)

    @pl.when(pl.program_id(1) == 0)
    def clear():
        in_grad_ref[...] = jnp.zeros_like(in_grad_ref)
        out_grad_ref[...] = jnp.zeros_like(out_grad_ref)

    for members in groups_of(states, GROUP_C):
        first, group = members[0], len(members)
        rates = [rate_ref[n] for n in members]

        def ahead(at, held):
            step = step_ref[at]
            driven = step * input_ref[at]
            grad = grad_ref[at]
            after = []
            for i, n in enumerate(members):
                states_ref[at, i] = held[i]
                decay = jnp.exp2(step * rates[i])
                decays_ref[at, i] = decay
                now = decay * held[i] + widened(mix_in_ref[at, n], lanes) * driven
                out_grad_ref[at, n] += narrowed(grad * now)
                after.append(now)
            return tuple(after)

        lax.fori_loop(0, steps, ahead, tuple(start_ref[n] for n in members), unroll=UNROLL_C)

        incoming = []
        for n in members:
            final = jnp.broadcast_to(enter_ref[n : n + 1], (SEGMENTS, lanes))
            inner = (
                pltpu.roll(adjoint_ref[n], SEGMENTS - 1, 0)
                + pltpu.roll(decay_ref[n], SEGMENTS - 1, 0) * final
            )
            incoming.append(jnp.where(row < SEGMENTS - 1, inner, final))

        def body(back, carry):
            at = steps - 1 - back
            incoming, decay_sums = carry
            step = step_ref[at]
            grad = grad_ref[at]
            driven = step * input_ref[at]
            in_sum = conv_ref[at] if first else zero
            rate_sum = pre_ref[at] if first else zero
            following, sums = [], []
            for i, n in enumerate(members):
                adjoint = widened(mix_out_ref[at, n], lanes) * grad + incoming[i]
                onward = decays_ref[at, i] * adjoint
                decay_grad = onward * states_ref[at, i]
                in_sum = in_sum + adjoint * widened(mix_in_ref[at, n], lanes)
                rate_sum = rate_sum + decay_grad * rates[i]
                sums.append(decay_sums[i] + decay_grad * step)
                in_grad_ref[at, n] += narrowed(adjoint * driven)
                following.append(onward)
            conv_ref[at] = in_sum
            pre_ref[at] = rate_sum
            return tuple(following), tuple(sums)

        _, sums = lax.fori_loop(
            0, steps, body, (tuple(incoming), (zero,) * group), unroll=UNROLL_D
        )
        for i, n in enumerate(members):
            decay_sum_ref[n : n + 1] = jnp.sum(sums[i], axis=0, keepdims=True)

    skip = skip_ref[...]

    def close(at, carry):
        pre_sum, skip_sum = carry
        step, inputs, grad, in_sum = step_ref[at], input_ref[at], grad_ref[at], conv_ref[at]
        step_grad = pre_ref[at] * (1.0 / LOG2E) + in_sum * inputs
        pre = step_grad * (1.0 - jnp.exp2(step * -LOG2E))
        pre_ref[at] = pre
        conv_ref[at] = in_sum * step + skip * grad
        return pre_sum + pre, skip_sum + grad * inputs

    pre_sum, skip_sum = lax.fori_loop(0, steps, close, (zero, zero), unroll=UNROLL_E)
    sums_ref[0:1] = jnp.sum(pre_sum, axis=0, keepdims=True)
    sums_ref[1:2] = jnp.sum(skip_sum, axis=0, keepdims=True)
    sums_ref[2:] = jnp.zeros((SEGMENTS - 2, lanes), F32)

    @pl.when(pl.program_id(1) == pl.num_programs(1) - 1)
    def across_lanes():
        lane = lax.broadcasted_iota(jnp.int32, (SEGMENTS, LANES), 1)

        def one(at, carry):
            total = jnp.zeros((SEGMENTS, LANES), F32)
            for n in range(states):
                for base, ref in ((0, in_grad_ref), (states, out_grad_ref)):
                    value = jnp.sum(ref[at, n], axis=1, keepdims=True)
                    total = jnp.where(lane == base + n, value, total)
            mix_ref[at] = total
            return carry

        lax.fori_loop(0, steps, one, 0, unroll=UNROLL_E)


class Scan:
    def __init__(self, steps, chains, states, width):
        lanes = LANES * math.gcd(width // LANES, BLOCKS)
        self.grid = (chains, width // lanes)
        self.rows_spec = pl.BlockSpec(
            (steps, None, SEGMENTS, lanes), lambda chain, block: (0, chain, 0, block)
        )
        self.mix_spec = pl.BlockSpec(
            (None, steps, states, SEGMENTS, LANES), lambda chain, block: (chain, 0, 0, 0, 0)
        )
        self.rate_spec = pl.BlockSpec((states, SEGMENTS, lanes), lambda chain, block: (0, 0, block))
        self.state_spec = pl.BlockSpec(
            (None, states, SEGMENTS, lanes), lambda chain, block: (chain, 0, 0, block)
        )
        self.edge_spec = pl.BlockSpec((None, states, lanes), lambda chain, block: (chain, 0, block))
        self.rows = jax.ShapeDtypeStruct((steps, chains, SEGMENTS, width), F32)
        self.mix = jax.ShapeDtypeStruct((chains, steps, states, SEGMENTS, LANES), F32)
        self.state = jax.ShapeDtypeStruct((chains, states, SEGMENTS, width), F32)
        self.edge = jax.ShapeDtypeStruct((chains, states, width), F32)
        self.sums = jax.ShapeDtypeStruct((chains, SEGMENTS, width), F32)
        self.sums_spec = pl.BlockSpec((None, SEGMENTS, lanes), lambda chain, block: (chain, 0, block))
        self.lane_sums = jax.ShapeDtypeStruct((steps, chains, SEGMENTS, LANES), F32)
        self.lane_spec = pl.BlockSpec(
            (steps, None, SEGMENTS, LANES), lambda chain, block: (0, chain, 0, 0)
        )
        self.skip_spec = pl.BlockSpec((1, lanes), lambda chain, block: (0, block))
        self.scratch = [
            pltpu.VMEM((steps, math.gcd(states, GROUP_C), SEGMENTS, lanes), F32),
            pltpu.VMEM((steps, math.gcd(states, GROUP_C), SEGMENTS, lanes), F32),
            pltpu.VMEM((steps, states, SEGMENTS, LANES), F32),
            pltpu.VMEM((steps, states, SEGMENTS, LANES), F32),
        ]
        self.work = steps * chains * SEGMENTS * width * states

    def call(self, kernel, ops, args, in_specs, outs, out_specs, scratch=()):
        size = sum(math.prod(a.shape) * a.dtype.itemsize for a in (*args, *outs))
        return pl.pallas_call(
            kernel,
            grid=self.grid,
            in_specs=in_specs,
            out_specs=out_specs,
            out_shape=outs,
            scratch_shapes=list(scratch),
            compiler_params=pltpu.CompilerParams(vmem_limit_bytes=VMEM_LIMIT),
            cost_estimate=pl.CostEstimate(
                flops=ops * self.work, transcendentals=self.work, bytes_accessed=size // COVER
            ),
        )(*args)

    def ends(self, step, inputs, mix_in, rate):
        return self.call(
            ends_kernel, 5, (step, inputs, mix_in, rate),
            [self.rows_spec, self.rows_spec, self.mix_spec, self.rate_spec],
            [self.state, self.state, self.edge],
            [self.state_spec, self.state_spec, self.edge_spec],
        )

    def run(self, step, inputs, mix_in, mix_out, rate, decay, state, enter):
        return self.call(
            states_kernel, 7, (step, inputs, mix_in, mix_out, rate, decay, state, enter),
            [self.rows_spec, self.rows_spec, self.mix_spec, self.mix_spec, self.rate_spec,
             self.state_spec, self.state_spec, self.edge_spec],
            [self.rows, self.state],
            [self.rows_spec, self.state_spec],
        )

    def adjoint_ends(self, step, mix_out, grad, rate):
        return self.call(
            adjoint_ends_kernel, 5, (step, mix_out, grad, rate),
            [self.rows_spec, self.mix_spec, self.rows_spec, self.rate_spec],
            [self.state, self.state, self.edge],
            [self.state_spec, self.state_spec, self.edge_spec],
        )

    def adjoint(self, args):
        return self.call(
            adjoint_kernel, 20, args,
            [self.rows_spec, self.rows_spec, self.mix_spec, self.mix_spec, self.rows_spec,
             self.rate_spec, self.state_spec, self.state_spec, self.state_spec, self.edge_spec,
             self.skip_spec],
            [self.rows, self.rows, self.edge, self.sums, self.lane_sums],
            [self.rows_spec, self.rows_spec, self.edge_spec, self.sums_spec, self.lane_spec],
            self.scratch,
        )


def conv_back_kernel(
    proj_ref, weight_ref, grad_ref, input_ref, taps_ref, shift_ref,
    out_ref, sums_ref, head_ref, tail_ref, product_ref, conv_ref,
):
    steps, rows, lanes = grad_ref.shape
    count = taps_ref.shape[0]
    reach = count - 1
    taps = [taps_ref[at : at + 1] for at in range(count)]
    shift = shift_ref[...]
    product_ref[...] = jnp.dot(
        proj_ref[...], weight_ref[...], preferred_element_type=F32
    ).reshape(steps, rows, lanes)

    def slopes(at, sums):
        inputs = [input_ref[at + tap].astype(F32) for tap in range(count)]
        pre = shift + sum(tap * value for tap, value in zip(taps, inputs))
        share = 1.0 / (1.0 + jnp.exp(-pre))
        conv = (grad_ref[at] + product_ref[at]) * (share * (1.0 + pre * (1.0 - share)))
        conv_ref[at] = conv
        return (*(total + conv * value for total, value in zip(sums, inputs)), sums[-1] + conv)

    zero = jnp.zeros((rows, lanes), F32)
    sums = lax.fori_loop(0, steps, slopes, (zero,) * (count + 1), unroll=2)
    for at, total in enumerate(sums):
        sums_ref[at : at + 1] = jnp.sum(total, axis=0, keepdims=True)
    sums_ref[count + 1 :] = jnp.zeros((sums_ref.shape[0] - count - 1, lanes), F32)
    row = sublane_rows(lanes)
    for at in range(reach):
        head_ref[at] = conv_ref[at]
        for low in range(0, rows, SEGMENTS):
            rolled = pltpu.roll(conv_ref[at, low : low + SEGMENTS], SEGMENTS - 1, 0)
            conv_ref[steps + at, low : low + SEGMENTS] = jnp.where(
                row < SEGMENTS - 1, rolled, 0.0
            )

    def back(at):
        return sum(taps[tap] * conv_ref[at + reach - tap] for tap in range(count))

    def store(at, carry):
        out_ref[at] = back(at).astype(BF16)
        return carry

    lax.fori_loop(0, steps, store, 0, unroll=2)
    for at in range(reach):
        tail_ref[at] = back(steps - reach + at)


def conv_back(proj, weight, grad, inputs, taps, shift):
    steps, rows, width = grad.shape
    reach = taps.shape[0] - 1
    lanes = LANES * math.gcd(width // LANES, BLOCKS)

    def block(count, dtype=F32):
        spec = pl.BlockSpec((count, rows, lanes), lambda at: (0, 0, at))
        return spec, jax.ShapeDtypeStruct((count, rows, width), dtype)

    def columns(count):
        return pl.BlockSpec((count, lanes), lambda at: (0, at))

    outs = [
        block(steps, BF16),
        (columns(SEGMENTS), jax.ShapeDtypeStruct((SEGMENTS, width), F32)),
        block(reach),
        block(reach),
    ]
    return pl.pallas_call(
        conv_back_kernel,
        grid=(width // lanes,),
        in_specs=[
            pl.BlockSpec(proj.shape, lambda at: (0, 0)),
            columns(weight.shape[0]),
            block(steps)[0],
            block(steps + reach)[0],
            columns(reach + 1),
            columns(1),
        ],
        out_specs=[spec for spec, _ in outs],
        out_shape=[shape for _, shape in outs],
        scratch_shapes=[
            pltpu.VMEM((steps, rows, lanes), F32),
            pltpu.VMEM((steps + reach, rows, lanes), F32),
        ],
        compiler_params=pltpu.CompilerParams(vmem_limit_bytes=VMEM_LIMIT),
        cost_estimate=pl.CostEstimate(flops=1, transcendentals=0, bytes_accessed=1),
    )(proj, weight, grad, inputs, taps, shift)


def expert_kernel(
    kept, rows_ref, cotan_ref, router_ref, mask_ref, up_a, down_a, up_b, down_b, *refs
):
    out_ref, picked_ref, prob_ref, copy_ref, grad_ref, active_a, active_b, hidden_a, hidden_b = refs[kept:]
    rows = rows_ref[...]
    copy_ref[...] = rows
    logits = contract_cols(rows, router_ref[...])
    shifted = jnp.exp(logits - jnp.max(logits, axis=1, keepdims=True))
    prob = shifted / jnp.sum(shifted, axis=1, keepdims=True)
    gate = jnp.sum(prob * mask_ref[...], axis=1, keepdims=True)
    grad = (gate * cotan_ref[...].astype(F32)).astype(BF16)
    prob_ref[...] = prob
    grad_ref[...] = grad
    out, picked = None, None
    for up, down, active_ref, hidden_ref in (
        (up_a, down_a, active_a, hidden_a),
        (up_b, down_b, active_b, hidden_b),
    ):
        up, down = (value[...].reshape(-1, value.shape[2]) for value in (up, down))
        hidden = jnp.dot(rows, up, preferred_element_type=F32)
        share = 0.5 + 0.5 * lax.erf(hidden * math.sqrt(0.5))
        slope = share + hidden * (jnp.exp(-0.5 * hidden * hidden) * (1.0 / math.sqrt(2 * math.pi)))
        active = (hidden * share).astype(BF16)
        active_ref[...] = active
        hidden_grad = (jnp.dot(grad, down, preferred_element_type=F32) * slope).astype(BF16)
        hidden_ref[...] = hidden_grad
        out_part = contract_cols(active, down)
        picked_part = contract_cols(hidden_grad, up)
        out = out_part if out is None else out + out_part
        picked = picked_part if picked is None else picked + picked_part
    out_ref[...] = out
    picked_ref[...] = picked


def expert_call(rows, cotan, router_t, mask, blocks, far_up, far_down, part, parts, kept):
    count, width = rows.shape
    shard, hidden = far_up.shape[1:]
    block = math.gcd(count, 512)
    base = part * (count // block)

    def rows_of(columns, low=0):
        return pl.BlockSpec((block, columns), lambda at: (at + low, 0))

    def whole(array):
        return pl.BlockSpec(array.shape, lambda at: (0, 0), pipeline_mode=pl.Buffered(1))

    def layer(array, at):
        return pl.BlockSpec(
            (array.shape[0], shard, hidden), lambda step: (0, at, 0), pipeline_mode=pl.Buffered(1)
        )

    experts = router_t.shape[0]
    inputs = (rows, cotan, router_t, mask, blocks, blocks, far_up, far_down)
    columns = (width, width, hidden, hidden, hidden, hidden)
    return pl.pallas_call(
        partial(expert_kernel, len(kept)),
        grid=(count // block,),
        in_specs=[
            rows_of(width), rows_of(width), whole(router_t), whole(mask),
            layer(blocks, 0), layer(blocks, 1), layer(far_up, 0), layer(far_down, 0),
            *[pl.BlockSpec(memory_space=pl.ANY)] * len(kept),
        ],
        out_specs=[
            rows_of(width), rows_of(width), rows_of(experts), *(rows_of(one, base) for one in columns)
        ],
        out_shape=[
            *(jax.ShapeDtypeStruct((count, one), F32) for one in (width, width, experts)),
            *(jax.ShapeDtypeStruct((parts * count, one), BF16) for one in columns),
        ],
        input_output_aliases={len(inputs) + at: 3 + at for at in range(len(kept))},
        compiler_params=pltpu.CompilerParams(vmem_limit_bytes=VMEM_LIMIT),
        cost_estimate=pl.CostEstimate(flops=1, transcendentals=0, bytes_accessed=1),
    )(*inputs, *kept)


def expert_exchange(value, experts):
    count = lax.axis_size("dp")
    groups = None
    if count != experts:
        groups = [
            [base + e for e in range(experts)] for base in range(0, count, experts)
        ]
    return lax.all_to_all(value, "dp", 0, 0, axis_index_groups=groups, tiled=True)


def by_ctx(first, second):
    lead = lax.axis_index("ctx") == 0
    return jnp.where(lead, first, second), jnp.where(lead, second, first)


def own_expert_blocks(up_shards, down_shards):
    experts, _, hidden = up_shards.shape
    count = lax.axis_size("dp")
    half = hidden // 2
    both = jnp.concatenate([up_shards, down_shards], axis=1)
    if lax.axis_size("ctx") == 2:
        both = by_ctx(both[:, :, :half], both[:, :, half:])[0]
    if count != experts:
        both = jnp.concatenate([both] * (count // experts), axis=0)
    return lax.all_to_all(both, "dp", 0, 0, tiled=True)


def other_hidden(both):
    rows = both.shape[1] // 2
    if lax.axis_size("ctx") == 2:
        return swapped(both[:, :rows], "ctx"), swapped(both[:, rows:], "ctx")
    half = both.shape[2] // 2
    return both[:, :rows, half:], both[:, rows:, half:]


def gather_kernel(count, parts, *refs):
    ins, outs = refs[:parts], refs[parts : 2 * parts]
    send_sem, recv_sem, own_sem = refs[2 * parts :]
    places = count // 2
    me = lax.axis_index("dp")
    place, side = lax.div(me, 2), lax.rem(me, 2)
    across = me + 1 - 2 * side
    barrier = pltpu.get_barrier_semaphore()

    def greet(device):
        pl.semaphore_signal(
            barrier, inc=1, device_id={"dp": device}, device_id_type=pl.DeviceIdType.MESH
        )

    greet(across)
    for step in (-1, 1):
        there = place + step

        @pl.when((there >= 0) & (there < places))
        def greet_place(step=step):
            greet(me + 2 * step)

    neighbours = 1 + (place > 0).astype(jnp.int32) + (place < places - 1).astype(jnp.int32)
    pl.semaphore_wait(barrier, neighbours)

    def copy(part, slot, kind, device, own):
        return pltpu.make_async_remote_copy(
            src_ref=ins[part] if own else outs[part].at[slot],
            dst_ref=outs[part].at[slot],
            send_sem=send_sem.at[kind, part, slot],
            recv_sem=recv_sem.at[part, slot],
            device_id={"dp": device},
            device_id_type=pl.DeviceIdType.MESH,
        )

    def passed_on(slot, steps, own, act):
        for step in steps:
            there = place + step

            @pl.when((there >= 0) & (there < places))
            def along(step=step):
                for part in range(parts):
                    act(copy(part, slot, step + 1, me + 2 * step, own))

        for part in range(parts):
            act(copy(part, slot, 1, across, own))

    def start(one):
        one.start()

    def sent(one):
        one.wait_send()

    mine = [
        pltpu.make_async_copy(ins[part], outs[part].at[me], own_sem.at[part])
        for part in range(parts)
    ]
    for one in mine:
        one.start()
    passed_on(me, (-1, 1), True, start)
    for far in range(1, places):
        for step in (-1, 1):
            origin = place - step * far

            @pl.when((origin >= 0) & (origin < places))
            def forward(step=step, far=far):
                slot = me - 2 * step * far
                for part in range(parts):
                    copy(part, slot, 1, across, False).wait_recv()
                passed_on(slot, (step,), False, start)

    for at in range(places):
        for part in range(parts):
            copy(part, 2 * at + 1 - side, 1, across, False).wait_recv()
    for one in mine:
        one.wait()
    passed_on(me, (-1, 1), True, sent)
    for far in range(1, places):
        for step in (-1, 1):
            origin = place - step * far

            @pl.when((origin >= 0) & (origin < places))
            def forwarded(step=step, far=far):
                passed_on(me - 2 * step * far, (step,), False, sent)


def gathered(*values):
    count = lax.axis_size("dp")
    parts = len(values)
    anywhere = pl.BlockSpec(memory_space=pl.ANY)
    size = sum(math.prod(value.shape) * 2 for value in values)
    return pl.pallas_call(
        partial(gather_kernel, count, parts),
        in_specs=[anywhere] * parts,
        out_specs=[anywhere] * parts,
        out_shape=[jax.ShapeDtypeStruct((count, *value.shape), value.dtype) for value in values],
        scratch_shapes=[
            pltpu.SemaphoreType.DMA((3, parts, count)),
            pltpu.SemaphoreType.DMA((parts, count)),
            pltpu.SemaphoreType.DMA((parts,)),
        ],
        compiler_params=pltpu.CompilerParams(collective_id=0, has_side_effects=True),
        cost_estimate=pl.CostEstimate(
            flops=0, transcendentals=0, bytes_accessed=2 * count * size
        ),
    )(*values)


def other_joined(own, first_shard, second_shard):
    count = lax.axis_size("ctx")
    if count == 2:
        return by_ctx(own, swapped(own, "ctx"))
    del first_shard, second_shard
    every = lax.all_gather(own, "ctx")
    return every[0], every[1]


def expert_weight_products(rows, hidden_grads, grads, actives):
    pairs = ((rows, hidden_grads), (grads, actives))
    far = [contract_rows(left, rights[1]) for left, rights in pairs]
    if lax.axis_size("ctx") == 2:
        far = [value.astype(BF16) for value in far]
    return [contract_rows(left, rights[0]) for left, rights in pairs], far


def sent_far(value):
    return swapped(value, "ctx") if lax.axis_size("ctx") == 2 else value


def expert_weight_parts(near, far):
    count = lax.axis_size("dp")
    parts = []
    for own, other in zip(near, far):
        if lax.axis_size("ctx") == 2:
            part = own + other.astype(F32)
        else:
            part = lax.psum_scatter(
                jnp.concatenate([own, other], axis=1), "ctx", scatter_dimension=1, tiled=True
            )
        parts.append(part.astype(BF16).reshape(count, part.shape[0] // count, part.shape[1]))
    return jnp.concatenate(parts, axis=1)


def expert_weight_blocks(blocks, experts):
    count = lax.axis_size("dp")
    if count != experts:
        blocks = jnp.sum(
            blocks.reshape(count // experts, experts, *blocks.shape[1:]).astype(F32), axis=0
        ).astype(BF16)
    shard = blocks.shape[1] // 2
    return blocks[:, :shard], blocks[:, shard:]


def far_hidden(blocks):
    if lax.axis_size("ctx") == 2:
        return swapped(blocks, "ctx")
    return lax.all_gather(blocks, "ctx", axis=2, tiled=True)


def expert_weight_grad(blocks, far_blocks):
    if lax.axis_size("ctx") == 2:
        far_blocks = jnp.concatenate(by_ctx(blocks, far_blocks), axis=2)
    return far_blocks.astype(F32)


def pair_products(first, second):
    if lax.axis_size("ctx") != 2:
        return contract_rows(*first), contract_rows(*second).astype(BF16)
    lefts, rights = by_ctx(first[0], second[0]), by_ctx(first[1], second[1])
    return contract_rows(lefts[0], rights[0]), contract_rows(lefts[1], rights[1]).astype(BF16)


def product_part(near, far):
    count = lax.axis_size("dp")

    def blocks(value):
        return value.astype(BF16).reshape(count, value.shape[0] // count, value.shape[1])

    if lax.axis_size("ctx") != 2:
        return jnp.concatenate([blocks(near), blocks(far)], axis=1)
    return blocks(near + far.astype(F32))


def product_shards(blocks):
    sums = jnp.sum(blocks.astype(F32), axis=0)
    if lax.axis_size("ctx") == 2:
        return by_ctx(sums, swapped(sums, "ctx"))
    sums = lax.psum(sums, "ctx")
    rows = sums.shape[0] // 2
    return sums[:rows], sums[rows:]


def local(
    hidden_in,
    out_grad,
    norm1_gain,
    in_weight,
    conv_weight,
    conv_bias,
    xproj_weight,
    dt_weight,
    dt_bias,
    decay_log,
    skip_weight,
    out_weight,
    norm2_gain,
    router_weight,
    fc1_weight,
    fc2_weight,
    expert_ids,
    keep_mask,
):
    batches, seqs, length, model_width = hidden_in.shape
    chains = batches * seqs
    tokens = chains * length
    steps = length // SEGMENTS
    shard, _, inner = in_weight.shape
    taps = conv_weight.shape[0]
    low_rank = dt_weight.shape[0]
    states = decay_log.shape[0]
    experts = fc1_weight.shape[0]
    dp_count = lax.axis_size("dp")
    tp_count = lax.axis_size("tp")
    capacity = tokens // 4
    part_cap = capacity // tp_count // HALVES
    slots = experts * part_cap
    tp_index = lax.axis_index("tp")
    scan = Scan(steps, chains, states, inner)

    def to_rows(value):
        value = value.reshape(chains, SEGMENTS, steps, -1).transpose(2, 0, 1, 3)
        return value.reshape(tokens, -1)

    def from_rows(value):
        value = value.reshape(steps, chains, SEGMENTS, -1).transpose(1, 2, 0, 3)
        return value.reshape(batches, seqs, length, -1)

    pieces = [
        norm1_gain[None],
        conv_weight,
        conv_bias[None],
        dt_weight,
        dt_bias[None],
        decay_log,
        skip_weight[None],
        norm2_gain[None],
        router_weight.T,
        xproj_weight.T,
    ]
    bounds = [0]
    for piece in pieces:
        bounds.append(bounds[-1] + piece.shape[0])
    small = sum(
        jnp.pad(piece, ((low, bounds[-1] - high), (0, 0)))
        for piece, low, high in zip(pieces, bounds, bounds[1:])
    )
    kinds = small.shape[0]
    small_wide = jnp.pad(small.T, ((0, 0), (0, -kinds % LANES)))
    in_x, small_all, later = gathered(
        in_weight[:, 0], small_wide, by_ctx(out_weight.T, in_weight[:, 1])[0]
    )
    in_x = in_x.reshape(dp_count * shard, inner)
    later = later.reshape(dp_count * shard, inner)
    small_all = small_all.reshape(dp_count * shard, -1)[:, :kinds].T
    small_all, up_shards, down_shards = together(
        small_all, fc1_weight, fc2_weight.transpose(0, 2, 1)
    )
    pieces = [small_all[bounds[i] : bounds[i + 1]] for i in range(len(bounds) - 1)]
    gain_one_f = pieces[0].astype(F32)
    tap_weights = pieces[1].astype(F32)
    conv_shift = pieces[2].astype(F32)
    dt_proj = pieces[3]
    dt_shift = pieces[4].astype(F32)
    decay_rate = -jnp.exp(pieces[5].astype(F32))
    skip_row = pieces[6].astype(F32)
    gain_two_f = pieces[7].astype(F32)
    router_t = pieces[8]
    x_proj_t = pieces[9]
    rate_rows = jnp.broadcast_to((decay_rate * LOG2E)[:, None, :], (states, SEGMENTS, inner))
    expert_blocks = own_expert_blocks(up_shards, down_shards)

    route = to_rows(expert_ids)[:, 0]
    keep = to_rows(keep_mask)[:, 0].astype(F32)
    onehot_int = (route[:, None] == jnp.arange(experts, dtype=jnp.int32)[None, :]).astype(jnp.int32)
    rank = jnp.sum((jnp.cumsum(onehot_int, axis=0) - 1) * onehot_int, axis=1)
    places = []
    for half in range(HALVES):
        own = rank - (tp_index * HALVES + half) * part_cap
        token_slot = jnp.where((own >= 0) & (own < part_cap), route * part_cap + own, -1)
        places.append(
            (token_slot[None, :] == jnp.arange(slots, dtype=jnp.int32)[:, None]).astype(BF16)
        )

    def slotted(value, half):
        sent = jnp.dot(places[half], value, preferred_element_type=F32).astype(BF16)
        return sent.reshape(experts, part_cap, -1)

    def landed(values):
        total = sum(
            contract_rows(place, value.reshape(slots, -1)) for place, value in zip(places, values)
        )
        return axis_sum(total.astype(BF16), "tp").astype(F32)

    def halves_of(value):
        return [value[:, at : at + part_cap] for at in range(0, value.shape[1], part_cap)]

    cotan_bf = to_rows(out_grad)
    cotan = cotan_bf.astype(F32)
    kept_cotan = (cotan * keep[:, None]).astype(BF16)
    sent_cotan = jnp.concatenate([slotted(kept_cotan, half) for half in range(HALVES)], axis=1)

    values = to_rows(hidden_in).astype(F32)
    normalized_rows, inverse_one = rms_forward(values, gain_one_f)
    normed_bf = normalized_rows.astype(BF16)
    x_pre = jnp.dot(normed_bf, in_x, preferred_element_type=F32).astype(BF16)
    x_pre = x_pre.reshape(steps, chains, SEGMENTS, inner)
    tail = x_pre[steps - taps + 1 :]
    edge_in = passed_along(tail[:, :, SEGMENTS - 1 :], "ctx", 1)
    edge_in, later = together(edge_in, later)
    out_proj_t, in_z = other_joined(later, out_weight.T, in_weight[:, 1])
    halo = jnp.concatenate([edge_in, tail[:, :, : SEGMENTS - 1]], axis=2)
    extended_bf = jnp.concatenate([halo, x_pre], axis=0)
    extended = extended_bf.astype(F32)
    conv_pre = jnp.broadcast_to(conv_shift[0], x_pre.shape)
    for tap in range(taps):
        conv_pre = conv_pre + tap_weights[tap] * extended[tap : tap + steps]
    xconv_bf = jax.nn.silu(conv_pre).astype(BF16)
    xconv = xconv_bf.astype(F32)
    xconv_rows = xconv_bf.reshape(tokens, inner)
    projected = axis_sum(contract_cols(xconv_rows, x_proj_t), "tp")
    dt_low = projected[:, :low_rank].astype(BF16)

    def mixes(value):
        value = value.reshape(steps, chains, SEGMENTS, states).transpose(1, 0, 3, 2)
        return jnp.broadcast_to(value[..., None], (*value.shape, LANES))

    mix_in = mixes(projected[:, low_rank : low_rank + states])
    mix_out = mixes(projected[:, low_rank + states :])
    dt_pre = (jnp.dot(dt_low, dt_proj, preferred_element_type=F32) + dt_shift).reshape(x_pre.shape)
    step_size = jax.nn.softplus(dt_pre)
    seg_decay, seg_state, last_state = scan.ends(step_size, xconv, mix_in, rate_rows)
    sent_cotan, expert_blocks, _ = together(sent_cotan, expert_blocks, seg_state)
    slot_cotan = expert_exchange(sent_cotan, experts)
    entering = entering_pieces(seg_decay[:, :, SEGMENTS - 1], last_state, "ctx", False)
    entering, expert_blocks = together(entering, expert_blocks)
    far_up, far_down = other_hidden(expert_blocks)
    scan_out, seg_start = scan.run(
        step_size, xconv, mix_in, mix_out, rate_rows, seg_decay, seg_state, entering
    )
    z_gate = jnp.dot(normed_bf, in_z, preferred_element_type=F32).reshape(x_pre.shape)
    scanned = scan_out + skip_row[0] * xconv
    z_silu = jax.nn.silu(z_gate)
    gated_bf = (scanned * z_silu).astype(BF16).reshape(tokens, inner)
    gated_bf, slot_cotan, far_up = together(gated_bf, slot_cotan, far_up)
    middle = values + axis_sum(contract_cols(gated_bf, out_proj_t), "tp")

    normed_two, inverse_two = rms_forward(middle, gain_two_f)
    normed_two_bf = normed_two.astype(BF16)
    expert_mask = (
        jnp.arange(experts, dtype=jnp.int32) == lax.rem(lax.axis_index("dp"), experts)
    ).astype(F32)[None, :]
    kept = ()
    got_grads, slot_outs, router_grad_t = [], [], 0.0
    for half, half_cotan in enumerate(halves_of(slot_cotan)):
        own_rows = expert_exchange(slotted(normed_two_bf, half), experts)
        if not half:
            own_rows, far_down = together(own_rows, far_down)
        else:
            own_rows, kept = together(own_rows, kept)
        own_rows = own_rows.reshape(slots, model_width)
        half_cotan = half_cotan.reshape(slots, model_width)
        far_rows, far_cotan = swapped(own_rows, "tp"), swapped(half_cotan, "tp")
        call = partial(
            expert_call, router_t=router_t, mask=expert_mask, blocks=expert_blocks, far_up=far_up,
            far_down=far_down, parts=2 * HALVES,
        )
        far = call(far_rows, far_cotan, part=2 * half, kept=kept)
        near = call(own_rows, half_cotan, part=2 * half + 1, kept=far[3:])
        if half:
            near, got_grads = together(near, got_grads)
        kept = near[3:]
        slot_out = near[0] + swapped(far[0], "tp")
        picked_grad = near[1] + swapped(far[1], "tp")
        slot_prob = near[2]
        slot_gate = jnp.sum(slot_prob * expert_mask, axis=1, keepdims=True)
        gate_grad = jnp.sum(slot_out * half_cotan.astype(F32), axis=1, keepdims=True)
        logit_grad = gate_grad * slot_gate * (expert_mask - slot_prob)
        router_grad_t = router_grad_t + contract_rows(logit_grad, own_rows.astype(F32), HIGHEST)
        picked_grad = picked_grad + jnp.dot(
            logit_grad, router_t.astype(F32), precision=HIGHEST, preferred_element_type=F32
        )
        got_grads.append(
            expert_exchange(picked_grad.astype(BF16).reshape(experts, part_cap, -1), experts)
        )
        slot_outs.append(slot_out.astype(BF16).reshape(experts, part_cap, -1))
    router_grad_t = axis_sum(router_grad_t, "tp")
    all_rows, all_grads, active_a, active_b, hidden_a, hidden_b = kept
    near_parts, far_parts = expert_weight_products(
        all_rows, (hidden_a, hidden_b), all_grads, (active_a, active_b)
    )
    far_first = sent_far(far_parts[0])
    got_grads, near_parts, far_second, far_first, slot_outs = together(
        got_grads, near_parts, far_parts[1], far_first, slot_outs
    )
    far_parts = far_first, sent_far(far_second)
    normed_two_grad = landed(got_grads)
    got_out = expert_exchange(jnp.concatenate(slot_outs, axis=1), experts)
    middle_norm_grad, gain_two_grad = rms_backward(middle, inverse_two, gain_two_f, normed_two_grad)
    middle_grad = cotan + middle_norm_grad
    mixer_grad_bf = middle_grad.astype(BF16)
    gated_grad = jnp.dot(mixer_grad_bf, out_proj_t, preferred_element_type=F32).reshape(x_pre.shape)
    scan_grad = gated_grad * z_silu
    z_grad = jax.vjp(jax.nn.silu, z_gate)[1](gated_grad * scanned)[0]
    z_grad_bf = z_grad.astype(BF16).reshape(tokens, inner)
    near_product, far_product = pair_products((mixer_grad_bf, gated_bf), (normed_bf, z_grad_bf))
    weight_parts = expert_weight_parts(near_parts, far_parts)
    scan_grad, weight_parts, got_out = together(scan_grad, weight_parts, got_out)
    weight_blocks = lax.all_to_all(weight_parts, "dp", 0, 0, tiled=True)
    back_decay, back_adjoint, first_adjoint = scan.adjoint_ends(
        step_size, mix_out, scan_grad, rate_rows
    )
    leaving = entering_pieces(back_decay[:, :, 0], first_adjoint, "ctx", True)
    leaving, near_product, far_product = together(leaving, near_product, far_product)
    far_product = sent_far(far_product)
    adjoint_args = (
        step_size, xconv, mix_in, mix_out, scan_grad, rate_rows, seg_start, back_decay, back_adjoint,
        leaving, skip_row,
    )
    pre_grad, xconv_grad, decay_sum, scan_sums, mix_grad = scan.adjoint(adjoint_args)
    pre_grad, far_product, weight_blocks = together(pre_grad, far_product, weight_blocks)
    weight_blocks = expert_weight_blocks(weight_blocks, experts)
    far_ups = far_hidden(weight_blocks[0])
    out_blocks = lax.all_to_all(product_part(near_product, far_product), "dp", 0, 0, tiled=True)
    decay_log_grad = jnp.sum(decay_sum, axis=0) * decay_rate
    dt_shift_grad, skip_grad = jnp.sum(scan_sums, axis=0)[:2]
    pre_grad = pre_grad.reshape(tokens, inner)
    dt_proj_grad = contract_rows(dt_low.astype(F32), pre_grad, HIGHEST)
    dt_low_grad = contract_cols(pre_grad, dt_proj.astype(F32), HIGHEST)
    mix_grad = mix_grad.reshape(tokens, LANES)[:, : 2 * states]
    proj_part = jnp.concatenate([dt_low_grad, mix_grad], axis=1)
    proj_grad_bf = axis_sum(proj_part, "tp").astype(BF16)
    x_proj_grad_t = contract_rows(proj_grad_bf, xconv_rows)
    flat = (chains * SEGMENTS, inner)
    x_grad_bf, conv_sums, head, last = conv_back(
        proj_grad_bf,
        x_proj_t,
        xconv_grad.reshape(steps, *flat),
        extended_bf.reshape(steps + taps - 1, *flat),
        tap_weights,
        conv_shift,
    )
    taps_grad, shift_grad = conv_sums[:taps], conv_sums[taps]
    edge_back = passed_along(
        head.reshape(taps - 1, chains, SEGMENTS, inner)[:, :, :1], "ctx", -1
    )
    edge_back, out_blocks, far_ups = together(edge_back, out_blocks, far_ups)
    reaching = jnp.stack(
        [
            sum(tap_weights[tap] * edge_back[at - tap] for tap in range(at + 1))
            for at in range(taps - 1)
        ]
    )
    reaching = jnp.pad(reaching, ((0, 0), (0, 0), (SEGMENTS - 1, 0), (0, 0)))
    last = (last + reaching.reshape(taps - 1, *flat)).astype(BF16)
    x_grad_bf = lax.dynamic_update_slice(x_grad_bf, last, (steps - taps + 1, 0, 0))
    x_grad_bf = x_grad_bf.reshape(tokens, inner)
    small_grads = jnp.concatenate(
        [
            taps_grad,
            shift_grad[None],
            dt_proj_grad,
            dt_shift_grad[None],
            decay_log_grad,
            skip_grad[None],
            gain_two_grad[None],
            router_grad_t,
            x_proj_grad_t,
        ],
        axis=0,
    )
    small_grads = small_grads.reshape(-1, dp_count, shard).transpose(1, 0, 2)
    x_grad_bf, small_grads, out_blocks = together(x_grad_bf, small_grads, out_blocks)
    small_blocks = lax.all_to_all(small_grads, "dp", 0, 0, tiled=True)
    normed_part = contract_cols(x_grad_bf, in_x) + contract_cols(z_grad_bf, in_z)
    normed_grad, small_blocks = together(axis_sum(normed_part, "tp"), small_blocks)
    values_norm_grad, gain_one_grad = rms_backward(values, inverse_one, gain_one_f, normed_grad)
    input_grad = from_rows((middle_grad + values_norm_grad).astype(BF16))

    in_x_part = contract_rows(normed_bf, x_grad_bf).astype(BF16).reshape(dp_count, shard, inner)
    gain_row = gain_one_grad.reshape(dp_count, 1, shard)
    gain_high = gain_row.astype(BF16)
    gain_low = (gain_row - gain_high.astype(F32)).astype(BF16)
    gain_rows = jnp.concatenate([gain_high, gain_low], axis=1)
    gain_rows = jnp.pad(gain_rows, ((0, 0), (0, 6), (0, inner - shard)))
    in_x_part, out_blocks = together(in_x_part, out_blocks)
    out_proj_grad, in_z_grad = product_shards(out_blocks)
    small_grads = axis_sum(jnp.sum(small_blocks, axis=0), "ctx")
    in_x_blocks = lax.all_to_all(
        jnp.concatenate([in_x_part, gain_rows], axis=1), "dp", 0, 0, tiled=True
    )
    out_proj_grad, in_z_grad, small_grads, far_down_blocks = together(
        out_proj_grad, in_z_grad, small_grads, weight_blocks[1]
    )
    far_downs, in_x_blocks = together(far_hidden(far_down_blocks), in_x_blocks)
    first_grad = expert_weight_grad(weight_blocks[0], far_ups)
    second_grad = expert_weight_grad(weight_blocks[1], far_downs)
    router_prob = jax.nn.softmax(contract_cols(normed_two_bf, router_t), axis=-1)
    gate_prob = jnp.sum(router_prob * onehot_int.astype(F32), axis=1) * keep
    result = from_rows((middle + gate_prob[:, None] * landed(halves_of(got_out))).astype(BF16))
    in_x_sums = axis_sum(jnp.sum(in_x_blocks.astype(F32), axis=0), "ctx")
    in_x_grad = in_x_sums[:shard]
    gain_one_grad = in_x_sums[shard : shard + 1, :shard] + in_x_sums[shard + 1 : shard + 2, :shard]
    small_grads = jnp.concatenate([gain_one_grad, small_grads], axis=0)
    sums = [small_grads[bounds[i] : bounds[i + 1]] for i in range(len(bounds) - 1)]
    return (
        result,
        input_grad,
        sums[0][0],
        jnp.stack([in_x_grad, in_z_grad], axis=1),
        sums[1],
        sums[2][0],
        sums[9].T,
        sums[3],
        sums[4][0],
        sums[5],
        sums[6][0],
        out_proj_grad.T,
        sums[7][0],
        sums[8].T,
        first_grad,
        second_grad.transpose(0, 2, 1),
    )


def solution(mesh):
    weights = (
        P("dp"),
        P("dp", None, "tp"),
        P(None, ("tp", "dp")),
        P(("tp", "dp")),
        P(("tp", "dp"), None),
        P(None, ("tp", "dp")),
        P(("tp", "dp")),
        P(None, ("tp", "dp")),
        P(("tp", "dp")),
        P("tp", "dp"),
        P("dp"),
        P("dp", None),
        P(None, "dp", "tp"),
        P(None, "tp", "dp"),
    )
    rows = P(None, "dp", "ctx", None)
    return jax.shard_map(
        local,
        mesh=mesh,
        in_specs=(rows, rows, *weights, P(("dp", "ctx"), None), P(("dp", "ctx"))),
        out_specs=(rows, rows, *weights),
        check_vma=False,
    )
```

```python
from functools import partial
import math

import jax
import jax.numpy as jnp
from jax import lax
from jax.experimental import pallas as pl
from jax.experimental.pallas import tpu as pltpu
from jax.sharding import PartitionSpec as P

EPSILON = 1e-05
HIGHEST = lax.Precision.HIGHEST
SEGMENTS = 8
LANES = 128
VMEM_LIMIT = 56 * 1024 * 1024
EXPERT_VMEM = 56 * 1024 * 1024
LOG2E = math.log2(math.e)
GROUP_A = 4
GROUP_B = 4
GROUP_C = 8
UNROLL_A = 8
UNROLL_B = 8
UNROLL_C = 8
UNROLL_D = 4
UNROLL_E = 8
BLOCKS = 3
COVER = 100
HALVES = 1
BF16 = jnp.bfloat16
F32 = jnp.float32


def swapped(value, axis):
    return lax.ppermute(value, axis, [(0, 1), (1, 0)])


def passed_along(value, axis, steps):
    count = lax.axis_size(axis)
    leading, last = (max(0, -steps), min(count, count - steps))
    return lax.ppermute(value, axis, [(source, source + steps) for source in range(leading, last)])


def axis_sum(value, axis):
    if lax.axis_size(axis) == 2:
        return value + swapped(value, axis)
    return lax.psum(value, axis)


def together(*values):
    return lax.optimization_barrier(values)


def entering_pieces(decay, value, axis, backward):
    count = lax.axis_size(axis)
    if count == 2:
        return passed_along(value, axis, -1 if backward else 1)
    mine = lax.axis_index(axis)
    decays = lax.all_gather(decay, axis)
    values = lax.all_gather(value, axis)
    running = jnp.zeros_like(value)
    for position in range(count - 1):
        at = count - 1 - position if backward else position
        longer = values[at] + decays[at] * running
        ahead = at > mine if backward else at < mine
        running = jnp.where(ahead, longer, running)
    return running


def contract_rows(left_side, right_side, precision=None):
    return lax.dot_general(
        left_side,
        right_side,
        (((0,), (0,)), ((), ())),
        precision=precision,
        preferred_element_type=F32,
    )


def contract_cols(left_side, right_side, precision=None):
    return lax.dot_general(
        left_side,
        right_side,
        (((1,), (1,)), ((), ())),
        precision=precision,
        preferred_element_type=F32,
    )


def rms_forward(values, gain_vec):
    inverse = lax.rsqrt(jnp.mean(values * values, axis=-1, keepdims=True) + EPSILON)
    return (values * inverse * gain_vec, inverse)


def rms_backward(values, inverse, gain_vec, grad_out):
    weighted = grad_out * gain_vec
    inner_mean = jnp.mean(values * weighted, axis=-1, keepdims=True)
    grad_values = inverse * weighted - values * inverse * inverse * inverse * inner_mean
    grad_gain = jnp.sum(grad_out * values * inverse, axis=0)
    return (grad_values, grad_gain)


def zeros_of(ref):
    return jnp.zeros(ref.shape[1:], F32)


def sublane_rows(lanes):
    return lax.broadcasted_iota(jnp.int32, (SEGMENTS, lanes), 0)


def widened(value, lanes):
    return jnp.concatenate([value] * (lanes // LANES), axis=1) if lanes > LANES else value


def narrowed(value):
    parts = [value[:, at : at + LANES] for at in range(0, value.shape[1], LANES)]
    return sum(parts[1:], parts[0])


def groups_of(states, size):
    size = math.gcd(states, size)
    return [range(first, first + size) for first in range(0, states, size)]


def joined_forward(decay, value, row):
    for reach in (1, 2, 4):
        inside = row >= reach
        value = value + jnp.where(inside, decay * pltpu.roll(value, reach, 0), 0.0)
        decay = jnp.where(inside, decay * pltpu.roll(decay, reach, 0), decay)
    return decay, value


def joined_backward(decay, value, row):
    for reach in (1, 2, 4):
        inside = row < SEGMENTS - reach
        value = value + jnp.where(inside, decay * pltpu.roll(value, SEGMENTS - reach, 0), 0.0)
        decay = jnp.where(inside, decay * pltpu.roll(decay, SEGMENTS - reach, 0), decay)
    return decay, value


def ends_kernel(step_ref, input_ref, mix_in_ref, rate_ref, decay_ref, state_ref, last_ref):
    steps, states, lanes = step_ref.shape[0], mix_in_ref.shape[1], step_ref.shape[2]
    zero = zeros_of(step_ref)
    row = sublane_rows(lanes)
    total = lax.fori_loop(0, steps, lambda at, total: total + step_ref[at], zero, unroll=UNROLL_E)
    for members in groups_of(states, GROUP_A):
        rates = [rate_ref[n] for n in members]

        def body(at, held):
            step = step_ref[at]
            driven = step * input_ref[at]
            return tuple(
                jnp.exp2(step * rate) * before + widened(mix_in_ref[at, n], lanes) * driven
                for n, rate, before in zip(members, rates, held)
            )

        held = lax.fori_loop(0, steps, body, (zero,) * len(members), unroll=UNROLL_A)
        for n, rate, end in zip(members, rates, held):
            decay, value = joined_forward(jnp.exp2(total * rate), end, row)
            decay_ref[n] = decay
            state_ref[n] = value
            last_ref[n : n + 1] = value[SEGMENTS - 1 :]


def states_kernel(
    step_ref, input_ref, mix_in_ref, mix_out_ref, rate_ref, decay_ref, state_ref, enter_ref,
    out_ref, start_ref,
):
    steps, states, lanes = step_ref.shape[0], mix_in_ref.shape[1], step_ref.shape[2]
    row = sublane_rows(lanes)
    for members in groups_of(states, GROUP_B):
        rates = [rate_ref[n] for n in members]
        held = []
        for n in members:
            first = jnp.broadcast_to(enter_ref[n : n + 1], (SEGMENTS, lanes))
            inner = pltpu.roll(state_ref[n], 1, 0) + pltpu.roll(decay_ref[n], 1, 0) * first
            start = jnp.where(row >= 1, inner, first)
            start_ref[n] = start
            held.append(start)

        def body(at, held):
            step = step_ref[at]
            driven = step * input_ref[at]
            held = tuple(
                jnp.exp2(step * rate) * before + widened(mix_in_ref[at, n], lanes) * driven
                for n, rate, before in zip(members, rates, held)
            )
            parts = [widened(mix_out_ref[at, n], lanes) * now for n, now in zip(members, held)]
            if members[0]:
                parts.append(out_ref[at])
            while len(parts) > 1:
                parts = [sum(parts[i + 1 : i + 2], parts[i]) for i in range(0, len(parts), 2)]
            out_ref[at] = parts[0]
            return held

        lax.fori_loop(0, steps, body, tuple(held), unroll=UNROLL_B)


def adjoint_ends_kernel(step_ref, mix_out_ref, grad_ref, rate_ref, decay_ref, adjoint_ref, first_ref):
    steps, states, lanes = step_ref.shape[0], mix_out_ref.shape[1], step_ref.shape[2]
    zero = zeros_of(step_ref)
    row = sublane_rows(lanes)
    total = lax.fori_loop(0, steps, lambda at, total: total + step_ref[at], zero, unroll=UNROLL_E)
    for members in groups_of(states, GROUP_A):
        rates = [rate_ref[n] for n in members]

        def body(back, incoming):
            at = steps - 1 - back
            step = step_ref[at]
            grad = grad_ref[at]
            return tuple(
                jnp.exp2(step * rate) * (widened(mix_out_ref[at, n], lanes) * grad + after)
                for n, rate, after in zip(members, rates, incoming)
            )

        incoming = lax.fori_loop(0, steps, body, (zero,) * len(members), unroll=UNROLL_A)
        for n, rate, end in zip(members, rates, incoming):
            decay, value = joined_backward(jnp.exp2(total * rate), end, row)
            decay_ref[n] = decay
            adjoint_ref[n] = value
            first_ref[n : n + 1] = value[:1]


def adjoint_kernel(
    step_ref, input_ref, mix_in_ref, mix_out_ref, grad_ref, rate_ref, start_ref, decay_ref, adjoint_ref,
    enter_ref, skip_ref,
    pre_ref, conv_ref, decay_sum_ref, sums_ref, mix_ref, states_ref, decays_ref, in_grad_ref, out_grad_ref,
):
    steps, states, lanes = step_ref.shape[0], mix_in_ref.shape[1], step_ref.shape[2]
    row = sublane_rows(lanes)
    zero = zeros_of(step_ref)

    @pl.when(pl.program_id(1) == 0)
    def clear():
        in_grad_ref[...] = jnp.zeros_like(in_grad_ref)
        out_grad_ref[...] = jnp.zeros_like(out_grad_ref)

    for members in groups_of(states, GROUP_C):
        first, group = members[0], len(members)
        rates = [rate_ref[n] for n in members]

        def ahead(at, held):
            step = step_ref[at]
            driven = step * input_ref[at]
            grad = grad_ref[at]
            after = []
            for i, n in enumerate(members):
                states_ref[at, i] = held[i]
                decay = jnp.exp2(step * rates[i])
                decays_ref[at, i] = decay
                now = decay * held[i] + widened(mix_in_ref[at, n], lanes) * driven
                out_grad_ref[at, n] += narrowed(grad * now)
                after.append(now)
            return tuple(after)

        lax.fori_loop(0, steps, ahead, tuple(start_ref[n] for n in members), unroll=UNROLL_C)

        incoming = []
        for n in members:
            final = jnp.broadcast_to(enter_ref[n : n + 1], (SEGMENTS, lanes))
            inner = (
                pltpu.roll(adjoint_ref[n], SEGMENTS - 1, 0)
                + pltpu.roll(decay_ref[n], SEGMENTS - 1, 0) * final
            )
            incoming.append(jnp.where(row < SEGMENTS - 1, inner, final))

        def body(back, carry):
            at = steps - 1 - back
            incoming, decay_sums = carry
            step = step_ref[at]
            grad = grad_ref[at]
            driven = step * input_ref[at]
            in_sum = conv_ref[at] if first else zero
            rate_sum = pre_ref[at] if first else zero
            following, sums = [], []
            for i, n in enumerate(members):
                adjoint = widened(mix_out_ref[at, n], lanes) * grad + incoming[i]
                onward = decays_ref[at, i] * adjoint
                decay_grad = onward * states_ref[at, i]
                in_sum = in_sum + adjoint * widened(mix_in_ref[at, n], lanes)
                rate_sum = rate_sum + decay_grad * rates[i]
                sums.append(decay_sums[i] + decay_grad * step)
                in_grad_ref[at, n] += narrowed(adjoint * driven)
                following.append(onward)
            conv_ref[at] = in_sum
            pre_ref[at] = rate_sum
            return tuple(following), tuple(sums)

        _, sums = lax.fori_loop(
            0, steps, body, (tuple(incoming), (zero,) * group), unroll=UNROLL_D
        )
        for i, n in enumerate(members):
            decay_sum_ref[n : n + 1] = jnp.sum(sums[i], axis=0, keepdims=True)

    skip = skip_ref[...]

    def close(at, carry):
        pre_sum, skip_sum = carry
        step, inputs, grad, in_sum = step_ref[at], input_ref[at], grad_ref[at], conv_ref[at]
        step_grad = pre_ref[at] * (1.0 / LOG2E) + in_sum * inputs
        pre = step_grad * (1.0 - jnp.exp2(step * -LOG2E))
        pre_ref[at] = pre
        conv_ref[at] = in_sum * step + skip * grad
        return pre_sum + pre, skip_sum + grad * inputs

    pre_sum, skip_sum = lax.fori_loop(0, steps, close, (zero, zero), unroll=UNROLL_E)
    sums_ref[0:1] = jnp.sum(pre_sum, axis=0, keepdims=True)
    sums_ref[1:2] = jnp.sum(skip_sum, axis=0, keepdims=True)
    sums_ref[2:] = jnp.zeros((SEGMENTS - 2, lanes), F32)

    @pl.when(pl.program_id(1) == pl.num_programs(1) - 1)
    def across_lanes():
        lane = lax.broadcasted_iota(jnp.int32, (SEGMENTS, LANES), 1)

        def one(at, carry):
            total = jnp.zeros((SEGMENTS, LANES), F32)
            for n in range(states):
                for base, ref in ((0, in_grad_ref), (states, out_grad_ref)):
                    value = jnp.sum(ref[at, n], axis=1, keepdims=True)
                    total = jnp.where(lane == base + n, value, total)
            mix_ref[at] = total
            return carry

        lax.fori_loop(0, steps, one, 0, unroll=UNROLL_E)


class Scan:
    def __init__(self, steps, chains, states, width):
        lanes = LANES * math.gcd(width // LANES, BLOCKS)
        self.grid = (chains, width // lanes)
        self.rows_spec = pl.BlockSpec(
            (steps, None, SEGMENTS, lanes), lambda chain, block: (0, chain, 0, block)
        )
        self.mix_spec = pl.BlockSpec(
            (None, steps, states, SEGMENTS, LANES), lambda chain, block: (chain, 0, 0, 0, 0)
        )
        self.rate_spec = pl.BlockSpec((states, SEGMENTS, lanes), lambda chain, block: (0, 0, block))
        self.state_spec = pl.BlockSpec(
            (None, states, SEGMENTS, lanes), lambda chain, block: (chain, 0, 0, block)
        )
        self.edge_spec = pl.BlockSpec((None, states, lanes), lambda chain, block: (chain, 0, block))
        self.rows = jax.ShapeDtypeStruct((steps, chains, SEGMENTS, width), F32)
        self.mix = jax.ShapeDtypeStruct((chains, steps, states, SEGMENTS, LANES), F32)
        self.state = jax.ShapeDtypeStruct((chains, states, SEGMENTS, width), F32)
        self.edge = jax.ShapeDtypeStruct((chains, states, width), F32)
        self.sums = jax.ShapeDtypeStruct((chains, SEGMENTS, width), F32)
        self.sums_spec = pl.BlockSpec((None, SEGMENTS, lanes), lambda chain, block: (chain, 0, block))
        self.lane_sums = jax.ShapeDtypeStruct((steps, chains, SEGMENTS, LANES), F32)
        self.lane_spec = pl.BlockSpec(
            (steps, None, SEGMENTS, LANES), lambda chain, block: (0, chain, 0, 0)
        )
        self.skip_spec = pl.BlockSpec((1, lanes), lambda chain, block: (0, block))
        self.scratch = [
            pltpu.VMEM((steps, math.gcd(states, GROUP_C), SEGMENTS, lanes), F32),
            pltpu.VMEM((steps, math.gcd(states, GROUP_C), SEGMENTS, lanes), F32),
            pltpu.VMEM((steps, states, SEGMENTS, LANES), F32),
            pltpu.VMEM((steps, states, SEGMENTS, LANES), F32),
        ]
        self.work = steps * chains * SEGMENTS * width * states

    def call(self, kernel, ops, args, in_specs, outs, out_specs, scratch=()):
        size = sum(math.prod(a.shape) * a.dtype.itemsize for a in (*args, *outs))
        return pl.pallas_call(
            kernel,
            grid=self.grid,
            in_specs=in_specs,
            out_specs=out_specs,
            out_shape=outs,
            scratch_shapes=list(scratch),
            compiler_params=pltpu.CompilerParams(vmem_limit_bytes=VMEM_LIMIT),
            cost_estimate=pl.CostEstimate(
                flops=ops * self.work, transcendentals=self.work, bytes_accessed=size // COVER
            ),
        )(*args)

    def ends(self, step, inputs, mix_in, rate):
        return self.call(
            ends_kernel, 5, (step, inputs, mix_in, rate),
            [self.rows_spec, self.rows_spec, self.mix_spec, self.rate_spec],
            [self.state, self.state, self.edge],
            [self.state_spec, self.state_spec, self.edge_spec],
        )

    def run(self, step, inputs, mix_in, mix_out, rate, decay, state, enter):
        return self.call(
            states_kernel, 7, (step, inputs, mix_in, mix_out, rate, decay, state, enter),
            [self.rows_spec, self.rows_spec, self.mix_spec, self.mix_spec, self.rate_spec,
             self.state_spec, self.state_spec, self.edge_spec],
            [self.rows, self.state],
            [self.rows_spec, self.state_spec],
        )

    def adjoint_ends(self, step, mix_out, grad, rate):
        return self.call(
            adjoint_ends_kernel, 5, (step, mix_out, grad, rate),
            [self.rows_spec, self.mix_spec, self.rows_spec, self.rate_spec],
            [self.state, self.state, self.edge],
            [self.state_spec, self.state_spec, self.edge_spec],
        )

    def adjoint(self, args):
        return self.call(
            adjoint_kernel, 20, args,
            [self.rows_spec, self.rows_spec, self.mix_spec, self.mix_spec, self.rows_spec,
             self.rate_spec, self.state_spec, self.state_spec, self.state_spec, self.edge_spec,
             self.skip_spec],
            [self.rows, self.rows, self.edge, self.sums, self.lane_sums],
            [self.rows_spec, self.rows_spec, self.edge_spec, self.sums_spec, self.lane_spec],
            self.scratch,
        )


def conv_back_kernel(
    proj_ref, weight_ref, grad_ref, input_ref, taps_ref, shift_ref,
    out_ref, sums_ref, head_ref, tail_ref, product_ref, conv_ref,
):
    steps, rows, lanes = grad_ref.shape
    count = taps_ref.shape[0]
    reach = count - 1
    taps = [taps_ref[at : at + 1] for at in range(count)]
    shift = shift_ref[...]
    product_ref[...] = jnp.dot(
        proj_ref[...], weight_ref[...], preferred_element_type=F32
    ).reshape(steps, rows, lanes)

    def slopes(at, sums):
        inputs = [input_ref[at + tap].astype(F32) for tap in range(count)]
        pre = shift + sum(tap * value for tap, value in zip(taps, inputs))
        share = 1.0 / (1.0 + jnp.exp(-pre))
        conv = (grad_ref[at] + product_ref[at]) * (share * (1.0 + pre * (1.0 - share)))
        conv_ref[at] = conv
        return (*(total + conv * value for total, value in zip(sums, inputs)), sums[-1] + conv)

    zero = jnp.zeros((rows, lanes), F32)
    sums = lax.fori_loop(0, steps, slopes, (zero,) * (count + 1), unroll=2)
    for at, total in enumerate(sums):
        sums_ref[at : at + 1] = jnp.sum(total, axis=0, keepdims=True)
    sums_ref[count + 1 :] = jnp.zeros((sums_ref.shape[0] - count - 1, lanes), F32)
    row = sublane_rows(lanes)
    for at in range(reach):
        head_ref[at] = conv_ref[at]
        for low in range(0, rows, SEGMENTS):
            rolled = pltpu.roll(conv_ref[at, low : low + SEGMENTS], SEGMENTS - 1, 0)
            conv_ref[steps + at, low : low + SEGMENTS] = jnp.where(
                row < SEGMENTS - 1, rolled, 0.0
            )

    def back(at):
        return sum(taps[tap] * conv_ref[at + reach - tap] for tap in range(count))

    def store(at, carry):
        out_ref[at] = back(at).astype(BF16)
        return carry

    lax.fori_loop(0, steps, store, 0, unroll=2)
    for at in range(reach):
        tail_ref[at] = back(steps - reach + at)


def conv_back(proj, weight, grad, inputs, taps, shift):
    steps, rows, width = grad.shape
    reach = taps.shape[0] - 1
    lanes = LANES * math.gcd(width // LANES, BLOCKS)

    def block(count, dtype=F32):
        spec = pl.BlockSpec((count, rows, lanes), lambda at: (0, 0, at))
        return spec, jax.ShapeDtypeStruct((count, rows, width), dtype)

    def columns(count):
        return pl.BlockSpec((count, lanes), lambda at: (0, at))

    outs = [
        block(steps, BF16),
        (columns(SEGMENTS), jax.ShapeDtypeStruct((SEGMENTS, width), F32)),
        block(reach),
        block(reach),
    ]
    return pl.pallas_call(
        conv_back_kernel,
        grid=(width // lanes,),
        in_specs=[
            pl.BlockSpec(proj.shape, lambda at: (0, 0)),
            columns(weight.shape[0]),
            block(steps)[0],
            block(steps + reach)[0],
            columns(reach + 1),
            columns(1),
        ],
        out_specs=[spec for spec, _ in outs],
        out_shape=[shape for _, shape in outs],
        scratch_shapes=[
            pltpu.VMEM((steps, rows, lanes), F32),
            pltpu.VMEM((steps + reach, rows, lanes), F32),
        ],
        compiler_params=pltpu.CompilerParams(vmem_limit_bytes=VMEM_LIMIT),
        cost_estimate=pl.CostEstimate(flops=1, transcendentals=0, bytes_accessed=1),
    )(proj, weight, grad, inputs, taps, shift)


def expert_kernel(
    kept, rows_ref, cotan_ref, router_ref, mask_ref, up_a, down_a, up_b, down_b, *refs
):
    out_ref, picked_ref, prob_ref, copy_ref, grad_ref, active_a, active_b, hidden_a, hidden_b = refs[kept:]
    rows = rows_ref[...]
    copy_ref[...] = rows
    logits = contract_cols(rows, router_ref[...])
    shifted = jnp.exp(logits - jnp.max(logits, axis=1, keepdims=True))
    prob = shifted / jnp.sum(shifted, axis=1, keepdims=True)
    gate = jnp.sum(prob * mask_ref[...], axis=1, keepdims=True)
    grad = (gate * cotan_ref[...].astype(F32)).astype(BF16)
    prob_ref[...] = prob
    grad_ref[...] = grad
    out, picked = None, None
    for up, down, active_ref, hidden_ref in (
        (up_a, down_a, active_a, hidden_a),
        (up_b, down_b, active_b, hidden_b),
    ):
        up, down = (value[...].reshape(-1, value.shape[2]) for value in (up, down))
        hidden = jnp.dot(rows, up, preferred_element_type=F32)
        share = 0.5 + 0.5 * lax.erf(hidden * math.sqrt(0.5))
        slope = share + hidden * (jnp.exp(-0.5 * hidden * hidden) * (1.0 / math.sqrt(2 * math.pi)))
        active = (hidden * share).astype(BF16)
        active_ref[...] = active
        hidden_grad = (jnp.dot(grad, down, preferred_element_type=F32) * slope).astype(BF16)
        hidden_ref[...] = hidden_grad
        out_part = contract_cols(active, down)
        picked_part = contract_cols(hidden_grad, up)
        out = out_part if out is None else out + out_part
        picked = picked_part if picked is None else picked + picked_part
    out_ref[...] = out
    picked_ref[...] = picked


def expert_call(rows, cotan, router_t, mask, blocks, far_up, far_down, part, parts, kept):
    count, width = rows.shape
    shard, hidden = far_up.shape[1:]
    block = math.gcd(count, 512)
    base = part * (count // block)

    def rows_of(columns, low=0):
        return pl.BlockSpec((block, columns), lambda at: (at + low, 0))

    def whole(array):
        return pl.BlockSpec(array.shape, lambda at: (0, 0), pipeline_mode=pl.Buffered(1))

    def layer(array, at):
        return pl.BlockSpec(
            (array.shape[0], shard, hidden), lambda step: (0, at, 0), pipeline_mode=pl.Buffered(1)
        )

    experts = router_t.shape[0]
    inputs = (rows, cotan, router_t, mask, blocks, blocks, far_up, far_down)
    columns = (width, width, hidden, hidden, hidden, hidden)
    return pl.pallas_call(
        partial(expert_kernel, len(kept)),
        grid=(count // block,),
        in_specs=[
            rows_of(width), rows_of(width), whole(router_t), whole(mask),
            layer(blocks, 0), layer(blocks, 1), layer(far_up, 0), layer(far_down, 0),
            *[pl.BlockSpec(memory_space=pl.ANY)] * len(kept),
        ],
        out_specs=[
            rows_of(width), rows_of(width), rows_of(experts), *(rows_of(one, base) for one in columns)
        ],
        out_shape=[
            *(jax.ShapeDtypeStruct((count, one), F32) for one in (width, width, experts)),
            *(jax.ShapeDtypeStruct((parts * count, one), BF16) for one in columns),
        ],
        input_output_aliases={len(inputs) + at: 3 + at for at in range(len(kept))},
        compiler_params=pltpu.CompilerParams(vmem_limit_bytes=EXPERT_VMEM),
        cost_estimate=pl.CostEstimate(
            flops=16 * count * width * hidden,
            transcendentals=4 * count * hidden,
            bytes_accessed=count * (14 * width + 8 * hidden) + 8 * width * hidden,
        ),
    )(*inputs, *kept)


def expert_exchange(value, experts):
    count = lax.axis_size("dp")
    groups = None
    if count != experts:
        groups = [
            [base + e for e in range(experts)] for base in range(0, count, experts)
        ]
    return lax.all_to_all(value, "dp", 0, 0, axis_index_groups=groups, tiled=True)


def by_ctx(first, second):
    lead = lax.axis_index("ctx") == 0
    return jnp.where(lead, first, second), jnp.where(lead, second, first)


def own_expert_blocks(up_shards, down_shards):
    experts, _, hidden = up_shards.shape
    count = lax.axis_size("dp")
    half = hidden // 2
    both = jnp.concatenate([up_shards, down_shards], axis=1)
    if lax.axis_size("ctx") == 2:
        both = by_ctx(both[:, :, :half], both[:, :, half:])[0]
    if count != experts:
        both = jnp.concatenate([both] * (count // experts), axis=0)
    return lax.all_to_all(both, "dp", 0, 0, tiled=True)


def other_hidden(both):
    rows = both.shape[1] // 2
    if lax.axis_size("ctx") == 2:
        return swapped(both[:, :rows], "ctx"), swapped(both[:, rows:], "ctx")
    half = both.shape[2] // 2
    return both[:, :rows, half:], both[:, rows:, half:]


def gather_kernel(count, parts, *refs):
    ins, outs = refs[:parts], refs[parts : 2 * parts]
    send_sem, recv_sem, own_sem = refs[2 * parts :]
    places = count // 2
    me = lax.axis_index("dp")
    place, side = lax.div(me, 2), lax.rem(me, 2)
    across = me + 1 - 2 * side
    barrier = pltpu.get_barrier_semaphore()

    def greet(device):
        pl.semaphore_signal(
            barrier, inc=1, device_id={"dp": device}, device_id_type=pl.DeviceIdType.MESH
        )

    greet(across)
    for step in (-1, 1):
        there = place + step

        @pl.when((there >= 0) & (there < places))
        def greet_place(step=step):
            greet(me + 2 * step)

    neighbours = 1 + (place > 0).astype(jnp.int32) + (place < places - 1).astype(jnp.int32)
    pl.semaphore_wait(barrier, neighbours)

    def copy(part, slot, kind, device, own):
        return pltpu.make_async_remote_copy(
            src_ref=ins[part] if own else outs[part].at[slot],
            dst_ref=outs[part].at[slot],
            send_sem=send_sem.at[kind, part, slot],
            recv_sem=recv_sem.at[part, slot],
            device_id={"dp": device},
            device_id_type=pl.DeviceIdType.MESH,
        )

    def passed_on(slot, steps, own, act):
        for step in steps:
            there = place + step

            @pl.when((there >= 0) & (there < places))
            def along(step=step):
                for part in range(parts):
                    act(copy(part, slot, step + 1, me + 2 * step, own))

        for part in range(parts):
            act(copy(part, slot, 1, across, own))

    def start(one):
        one.start()

    def sent(one):
        one.wait_send()

    mine = [
        pltpu.make_async_copy(ins[part], outs[part].at[me], own_sem.at[part])
        for part in range(parts)
    ]
    for one in mine:
        one.start()
    passed_on(me, (-1, 1), True, start)
    for far in range(1, places):
        for step in (-1, 1):
            origin = place - step * far

            @pl.when((origin >= 0) & (origin < places))
            def forward(step=step, far=far):
                slot = me - 2 * step * far
                for part in range(parts):
                    copy(part, slot, 1, across, False).wait_recv()
                passed_on(slot, (step,), False, start)

    for at in range(places):
        for part in range(parts):
            copy(part, 2 * at + 1 - side, 1, across, False).wait_recv()
    for one in mine:
        one.wait()
    passed_on(me, (-1, 1), True, sent)
    for far in range(1, places):
        for step in (-1, 1):
            origin = place - step * far

            @pl.when((origin >= 0) & (origin < places))
            def forwarded(step=step, far=far):
                passed_on(me - 2 * step * far, (step,), False, sent)


def gathered(*values):
    count = lax.axis_size("dp")
    parts = len(values)
    anywhere = pl.BlockSpec(memory_space=pl.ANY)
    size = sum(math.prod(value.shape) * 2 for value in values)
    return pl.pallas_call(
        partial(gather_kernel, count, parts),
        in_specs=[anywhere] * parts,
        out_specs=[anywhere] * parts,
        out_shape=[jax.ShapeDtypeStruct((count, *value.shape), value.dtype) for value in values],
        scratch_shapes=[
            pltpu.SemaphoreType.DMA((3, parts, count)),
            pltpu.SemaphoreType.DMA((parts, count)),
            pltpu.SemaphoreType.DMA((parts,)),
        ],
        compiler_params=pltpu.CompilerParams(collective_id=0, has_side_effects=True),
        cost_estimate=pl.CostEstimate(
            flops=0, transcendentals=0, bytes_accessed=2 * count * size
        ),
    )(*values)


def other_joined(own, first_shard, second_shard):
    count = lax.axis_size("ctx")
    if count == 2:
        return by_ctx(own, swapped(own, "ctx"))
    del first_shard, second_shard
    every = lax.all_gather(own, "ctx")
    return every[0], every[1]


def expert_weight_products(rows, hidden_grads, grads, actives):
    pairs = ((rows, hidden_grads), (grads, actives))
    far = [contract_rows(left, rights[1]) for left, rights in pairs]
    if lax.axis_size("ctx") == 2:
        far = [value.astype(BF16) for value in far]
    return [contract_rows(left, rights[0]) for left, rights in pairs], far


def sent_far(value):
    return swapped(value, "ctx") if lax.axis_size("ctx") == 2 else value


def expert_weight_parts(near, far):
    count = lax.axis_size("dp")
    parts = []
    for own, other in zip(near, far):
        if lax.axis_size("ctx") == 2:
            part = own + other.astype(F32)
        else:
            part = lax.psum_scatter(
                jnp.concatenate([own, other], axis=1), "ctx", scatter_dimension=1, tiled=True
            )
        parts.append(part.astype(BF16).reshape(count, part.shape[0] // count, part.shape[1]))
    return jnp.concatenate(parts, axis=1)


def expert_weight_blocks(blocks, experts):
    count = lax.axis_size("dp")
    if count != experts:
        blocks = jnp.sum(
            blocks.reshape(count // experts, experts, *blocks.shape[1:]).astype(F32), axis=0
        ).astype(BF16)
    shard = blocks.shape[1] // 2
    return blocks[:, :shard], blocks[:, shard:]


def far_hidden(blocks):
    if lax.axis_size("ctx") == 2:
        return swapped(blocks, "ctx")
    return lax.all_gather(blocks, "ctx", axis=2, tiled=True)


def expert_weight_grad(blocks, far_blocks):
    if lax.axis_size("ctx") == 2:
        far_blocks = jnp.concatenate(by_ctx(blocks, far_blocks), axis=2)
    return far_blocks.astype(F32)


def pair_products(first, second):
    if lax.axis_size("ctx") != 2:
        return contract_rows(*first), contract_rows(*second).astype(BF16)
    lefts, rights = by_ctx(first[0], second[0]), by_ctx(first[1], second[1])
    return contract_rows(lefts[0], rights[0]), contract_rows(lefts[1], rights[1]).astype(BF16)


def product_part(near, far):
    count = lax.axis_size("dp")

    def blocks(value):
        return value.astype(BF16).reshape(count, value.shape[0] // count, value.shape[1])

    if lax.axis_size("ctx") != 2:
        return jnp.concatenate([blocks(near), blocks(far)], axis=1)
    return blocks(near + far.astype(F32))


def product_shards(blocks):
    sums = jnp.sum(blocks.astype(F32), axis=0)
    if lax.axis_size("ctx") == 2:
        return by_ctx(sums, swapped(sums, "ctx"))
    sums = lax.psum(sums, "ctx")
    rows = sums.shape[0] // 2
    return sums[:rows], sums[rows:]


def local(
    hidden_in,
    out_grad,
    norm1_gain,
    in_weight,
    conv_weight,
    conv_bias,
    xproj_weight,
    dt_weight,
    dt_bias,
    decay_log,
    skip_weight,
    out_weight,
    norm2_gain,
    router_weight,
    fc1_weight,
    fc2_weight,
    expert_ids,
    keep_mask,
):
    batches, seqs, length, model_width = hidden_in.shape
    chains = batches * seqs
    tokens = chains * length
    steps = length // SEGMENTS
    shard, _, inner = in_weight.shape
    taps = conv_weight.shape[0]
    low_rank = dt_weight.shape[0]
    states = decay_log.shape[0]
    experts = fc1_weight.shape[0]
    dp_count = lax.axis_size("dp")
    tp_count = lax.axis_size("tp")
    capacity = tokens // 4
    part_cap = capacity // tp_count // HALVES
    slots = experts * part_cap
    tp_index = lax.axis_index("tp")
    scan = Scan(steps, chains, states, inner)

    def to_rows(value):
        value = value.reshape(chains, SEGMENTS, steps, -1).transpose(2, 0, 1, 3)
        return value.reshape(tokens, -1)

    def from_rows(value):
        value = value.reshape(steps, chains, SEGMENTS, -1).transpose(1, 2, 0, 3)
        return value.reshape(batches, seqs, length, -1)

    pieces = [
        norm1_gain[None],
        conv_weight,
        conv_bias[None],
        dt_weight,
        dt_bias[None],
        decay_log,
        skip_weight[None],
        norm2_gain[None],
        router_weight.T,
        xproj_weight.T,
    ]
    bounds = [0]
    for piece in pieces:
        bounds.append(bounds[-1] + piece.shape[0])
    small = sum(
        jnp.pad(piece, ((low, bounds[-1] - high), (0, 0)))
        for piece, low, high in zip(pieces, bounds, bounds[1:])
    )
    kinds = small.shape[0]
    small_wide = jnp.pad(small.T, ((0, 0), (0, -kinds % LANES)))
    in_x, small_all, later = gathered(
        in_weight[:, 0], small_wide, by_ctx(out_weight.T, in_weight[:, 1])[0]
    )
    in_x = in_x.reshape(dp_count * shard, inner)
    later = later.reshape(dp_count * shard, inner)
    small_all = small_all.reshape(dp_count * shard, -1)[:, :kinds].T
    small_all, up_shards, down_shards = together(
        small_all, fc1_weight, fc2_weight.transpose(0, 2, 1)
    )
    pieces = [small_all[bounds[i] : bounds[i + 1]] for i in range(len(bounds) - 1)]
    gain_one_f = pieces[0].astype(F32)
    tap_weights = pieces[1].astype(F32)
    conv_shift = pieces[2].astype(F32)
    dt_proj = pieces[3]
    dt_shift = pieces[4].astype(F32)
    decay_rate = -jnp.exp(pieces[5].astype(F32))
    skip_row = pieces[6].astype(F32)
    gain_two_f = pieces[7].astype(F32)
    router_t = pieces[8]
    x_proj_t = pieces[9]
    rate_rows = jnp.broadcast_to((decay_rate * LOG2E)[:, None, :], (states, SEGMENTS, inner))
    expert_blocks = own_expert_blocks(up_shards, down_shards)

    values = to_rows(hidden_in).astype(F32)
    normalized_rows, inverse_one = rms_forward(values, gain_one_f)
    normed_bf = normalized_rows.astype(BF16)
    x_pre = jnp.dot(normed_bf, in_x, preferred_element_type=F32).astype(BF16)
    x_pre = x_pre.reshape(steps, chains, SEGMENTS, inner)
    tail = x_pre[steps - taps + 1 :]
    edge_in = passed_along(tail[:, :, SEGMENTS - 1 :], "ctx", 1)
    edge_in, later = together(edge_in, later)
    out_proj_t, in_z = other_joined(later, out_weight.T, in_weight[:, 1])
    halo = jnp.concatenate([edge_in, tail[:, :, : SEGMENTS - 1]], axis=2)
    extended_bf = jnp.concatenate([halo, x_pre], axis=0)
    extended = extended_bf.astype(F32)
    conv_pre = jnp.broadcast_to(conv_shift[0], x_pre.shape)
    for tap in range(taps):
        conv_pre = conv_pre + tap_weights[tap] * extended[tap : tap + steps]
    xconv_bf = jax.nn.silu(conv_pre).astype(BF16)
    xconv = xconv_bf.astype(F32)
    xconv_rows = xconv_bf.reshape(tokens, inner)
    projected = axis_sum(contract_cols(xconv_rows, x_proj_t), "tp")
    dt_low = projected[:, :low_rank].astype(BF16)

    def mixes(value):
        value = value.reshape(steps, chains, SEGMENTS, states).transpose(1, 0, 3, 2)
        return jnp.broadcast_to(value[..., None], (*value.shape, LANES))

    mix_in = mixes(projected[:, low_rank : low_rank + states])
    mix_out = mixes(projected[:, low_rank + states :])
    dt_pre = (jnp.dot(dt_low, dt_proj, preferred_element_type=F32) + dt_shift).reshape(x_pre.shape)
    step_size = jax.nn.softplus(dt_pre)
    seg_decay, seg_state, last_state = scan.ends(step_size, xconv, mix_in, rate_rows)
    later_ids, later_mask, later_grad, _ = together(expert_ids, keep_mask, out_grad, seg_state)
    route = to_rows(later_ids)[:, 0]
    keep = to_rows(later_mask)[:, 0].astype(F32)
    onehot_int = (route[:, None] == jnp.arange(experts, dtype=jnp.int32)[None, :]).astype(jnp.int32)
    rank = jnp.sum((jnp.cumsum(onehot_int, axis=0) - 1) * onehot_int, axis=1)
    places = []
    for half in range(HALVES):
        own = rank - (tp_index * HALVES + half) * part_cap
        token_slot = jnp.where((own >= 0) & (own < part_cap), route * part_cap + own, -1)
        places.append(
            (token_slot[None, :] == jnp.arange(slots, dtype=jnp.int32)[:, None]).astype(BF16)
        )

    def slotted(value, half):
        sent = jnp.dot(places[half], value, preferred_element_type=F32).astype(BF16)
        return sent.reshape(experts, part_cap, -1)

    def landed(values):
        total = sum(
            contract_rows(place, value.reshape(slots, -1)) for place, value in zip(places, values)
        )
        return axis_sum(total.astype(BF16), "tp").astype(F32)

    def halves_of(value):
        return [value[:, at : at + part_cap] for at in range(0, value.shape[1], part_cap)]

    cotan_bf = to_rows(later_grad)
    cotan = cotan_bf.astype(F32)
    kept_cotan = (cotan * keep[:, None]).astype(BF16)
    sent_cotan = jnp.concatenate([slotted(kept_cotan, half) for half in range(HALVES)], axis=1)
    sent_cotan, expert_blocks = together(sent_cotan, expert_blocks)
    slot_cotan = expert_exchange(sent_cotan, experts)
    entering = entering_pieces(seg_decay[:, :, SEGMENTS - 1], last_state, "ctx", False)
    entering, expert_blocks = together(entering, expert_blocks)
    far_up, far_down = other_hidden(expert_blocks)
    scan_out, seg_start = scan.run(
        step_size, xconv, mix_in, mix_out, rate_rows, seg_decay, seg_state, entering
    )
    z_gate = jnp.dot(normed_bf, in_z, preferred_element_type=F32).reshape(x_pre.shape)
    scanned = scan_out + skip_row[0] * xconv
    z_silu = jax.nn.silu(z_gate)
    gated_bf = (scanned * z_silu).astype(BF16).reshape(tokens, inner)
    gated_bf, slot_cotan, far_up = together(gated_bf, slot_cotan, far_up)
    middle = values + axis_sum(contract_cols(gated_bf, out_proj_t), "tp")

    normed_two, inverse_two = rms_forward(middle, gain_two_f)
    normed_two_bf = normed_two.astype(BF16)
    expert_mask = (
        jnp.arange(experts, dtype=jnp.int32) == lax.rem(lax.axis_index("dp"), experts)
    ).astype(F32)[None, :]
    kept = ()
    got_grads, slot_outs, router_grad_t = [], [], 0.0
    for half, half_cotan in enumerate(halves_of(slot_cotan)):
        own_rows = expert_exchange(slotted(normed_two_bf, half), experts)
        if not half:
            own_rows, far_down = together(own_rows, far_down)
        else:
            own_rows, kept = together(own_rows, kept)
        own_rows = own_rows.reshape(slots, model_width)
        half_cotan = half_cotan.reshape(slots, model_width)
        far_rows, far_cotan = swapped(own_rows, "tp"), swapped(half_cotan, "tp")
        call = partial(
            expert_call, router_t=router_t, mask=expert_mask, blocks=expert_blocks, far_up=far_up,
            far_down=far_down, parts=2 * HALVES,
        )
        far = call(far_rows, far_cotan, part=2 * half, kept=kept)
        near = call(own_rows, half_cotan, part=2 * half + 1, kept=far[3:])
        if half:
            near, got_grads = together(near, got_grads)
        kept = near[3:]
        slot_out = near[0] + swapped(far[0], "tp")
        picked_grad = near[1] + swapped(far[1], "tp")
        slot_prob = near[2]
        slot_gate = jnp.sum(slot_prob * expert_mask, axis=1, keepdims=True)
        gate_grad = jnp.sum(slot_out * half_cotan.astype(F32), axis=1, keepdims=True)
        logit_grad = gate_grad * slot_gate * (expert_mask - slot_prob)
        router_grad_t = router_grad_t + contract_rows(logit_grad, own_rows.astype(F32), HIGHEST)
        picked_grad = picked_grad + jnp.dot(
            logit_grad, router_t.astype(F32), precision=HIGHEST, preferred_element_type=F32
        )
        got_grads.append(
            expert_exchange(picked_grad.astype(BF16).reshape(experts, part_cap, -1), experts)
        )
        slot_outs.append(slot_out.astype(BF16).reshape(experts, part_cap, -1))
    router_grad_t = axis_sum(router_grad_t, "tp")
    all_rows, all_grads, active_a, active_b, hidden_a, hidden_b = kept
    near_parts, far_parts = expert_weight_products(
        all_rows, (hidden_a, hidden_b), all_grads, (active_a, active_b)
    )
    far_first = sent_far(far_parts[0])
    got_grads, near_parts, far_second, far_first, slot_outs = together(
        got_grads, near_parts, far_parts[1], far_first, slot_outs
    )
    far_parts = far_first, sent_far(far_second)
    normed_two_grad = landed(got_grads)
    got_out = expert_exchange(jnp.concatenate(slot_outs, axis=1), experts)
    middle_norm_grad, gain_two_grad = rms_backward(middle, inverse_two, gain_two_f, normed_two_grad)
    middle_grad = cotan + middle_norm_grad
    mixer_grad_bf = middle_grad.astype(BF16)
    gated_grad = jnp.dot(mixer_grad_bf, out_proj_t, preferred_element_type=F32).reshape(x_pre.shape)
    scan_grad = gated_grad * z_silu
    z_grad = jax.vjp(jax.nn.silu, z_gate)[1](gated_grad * scanned)[0]
    z_grad_bf = z_grad.astype(BF16).reshape(tokens, inner)
    near_product, far_product = pair_products((mixer_grad_bf, gated_bf), (normed_bf, z_grad_bf))
    back_decay, back_adjoint, first_adjoint = scan.adjoint_ends(
        step_size, mix_out, scan_grad, rate_rows
    )
    far_parts, got_out, _ = together(far_parts, got_out, first_adjoint)
    weight_blocks = lax.all_to_all(
        expert_weight_parts(near_parts, far_parts), "dp", 0, 0, tiled=True
    )
    leaving = entering_pieces(back_decay[:, :, 0], first_adjoint, "ctx", True)
    leaving, near_product, far_product = together(leaving, near_product, far_product)
    far_product = sent_far(far_product)
    adjoint_args = (
        step_size, xconv, mix_in, mix_out, scan_grad, rate_rows, seg_start, back_decay, back_adjoint,
        leaving, skip_row,
    )
    pre_grad, xconv_grad, decay_sum, scan_sums, mix_grad = scan.adjoint(adjoint_args)
    pre_grad, far_product, weight_blocks = together(pre_grad, far_product, weight_blocks)
    weight_blocks = expert_weight_blocks(weight_blocks, experts)
    far_ups = far_hidden(weight_blocks[0])
    out_blocks = lax.all_to_all(product_part(near_product, far_product), "dp", 0, 0, tiled=True)
    decay_log_grad = jnp.sum(decay_sum, axis=0) * decay_rate
    dt_shift_grad, skip_grad = jnp.sum(scan_sums, axis=0)[:2]
    pre_grad = pre_grad.reshape(tokens, inner)
    dt_proj_grad = contract_rows(dt_low.astype(F32), pre_grad, HIGHEST)
    dt_low_grad = contract_cols(pre_grad, dt_proj.astype(F32), HIGHEST)
    mix_grad = mix_grad.reshape(tokens, LANES)[:, : 2 * states]
    proj_part = jnp.concatenate([dt_low_grad, mix_grad], axis=1)
    proj_grad_bf = axis_sum(proj_part, "tp").astype(BF16)
    x_proj_grad_t = contract_rows(proj_grad_bf, xconv_rows)
    flat = (chains * SEGMENTS, inner)
    x_grad_bf, conv_sums, head, last = conv_back(
        proj_grad_bf,
        x_proj_t,
        xconv_grad.reshape(steps, *flat),
        extended_bf.reshape(steps + taps - 1, *flat),
        tap_weights,
        conv_shift,
    )
    taps_grad, shift_grad = conv_sums[:taps], conv_sums[taps]
    edge_back = passed_along(
        head.reshape(taps - 1, chains, SEGMENTS, inner)[:, :, :1], "ctx", -1
    )
    edge_back, out_blocks, far_ups = together(edge_back, out_blocks, far_ups)
    reaching = jnp.stack(
        [
            sum(tap_weights[tap] * edge_back[at - tap] for tap in range(at + 1))
            for at in range(taps - 1)
        ]
    )
    reaching = jnp.pad(reaching, ((0, 0), (0, 0), (SEGMENTS - 1, 0), (0, 0)))
    last = (last + reaching.reshape(taps - 1, *flat)).astype(BF16)
    x_grad_bf = lax.dynamic_update_slice(x_grad_bf, last, (steps - taps + 1, 0, 0))
    x_grad_bf = x_grad_bf.reshape(tokens, inner)
    small_grads = jnp.concatenate(
        [
            taps_grad,
            shift_grad[None],
            dt_proj_grad,
            dt_shift_grad[None],
            decay_log_grad,
            skip_grad[None],
            gain_two_grad[None],
            router_grad_t,
            x_proj_grad_t,
        ],
        axis=0,
    )
    small_grads = small_grads.reshape(-1, dp_count, shard).transpose(1, 0, 2)
    small_size = small_grads.shape[1] * shard
    small_rows = small_grads.astype(BF16).reshape(dp_count, small_size)
    small_rows = jnp.pad(small_rows, ((0, 0), (0, -small_size % inner))).reshape(dp_count, -1, inner)
    x_grad_bf, small_rows, out_blocks = together(x_grad_bf, small_rows, out_blocks)
    normed_part = contract_cols(x_grad_bf, in_x) + contract_cols(z_grad_bf, in_z)
    normed_grad = axis_sum(normed_part, "tp")
    values_norm_grad, gain_one_grad = rms_backward(values, inverse_one, gain_one_f, normed_grad)
    input_grad = from_rows((middle_grad + values_norm_grad).astype(BF16))

    in_x_part = contract_rows(normed_bf, x_grad_bf).astype(BF16).reshape(dp_count, shard, inner)
    gain_row = gain_one_grad.reshape(dp_count, 1, shard)
    gain_high = gain_row.astype(BF16)
    gain_low = (gain_row - gain_high.astype(F32)).astype(BF16)
    gain_rows = jnp.concatenate([gain_high, gain_low], axis=1)
    gain_rows = jnp.pad(gain_rows, ((0, 0), (0, 6), (0, inner - shard)))
    in_x_part, out_blocks = together(in_x_part, out_blocks)
    out_proj_grad, in_z_grad = product_shards(out_blocks)
    in_x_blocks = lax.all_to_all(
        jnp.concatenate([in_x_part, gain_rows, small_rows], axis=1), "dp", 0, 0, tiled=True
    )
    out_proj_grad, in_z_grad, far_down_blocks = together(
        out_proj_grad, in_z_grad, weight_blocks[1]
    )
    far_downs, in_x_blocks = together(far_hidden(far_down_blocks), in_x_blocks)
    first_grad = expert_weight_grad(weight_blocks[0], far_ups)
    second_grad = expert_weight_grad(weight_blocks[1], far_downs)
    router_prob = jax.nn.softmax(contract_cols(normed_two_bf, router_t), axis=-1)
    gate_prob = jnp.sum(router_prob * onehot_int.astype(F32), axis=1) * keep
    result = from_rows((middle + gate_prob[:, None] * landed(halves_of(got_out))).astype(BF16))
    in_x_sums = axis_sum(jnp.sum(in_x_blocks.astype(F32), axis=0), "ctx")
    in_x_grad = in_x_sums[:shard]
    gain_one_grad = in_x_sums[shard : shard + 1, :shard] + in_x_sums[shard + 1 : shard + 2, :shard]
    small_grads = in_x_sums[shard + 8 :].reshape(-1)[:small_size].reshape(-1, shard)
    small_grads = jnp.concatenate([gain_one_grad, small_grads], axis=0)
    sums = [small_grads[bounds[i] : bounds[i + 1]] for i in range(len(bounds) - 1)]
    return (
        result,
        input_grad,
        sums[0][0],
        jnp.stack([in_x_grad, in_z_grad], axis=1),
        sums[1],
        sums[2][0],
        sums[9].T,
        sums[3],
        sums[4][0],
        sums[5],
        sums[6][0],
        out_proj_grad.T,
        sums[7][0],
        sums[8].T,
        first_grad,
        second_grad.transpose(0, 2, 1),
    )


def solution(mesh):
    weights = (
        P("dp"),
        P("dp", None, "tp"),
        P(None, ("tp", "dp")),
        P(("tp", "dp")),
        P(("tp", "dp"), None),
        P(None, ("tp", "dp")),
        P(("tp", "dp")),
        P(None, ("tp", "dp")),
        P(("tp", "dp")),
        P("tp", "dp"),
        P("dp"),
        P("dp", None),
        P(None, "dp", "tp"),
        P(None, "tp", "dp"),
    )
    rows = P(None, "dp", "ctx", None)
    return jax.shard_map(
        local,
        mesh=mesh,
        in_specs=(rows, rows, *weights, P(("dp", "ctx"), None), P(("dp", "ctx"))),
        out_specs=(rows, rows, *weights),
        check_vma=False,
    )
```

```python
from functools import partial
import math

import jax
import jax.numpy as jnp
from jax import lax
from jax.experimental import pallas as pl
from jax.experimental.pallas import tpu as pltpu
from jax.sharding import PartitionSpec as P

EPSILON = 1e-05
HIGHEST = lax.Precision.HIGHEST
SEGMENTS = 8
LANES = 128
VMEM_LIMIT = 56 * 1024 * 1024
EXPERT_VMEM = 56 * 1024 * 1024
LOG2E = math.log2(math.e)
GROUP_A = 4
GROUP_B = 4
GROUP_C = 8
UNROLL_A = 8
UNROLL_B = 8
UNROLL_C = 8
UNROLL_D = 4
UNROLL_E = 8
BLOCKS = 3
COVER = 100
HALVES = 1
BF16 = jnp.bfloat16
F32 = jnp.float32


def swapped(value, axis):
    return lax.ppermute(value, axis, [(0, 1), (1, 0)])


def passed_along(value, axis, steps):
    count = lax.axis_size(axis)
    leading, last = (max(0, -steps), min(count, count - steps))
    return lax.ppermute(value, axis, [(source, source + steps) for source in range(leading, last)])


def axis_sum(value, axis):
    if lax.axis_size(axis) == 2:
        return value + swapped(value, axis)
    return lax.psum(value, axis)


def together(*values):
    return lax.optimization_barrier(values)


def entering_pieces(decay, value, axis, backward):
    count = lax.axis_size(axis)
    if count == 2:
        return passed_along(value, axis, -1 if backward else 1)
    mine = lax.axis_index(axis)
    decays = lax.all_gather(decay, axis)
    values = lax.all_gather(value, axis)
    running = jnp.zeros_like(value)
    for position in range(count - 1):
        at = count - 1 - position if backward else position
        longer = values[at] + decays[at] * running
        ahead = at > mine if backward else at < mine
        running = jnp.where(ahead, longer, running)
    return running


def contract_rows(left_side, right_side, precision=None):
    return lax.dot_general(
        left_side,
        right_side,
        (((0,), (0,)), ((), ())),
        precision=precision,
        preferred_element_type=F32,
    )


def contract_cols(left_side, right_side, precision=None):
    return lax.dot_general(
        left_side,
        right_side,
        (((1,), (1,)), ((), ())),
        precision=precision,
        preferred_element_type=F32,
    )


def rms_forward(values, gain_vec):
    inverse = lax.rsqrt(jnp.mean(values * values, axis=-1, keepdims=True) + EPSILON)
    return (values * inverse * gain_vec, inverse)


def rms_backward(values, inverse, gain_vec, grad_out):
    weighted = grad_out * gain_vec
    inner_mean = jnp.mean(values * weighted, axis=-1, keepdims=True)
    grad_values = inverse * weighted - values * inverse * inverse * inverse * inner_mean
    grad_gain = jnp.sum(grad_out * values * inverse, axis=0)
    return (grad_values, grad_gain)


def zeros_of(ref):
    return jnp.zeros(ref.shape[1:], F32)


def sublane_rows(lanes):
    return lax.broadcasted_iota(jnp.int32, (SEGMENTS, lanes), 0)


def widened(value, lanes):
    return jnp.concatenate([value] * (lanes // LANES), axis=1) if lanes > LANES else value


def narrowed(value):
    parts = [value[:, at : at + LANES] for at in range(0, value.shape[1], LANES)]
    return sum(parts[1:], parts[0])


def groups_of(states, size):
    size = math.gcd(states, size)
    return [range(first, first + size) for first in range(0, states, size)]


def joined_forward(decay, value, row):
    for reach in (1, 2, 4):
        inside = row >= reach
        value = value + jnp.where(inside, decay * pltpu.roll(value, reach, 0), 0.0)
        decay = jnp.where(inside, decay * pltpu.roll(decay, reach, 0), decay)
    return decay, value


def joined_backward(decay, value, row):
    for reach in (1, 2, 4):
        inside = row < SEGMENTS - reach
        value = value + jnp.where(inside, decay * pltpu.roll(value, SEGMENTS - reach, 0), 0.0)
        decay = jnp.where(inside, decay * pltpu.roll(decay, SEGMENTS - reach, 0), decay)
    return decay, value


def ends_kernel(step_ref, input_ref, mix_in_ref, rate_ref, decay_ref, state_ref, last_ref):
    steps, states, lanes = step_ref.shape[0], mix_in_ref.shape[1], step_ref.shape[2]
    zero = zeros_of(step_ref)
    row = sublane_rows(lanes)
    total = lax.fori_loop(0, steps, lambda at, total: total + step_ref[at], zero, unroll=UNROLL_E)
    for members in groups_of(states, GROUP_A):
        rates = [rate_ref[n] for n in members]

        def body(at, held):
            step = step_ref[at]
            driven = step * input_ref[at]
            return tuple(
                jnp.exp2(step * rate) * before + widened(mix_in_ref[at, n], lanes) * driven
                for n, rate, before in zip(members, rates, held)
            )

        held = lax.fori_loop(0, steps, body, (zero,) * len(members), unroll=UNROLL_A)
        for n, rate, end in zip(members, rates, held):
            decay, value = joined_forward(jnp.exp2(total * rate), end, row)
            decay_ref[n] = decay
            state_ref[n] = value
            last_ref[n : n + 1] = value[SEGMENTS - 1 :]


def states_kernel(
    step_ref, input_ref, mix_in_ref, mix_out_ref, rate_ref, decay_ref, state_ref, enter_ref,
    out_ref, start_ref,
):
    steps, states, lanes = step_ref.shape[0], mix_in_ref.shape[1], step_ref.shape[2]
    row = sublane_rows(lanes)
    for members in groups_of(states, GROUP_B):
        rates = [rate_ref[n] for n in members]
        held = []
        for n in members:
            first = jnp.broadcast_to(enter_ref[n : n + 1], (SEGMENTS, lanes))
            inner = pltpu.roll(state_ref[n], 1, 0) + pltpu.roll(decay_ref[n], 1, 0) * first
            start = jnp.where(row >= 1, inner, first)
            start_ref[n] = start
            held.append(start)

        def body(at, held):
            step = step_ref[at]
            driven = step * input_ref[at]
            held = tuple(
                jnp.exp2(step * rate) * before + widened(mix_in_ref[at, n], lanes) * driven
                for n, rate, before in zip(members, rates, held)
            )
            parts = [widened(mix_out_ref[at, n], lanes) * now for n, now in zip(members, held)]
            if members[0]:
                parts.append(out_ref[at])
            while len(parts) > 1:
                parts = [sum(parts[i + 1 : i + 2], parts[i]) for i in range(0, len(parts), 2)]
            out_ref[at] = parts[0]
            return held

        lax.fori_loop(0, steps, body, tuple(held), unroll=UNROLL_B)


def adjoint_ends_kernel(step_ref, mix_out_ref, grad_ref, rate_ref, decay_ref, adjoint_ref, first_ref):
    steps, states, lanes = step_ref.shape[0], mix_out_ref.shape[1], step_ref.shape[2]
    zero = zeros_of(step_ref)
    row = sublane_rows(lanes)
    total = lax.fori_loop(0, steps, lambda at, total: total + step_ref[at], zero, unroll=UNROLL_E)
    for members in groups_of(states, GROUP_A):
        rates = [rate_ref[n] for n in members]

        def body(back, incoming):
            at = steps - 1 - back
            step = step_ref[at]
            grad = grad_ref[at]
            return tuple(
                jnp.exp2(step * rate) * (widened(mix_out_ref[at, n], lanes) * grad + after)
                for n, rate, after in zip(members, rates, incoming)
            )

        incoming = lax.fori_loop(0, steps, body, (zero,) * len(members), unroll=UNROLL_A)
        for n, rate, end in zip(members, rates, incoming):
            decay, value = joined_backward(jnp.exp2(total * rate), end, row)
            decay_ref[n] = decay
            adjoint_ref[n] = value
            first_ref[n : n + 1] = value[:1]


def adjoint_kernel(
    step_ref, input_ref, mix_in_ref, mix_out_ref, grad_ref, rate_ref, start_ref, decay_ref, adjoint_ref,
    enter_ref, skip_ref,
    pre_ref, conv_ref, decay_sum_ref, sums_ref, mix_ref, states_ref, decays_ref, in_grad_ref, out_grad_ref,
):
    steps, states, lanes = step_ref.shape[0], mix_in_ref.shape[1], step_ref.shape[2]
    row = sublane_rows(lanes)
    zero = zeros_of(step_ref)

    @pl.when(pl.program_id(1) == 0)
    def clear():
        in_grad_ref[...] = jnp.zeros_like(in_grad_ref)
        out_grad_ref[...] = jnp.zeros_like(out_grad_ref)

    for members in groups_of(states, GROUP_C):
        first, group = members[0], len(members)
        rates = [rate_ref[n] for n in members]

        def ahead(at, held):
            step = step_ref[at]
            driven = step * input_ref[at]
            grad = grad_ref[at]
            after = []
            for i, n in enumerate(members):
                states_ref[at, i] = held[i]
                decay = jnp.exp2(step * rates[i])
                decays_ref[at, i] = decay
                now = decay * held[i] + widened(mix_in_ref[at, n], lanes) * driven
                out_grad_ref[at, n] += narrowed(grad * now)
                after.append(now)
            return tuple(after)

        lax.fori_loop(0, steps, ahead, tuple(start_ref[n] for n in members), unroll=UNROLL_C)

        incoming = []
        for n in members:
            final = jnp.broadcast_to(enter_ref[n : n + 1], (SEGMENTS, lanes))
            inner = (
                pltpu.roll(adjoint_ref[n], SEGMENTS - 1, 0)
                + pltpu.roll(decay_ref[n], SEGMENTS - 1, 0) * final
            )
            incoming.append(jnp.where(row < SEGMENTS - 1, inner, final))

        def body(back, carry):
            at = steps - 1 - back
            incoming, decay_sums = carry
            step = step_ref[at]
            grad = grad_ref[at]
            driven = step * input_ref[at]
            in_sum = conv_ref[at] if first else zero
            rate_sum = pre_ref[at] if first else zero
            following, sums = [], []
            for i, n in enumerate(members):
                adjoint = widened(mix_out_ref[at, n], lanes) * grad + incoming[i]
                onward = decays_ref[at, i] * adjoint
                decay_grad = onward * states_ref[at, i]
                in_sum = in_sum + adjoint * widened(mix_in_ref[at, n], lanes)
                rate_sum = rate_sum + decay_grad * rates[i]
                sums.append(decay_sums[i] + decay_grad * step)
                in_grad_ref[at, n] += narrowed(adjoint * driven)
                following.append(onward)
            conv_ref[at] = in_sum
            pre_ref[at] = rate_sum
            return tuple(following), tuple(sums)

        _, sums = lax.fori_loop(
            0, steps, body, (tuple(incoming), (zero,) * group), unroll=UNROLL_D
        )
        for i, n in enumerate(members):
            decay_sum_ref[n : n + 1] = jnp.sum(sums[i], axis=0, keepdims=True)

    skip = skip_ref[...]

    def close(at, carry):
        pre_sum, skip_sum = carry
        step, inputs, grad, in_sum = step_ref[at], input_ref[at], grad_ref[at], conv_ref[at]
        step_grad = pre_ref[at] * (1.0 / LOG2E) + in_sum * inputs
        pre = step_grad * (1.0 - jnp.exp2(step * -LOG2E))
        pre_ref[at] = pre
        conv_ref[at] = in_sum * step + skip * grad
        return pre_sum + pre, skip_sum + grad * inputs

    pre_sum, skip_sum = lax.fori_loop(0, steps, close, (zero, zero), unroll=UNROLL_E)
    sums_ref[0:1] = jnp.sum(pre_sum, axis=0, keepdims=True)
    sums_ref[1:2] = jnp.sum(skip_sum, axis=0, keepdims=True)
    sums_ref[2:] = jnp.zeros((SEGMENTS - 2, lanes), F32)

    @pl.when(pl.program_id(1) == pl.num_programs(1) - 1)
    def across_lanes():
        lane = lax.broadcasted_iota(jnp.int32, (SEGMENTS, LANES), 1)

        def one(at, carry):
            total = jnp.zeros((SEGMENTS, LANES), F32)
            for n in range(states):
                for base, ref in ((0, in_grad_ref), (states, out_grad_ref)):
                    value = jnp.sum(ref[at, n], axis=1, keepdims=True)
                    total = jnp.where(lane == base + n, value, total)
            mix_ref[at] = total
            return carry

        lax.fori_loop(0, steps, one, 0, unroll=UNROLL_E)


class Scan:
    def __init__(self, steps, chains, states, width):
        lanes = LANES * math.gcd(width // LANES, BLOCKS)
        self.grid = (chains, width // lanes)
        self.rows_spec = pl.BlockSpec(
            (steps, None, SEGMENTS, lanes), lambda chain, block: (0, chain, 0, block)
        )
        self.mix_spec = pl.BlockSpec(
            (None, steps, states, SEGMENTS, LANES), lambda chain, block: (chain, 0, 0, 0, 0)
        )
        self.rate_spec = pl.BlockSpec((states, SEGMENTS, lanes), lambda chain, block: (0, 0, block))
        self.state_spec = pl.BlockSpec(
            (None, states, SEGMENTS, lanes), lambda chain, block: (chain, 0, 0, block)
        )
        self.edge_spec = pl.BlockSpec((None, states, lanes), lambda chain, block: (chain, 0, block))
        self.rows = jax.ShapeDtypeStruct((steps, chains, SEGMENTS, width), F32)
        self.mix = jax.ShapeDtypeStruct((chains, steps, states, SEGMENTS, LANES), F32)
        self.state = jax.ShapeDtypeStruct((chains, states, SEGMENTS, width), F32)
        self.edge = jax.ShapeDtypeStruct((chains, states, width), F32)
        self.sums = jax.ShapeDtypeStruct((chains, SEGMENTS, width), F32)
        self.sums_spec = pl.BlockSpec((None, SEGMENTS, lanes), lambda chain, block: (chain, 0, block))
        self.lane_sums = jax.ShapeDtypeStruct((steps, chains, SEGMENTS, LANES), F32)
        self.lane_spec = pl.BlockSpec(
            (steps, None, SEGMENTS, LANES), lambda chain, block: (0, chain, 0, 0)
        )
        self.skip_spec = pl.BlockSpec((1, lanes), lambda chain, block: (0, block))
        self.scratch = [
            pltpu.VMEM((steps, math.gcd(states, GROUP_C), SEGMENTS, lanes), F32),
            pltpu.VMEM((steps, math.gcd(states, GROUP_C), SEGMENTS, lanes), F32),
            pltpu.VMEM((steps, states, SEGMENTS, LANES), F32),
            pltpu.VMEM((steps, states, SEGMENTS, LANES), F32),
        ]
        self.work = steps * chains * SEGMENTS * width * states

    def call(self, kernel, ops, args, in_specs, outs, out_specs, scratch=()):
        size = sum(math.prod(a.shape) * a.dtype.itemsize for a in (*args, *outs))
        return pl.pallas_call(
            kernel,
            grid=self.grid,
            in_specs=in_specs,
            out_specs=out_specs,
            out_shape=outs,
            scratch_shapes=list(scratch),
            compiler_params=pltpu.CompilerParams(vmem_limit_bytes=VMEM_LIMIT),
            cost_estimate=pl.CostEstimate(
                flops=ops * self.work, transcendentals=self.work, bytes_accessed=size // COVER
            ),
        )(*args)

    def ends(self, step, inputs, mix_in, rate):
        return self.call(
            ends_kernel, 5, (step, inputs, mix_in, rate),
            [self.rows_spec, self.rows_spec, self.mix_spec, self.rate_spec],
            [self.state, self.state, self.edge],
            [self.state_spec, self.state_spec, self.edge_spec],
        )

    def run(self, step, inputs, mix_in, mix_out, rate, decay, state, enter):
        return self.call(
            states_kernel, 7, (step, inputs, mix_in, mix_out, rate, decay, state, enter),
            [self.rows_spec, self.rows_spec, self.mix_spec, self.mix_spec, self.rate_spec,
             self.state_spec, self.state_spec, self.edge_spec],
            [self.rows, self.state],
            [self.rows_spec, self.state_spec],
        )

    def adjoint_ends(self, step, mix_out, grad, rate):
        return self.call(
            adjoint_ends_kernel, 5, (step, mix_out, grad, rate),
            [self.rows_spec, self.mix_spec, self.rows_spec, self.rate_spec],
            [self.state, self.state, self.edge],
            [self.state_spec, self.state_spec, self.edge_spec],
        )

    def adjoint(self, args):
        return self.call(
            adjoint_kernel, 20, args,
            [self.rows_spec, self.rows_spec, self.mix_spec, self.mix_spec, self.rows_spec,
             self.rate_spec, self.state_spec, self.state_spec, self.state_spec, self.edge_spec,
             self.skip_spec],
            [self.rows, self.rows, self.edge, self.sums, self.lane_sums],
            [self.rows_spec, self.rows_spec, self.edge_spec, self.sums_spec, self.lane_spec],
            self.scratch,
        )


def conv_back_kernel(
    proj_ref, weight_ref, grad_ref, input_ref, taps_ref, shift_ref,
    out_ref, sums_ref, head_ref, tail_ref, product_ref, conv_ref,
):
    steps, rows, lanes = grad_ref.shape
    count = taps_ref.shape[0]
    reach = count - 1
    taps = [taps_ref[at : at + 1] for at in range(count)]
    shift = shift_ref[...]
    product_ref[...] = jnp.dot(
        proj_ref[...], weight_ref[...], preferred_element_type=F32
    ).reshape(steps, rows, lanes)

    def slopes(at, sums):
        inputs = [input_ref[at + tap].astype(F32) for tap in range(count)]
        pre = shift + sum(tap * value for tap, value in zip(taps, inputs))
        share = 1.0 / (1.0 + jnp.exp(-pre))
        conv = (grad_ref[at] + product_ref[at]) * (share * (1.0 + pre * (1.0 - share)))
        conv_ref[at] = conv
        return (*(total + conv * value for total, value in zip(sums, inputs)), sums[-1] + conv)

    zero = jnp.zeros((rows, lanes), F32)
    sums = lax.fori_loop(0, steps, slopes, (zero,) * (count + 1), unroll=2)
    for at, total in enumerate(sums):
        sums_ref[at : at + 1] = jnp.sum(total, axis=0, keepdims=True)
    sums_ref[count + 1 :] = jnp.zeros((sums_ref.shape[0] - count - 1, lanes), F32)
    row = sublane_rows(lanes)
    for at in range(reach):
        head_ref[at] = conv_ref[at]
        for low in range(0, rows, SEGMENTS):
            rolled = pltpu.roll(conv_ref[at, low : low + SEGMENTS], SEGMENTS - 1, 0)
            conv_ref[steps + at, low : low + SEGMENTS] = jnp.where(
                row < SEGMENTS - 1, rolled, 0.0
            )

    def back(at):
        return sum(taps[tap] * conv_ref[at + reach - tap] for tap in range(count))

    def store(at, carry):
        out_ref[at] = back(at).astype(BF16)
        return carry

    lax.fori_loop(0, steps, store, 0, unroll=2)
    for at in range(reach):
        tail_ref[at] = back(steps - reach + at)


def conv_back(proj, weight, grad, inputs, taps, shift):
    steps, rows, width = grad.shape
    reach = taps.shape[0] - 1
    lanes = LANES * math.gcd(width // LANES, BLOCKS)

    def block(count, dtype=F32):
        spec = pl.BlockSpec((count, rows, lanes), lambda at: (0, 0, at))
        return spec, jax.ShapeDtypeStruct((count, rows, width), dtype)

    def columns(count):
        return pl.BlockSpec((count, lanes), lambda at: (0, at))

    outs = [
        block(steps, BF16),
        (columns(SEGMENTS), jax.ShapeDtypeStruct((SEGMENTS, width), F32)),
        block(reach),
        block(reach),
    ]
    return pl.pallas_call(
        conv_back_kernel,
        grid=(width // lanes,),
        in_specs=[
            pl.BlockSpec(proj.shape, lambda at: (0, 0)),
            columns(weight.shape[0]),
            block(steps)[0],
            block(steps + reach)[0],
            columns(reach + 1),
            columns(1),
        ],
        out_specs=[spec for spec, _ in outs],
        out_shape=[shape for _, shape in outs],
        scratch_shapes=[
            pltpu.VMEM((steps, rows, lanes), F32),
            pltpu.VMEM((steps + reach, rows, lanes), F32),
        ],
        compiler_params=pltpu.CompilerParams(vmem_limit_bytes=VMEM_LIMIT),
        cost_estimate=pl.CostEstimate(flops=1, transcendentals=0, bytes_accessed=1),
    )(proj, weight, grad, inputs, taps, shift)


def expert_kernel(
    kept, rows_ref, cotan_ref, router_ref, mask_ref, up_a, down_a, up_b, down_b, *refs
):
    out_ref, picked_ref, prob_ref, copy_ref, grad_ref, active_a, active_b, hidden_a, hidden_b = refs[kept:]
    rows = rows_ref[...]
    copy_ref[...] = rows
    logits = contract_cols(rows, router_ref[...])
    shifted = jnp.exp(logits - jnp.max(logits, axis=1, keepdims=True))
    prob = shifted / jnp.sum(shifted, axis=1, keepdims=True)
    gate = jnp.sum(prob * mask_ref[...], axis=1, keepdims=True)
    grad = (gate * cotan_ref[...].astype(F32)).astype(BF16)
    prob_ref[...] = prob
    grad_ref[...] = grad
    out, picked = None, None
    for up, down, active_ref, hidden_ref in (
        (up_a, down_a, active_a, hidden_a),
        (up_b, down_b, active_b, hidden_b),
    ):
        up, down = (value[...].reshape(-1, value.shape[2]) for value in (up, down))
        hidden = jnp.dot(rows, up, preferred_element_type=F32)
        share = 0.5 + 0.5 * lax.erf(hidden * math.sqrt(0.5))
        slope = share + hidden * (jnp.exp(-0.5 * hidden * hidden) * (1.0 / math.sqrt(2 * math.pi)))
        active = (hidden * share).astype(BF16)
        active_ref[...] = active
        hidden_grad = (jnp.dot(grad, down, preferred_element_type=F32) * slope).astype(BF16)
        hidden_ref[...] = hidden_grad
        out_part = contract_cols(active, down)
        picked_part = contract_cols(hidden_grad, up)
        out = out_part if out is None else out + out_part
        picked = picked_part if picked is None else picked + picked_part
    out_ref[...] = out
    picked_ref[...] = picked


def expert_call(rows, cotan, router_t, mask, blocks, far_up, far_down, part, parts, kept):
    count, width = rows.shape
    shard, hidden = far_up.shape[1:]
    block = math.gcd(count, 512)
    base = part * (count // block)

    def rows_of(columns, low=0):
        return pl.BlockSpec((block, columns), lambda at: (at + low, 0))

    def whole(array):
        return pl.BlockSpec(array.shape, lambda at: (0, 0), pipeline_mode=pl.Buffered(1))

    def layer(array, at):
        return pl.BlockSpec(
            (array.shape[0], shard, hidden), lambda step: (0, at, 0), pipeline_mode=pl.Buffered(1)
        )

    experts = router_t.shape[0]
    inputs = (rows, cotan, router_t, mask, blocks, blocks, far_up, far_down)
    columns = (width, width, hidden, hidden, hidden, hidden)
    return pl.pallas_call(
        partial(expert_kernel, len(kept)),
        grid=(count // block,),
        in_specs=[
            rows_of(width), rows_of(width), whole(router_t), whole(mask),
            layer(blocks, 0), layer(blocks, 1), layer(far_up, 0), layer(far_down, 0),
            *[pl.BlockSpec(memory_space=pl.ANY)] * len(kept),
        ],
        out_specs=[
            rows_of(width), rows_of(width), rows_of(experts), *(rows_of(one, base) for one in columns)
        ],
        out_shape=[
            *(jax.ShapeDtypeStruct((count, one), F32) for one in (width, width, experts)),
            *(jax.ShapeDtypeStruct((parts * count, one), BF16) for one in columns),
        ],
        input_output_aliases={len(inputs) + at: 3 + at for at in range(len(kept))},
        compiler_params=pltpu.CompilerParams(vmem_limit_bytes=EXPERT_VMEM),
        cost_estimate=pl.CostEstimate(
            flops=16 * count * width * hidden,
            transcendentals=4 * count * hidden,
            bytes_accessed=count * (14 * width + 8 * hidden) + 8 * width * hidden,
        ),
    )(*inputs, *kept)


def expert_exchange(value, experts):
    count = lax.axis_size("dp")
    groups = None
    if count != experts:
        groups = [
            [base + e for e in range(experts)] for base in range(0, count, experts)
        ]
    return lax.all_to_all(value, "dp", 0, 0, axis_index_groups=groups, tiled=True)


def by_ctx(first, second):
    lead = lax.axis_index("ctx") == 0
    return jnp.where(lead, first, second), jnp.where(lead, second, first)


def own_expert_blocks(up_shards, down_shards):
    experts, _, hidden = up_shards.shape
    count = lax.axis_size("dp")
    half = hidden // 2
    both = jnp.concatenate([up_shards, down_shards], axis=1)
    if lax.axis_size("ctx") == 2:
        both = by_ctx(both[:, :, :half], both[:, :, half:])[0]
    if count != experts:
        both = jnp.concatenate([both] * (count // experts), axis=0)
    return lax.all_to_all(both, "dp", 0, 0, tiled=True)


def other_hidden(both):
    rows = both.shape[1] // 2
    if lax.axis_size("ctx") == 2:
        return swapped(both[:, :rows], "ctx"), swapped(both[:, rows:], "ctx")
    half = both.shape[2] // 2
    return both[:, :rows, half:], both[:, rows:, half:]


def gather_kernel(count, parts, *refs):
    ins, outs = refs[:parts], refs[parts : 2 * parts]
    send_sem, recv_sem, own_sem = refs[2 * parts :]
    places = count // 2
    me = lax.axis_index("dp")
    place, side = lax.div(me, 2), lax.rem(me, 2)
    across = me + 1 - 2 * side
    barrier = pltpu.get_barrier_semaphore()

    def greet(device):
        pl.semaphore_signal(
            barrier, inc=1, device_id={"dp": device}, device_id_type=pl.DeviceIdType.MESH
        )

    greet(across)
    for step in (-1, 1):
        there = place + step

        @pl.when((there >= 0) & (there < places))
        def greet_place(step=step):
            greet(me + 2 * step)

    neighbours = 1 + (place > 0).astype(jnp.int32) + (place < places - 1).astype(jnp.int32)
    pl.semaphore_wait(barrier, neighbours)

    def copy(part, slot, kind, device, own):
        return pltpu.make_async_remote_copy(
            src_ref=ins[part] if own else outs[part].at[slot],
            dst_ref=outs[part].at[slot],
            send_sem=send_sem.at[kind, part, slot],
            recv_sem=recv_sem.at[part, slot],
            device_id={"dp": device},
            device_id_type=pl.DeviceIdType.MESH,
        )

    def passed_on(slot, steps, own, act):
        for step in steps:
            there = place + step

            @pl.when((there >= 0) & (there < places))
            def along(step=step):
                for part in range(parts):
                    act(copy(part, slot, step + 1, me + 2 * step, own))

        for part in range(parts):
            act(copy(part, slot, 1, across, own))

    def start(one):
        one.start()

    def sent(one):
        one.wait_send()

    mine = [
        pltpu.make_async_copy(ins[part], outs[part].at[me], own_sem.at[part])
        for part in range(parts)
    ]
    for one in mine:
        one.start()
    passed_on(me, (-1, 1), True, start)
    for far in range(1, places):
        for step in (-1, 1):
            origin = place - step * far

            @pl.when((origin >= 0) & (origin < places))
            def forward(step=step, far=far):
                slot = me - 2 * step * far
                for part in range(parts):
                    copy(part, slot, 1, across, False).wait_recv()
                passed_on(slot, (step,), False, start)

    for at in range(places):
        for part in range(parts):
            copy(part, 2 * at + 1 - side, 1, across, False).wait_recv()
    for one in mine:
        one.wait()
    passed_on(me, (-1, 1), True, sent)
    for far in range(1, places):
        for step in (-1, 1):
            origin = place - step * far

            @pl.when((origin >= 0) & (origin < places))
            def forwarded(step=step, far=far):
                passed_on(me - 2 * step * far, (step,), False, sent)


def gathered(*values):
    count = lax.axis_size("dp")
    parts = len(values)
    anywhere = pl.BlockSpec(memory_space=pl.ANY)
    size = sum(math.prod(value.shape) * 2 for value in values)
    return pl.pallas_call(
        partial(gather_kernel, count, parts),
        in_specs=[anywhere] * parts,
        out_specs=[anywhere] * parts,
        out_shape=[jax.ShapeDtypeStruct((count, *value.shape), value.dtype) for value in values],
        scratch_shapes=[
            pltpu.SemaphoreType.DMA((3, parts, count)),
            pltpu.SemaphoreType.DMA((parts, count)),
            pltpu.SemaphoreType.DMA((parts,)),
        ],
        compiler_params=pltpu.CompilerParams(collective_id=0, has_side_effects=True),
        cost_estimate=pl.CostEstimate(
            flops=0, transcendentals=0, bytes_accessed=2 * count * size
        ),
    )(*values)


def other_joined(own, first_shard, second_shard):
    count = lax.axis_size("ctx")
    if count == 2:
        return by_ctx(own, swapped(own, "ctx"))
    del first_shard, second_shard
    every = lax.all_gather(own, "ctx")
    return every[0], every[1]


def expert_weight_products(rows, hidden_grads, grads, actives):
    pairs = ((rows, hidden_grads), (grads, actives))
    far = [contract_rows(left, rights[1]) for left, rights in pairs]
    if lax.axis_size("ctx") == 2:
        far = [value.astype(BF16) for value in far]
    return [contract_rows(left, rights[0]) for left, rights in pairs], far


def sent_far(value):
    return swapped(value, "ctx") if lax.axis_size("ctx") == 2 else value


def expert_weight_parts(near, far):
    count = lax.axis_size("dp")
    parts = []
    for own, other in zip(near, far):
        if lax.axis_size("ctx") == 2:
            part = own + other.astype(F32)
        else:
            part = lax.psum_scatter(
                jnp.concatenate([own, other], axis=1), "ctx", scatter_dimension=1, tiled=True
            )
        parts.append(part.astype(BF16).reshape(count, part.shape[0] // count, part.shape[1]))
    return jnp.concatenate(parts, axis=1)


def expert_weight_blocks(blocks, experts):
    count = lax.axis_size("dp")
    if count != experts:
        blocks = jnp.sum(
            blocks.reshape(count // experts, experts, *blocks.shape[1:]).astype(F32), axis=0
        ).astype(BF16)
    shard = blocks.shape[1] // 2
    return blocks[:, :shard], blocks[:, shard:]


def far_hidden(blocks):
    if lax.axis_size("ctx") == 2:
        return swapped(blocks, "ctx")
    return lax.all_gather(blocks, "ctx", axis=2, tiled=True)


def expert_weight_grad(blocks, far_blocks):
    if lax.axis_size("ctx") == 2:
        far_blocks = jnp.concatenate(by_ctx(blocks, far_blocks), axis=2)
    return far_blocks.astype(F32)


def pair_products(first, second):
    if lax.axis_size("ctx") != 2:
        return contract_rows(*first), contract_rows(*second).astype(BF16)
    lefts, rights = by_ctx(first[0], second[0]), by_ctx(first[1], second[1])
    return contract_rows(lefts[0], rights[0]), contract_rows(lefts[1], rights[1]).astype(BF16)


def product_part(near, far):
    count = lax.axis_size("dp")

    def blocks(value):
        return value.astype(BF16).reshape(count, value.shape[0] // count, value.shape[1])

    if lax.axis_size("ctx") != 2:
        return jnp.concatenate([blocks(near), blocks(far)], axis=1)
    return blocks(near + far.astype(F32))


def product_shards(blocks):
    sums = jnp.sum(blocks.astype(F32), axis=0)
    if lax.axis_size("ctx") == 2:
        return by_ctx(sums, swapped(sums, "ctx"))
    sums = lax.psum(sums, "ctx")
    rows = sums.shape[0] // 2
    return sums[:rows], sums[rows:]


def local(
    hidden_in,
    out_grad,
    norm1_gain,
    in_weight,
    conv_weight,
    conv_bias,
    xproj_weight,
    dt_weight,
    dt_bias,
    decay_log,
    skip_weight,
    out_weight,
    norm2_gain,
    router_weight,
    fc1_weight,
    fc2_weight,
    expert_ids,
    keep_mask,
):
    batches, seqs, length, model_width = hidden_in.shape
    chains = batches * seqs
    tokens = chains * length
    steps = length // SEGMENTS
    shard, _, inner = in_weight.shape
    taps = conv_weight.shape[0]
    low_rank = dt_weight.shape[0]
    states = decay_log.shape[0]
    experts = fc1_weight.shape[0]
    dp_count = lax.axis_size("dp")
    tp_count = lax.axis_size("tp")
    capacity = tokens // 4
    part_cap = capacity // tp_count // HALVES
    slots = experts * part_cap
    tp_index = lax.axis_index("tp")
    scan = Scan(steps, chains, states, inner)

    def to_rows(value):
        value = value.reshape(chains, SEGMENTS, steps, -1).transpose(2, 0, 1, 3)
        return value.reshape(tokens, -1)

    def from_rows(value):
        value = value.reshape(steps, chains, SEGMENTS, -1).transpose(1, 2, 0, 3)
        return value.reshape(batches, seqs, length, -1)

    pieces = [
        norm1_gain[None],
        conv_weight,
        conv_bias[None],
        dt_weight,
        dt_bias[None],
        decay_log,
        skip_weight[None],
        norm2_gain[None],
        router_weight.T,
        xproj_weight.T,
    ]
    bounds = [0]
    for piece in pieces:
        bounds.append(bounds[-1] + piece.shape[0])
    small = sum(
        jnp.pad(piece, ((low, bounds[-1] - high), (0, 0)))
        for piece, low, high in zip(pieces, bounds, bounds[1:])
    )
    kinds = small.shape[0]
    small_wide = jnp.pad(small.T, ((0, 0), (0, -kinds % LANES)))
    in_x, small_all, later = gathered(
        in_weight[:, 0], small_wide, by_ctx(out_weight.T, in_weight[:, 1])[0]
    )
    in_x = in_x.reshape(dp_count * shard, inner)
    later = later.reshape(dp_count * shard, inner)
    small_all = small_all.reshape(dp_count * shard, -1)[:, :kinds].T
    small_all, up_shards, down_shards = together(
        small_all, fc1_weight, fc2_weight.transpose(0, 2, 1)
    )
    pieces = [small_all[bounds[i] : bounds[i + 1]] for i in range(len(bounds) - 1)]
    gain_one_f = pieces[0].astype(F32)
    tap_weights = pieces[1].astype(F32)
    conv_shift = pieces[2].astype(F32)
    dt_proj = pieces[3]
    dt_shift = pieces[4].astype(F32)
    decay_rate = -jnp.exp(pieces[5].astype(F32))
    skip_row = pieces[6].astype(F32)
    gain_two_f = pieces[7].astype(F32)
    router_t = pieces[8]
    x_proj_t = pieces[9]
    rate_rows = jnp.broadcast_to((decay_rate * LOG2E)[:, None, :], (states, SEGMENTS, inner))
    expert_blocks = own_expert_blocks(up_shards, down_shards)

    values = to_rows(hidden_in).astype(F32)
    normalized_rows, inverse_one = rms_forward(values, gain_one_f)
    normed_bf = normalized_rows.astype(BF16)
    x_pre = jnp.dot(normed_bf, in_x, preferred_element_type=F32).astype(BF16)
    x_pre = x_pre.reshape(steps, chains, SEGMENTS, inner)
    tail = x_pre[steps - taps + 1 :]
    edge_in = passed_along(tail[:, :, SEGMENTS - 1 :], "ctx", 1)
    edge_in, later = together(edge_in, later)
    out_proj_t, in_z = other_joined(later, out_weight.T, in_weight[:, 1])
    halo = jnp.concatenate([edge_in, tail[:, :, : SEGMENTS - 1]], axis=2)
    extended_bf = jnp.concatenate([halo, x_pre], axis=0)
    extended = extended_bf.astype(F32)
    conv_pre = jnp.broadcast_to(conv_shift[0], x_pre.shape)
    for tap in range(taps):
        conv_pre = conv_pre + tap_weights[tap] * extended[tap : tap + steps]
    xconv_bf = jax.nn.silu(conv_pre).astype(BF16)
    xconv = xconv_bf.astype(F32)
    xconv_rows = xconv_bf.reshape(tokens, inner)
    projected = axis_sum(contract_cols(xconv_rows, x_proj_t), "tp")
    dt_low = projected[:, :low_rank].astype(BF16)

    def mixes(value):
        value = value.reshape(steps, chains, SEGMENTS, states).transpose(1, 0, 3, 2)
        return jnp.broadcast_to(value[..., None], (*value.shape, LANES))

    mix_in = mixes(projected[:, low_rank : low_rank + states])
    mix_out = mixes(projected[:, low_rank + states :])
    dt_pre = (jnp.dot(dt_low, dt_proj, preferred_element_type=F32) + dt_shift).reshape(x_pre.shape)
    step_size = jax.nn.softplus(dt_pre)
    seg_decay, seg_state, last_state = scan.ends(step_size, xconv, mix_in, rate_rows)
    later_ids, later_mask, later_grad, _ = together(expert_ids, keep_mask, out_grad, seg_state)
    route = to_rows(later_ids)[:, 0]
    keep = to_rows(later_mask)[:, 0].astype(F32)
    onehot_int = (route[:, None] == jnp.arange(experts, dtype=jnp.int32)[None, :]).astype(jnp.int32)
    rank = jnp.sum((jnp.cumsum(onehot_int, axis=0) - 1) * onehot_int, axis=1)
    places = []
    for half in range(HALVES):
        own = rank - (tp_index * HALVES + half) * part_cap
        token_slot = jnp.where((own >= 0) & (own < part_cap), route * part_cap + own, -1)
        places.append(
            (token_slot[None, :] == jnp.arange(slots, dtype=jnp.int32)[:, None]).astype(BF16)
        )

    def slotted(value, half):
        sent = jnp.dot(places[half], value, preferred_element_type=F32).astype(BF16)
        return sent.reshape(experts, part_cap, -1)

    def landed(values):
        total = sum(
            contract_rows(place, value.reshape(slots, -1)) for place, value in zip(places, values)
        )
        return axis_sum(total.astype(BF16), "tp").astype(F32)

    def halves_of(value):
        return [value[:, at : at + part_cap] for at in range(0, value.shape[1], part_cap)]

    cotan_bf = to_rows(later_grad)
    cotan = cotan_bf.astype(F32)
    kept_cotan = (cotan * keep[:, None]).astype(BF16)
    sent_cotan = jnp.concatenate([slotted(kept_cotan, half) for half in range(HALVES)], axis=1)
    entering = entering_pieces(seg_decay[:, :, SEGMENTS - 1], last_state, "ctx", False)
    entering, mix_out, expert_blocks, sent_cotan = together(
        entering, mix_out, expert_blocks, sent_cotan
    )
    slot_cotan = expert_exchange(sent_cotan, experts)
    far_up, far_down = other_hidden(expert_blocks)
    scan_out, seg_start = scan.run(
        step_size, xconv, mix_in, mix_out, rate_rows, seg_decay, seg_state, entering
    )
    z_gate = jnp.dot(normed_bf, in_z, preferred_element_type=F32).reshape(x_pre.shape)
    scanned = scan_out + skip_row[0] * xconv
    z_silu = jax.nn.silu(z_gate)
    gated_bf = (scanned * z_silu).astype(BF16).reshape(tokens, inner)
    gated_bf, slot_cotan, far_up = together(gated_bf, slot_cotan, far_up)
    middle = values + axis_sum(contract_cols(gated_bf, out_proj_t), "tp")

    normed_two, inverse_two = rms_forward(middle, gain_two_f)
    normed_two_bf = normed_two.astype(BF16)
    expert_mask = (
        jnp.arange(experts, dtype=jnp.int32) == lax.rem(lax.axis_index("dp"), experts)
    ).astype(F32)[None, :]
    kept = ()
    got_grads, slot_outs, router_grad_t = [], [], 0.0
    for half, half_cotan in enumerate(halves_of(slot_cotan)):
        own_rows = expert_exchange(slotted(normed_two_bf, half), experts)
        if not half:
            own_rows, far_down = together(own_rows, far_down)
        else:
            own_rows, kept = together(own_rows, kept)
        own_rows = own_rows.reshape(slots, model_width)
        half_cotan = half_cotan.reshape(slots, model_width)
        far_rows, far_cotan = swapped(own_rows, "tp"), swapped(half_cotan, "tp")
        call = partial(
            expert_call, router_t=router_t, mask=expert_mask, blocks=expert_blocks, far_up=far_up,
            far_down=far_down, parts=2 * HALVES,
        )
        far = call(far_rows, far_cotan, part=2 * half, kept=kept)
        near = call(own_rows, half_cotan, part=2 * half + 1, kept=far[3:])
        if half:
            near, got_grads = together(near, got_grads)
        kept = near[3:]
        slot_out = near[0] + swapped(far[0], "tp")
        picked_grad = near[1] + swapped(far[1], "tp")
        slot_prob = near[2]
        slot_gate = jnp.sum(slot_prob * expert_mask, axis=1, keepdims=True)
        gate_grad = jnp.sum(slot_out * half_cotan.astype(F32), axis=1, keepdims=True)
        logit_grad = gate_grad * slot_gate * (expert_mask - slot_prob)
        router_grad_t = router_grad_t + contract_rows(logit_grad, own_rows.astype(F32), HIGHEST)
        picked_grad = picked_grad + jnp.dot(
            logit_grad, router_t.astype(F32), precision=HIGHEST, preferred_element_type=F32
        )
        got_grads.append(
            expert_exchange(picked_grad.astype(BF16).reshape(experts, part_cap, -1), experts)
        )
        slot_outs.append(slot_out.astype(BF16).reshape(experts, part_cap, -1))
    router_grad_t = axis_sum(router_grad_t, "tp")
    all_rows, all_grads, active_a, active_b, hidden_a, hidden_b = kept
    near_parts, far_parts = expert_weight_products(
        all_rows, (hidden_a, hidden_b), all_grads, (active_a, active_b)
    )
    far_first = sent_far(far_parts[0])
    got_grads, near_parts, far_second, far_first, slot_outs, router_grad_t = together(
        got_grads, near_parts, far_parts[1], far_first, slot_outs, router_grad_t
    )
    far_parts = far_first, sent_far(far_second)
    normed_two_grad = landed(got_grads)
    got_out = expert_exchange(jnp.concatenate(slot_outs, axis=1), experts)
    middle_norm_grad, gain_two_grad = rms_backward(middle, inverse_two, gain_two_f, normed_two_grad)
    middle_grad = cotan + middle_norm_grad
    mixer_grad_bf = middle_grad.astype(BF16)
    gated_grad = jnp.dot(mixer_grad_bf, out_proj_t, preferred_element_type=F32).reshape(x_pre.shape)
    scan_grad = gated_grad * z_silu
    z_grad = jax.vjp(jax.nn.silu, z_gate)[1](gated_grad * scanned)[0]
    z_grad_bf = z_grad.astype(BF16).reshape(tokens, inner)
    near_product, far_product = pair_products((mixer_grad_bf, gated_bf), (normed_bf, z_grad_bf))
    back_decay, back_adjoint, first_adjoint = scan.adjoint_ends(
        step_size, mix_out, scan_grad, rate_rows
    )
    normed_part = contract_cols(z_grad_bf, in_z)
    far_parts, got_out, near_product, far_product, normed_part, _ = together(
        far_parts, got_out, near_product, far_product, normed_part, first_adjoint
    )
    weight_blocks = lax.all_to_all(
        expert_weight_parts(near_parts, far_parts), "dp", 0, 0, tiled=True
    )
    leaving = entering_pieces(back_decay[:, :, 0], first_adjoint, "ctx", True)
    leaving, near_product, far_product = together(leaving, near_product, far_product)
    far_product = sent_far(far_product)
    adjoint_args = (
        step_size, xconv, mix_in, mix_out, scan_grad, rate_rows, seg_start, back_decay, back_adjoint,
        leaving, skip_row,
    )
    pre_grad, xconv_grad, decay_sum, scan_sums, mix_grad = scan.adjoint(adjoint_args)
    pre_grad, far_product, weight_blocks = together(pre_grad, far_product, weight_blocks)
    weight_blocks = expert_weight_blocks(weight_blocks, experts)
    far_ups = far_hidden(weight_blocks[0])
    out_blocks = lax.all_to_all(product_part(near_product, far_product), "dp", 0, 0, tiled=True)
    decay_log_grad = jnp.sum(decay_sum, axis=0) * decay_rate
    dt_shift_grad, skip_grad = jnp.sum(scan_sums, axis=0)[:2]
    pre_grad = pre_grad.reshape(tokens, inner)
    dt_proj_grad = contract_rows(dt_low.astype(F32), pre_grad, HIGHEST)
    dt_low_grad = contract_cols(pre_grad, dt_proj.astype(F32), HIGHEST)
    mix_grad = mix_grad.reshape(tokens, LANES)[:, : 2 * states]
    proj_part = jnp.concatenate([dt_low_grad, mix_grad], axis=1)
    proj_grad_bf = axis_sum(proj_part, "tp").astype(BF16)
    x_proj_grad_t = contract_rows(proj_grad_bf, xconv_rows)
    flat = (chains * SEGMENTS, inner)
    x_grad_bf, conv_sums, head, last = conv_back(
        proj_grad_bf,
        x_proj_t,
        xconv_grad.reshape(steps, *flat),
        extended_bf.reshape(steps + taps - 1, *flat),
        tap_weights,
        conv_shift,
    )
    taps_grad, shift_grad = conv_sums[:taps], conv_sums[taps]
    edge_back = passed_along(
        head.reshape(taps - 1, chains, SEGMENTS, inner)[:, :, :1], "ctx", -1
    )
    edge_back, out_blocks, far_ups = together(edge_back, out_blocks, far_ups)
    reaching = jnp.stack(
        [
            sum(tap_weights[tap] * edge_back[at - tap] for tap in range(at + 1))
            for at in range(taps - 1)
        ]
    )
    reaching = jnp.pad(reaching, ((0, 0), (0, 0), (SEGMENTS - 1, 0), (0, 0)))
    last = (last + reaching.reshape(taps - 1, *flat)).astype(BF16)
    x_grad_bf = lax.dynamic_update_slice(x_grad_bf, last, (steps - taps + 1, 0, 0))
    x_grad_bf = x_grad_bf.reshape(tokens, inner)
    small_grads = jnp.concatenate(
        [
            taps_grad,
            shift_grad[None],
            dt_proj_grad,
            dt_shift_grad[None],
            decay_log_grad,
            skip_grad[None],
            gain_two_grad[None],
            router_grad_t,
            x_proj_grad_t,
        ],
        axis=0,
    )
    small_grads = small_grads.reshape(-1, dp_count, shard).transpose(1, 0, 2)
    small_size = small_grads.shape[1] * shard
    small_rows = small_grads.astype(BF16).reshape(dp_count, small_size)
    small_rows = jnp.pad(small_rows, ((0, 0), (0, -small_size % inner))).reshape(dp_count, -1, inner)
    x_grad_bf, small_rows, out_blocks = together(x_grad_bf, small_rows, out_blocks)
    normed_part = normed_part + contract_cols(x_grad_bf, in_x)
    normed_grad = axis_sum(normed_part, "tp")
    values_norm_grad, gain_one_grad = rms_backward(values, inverse_one, gain_one_f, normed_grad)
    input_grad = from_rows((middle_grad + values_norm_grad).astype(BF16))

    in_x_part = contract_rows(normed_bf, x_grad_bf).astype(BF16).reshape(dp_count, shard, inner)
    gain_row = gain_one_grad.reshape(dp_count, 1, shard)
    gain_high = gain_row.astype(BF16)
    gain_low = (gain_row - gain_high.astype(F32)).astype(BF16)
    gain_rows = jnp.concatenate([gain_high, gain_low], axis=1)
    gain_rows = jnp.pad(gain_rows, ((0, 0), (0, 6), (0, inner - shard)))
    in_x_part, out_blocks = together(in_x_part, out_blocks)
    out_proj_grad, in_z_grad = product_shards(out_blocks)
    in_x_blocks = lax.all_to_all(
        jnp.concatenate([in_x_part, gain_rows, small_rows], axis=1), "dp", 0, 0, tiled=True
    )
    out_proj_grad, in_z_grad, far_down_blocks = together(
        out_proj_grad, in_z_grad, weight_blocks[1]
    )
    far_downs, in_x_blocks = together(far_hidden(far_down_blocks), in_x_blocks)
    first_grad = expert_weight_grad(weight_blocks[0], far_ups)
    second_grad = expert_weight_grad(weight_blocks[1], far_downs)
    router_prob = jax.nn.softmax(contract_cols(normed_two_bf, router_t), axis=-1)
    gate_prob = jnp.sum(router_prob * onehot_int.astype(F32), axis=1) * keep
    result = from_rows((middle + gate_prob[:, None] * landed(halves_of(got_out))).astype(BF16))
    in_x_sums = axis_sum(jnp.sum(in_x_blocks.astype(F32), axis=0), "ctx")
    in_x_grad = in_x_sums[:shard]
    gain_one_grad = in_x_sums[shard : shard + 1, :shard] + in_x_sums[shard + 1 : shard + 2, :shard]
    small_grads = in_x_sums[shard + 8 :].reshape(-1)[:small_size].reshape(-1, shard)
    small_grads = jnp.concatenate([gain_one_grad, small_grads], axis=0)
    sums = [small_grads[bounds[i] : bounds[i + 1]] for i in range(len(bounds) - 1)]
    return (
        result,
        input_grad,
        sums[0][0],
        jnp.stack([in_x_grad, in_z_grad], axis=1),
        sums[1],
        sums[2][0],
        sums[9].T,
        sums[3],
        sums[4][0],
        sums[5],
        sums[6][0],
        out_proj_grad.T,
        sums[7][0],
        sums[8].T,
        first_grad,
        second_grad.transpose(0, 2, 1),
    )


def solution(mesh):
    weights = (
        P("dp"),
        P("dp", None, "tp"),
        P(None, ("tp", "dp")),
        P(("tp", "dp")),
        P(("tp", "dp"), None),
        P(None, ("tp", "dp")),
        P(("tp", "dp")),
        P(None, ("tp", "dp")),
        P(("tp", "dp")),
        P("tp", "dp"),
        P("dp"),
        P("dp", None),
        P(None, "dp", "tp"),
        P(None, "tp", "dp"),
    )
    rows = P(None, "dp", "ctx", None)
    return jax.shard_map(
        local,
        mesh=mesh,
        in_specs=(rows, rows, *weights, P(("dp", "ctx"), None), P(("dp", "ctx"))),
        out_specs=(rows, rows, *weights),
        check_vma=False,
    )
```

```python
from functools import partial
import math

import jax
import jax.numpy as jnp
from jax import lax
from jax.experimental import pallas as pl
from jax.experimental.pallas import tpu as pltpu
from jax.sharding import PartitionSpec as P

EPSILON = 1e-05
HIGHEST = lax.Precision.HIGHEST
SEGMENTS = 8
LANES = 128
VMEM_LIMIT = 56 * 1024 * 1024
EXPERT_VMEM = 56 * 1024 * 1024
LOG2E = math.log2(math.e)
GROUP_A = 4
GROUP_B = 4
GROUP_C = 8
UNROLL_A = 8
UNROLL_B = 8
UNROLL_C = 8
UNROLL_D = 4
UNROLL_E = 8
BLOCKS = 3
COVER = 100
HALVES = 1
BF16 = jnp.bfloat16
F32 = jnp.float32


def swapped(value, axis):
    return lax.ppermute(value, axis, [(0, 1), (1, 0)])


def passed_along(value, axis, steps):
    count = lax.axis_size(axis)
    leading, last = (max(0, -steps), min(count, count - steps))
    return lax.ppermute(value, axis, [(source, source + steps) for source in range(leading, last)])


def axis_sum(value, axis):
    if lax.axis_size(axis) == 2:
        return value + swapped(value, axis)
    return lax.psum(value, axis)


def together(*values):
    return lax.optimization_barrier(values)


def entering_pieces(decay, value, axis, backward):
    count = lax.axis_size(axis)
    if count == 2:
        return passed_along(value, axis, -1 if backward else 1)
    mine = lax.axis_index(axis)
    decays = lax.all_gather(decay, axis)
    values = lax.all_gather(value, axis)
    running = jnp.zeros_like(value)
    for position in range(count - 1):
        at = count - 1 - position if backward else position
        longer = values[at] + decays[at] * running
        ahead = at > mine if backward else at < mine
        running = jnp.where(ahead, longer, running)
    return running


def contract_rows(left_side, right_side, precision=None):
    return lax.dot_general(
        left_side,
        right_side,
        (((0,), (0,)), ((), ())),
        precision=precision,
        preferred_element_type=F32,
    )


def contract_cols(left_side, right_side, precision=None):
    return lax.dot_general(
        left_side,
        right_side,
        (((1,), (1,)), ((), ())),
        precision=precision,
        preferred_element_type=F32,
    )


def rms_forward(values, gain_vec):
    inverse = lax.rsqrt(jnp.mean(values * values, axis=-1, keepdims=True) + EPSILON)
    return (values * inverse * gain_vec, inverse)


def rms_backward(values, inverse, gain_vec, grad_out):
    weighted = grad_out * gain_vec
    inner_mean = jnp.mean(values * weighted, axis=-1, keepdims=True)
    grad_values = inverse * weighted - values * inverse * inverse * inverse * inner_mean
    grad_gain = jnp.sum(grad_out * values * inverse, axis=0)
    return (grad_values, grad_gain)


def zeros_of(ref):
    return jnp.zeros(ref.shape[1:], F32)


def sublane_rows(lanes):
    return lax.broadcasted_iota(jnp.int32, (SEGMENTS, lanes), 0)


def widened(value, lanes):
    return jnp.concatenate([value] * (lanes // LANES), axis=1) if lanes > LANES else value


def narrowed(value):
    parts = [value[:, at : at + LANES] for at in range(0, value.shape[1], LANES)]
    return sum(parts[1:], parts[0])


def groups_of(states, size):
    size = math.gcd(states, size)
    return [range(first, first + size) for first in range(0, states, size)]


def joined_forward(decay, value, row):
    for reach in (1, 2, 4):
        inside = row >= reach
        value = value + jnp.where(inside, decay * pltpu.roll(value, reach, 0), 0.0)
        decay = jnp.where(inside, decay * pltpu.roll(decay, reach, 0), decay)
    return decay, value


def joined_backward(decay, value, row):
    for reach in (1, 2, 4):
        inside = row < SEGMENTS - reach
        value = value + jnp.where(inside, decay * pltpu.roll(value, SEGMENTS - reach, 0), 0.0)
        decay = jnp.where(inside, decay * pltpu.roll(decay, SEGMENTS - reach, 0), decay)
    return decay, value


def ends_kernel(step_ref, input_ref, mix_in_ref, rate_ref, decay_ref, state_ref, last_ref):
    steps, states, lanes = step_ref.shape[0], mix_in_ref.shape[1], step_ref.shape[2]
    zero = zeros_of(step_ref)
    row = sublane_rows(lanes)
    total = lax.fori_loop(0, steps, lambda at, total: total + step_ref[at], zero, unroll=UNROLL_E)
    for members in groups_of(states, GROUP_A):
        rates = [rate_ref[n] for n in members]

        def body(at, held):
            step = step_ref[at]
            driven = step * input_ref[at]
            return tuple(
                jnp.exp2(step * rate) * before + widened(mix_in_ref[at, n], lanes) * driven
                for n, rate, before in zip(members, rates, held)
            )

        held = lax.fori_loop(0, steps, body, (zero,) * len(members), unroll=UNROLL_A)
        for n, rate, end in zip(members, rates, held):
            decay, value = joined_forward(jnp.exp2(total * rate), end, row)
            decay_ref[n] = decay
            state_ref[n] = value
            last_ref[n : n + 1] = value[SEGMENTS - 1 :]


def states_kernel(
    step_ref, input_ref, mix_in_ref, mix_out_ref, rate_ref, decay_ref, state_ref, enter_ref,
    out_ref, start_ref,
):
    steps, states, lanes = step_ref.shape[0], mix_in_ref.shape[1], step_ref.shape[2]
    row = sublane_rows(lanes)
    for members in groups_of(states, GROUP_B):
        rates = [rate_ref[n] for n in members]
        held = []
        for n in members:
            first = jnp.broadcast_to(enter_ref[n : n + 1], (SEGMENTS, lanes))
            inner = pltpu.roll(state_ref[n], 1, 0) + pltpu.roll(decay_ref[n], 1, 0) * first
            start = jnp.where(row >= 1, inner, first)
            start_ref[n] = start
            held.append(start)

        def body(at, held):
            step = step_ref[at]
            driven = step * input_ref[at]
            held = tuple(
                jnp.exp2(step * rate) * before + widened(mix_in_ref[at, n], lanes) * driven
                for n, rate, before in zip(members, rates, held)
            )
            parts = [widened(mix_out_ref[at, n], lanes) * now for n, now in zip(members, held)]
            if members[0]:
                parts.append(out_ref[at])
            while len(parts) > 1:
                parts = [sum(parts[i + 1 : i + 2], parts[i]) for i in range(0, len(parts), 2)]
            out_ref[at] = parts[0]
            return held

        lax.fori_loop(0, steps, body, tuple(held), unroll=UNROLL_B)


def adjoint_ends_kernel(step_ref, mix_out_ref, grad_ref, rate_ref, decay_ref, adjoint_ref, first_ref):
    steps, states, lanes = step_ref.shape[0], mix_out_ref.shape[1], step_ref.shape[2]
    zero = zeros_of(step_ref)
    row = sublane_rows(lanes)
    total = lax.fori_loop(0, steps, lambda at, total: total + step_ref[at], zero, unroll=UNROLL_E)
    for members in groups_of(states, GROUP_A):
        rates = [rate_ref[n] for n in members]

        def body(back, incoming):
            at = steps - 1 - back
            step = step_ref[at]
            grad = grad_ref[at]
            return tuple(
                jnp.exp2(step * rate) * (widened(mix_out_ref[at, n], lanes) * grad + after)
                for n, rate, after in zip(members, rates, incoming)
            )

        incoming = lax.fori_loop(0, steps, body, (zero,) * len(members), unroll=UNROLL_A)
        for n, rate, end in zip(members, rates, incoming):
            decay, value = joined_backward(jnp.exp2(total * rate), end, row)
            decay_ref[n] = decay
            adjoint_ref[n] = value
            first_ref[n : n + 1] = value[:1]


def adjoint_kernel(
    step_ref, input_ref, mix_in_ref, mix_out_ref, grad_ref, rate_ref, start_ref, decay_ref, adjoint_ref,
    enter_ref, skip_ref,
    pre_out_ref, conv_ref, decay_sum_ref, sums_ref, mix_ref,
    states_ref, decays_ref, in_grad_ref, out_grad_ref, pre_ref,
):
    steps, states, lanes = step_ref.shape[0], mix_in_ref.shape[1], step_ref.shape[2]
    row = sublane_rows(lanes)
    zero = zeros_of(step_ref)

    @pl.when(pl.program_id(1) == 0)
    def clear():
        in_grad_ref[...] = jnp.zeros_like(in_grad_ref)
        out_grad_ref[...] = jnp.zeros_like(out_grad_ref)

    for members in groups_of(states, GROUP_C):
        first, group = members[0], len(members)
        rates = [rate_ref[n] for n in members]

        def ahead(at, held):
            step = step_ref[at]
            driven = step * input_ref[at]
            grad = grad_ref[at]
            after = []
            for i, n in enumerate(members):
                states_ref[at, i] = held[i]
                decay = jnp.exp2(step * rates[i])
                decays_ref[at, i] = decay
                now = decay * held[i] + widened(mix_in_ref[at, n], lanes) * driven
                out_grad_ref[at, n] += narrowed(grad * now)
                after.append(now)
            return tuple(after)

        lax.fori_loop(0, steps, ahead, tuple(start_ref[n] for n in members), unroll=UNROLL_C)

        incoming = []
        for n in members:
            final = jnp.broadcast_to(enter_ref[n : n + 1], (SEGMENTS, lanes))
            inner = (
                pltpu.roll(adjoint_ref[n], SEGMENTS - 1, 0)
                + pltpu.roll(decay_ref[n], SEGMENTS - 1, 0) * final
            )
            incoming.append(jnp.where(row < SEGMENTS - 1, inner, final))

        def body(back, carry):
            at = steps - 1 - back
            incoming, decay_sums = carry
            step = step_ref[at]
            grad = grad_ref[at]
            driven = step * input_ref[at]
            in_sum = conv_ref[at] if first else zero
            rate_sum = pre_ref[at] if first else zero
            following, sums = [], []
            for i, n in enumerate(members):
                adjoint = widened(mix_out_ref[at, n], lanes) * grad + incoming[i]
                onward = decays_ref[at, i] * adjoint
                decay_grad = onward * states_ref[at, i]
                in_sum = in_sum + adjoint * widened(mix_in_ref[at, n], lanes)
                rate_sum = rate_sum + decay_grad * rates[i]
                sums.append(decay_sums[i] + decay_grad * step)
                in_grad_ref[at, n] += narrowed(adjoint * driven)
                following.append(onward)
            conv_ref[at] = in_sum
            pre_ref[at] = rate_sum
            return tuple(following), tuple(sums)

        _, sums = lax.fori_loop(
            0, steps, body, (tuple(incoming), (zero,) * group), unroll=UNROLL_D
        )
        for i, n in enumerate(members):
            decay_sum_ref[n : n + 1] = jnp.sum(sums[i], axis=0, keepdims=True)

    skip = skip_ref[...]

    def close(at, carry):
        pre_sum, skip_sum = carry
        step, inputs, grad, in_sum = step_ref[at], input_ref[at], grad_ref[at], conv_ref[at]
        step_grad = pre_ref[at] * (1.0 / LOG2E) + in_sum * inputs
        pre = step_grad * (1.0 - jnp.exp2(step * -LOG2E))
        pre_out_ref[at] = pre.astype(BF16)
        conv_ref[at] = in_sum * step + skip * grad
        return pre_sum + pre, skip_sum + grad * inputs

    pre_sum, skip_sum = lax.fori_loop(0, steps, close, (zero, zero), unroll=UNROLL_E)
    sums_ref[0:1] = jnp.sum(pre_sum, axis=0, keepdims=True)
    sums_ref[1:2] = jnp.sum(skip_sum, axis=0, keepdims=True)
    sums_ref[2:] = jnp.zeros((SEGMENTS - 2, lanes), F32)

    @pl.when(pl.program_id(1) == pl.num_programs(1) - 1)
    def across_lanes():
        lane = lax.broadcasted_iota(jnp.int32, (SEGMENTS, LANES), 1)

        def one(at, carry):
            total = jnp.zeros((SEGMENTS, LANES), F32)
            for n in range(states):
                for base, ref in ((0, in_grad_ref), (states, out_grad_ref)):
                    value = jnp.sum(ref[at, n], axis=1, keepdims=True)
                    total = jnp.where(lane == base + n, value, total)
            mix_ref[at] = total
            return carry

        lax.fori_loop(0, steps, one, 0, unroll=UNROLL_E)


class Scan:
    def __init__(self, steps, chains, states, width):
        lanes = LANES * math.gcd(width // LANES, BLOCKS)
        self.grid = (chains, width // lanes)
        self.rows_spec = pl.BlockSpec(
            (steps, None, SEGMENTS, lanes), lambda chain, block: (0, chain, 0, block)
        )
        self.mix_spec = pl.BlockSpec(
            (None, steps, states, SEGMENTS, LANES), lambda chain, block: (chain, 0, 0, 0, 0)
        )
        self.rate_spec = pl.BlockSpec((states, SEGMENTS, lanes), lambda chain, block: (0, 0, block))
        self.state_spec = pl.BlockSpec(
            (None, states, SEGMENTS, lanes), lambda chain, block: (chain, 0, 0, block)
        )
        self.edge_spec = pl.BlockSpec((None, states, lanes), lambda chain, block: (chain, 0, block))
        self.rows = jax.ShapeDtypeStruct((steps, chains, SEGMENTS, width), F32)
        self.mix = jax.ShapeDtypeStruct((chains, steps, states, SEGMENTS, LANES), F32)
        self.state = jax.ShapeDtypeStruct((chains, states, SEGMENTS, width), F32)
        self.edge = jax.ShapeDtypeStruct((chains, states, width), F32)
        self.sums = jax.ShapeDtypeStruct((chains, SEGMENTS, width), F32)
        self.sums_spec = pl.BlockSpec((None, SEGMENTS, lanes), lambda chain, block: (chain, 0, block))
        self.lane_sums = jax.ShapeDtypeStruct((steps, chains, SEGMENTS, LANES), F32)
        self.lane_spec = pl.BlockSpec(
            (steps, None, SEGMENTS, LANES), lambda chain, block: (0, chain, 0, 0)
        )
        self.skip_spec = pl.BlockSpec((1, lanes), lambda chain, block: (0, block))
        self.scratch = [
            pltpu.VMEM((steps, math.gcd(states, GROUP_C), SEGMENTS, lanes), F32),
            pltpu.VMEM((steps, math.gcd(states, GROUP_C), SEGMENTS, lanes), F32),
            pltpu.VMEM((steps, states, SEGMENTS, LANES), F32),
            pltpu.VMEM((steps, states, SEGMENTS, LANES), F32),
            pltpu.VMEM((steps, SEGMENTS, lanes), F32),
        ]
        self.narrow_rows = jax.ShapeDtypeStruct((steps, chains, SEGMENTS, width), BF16)
        self.work = steps * chains * SEGMENTS * width * states

    def call(self, kernel, ops, args, in_specs, outs, out_specs, scratch=()):
        size = sum(math.prod(a.shape) * a.dtype.itemsize for a in (*args, *outs))
        return pl.pallas_call(
            kernel,
            grid=self.grid,
            in_specs=in_specs,
            out_specs=out_specs,
            out_shape=outs,
            scratch_shapes=list(scratch),
            compiler_params=pltpu.CompilerParams(vmem_limit_bytes=VMEM_LIMIT),
            cost_estimate=pl.CostEstimate(
                flops=ops * self.work, transcendentals=self.work, bytes_accessed=size // COVER
            ),
        )(*args)

    def ends(self, step, inputs, mix_in, rate):
        return self.call(
            ends_kernel, 5, (step, inputs, mix_in, rate),
            [self.rows_spec, self.rows_spec, self.mix_spec, self.rate_spec],
            [self.state, self.state, self.edge],
            [self.state_spec, self.state_spec, self.edge_spec],
        )

    def run(self, step, inputs, mix_in, mix_out, rate, decay, state, enter):
        return self.call(
            states_kernel, 7, (step, inputs, mix_in, mix_out, rate, decay, state, enter),
            [self.rows_spec, self.rows_spec, self.mix_spec, self.mix_spec, self.rate_spec,
             self.state_spec, self.state_spec, self.edge_spec],
            [self.rows, self.state],
            [self.rows_spec, self.state_spec],
        )

    def adjoint_ends(self, step, mix_out, grad, rate):
        return self.call(
            adjoint_ends_kernel, 5, (step, mix_out, grad, rate),
            [self.rows_spec, self.mix_spec, self.rows_spec, self.rate_spec],
            [self.state, self.state, self.edge],
            [self.state_spec, self.state_spec, self.edge_spec],
        )

    def adjoint(self, args):
        return self.call(
            adjoint_kernel, 20, args,
            [self.rows_spec, self.rows_spec, self.mix_spec, self.mix_spec, self.rows_spec,
             self.rate_spec, self.state_spec, self.state_spec, self.state_spec, self.edge_spec,
             self.skip_spec],
            [self.narrow_rows, self.rows, self.edge, self.sums, self.lane_sums],
            [self.rows_spec, self.rows_spec, self.edge_spec, self.sums_spec, self.lane_spec],
            self.scratch,
        )


def conv_back_kernel(
    proj_ref, weight_ref, grad_ref, input_ref, taps_ref, shift_ref,
    out_ref, sums_ref, head_ref, tail_ref, product_ref, conv_ref,
):
    steps, rows, lanes = grad_ref.shape
    count = taps_ref.shape[0]
    reach = count - 1
    taps = [taps_ref[at : at + 1] for at in range(count)]
    shift = shift_ref[...]
    product_ref[...] = jnp.dot(
        proj_ref[...], weight_ref[...], preferred_element_type=F32
    ).reshape(steps, rows, lanes)

    def slopes(at, sums):
        inputs = [input_ref[at + tap].astype(F32) for tap in range(count)]
        pre = shift + sum(tap * value for tap, value in zip(taps, inputs))
        share = 1.0 / (1.0 + jnp.exp(-pre))
        conv = (grad_ref[at] + product_ref[at]) * (share * (1.0 + pre * (1.0 - share)))
        conv_ref[at] = conv
        return (*(total + conv * value for total, value in zip(sums, inputs)), sums[-1] + conv)

    zero = jnp.zeros((rows, lanes), F32)
    sums = lax.fori_loop(0, steps, slopes, (zero,) * (count + 1), unroll=2)
    for at, total in enumerate(sums):
        sums_ref[at : at + 1] = jnp.sum(total, axis=0, keepdims=True)
    sums_ref[count + 1 :] = jnp.zeros((sums_ref.shape[0] - count - 1, lanes), F32)
    row = sublane_rows(lanes)
    for at in range(reach):
        head_ref[at] = conv_ref[at]
        for low in range(0, rows, SEGMENTS):
            rolled = pltpu.roll(conv_ref[at, low : low + SEGMENTS], SEGMENTS - 1, 0)
            conv_ref[steps + at, low : low + SEGMENTS] = jnp.where(
                row < SEGMENTS - 1, rolled, 0.0
            )

    def back(at):
        return sum(taps[tap] * conv_ref[at + reach - tap] for tap in range(count))

    def store(at, carry):
        out_ref[at] = back(at).astype(BF16)
        return carry

    lax.fori_loop(0, steps, store, 0, unroll=2)
    for at in range(reach):
        tail_ref[at] = back(steps - reach + at)


def conv_back(proj, weight, grad, inputs, taps, shift):
    steps, rows, width = grad.shape
    reach = taps.shape[0] - 1
    lanes = LANES * math.gcd(width // LANES, BLOCKS)

    def block(count, dtype=F32):
        spec = pl.BlockSpec((count, rows, lanes), lambda at: (0, 0, at))
        return spec, jax.ShapeDtypeStruct((count, rows, width), dtype)

    def columns(count):
        return pl.BlockSpec((count, lanes), lambda at: (0, at))

    outs = [
        block(steps, BF16),
        (columns(SEGMENTS), jax.ShapeDtypeStruct((SEGMENTS, width), F32)),
        block(reach),
        block(reach),
    ]
    return pl.pallas_call(
        conv_back_kernel,
        grid=(width // lanes,),
        in_specs=[
            pl.BlockSpec(proj.shape, lambda at: (0, 0)),
            columns(weight.shape[0]),
            block(steps)[0],
            block(steps + reach)[0],
            columns(reach + 1),
            columns(1),
        ],
        out_specs=[spec for spec, _ in outs],
        out_shape=[shape for _, shape in outs],
        scratch_shapes=[
            pltpu.VMEM((steps, rows, lanes), F32),
            pltpu.VMEM((steps + reach, rows, lanes), F32),
        ],
        compiler_params=pltpu.CompilerParams(vmem_limit_bytes=VMEM_LIMIT),
        cost_estimate=pl.CostEstimate(flops=1, transcendentals=0, bytes_accessed=1),
    )(proj, weight, grad, inputs, taps, shift)


def expert_kernel(
    kept, rows_ref, cotan_ref, router_ref, mask_ref, up_a, down_a, up_b, down_b, *refs
):
    out_ref, picked_ref, prob_ref, copy_ref, grad_ref, active_a, active_b, hidden_a, hidden_b = refs[kept:]
    rows = rows_ref[...]
    copy_ref[...] = rows
    logits = contract_cols(rows, router_ref[...])
    shifted = jnp.exp(logits - jnp.max(logits, axis=1, keepdims=True))
    prob = shifted / jnp.sum(shifted, axis=1, keepdims=True)
    gate = jnp.sum(prob * mask_ref[...], axis=1, keepdims=True)
    grad = (gate * cotan_ref[...].astype(F32)).astype(BF16)
    prob_ref[...] = prob
    grad_ref[...] = grad
    out, picked = None, None
    for up, down, active_ref, hidden_ref in (
        (up_a, down_a, active_a, hidden_a),
        (up_b, down_b, active_b, hidden_b),
    ):
        up, down = (value[...].reshape(-1, value.shape[2]) for value in (up, down))
        hidden = jnp.dot(rows, up, preferred_element_type=F32)
        share = 0.5 + 0.5 * lax.erf(hidden * math.sqrt(0.5))
        slope = share + hidden * (jnp.exp(-0.5 * hidden * hidden) * (1.0 / math.sqrt(2 * math.pi)))
        active = (hidden * share).astype(BF16)
        active_ref[...] = active
        hidden_grad = (jnp.dot(grad, down, preferred_element_type=F32) * slope).astype(BF16)
        hidden_ref[...] = hidden_grad
        out_part = contract_cols(active, down)
        picked_part = contract_cols(hidden_grad, up)
        out = out_part if out is None else out + out_part
        picked = picked_part if picked is None else picked + picked_part
    out_ref[...] = out
    picked_ref[...] = picked


def expert_call(rows, cotan, router_t, mask, blocks, far_up, far_down, part, parts, kept):
    count, width = rows.shape
    shard, hidden = far_up.shape[1:]
    block = math.gcd(count, 512)
    base = part * (count // block)

    def rows_of(columns, low=0):
        return pl.BlockSpec((block, columns), lambda at: (at + low, 0))

    def whole(array):
        return pl.BlockSpec(array.shape, lambda at: (0, 0), pipeline_mode=pl.Buffered(1))

    def layer(array, at):
        return pl.BlockSpec(
            (array.shape[0], shard, hidden), lambda step: (0, at, 0), pipeline_mode=pl.Buffered(1)
        )

    experts = router_t.shape[0]
    inputs = (rows, cotan, router_t, mask, blocks, blocks, far_up, far_down)
    columns = (width, width, hidden, hidden, hidden, hidden)
    return pl.pallas_call(
        partial(expert_kernel, len(kept)),
        grid=(count // block,),
        in_specs=[
            rows_of(width), rows_of(width), whole(router_t), whole(mask),
            layer(blocks, 0), layer(blocks, 1), layer(far_up, 0), layer(far_down, 0),
            *[pl.BlockSpec(memory_space=pl.ANY)] * len(kept),
        ],
        out_specs=[
            rows_of(width), rows_of(width), rows_of(experts), *(rows_of(one, base) for one in columns)
        ],
        out_shape=[
            *(jax.ShapeDtypeStruct((count, one), F32) for one in (width, width, experts)),
            *(jax.ShapeDtypeStruct((parts * count, one), BF16) for one in columns),
        ],
        input_output_aliases={len(inputs) + at: 3 + at for at in range(len(kept))},
        compiler_params=pltpu.CompilerParams(vmem_limit_bytes=EXPERT_VMEM),
        cost_estimate=pl.CostEstimate(
            flops=16 * count * width * hidden,
            transcendentals=4 * count * hidden,
            bytes_accessed=count * (14 * width + 8 * hidden) + 8 * width * hidden,
        ),
    )(*inputs, *kept)


def expert_exchange(value, experts):
    count = lax.axis_size("dp")
    groups = None
    if count != experts:
        groups = [
            [base + e for e in range(experts)] for base in range(0, count, experts)
        ]
    return lax.all_to_all(value, "dp", 0, 0, axis_index_groups=groups, tiled=True)


def by_ctx(first, second):
    lead = lax.axis_index("ctx") == 0
    return jnp.where(lead, first, second), jnp.where(lead, second, first)


def own_expert_blocks(up_shards, down_shards):
    experts, _, hidden = up_shards.shape
    count = lax.axis_size("dp")
    half = hidden // 2
    both = jnp.concatenate([up_shards, down_shards], axis=1)
    if lax.axis_size("ctx") == 2:
        both = by_ctx(both[:, :, :half], both[:, :, half:])[0]
    if count != experts:
        both = jnp.concatenate([both] * (count // experts), axis=0)
    return lax.all_to_all(both, "dp", 0, 0, tiled=True)


def other_hidden(both):
    rows = both.shape[1] // 2
    if lax.axis_size("ctx") == 2:
        return swapped(both[:, :rows], "ctx"), swapped(both[:, rows:], "ctx")
    half = both.shape[2] // 2
    return both[:, :rows, half:], both[:, rows:, half:]


def gather_kernel(count, parts, *refs):
    ins, outs = refs[:parts], refs[parts : 2 * parts]
    send_sem, recv_sem, own_sem = refs[2 * parts :]
    places = count // 2
    me = lax.axis_index("dp")
    place, side = lax.div(me, 2), lax.rem(me, 2)
    across = me + 1 - 2 * side
    barrier = pltpu.get_barrier_semaphore()

    def greet(device):
        pl.semaphore_signal(
            barrier, inc=1, device_id={"dp": device}, device_id_type=pl.DeviceIdType.MESH
        )

    greet(across)
    for step in (-1, 1):
        there = place + step

        @pl.when((there >= 0) & (there < places))
        def greet_place(step=step):
            greet(me + 2 * step)

    neighbours = 1 + (place > 0).astype(jnp.int32) + (place < places - 1).astype(jnp.int32)
    pl.semaphore_wait(barrier, neighbours)

    def copy(part, slot, kind, device, own):
        return pltpu.make_async_remote_copy(
            src_ref=ins[part] if own else outs[part].at[slot],
            dst_ref=outs[part].at[slot],
            send_sem=send_sem.at[kind, part, slot],
            recv_sem=recv_sem.at[part, slot],
            device_id={"dp": device},
            device_id_type=pl.DeviceIdType.MESH,
        )

    def passed_on(slot, steps, own, act):
        for step in steps:
            there = place + step

            @pl.when((there >= 0) & (there < places))
            def along(step=step):
                for part in range(parts):
                    act(copy(part, slot, step + 1, me + 2 * step, own))

        for part in range(parts):
            act(copy(part, slot, 1, across, own))

    def start(one):
        one.start()

    def sent(one):
        one.wait_send()

    mine = [
        pltpu.make_async_copy(ins[part], outs[part].at[me], own_sem.at[part])
        for part in range(parts)
    ]
    for one in mine:
        one.start()
    passed_on(me, (-1, 1), True, start)
    for far in range(1, places):
        for step in (-1, 1):
            origin = place - step * far

            @pl.when((origin >= 0) & (origin < places))
            def forward(step=step, far=far):
                slot = me - 2 * step * far
                for part in range(parts):
                    copy(part, slot, 1, across, False).wait_recv()
                passed_on(slot, (step,), False, start)

    for at in range(places):
        for part in range(parts):
            copy(part, 2 * at + 1 - side, 1, across, False).wait_recv()
    for one in mine:
        one.wait()
    passed_on(me, (-1, 1), True, sent)
    for far in range(1, places):
        for step in (-1, 1):
            origin = place - step * far

            @pl.when((origin >= 0) & (origin < places))
            def forwarded(step=step, far=far):
                passed_on(me - 2 * step * far, (step,), False, sent)


def gathered(*values):
    count = lax.axis_size("dp")
    parts = len(values)
    anywhere = pl.BlockSpec(memory_space=pl.ANY)
    size = sum(math.prod(value.shape) * 2 for value in values)
    return pl.pallas_call(
        partial(gather_kernel, count, parts),
        in_specs=[anywhere] * parts,
        out_specs=[anywhere] * parts,
        out_shape=[jax.ShapeDtypeStruct((count, *value.shape), value.dtype) for value in values],
        scratch_shapes=[
            pltpu.SemaphoreType.DMA((3, parts, count)),
            pltpu.SemaphoreType.DMA((parts, count)),
            pltpu.SemaphoreType.DMA((parts,)),
        ],
        compiler_params=pltpu.CompilerParams(collective_id=0, has_side_effects=True),
        cost_estimate=pl.CostEstimate(
            flops=0, transcendentals=0, bytes_accessed=2 * count * size
        ),
    )(*values)


def other_joined(own, first_shard, second_shard):
    count = lax.axis_size("ctx")
    if count == 2:
        return by_ctx(own, swapped(own, "ctx"))
    del first_shard, second_shard
    every = lax.all_gather(own, "ctx")
    return every[0], every[1]


def expert_weight_products(rows, hidden_grads, grads, actives):
    pairs = ((rows, hidden_grads), (grads, actives))
    far = [contract_rows(left, rights[1]) for left, rights in pairs]
    if lax.axis_size("ctx") == 2:
        far = [value.astype(BF16) for value in far]
    return [contract_rows(left, rights[0]) for left, rights in pairs], far


def sent_far(value):
    return swapped(value, "ctx") if lax.axis_size("ctx") == 2 else value


def expert_weight_parts(near, far):
    count = lax.axis_size("dp")
    parts = []
    for own, other in zip(near, far):
        if lax.axis_size("ctx") == 2:
            part = own + other.astype(F32)
        else:
            part = lax.psum_scatter(
                jnp.concatenate([own, other], axis=1), "ctx", scatter_dimension=1, tiled=True
            )
        parts.append(part.astype(BF16).reshape(count, part.shape[0] // count, part.shape[1]))
    return jnp.concatenate(parts, axis=1)


def expert_weight_blocks(blocks, experts):
    count = lax.axis_size("dp")
    if count != experts:
        blocks = jnp.sum(
            blocks.reshape(count // experts, experts, *blocks.shape[1:]).astype(F32), axis=0
        ).astype(BF16)
    shard = blocks.shape[1] // 2
    return blocks[:, :shard], blocks[:, shard:]


def far_hidden(blocks):
    if lax.axis_size("ctx") == 2:
        return swapped(blocks, "ctx")
    return lax.all_gather(blocks, "ctx", axis=2, tiled=True)


def expert_weight_grad(blocks, far_blocks):
    if lax.axis_size("ctx") == 2:
        far_blocks = jnp.concatenate(by_ctx(blocks, far_blocks), axis=2)
    return far_blocks.astype(F32)


def pair_products(first, second):
    if lax.axis_size("ctx") != 2:
        return contract_rows(*first), contract_rows(*second).astype(BF16)
    lefts, rights = by_ctx(first[0], second[0]), by_ctx(first[1], second[1])
    return contract_rows(lefts[0], rights[0]), contract_rows(lefts[1], rights[1]).astype(BF16)


def product_part(near, far):
    count = lax.axis_size("dp")

    def blocks(value):
        return value.astype(BF16).reshape(count, value.shape[0] // count, value.shape[1])

    if lax.axis_size("ctx") != 2:
        return jnp.concatenate([blocks(near), blocks(far)], axis=1)
    return blocks(near + far.astype(F32))


def product_shards(blocks):
    sums = jnp.sum(blocks.astype(F32), axis=0)
    if lax.axis_size("ctx") == 2:
        return by_ctx(sums, swapped(sums, "ctx"))
    sums = lax.psum(sums, "ctx")
    rows = sums.shape[0] // 2
    return sums[:rows], sums[rows:]


def local(
    hidden_in,
    out_grad,
    norm1_gain,
    in_weight,
    conv_weight,
    conv_bias,
    xproj_weight,
    dt_weight,
    dt_bias,
    decay_log,
    skip_weight,
    out_weight,
    norm2_gain,
    router_weight,
    fc1_weight,
    fc2_weight,
    expert_ids,
    keep_mask,
):
    batches, seqs, length, model_width = hidden_in.shape
    chains = batches * seqs
    tokens = chains * length
    steps = length // SEGMENTS
    shard, _, inner = in_weight.shape
    taps = conv_weight.shape[0]
    low_rank = dt_weight.shape[0]
    states = decay_log.shape[0]
    experts = fc1_weight.shape[0]
    dp_count = lax.axis_size("dp")
    tp_count = lax.axis_size("tp")
    capacity = tokens // 4
    part_cap = capacity // tp_count // HALVES
    slots = experts * part_cap
    tp_index = lax.axis_index("tp")
    scan = Scan(steps, chains, states, inner)

    def to_rows(value):
        value = value.reshape(chains, SEGMENTS, steps, -1).transpose(2, 0, 1, 3)
        return value.reshape(tokens, -1)

    def from_rows(value):
        value = value.reshape(steps, chains, SEGMENTS, -1).transpose(1, 2, 0, 3)
        return value.reshape(batches, seqs, length, -1)

    pieces = [
        norm1_gain[None],
        conv_weight,
        conv_bias[None],
        dt_weight,
        dt_bias[None],
        decay_log,
        skip_weight[None],
        norm2_gain[None],
        router_weight.T,
        xproj_weight.T,
    ]
    bounds = [0]
    for piece in pieces:
        bounds.append(bounds[-1] + piece.shape[0])
    small = sum(
        jnp.pad(piece, ((low, bounds[-1] - high), (0, 0)))
        for piece, low, high in zip(pieces, bounds, bounds[1:])
    )
    kinds = small.shape[0]
    small_wide = jnp.pad(small.T, ((0, 0), (0, -kinds % LANES)))
    in_x, small_all, later = gathered(
        in_weight[:, 0], small_wide, by_ctx(out_weight.T, in_weight[:, 1])[0]
    )
    in_x = in_x.reshape(dp_count * shard, inner)
    later = later.reshape(dp_count * shard, inner)
    small_all = small_all.reshape(dp_count * shard, -1)[:, :kinds].T
    small_all, up_shards, down_shards = together(
        small_all, fc1_weight, fc2_weight.transpose(0, 2, 1)
    )
    pieces = [small_all[bounds[i] : bounds[i + 1]] for i in range(len(bounds) - 1)]
    gain_one_f = pieces[0].astype(F32)
    tap_weights = pieces[1].astype(F32)
    conv_shift = pieces[2].astype(F32)
    dt_proj = pieces[3]
    dt_shift = pieces[4].astype(F32)
    decay_rate = -jnp.exp(pieces[5].astype(F32))
    skip_row = pieces[6].astype(F32)
    gain_two_f = pieces[7].astype(F32)
    router_t = pieces[8]
    x_proj_t = pieces[9]
    rate_rows = jnp.broadcast_to((decay_rate * LOG2E)[:, None, :], (states, SEGMENTS, inner))
    expert_blocks = own_expert_blocks(up_shards, down_shards)

    values = to_rows(hidden_in).astype(F32)
    normalized_rows, inverse_one = rms_forward(values, gain_one_f)
    normed_bf = normalized_rows.astype(BF16)
    x_pre = jnp.dot(normed_bf, in_x, preferred_element_type=F32).astype(BF16)
    x_pre = x_pre.reshape(steps, chains, SEGMENTS, inner)
    tail = x_pre[steps - taps + 1 :]
    edge_in = passed_along(tail[:, :, SEGMENTS - 1 :], "ctx", 1)
    edge_in, later = together(edge_in, later)
    out_proj_t, in_z = other_joined(later, out_weight.T, in_weight[:, 1])
    halo = jnp.concatenate([edge_in, tail[:, :, : SEGMENTS - 1]], axis=2)
    extended_bf = jnp.concatenate([halo, x_pre], axis=0)
    extended = extended_bf.astype(F32)
    conv_pre = jnp.broadcast_to(conv_shift[0], x_pre.shape)
    for tap in range(taps):
        conv_pre = conv_pre + tap_weights[tap] * extended[tap : tap + steps]
    xconv_bf = jax.nn.silu(conv_pre).astype(BF16)
    xconv = xconv_bf.astype(F32)
    xconv_rows = xconv_bf.reshape(tokens, inner)
    projected = axis_sum(contract_cols(xconv_rows, x_proj_t), "tp")
    dt_low = projected[:, :low_rank].astype(BF16)

    def mixes(value):
        value = value.reshape(steps, chains, SEGMENTS, states).transpose(1, 0, 3, 2)
        return jnp.broadcast_to(value[..., None], (*value.shape, LANES))

    mix_in = mixes(projected[:, low_rank : low_rank + states])
    mix_out = mixes(projected[:, low_rank + states :])
    dt_pre = (jnp.dot(dt_low, dt_proj, preferred_element_type=F32) + dt_shift).reshape(x_pre.shape)
    step_size = jax.nn.softplus(dt_pre)
    seg_decay, seg_state, last_state = scan.ends(step_size, xconv, mix_in, rate_rows)
    later_ids, later_mask, later_grad, _ = together(expert_ids, keep_mask, out_grad, seg_state)
    route = to_rows(later_ids)[:, 0]
    keep = to_rows(later_mask)[:, 0].astype(F32)
    onehot_int = (route[:, None] == jnp.arange(experts, dtype=jnp.int32)[None, :]).astype(jnp.int32)
    rank = jnp.sum((jnp.cumsum(onehot_int, axis=0) - 1) * onehot_int, axis=1)
    places = []
    for half in range(HALVES):
        own = rank - (tp_index * HALVES + half) * part_cap
        token_slot = jnp.where((own >= 0) & (own < part_cap), route * part_cap + own, -1)
        places.append(
            (token_slot[None, :] == jnp.arange(slots, dtype=jnp.int32)[:, None]).astype(BF16)
        )

    def slotted(value, half):
        sent = jnp.dot(places[half], value, preferred_element_type=F32).astype(BF16)
        return sent.reshape(experts, part_cap, -1)

    def landed(values):
        total = sum(
            contract_rows(place, value.reshape(slots, -1)) for place, value in zip(places, values)
        )
        return axis_sum(total.astype(BF16), "tp").astype(F32)

    def halves_of(value):
        return [value[:, at : at + part_cap] for at in range(0, value.shape[1], part_cap)]

    cotan_bf = to_rows(later_grad)
    cotan = cotan_bf.astype(F32)
    kept_cotan = (cotan * keep[:, None]).astype(BF16)
    sent_cotan = jnp.concatenate([slotted(kept_cotan, half) for half in range(HALVES)], axis=1)
    entering = entering_pieces(seg_decay[:, :, SEGMENTS - 1], last_state, "ctx", False)
    entering, mix_out, expert_blocks, sent_cotan = together(
        entering, mix_out, expert_blocks, sent_cotan
    )
    slot_cotan = expert_exchange(sent_cotan, experts)
    far_up, far_down = other_hidden(expert_blocks)
    scan_out, seg_start = scan.run(
        step_size, xconv, mix_in, mix_out, rate_rows, seg_decay, seg_state, entering
    )
    z_gate = jnp.dot(normed_bf, in_z, preferred_element_type=F32).reshape(x_pre.shape)
    scanned = scan_out + skip_row[0] * xconv
    z_silu = jax.nn.silu(z_gate)
    gated_bf = (scanned * z_silu).astype(BF16).reshape(tokens, inner)
    gated_bf, far_up = together(gated_bf, far_up)
    mixer_part, slot_cotan = together(contract_cols(gated_bf, out_proj_t), slot_cotan)
    middle = values + axis_sum(mixer_part, "tp")

    normed_two, inverse_two = rms_forward(middle, gain_two_f)
    normed_two_bf = normed_two.astype(BF16)
    expert_mask = (
        jnp.arange(experts, dtype=jnp.int32) == lax.rem(lax.axis_index("dp"), experts)
    ).astype(F32)[None, :]
    kept = ()
    got_grads, slot_outs, router_grad_t = [], [], 0.0
    for half, half_cotan in enumerate(halves_of(slot_cotan)):
        own_rows = expert_exchange(slotted(normed_two_bf, half), experts)
        if not half:
            own_rows, far_down = together(own_rows, far_down)
        else:
            own_rows, kept = together(own_rows, kept)
        own_rows = own_rows.reshape(slots, model_width)
        half_cotan = half_cotan.reshape(slots, model_width)
        far_rows, far_cotan = swapped(own_rows, "tp"), swapped(half_cotan, "tp")
        call = partial(
            expert_call, router_t=router_t, mask=expert_mask, blocks=expert_blocks, far_up=far_up,
            far_down=far_down, parts=2 * HALVES,
        )
        far = call(far_rows, far_cotan, part=2 * half, kept=kept)
        near = call(own_rows, half_cotan, part=2 * half + 1, kept=far[3:])
        if half:
            near, got_grads = together(near, got_grads)
        kept = near[3:]
        slot_out = near[0] + swapped(far[0], "tp")
        picked_grad = near[1] + swapped(far[1], "tp")
        slot_prob = near[2]
        slot_gate = jnp.sum(slot_prob * expert_mask, axis=1, keepdims=True)
        gate_grad = jnp.sum(slot_out * half_cotan.astype(F32), axis=1, keepdims=True)
        logit_grad = gate_grad * slot_gate * (expert_mask - slot_prob)
        router_grad_t = router_grad_t + contract_rows(logit_grad, own_rows.astype(F32), HIGHEST)
        picked_grad = picked_grad + jnp.dot(
            logit_grad, router_t.astype(F32), precision=HIGHEST, preferred_element_type=F32
        )
        got_grads.append(
            expert_exchange(picked_grad.astype(BF16).reshape(experts, part_cap, -1), experts)
        )
        slot_outs.append(slot_out.astype(BF16).reshape(experts, part_cap, -1))
    router_grad_t = axis_sum(router_grad_t, "tp")
    all_rows, all_grads, active_a, active_b, hidden_a, hidden_b = kept
    near_parts, far_parts = expert_weight_products(
        all_rows, (hidden_a, hidden_b), all_grads, (active_a, active_b)
    )
    far_first = sent_far(far_parts[0])
    got_grads, near_parts, far_second, far_first, slot_outs, router_grad_t = together(
        got_grads, near_parts, far_parts[1], far_first, slot_outs, router_grad_t
    )
    far_parts = far_first, sent_far(far_second)
    normed_two_grad = landed(got_grads)
    got_out = expert_exchange(jnp.concatenate(slot_outs, axis=1), experts)
    middle_norm_grad, gain_two_grad = rms_backward(middle, inverse_two, gain_two_f, normed_two_grad)
    middle_grad = cotan + middle_norm_grad
    mixer_grad_bf = middle_grad.astype(BF16)
    gated_grad = jnp.dot(mixer_grad_bf, out_proj_t, preferred_element_type=F32).reshape(x_pre.shape)
    scan_grad = gated_grad * z_silu
    z_grad = jax.vjp(jax.nn.silu, z_gate)[1](gated_grad * scanned)[0]
    z_grad_bf = z_grad.astype(BF16).reshape(tokens, inner)
    near_product, far_product = pair_products((mixer_grad_bf, gated_bf), (normed_bf, z_grad_bf))
    back_decay, back_adjoint, first_adjoint = scan.adjoint_ends(
        step_size, mix_out, scan_grad, rate_rows
    )
    normed_part = contract_cols(z_grad_bf, in_z)
    far_parts, got_out, near_product, far_product, normed_part, _ = together(
        far_parts, got_out, near_product, far_product, normed_part, first_adjoint
    )
    weight_blocks = lax.all_to_all(
        expert_weight_parts(near_parts, far_parts), "dp", 0, 0, tiled=True
    )
    leaving = entering_pieces(back_decay[:, :, 0], first_adjoint, "ctx", True)
    leaving, near_product, far_product = together(leaving, near_product, far_product)
    far_product = sent_far(far_product)
    adjoint_args = (
        step_size, xconv, mix_in, mix_out, scan_grad, rate_rows, seg_start, back_decay, back_adjoint,
        leaving, skip_row,
    )
    pre_grad, xconv_grad, decay_sum, scan_sums, mix_grad = scan.adjoint(adjoint_args)
    pre_grad, far_product, weight_blocks = together(pre_grad, far_product, weight_blocks)
    weight_blocks = expert_weight_blocks(weight_blocks, experts)
    far_ups = far_hidden(weight_blocks[0])
    out_blocks = lax.all_to_all(product_part(near_product, far_product), "dp", 0, 0, tiled=True)
    decay_log_grad = jnp.sum(decay_sum, axis=0) * decay_rate
    dt_shift_grad, skip_grad = jnp.sum(scan_sums, axis=0)[:2]
    pre_grad = pre_grad.reshape(tokens, inner)
    dt_proj_grad = contract_rows(dt_low, pre_grad)
    dt_low_grad = contract_cols(pre_grad, dt_proj)
    mix_grad = mix_grad.reshape(tokens, LANES)[:, : 2 * states]
    proj_part = jnp.concatenate([dt_low_grad, mix_grad], axis=1)
    proj_grad_bf = axis_sum(proj_part, "tp").astype(BF16)
    x_proj_grad_t = contract_rows(proj_grad_bf, xconv_rows)
    flat = (chains * SEGMENTS, inner)
    x_grad_bf, conv_sums, head, last = conv_back(
        proj_grad_bf,
        x_proj_t,
        xconv_grad.reshape(steps, *flat),
        extended_bf.reshape(steps + taps - 1, *flat),
        tap_weights,
        conv_shift,
    )
    taps_grad, shift_grad = conv_sums[:taps], conv_sums[taps]
    edge_back = passed_along(
        head.reshape(taps - 1, chains, SEGMENTS, inner)[:, :, :1], "ctx", -1
    )
    edge_back, out_blocks, far_ups = together(edge_back, out_blocks, far_ups)
    reaching = jnp.stack(
        [
            sum(tap_weights[tap] * edge_back[at - tap] for tap in range(at + 1))
            for at in range(taps - 1)
        ]
    )
    reaching = jnp.pad(reaching, ((0, 0), (0, 0), (SEGMENTS - 1, 0), (0, 0)))
    last = (last + reaching.reshape(taps - 1, *flat)).astype(BF16)
    x_grad_bf = lax.dynamic_update_slice(x_grad_bf, last, (steps - taps + 1, 0, 0))
    x_grad_bf = x_grad_bf.reshape(tokens, inner)
    small_grads = jnp.concatenate(
        [
            taps_grad,
            shift_grad[None],
            dt_proj_grad,
            dt_shift_grad[None],
            decay_log_grad,
            skip_grad[None],
            gain_two_grad[None],
            router_grad_t,
            x_proj_grad_t,
        ],
        axis=0,
    )
    small_grads = small_grads.reshape(-1, dp_count, shard).transpose(1, 0, 2)
    small_size = small_grads.shape[1] * shard
    small_rows = small_grads.astype(BF16).reshape(dp_count, small_size)
    small_rows = jnp.pad(small_rows, ((0, 0), (0, -small_size % inner))).reshape(dp_count, -1, inner)
    x_grad_bf, small_rows, out_blocks = together(x_grad_bf, small_rows, out_blocks)
    normed_part = normed_part + contract_cols(x_grad_bf, in_x)
    normed_grad = axis_sum(normed_part, "tp")
    values_norm_grad, gain_one_grad = rms_backward(values, inverse_one, gain_one_f, normed_grad)
    input_grad = from_rows((middle_grad + values_norm_grad).astype(BF16))

    in_x_part = contract_rows(normed_bf, x_grad_bf).astype(BF16).reshape(dp_count, shard, inner)
    gain_row = gain_one_grad.reshape(dp_count, 1, shard)
    gain_high = gain_row.astype(BF16)
    gain_low = (gain_row - gain_high.astype(F32)).astype(BF16)
    gain_rows = jnp.concatenate([gain_high, gain_low], axis=1)
    gain_rows = jnp.pad(gain_rows, ((0, 0), (0, 6), (0, inner - shard)))
    in_x_part, out_blocks = together(in_x_part, out_blocks)
    out_proj_grad, in_z_grad = product_shards(out_blocks)
    in_x_blocks = lax.all_to_all(
        jnp.concatenate([in_x_part, gain_rows, small_rows], axis=1), "dp", 0, 0, tiled=True
    )
    out_proj_grad, in_z_grad, far_down_blocks = together(
        out_proj_grad, in_z_grad, weight_blocks[1]
    )
    far_downs, in_x_blocks = together(far_hidden(far_down_blocks), in_x_blocks)
    first_grad = expert_weight_grad(weight_blocks[0], far_ups)
    second_grad = expert_weight_grad(weight_blocks[1], far_downs)
    router_prob = jax.nn.softmax(contract_cols(normed_two_bf, router_t), axis=-1)
    gate_prob = jnp.sum(router_prob * onehot_int.astype(F32), axis=1) * keep
    result = from_rows((middle + gate_prob[:, None] * landed(halves_of(got_out))).astype(BF16))
    in_x_sums = axis_sum(jnp.sum(in_x_blocks.astype(F32), axis=0), "ctx")
    in_x_grad = in_x_sums[:shard]
    gain_one_grad = in_x_sums[shard : shard + 1, :shard] + in_x_sums[shard + 1 : shard + 2, :shard]
    small_grads = in_x_sums[shard + 8 :].reshape(-1)[:small_size].reshape(-1, shard)
    small_grads = jnp.concatenate([gain_one_grad, small_grads], axis=0)
    sums = [small_grads[bounds[i] : bounds[i + 1]] for i in range(len(bounds) - 1)]
    return (
        result,
        input_grad,
        sums[0][0],
        jnp.stack([in_x_grad, in_z_grad], axis=1),
        sums[1],
        sums[2][0],
        sums[9].T,
        sums[3],
        sums[4][0],
        sums[5],
        sums[6][0],
        out_proj_grad.T,
        sums[7][0],
        sums[8].T,
        first_grad,
        second_grad.transpose(0, 2, 1),
    )


def solution(mesh):
    weights = (
        P("dp"),
        P("dp", None, "tp"),
        P(None, ("tp", "dp")),
        P(("tp", "dp")),
        P(("tp", "dp"), None),
        P(None, ("tp", "dp")),
        P(("tp", "dp")),
        P(None, ("tp", "dp")),
        P(("tp", "dp")),
        P("tp", "dp"),
        P("dp"),
        P("dp", None),
        P(None, "dp", "tp"),
        P(None, "tp", "dp"),
    )
    rows = P(None, "dp", "ctx", None)
    return jax.shard_map(
        local,
        mesh=mesh,
        in_specs=(rows, rows, *weights, P(("dp", "ctx"), None), P(("dp", "ctx"))),
        out_specs=(rows, rows, *weights),
        check_vma=False,
    )
```

```python
from functools import partial
import math

import jax
import jax.numpy as jnp
from jax import lax
from jax.experimental import pallas as pl
from jax.experimental.pallas import tpu as pltpu
from jax.sharding import PartitionSpec as P

EPSILON = 1e-05
HIGHEST = lax.Precision.HIGHEST
SEGMENTS = 8
LANES = 128
VMEM_LIMIT = 56 * 1024 * 1024
EXPERT_VMEM = 56 * 1024 * 1024
LOG2E = math.log2(math.e)
GROUP_A = 4
GROUP_B = 4
GROUP_C = 8
UNROLL_A = 8
UNROLL_B = 8
UNROLL_C = 8
UNROLL_D = 4
UNROLL_E = 8
BLOCKS = 3
COVER = 100
HALVES = 1
BF16 = jnp.bfloat16
F32 = jnp.float32


def swapped(value, axis):
    return lax.ppermute(value, axis, [(0, 1), (1, 0)])


def passed_along(value, axis, steps):
    count = lax.axis_size(axis)
    leading, last = (max(0, -steps), min(count, count - steps))
    return lax.ppermute(value, axis, [(source, source + steps) for source in range(leading, last)])


def axis_sum(value, axis):
    if lax.axis_size(axis) == 2:
        return value + swapped(value, axis)
    return lax.psum(value, axis)


def together(*values):
    return lax.optimization_barrier(values)


def narrow_sum(value, axis):
    if lax.axis_size(axis) == 2:
        return value.astype(F32) + swapped(value, axis).astype(F32)
    return lax.psum(value.astype(F32), axis)


def entering_pieces(decay, value, axis, backward):
    count = lax.axis_size(axis)
    if count == 2:
        return passed_along(value, axis, -1 if backward else 1)
    mine = lax.axis_index(axis)
    decays = lax.all_gather(decay, axis)
    values = lax.all_gather(value, axis)
    running = jnp.zeros_like(value)
    for position in range(count - 1):
        at = count - 1 - position if backward else position
        longer = values[at] + decays[at] * running
        ahead = at > mine if backward else at < mine
        running = jnp.where(ahead, longer, running)
    return running


def contract_rows(left_side, right_side, precision=None):
    return lax.dot_general(
        left_side,
        right_side,
        (((0,), (0,)), ((), ())),
        precision=precision,
        preferred_element_type=F32,
    )


def contract_cols(left_side, right_side, precision=None):
    return lax.dot_general(
        left_side,
        right_side,
        (((1,), (1,)), ((), ())),
        precision=precision,
        preferred_element_type=F32,
    )


def rms_forward(values, gain_vec):
    inverse = lax.rsqrt(jnp.mean(values * values, axis=-1, keepdims=True) + EPSILON)
    return (values * inverse * gain_vec, inverse)


def rms_backward(values, inverse, gain_vec, grad_out):
    weighted = grad_out * gain_vec
    inner_mean = jnp.mean(values * weighted, axis=-1, keepdims=True)
    grad_values = inverse * weighted - values * inverse * inverse * inverse * inner_mean
    grad_gain = jnp.sum(grad_out * values * inverse, axis=0)
    return (grad_values, grad_gain)


def zeros_of(ref):
    return jnp.zeros(ref.shape[1:], F32)


def sublane_rows(lanes):
    return lax.broadcasted_iota(jnp.int32, (SEGMENTS, lanes), 0)


def widened(value, lanes):
    return jnp.concatenate([value] * (lanes // LANES), axis=1) if lanes > LANES else value


def narrowed(value):
    parts = [value[:, at : at + LANES] for at in range(0, value.shape[1], LANES)]
    return sum(parts[1:], parts[0])


def groups_of(states, size):
    size = math.gcd(states, size)
    return [range(first, first + size) for first in range(0, states, size)]


def joined_forward(decay, value, row):
    for reach in (1, 2, 4):
        inside = row >= reach
        value = value + jnp.where(inside, decay * pltpu.roll(value, reach, 0), 0.0)
        decay = jnp.where(inside, decay * pltpu.roll(decay, reach, 0), decay)
    return decay, value


def joined_backward(decay, value, row):
    for reach in (1, 2, 4):
        inside = row < SEGMENTS - reach
        value = value + jnp.where(inside, decay * pltpu.roll(value, SEGMENTS - reach, 0), 0.0)
        decay = jnp.where(inside, decay * pltpu.roll(decay, SEGMENTS - reach, 0), decay)
    return decay, value


def ends_kernel(step_ref, input_ref, mix_in_ref, rate_ref, decay_ref, state_ref, last_ref):
    steps, states, lanes = step_ref.shape[0], mix_in_ref.shape[1], step_ref.shape[2]
    zero = zeros_of(step_ref)
    row = sublane_rows(lanes)
    total = lax.fori_loop(0, steps, lambda at, total: total + step_ref[at], zero, unroll=UNROLL_E)
    for members in groups_of(states, GROUP_A):
        rates = [rate_ref[n] for n in members]

        def body(at, held):
            step = step_ref[at]
            driven = step * input_ref[at]
            return tuple(
                jnp.exp2(step * rate) * before + widened(mix_in_ref[at, n], lanes) * driven
                for n, rate, before in zip(members, rates, held)
            )

        held = lax.fori_loop(0, steps, body, (zero,) * len(members), unroll=UNROLL_A)
        for n, rate, end in zip(members, rates, held):
            decay, value = joined_forward(jnp.exp2(total * rate), end, row)
            decay_ref[n] = decay
            state_ref[n] = value
            last_ref[n : n + 1] = value[SEGMENTS - 1 :]


def states_kernel(
    step_ref, input_ref, mix_in_ref, mix_out_ref, rate_ref, decay_ref, state_ref, enter_ref,
    out_ref, start_ref,
):
    steps, states, lanes = step_ref.shape[0], mix_in_ref.shape[1], step_ref.shape[2]
    row = sublane_rows(lanes)
    for members in groups_of(states, GROUP_B):
        rates = [rate_ref[n] for n in members]
        held = []
        for n in members:
            first = jnp.broadcast_to(enter_ref[n : n + 1], (SEGMENTS, lanes))
            inner = pltpu.roll(state_ref[n], 1, 0) + pltpu.roll(decay_ref[n], 1, 0) * first
            start = jnp.where(row >= 1, inner, first)
            start_ref[n] = start
            held.append(start)

        def body(at, held):
            step = step_ref[at]
            driven = step * input_ref[at]
            held = tuple(
                jnp.exp2(step * rate) * before + widened(mix_in_ref[at, n], lanes) * driven
                for n, rate, before in zip(members, rates, held)
            )
            parts = [widened(mix_out_ref[at, n], lanes) * now for n, now in zip(members, held)]
            if members[0]:
                parts.append(out_ref[at])
            while len(parts) > 1:
                parts = [sum(parts[i + 1 : i + 2], parts[i]) for i in range(0, len(parts), 2)]
            out_ref[at] = parts[0]
            return held

        lax.fori_loop(0, steps, body, tuple(held), unroll=UNROLL_B)


def adjoint_ends_kernel(step_ref, mix_out_ref, grad_ref, rate_ref, decay_ref, adjoint_ref, first_ref):
    steps, states, lanes = step_ref.shape[0], mix_out_ref.shape[1], step_ref.shape[2]
    zero = zeros_of(step_ref)
    row = sublane_rows(lanes)
    total = lax.fori_loop(0, steps, lambda at, total: total + step_ref[at], zero, unroll=UNROLL_E)
    for members in groups_of(states, GROUP_A):
        rates = [rate_ref[n] for n in members]

        def body(back, incoming):
            at = steps - 1 - back
            step = step_ref[at]
            grad = grad_ref[at]
            return tuple(
                jnp.exp2(step * rate) * (widened(mix_out_ref[at, n], lanes) * grad + after)
                for n, rate, after in zip(members, rates, incoming)
            )

        incoming = lax.fori_loop(0, steps, body, (zero,) * len(members), unroll=UNROLL_A)
        for n, rate, end in zip(members, rates, incoming):
            decay, value = joined_backward(jnp.exp2(total * rate), end, row)
            decay_ref[n] = decay
            adjoint_ref[n] = value
            first_ref[n : n + 1] = value[:1]


def adjoint_kernel(
    step_ref, input_ref, mix_in_ref, mix_out_ref, grad_ref, rate_ref, start_ref, decay_ref, adjoint_ref,
    enter_ref, skip_ref,
    pre_out_ref, conv_ref, decay_sum_ref, sums_ref, mix_ref,
    states_ref, decays_ref, in_grad_ref, out_grad_ref, pre_ref,
):
    steps, states, lanes = step_ref.shape[0], mix_in_ref.shape[1], step_ref.shape[2]
    row = sublane_rows(lanes)
    zero = zeros_of(step_ref)

    @pl.when(pl.program_id(1) == 0)
    def clear():
        in_grad_ref[...] = jnp.zeros_like(in_grad_ref)
        out_grad_ref[...] = jnp.zeros_like(out_grad_ref)

    for members in groups_of(states, GROUP_C):
        first, group = members[0], len(members)
        rates = [rate_ref[n] for n in members]

        def ahead(at, held):
            step = step_ref[at]
            driven = step * input_ref[at]
            grad = grad_ref[at]
            after = []
            for i, n in enumerate(members):
                states_ref[at, i] = held[i]
                decay = jnp.exp2(step * rates[i])
                decays_ref[at, i] = decay
                now = decay * held[i] + widened(mix_in_ref[at, n], lanes) * driven
                out_grad_ref[at, n] += narrowed(grad * now)
                after.append(now)
            return tuple(after)

        lax.fori_loop(0, steps, ahead, tuple(start_ref[n] for n in members), unroll=UNROLL_C)

        incoming = []
        for n in members:
            final = jnp.broadcast_to(enter_ref[n : n + 1], (SEGMENTS, lanes))
            inner = (
                pltpu.roll(adjoint_ref[n], SEGMENTS - 1, 0)
                + pltpu.roll(decay_ref[n], SEGMENTS - 1, 0) * final
            )
            incoming.append(jnp.where(row < SEGMENTS - 1, inner, final))

        def body(back, carry):
            at = steps - 1 - back
            incoming, decay_sums = carry
            step = step_ref[at]
            grad = grad_ref[at]
            driven = step * input_ref[at]
            in_sum = conv_ref[at] if first else zero
            rate_sum = pre_ref[at] if first else zero
            following, sums = [], []
            for i, n in enumerate(members):
                adjoint = widened(mix_out_ref[at, n], lanes) * grad + incoming[i]
                onward = decays_ref[at, i] * adjoint
                decay_grad = onward * states_ref[at, i]
                in_sum = in_sum + adjoint * widened(mix_in_ref[at, n], lanes)
                rate_sum = rate_sum + decay_grad * rates[i]
                sums.append(decay_sums[i] + decay_grad * step)
                in_grad_ref[at, n] += narrowed(adjoint * driven)
                following.append(onward)
            conv_ref[at] = in_sum
            pre_ref[at] = rate_sum
            return tuple(following), tuple(sums)

        _, sums = lax.fori_loop(
            0, steps, body, (tuple(incoming), (zero,) * group), unroll=UNROLL_D
        )
        for i, n in enumerate(members):
            decay_sum_ref[n : n + 1] = jnp.sum(sums[i], axis=0, keepdims=True)

    skip = skip_ref[...]

    def close(at, carry):
        pre_sum, skip_sum = carry
        step, inputs, grad, in_sum = step_ref[at], input_ref[at], grad_ref[at], conv_ref[at]
        step_grad = pre_ref[at] * (1.0 / LOG2E) + in_sum * inputs
        pre = step_grad * (1.0 - jnp.exp2(step * -LOG2E))
        pre_out_ref[at] = pre.astype(BF16)
        conv_ref[at] = in_sum * step + skip * grad
        return pre_sum + pre, skip_sum + grad * inputs

    pre_sum, skip_sum = lax.fori_loop(0, steps, close, (zero, zero), unroll=UNROLL_E)
    sums_ref[0:1] = jnp.sum(pre_sum, axis=0, keepdims=True)
    sums_ref[1:2] = jnp.sum(skip_sum, axis=0, keepdims=True)
    sums_ref[2:] = jnp.zeros((SEGMENTS - 2, lanes), F32)

    @pl.when(pl.program_id(1) == pl.num_programs(1) - 1)
    def across_lanes():
        lane = lax.broadcasted_iota(jnp.int32, (SEGMENTS, LANES), 1)

        def one(at, carry):
            total = jnp.zeros((SEGMENTS, LANES), F32)
            for n in range(states):
                for base, ref in ((0, in_grad_ref), (states, out_grad_ref)):
                    value = jnp.sum(ref[at, n], axis=1, keepdims=True)
                    total = jnp.where(lane == base + n, value, total)
            mix_ref[at] = total
            return carry

        lax.fori_loop(0, steps, one, 0, unroll=UNROLL_E)


class Scan:
    def __init__(self, steps, chains, states, width):
        lanes = LANES * math.gcd(width // LANES, BLOCKS)
        self.grid = (chains, width // lanes)
        self.rows_spec = pl.BlockSpec(
            (steps, None, SEGMENTS, lanes), lambda chain, block: (0, chain, 0, block)
        )
        self.mix_spec = pl.BlockSpec(
            (None, steps, states, SEGMENTS, LANES), lambda chain, block: (chain, 0, 0, 0, 0)
        )
        self.rate_spec = pl.BlockSpec((states, SEGMENTS, lanes), lambda chain, block: (0, 0, block))
        self.state_spec = pl.BlockSpec(
            (None, states, SEGMENTS, lanes), lambda chain, block: (chain, 0, 0, block)
        )
        self.edge_spec = pl.BlockSpec((None, states, lanes), lambda chain, block: (chain, 0, block))
        self.rows = jax.ShapeDtypeStruct((steps, chains, SEGMENTS, width), F32)
        self.mix = jax.ShapeDtypeStruct((chains, steps, states, SEGMENTS, LANES), F32)
        self.state = jax.ShapeDtypeStruct((chains, states, SEGMENTS, width), F32)
        self.edge = jax.ShapeDtypeStruct((chains, states, width), F32)
        self.sums = jax.ShapeDtypeStruct((chains, SEGMENTS, width), F32)
        self.sums_spec = pl.BlockSpec((None, SEGMENTS, lanes), lambda chain, block: (chain, 0, block))
        self.lane_sums = jax.ShapeDtypeStruct((steps, chains, SEGMENTS, LANES), F32)
        self.lane_spec = pl.BlockSpec(
            (steps, None, SEGMENTS, LANES), lambda chain, block: (0, chain, 0, 0)
        )
        self.skip_spec = pl.BlockSpec((1, lanes), lambda chain, block: (0, block))
        self.scratch = [
            pltpu.VMEM((steps, math.gcd(states, GROUP_C), SEGMENTS, lanes), F32),
            pltpu.VMEM((steps, math.gcd(states, GROUP_C), SEGMENTS, lanes), F32),
            pltpu.VMEM((steps, states, SEGMENTS, LANES), F32),
            pltpu.VMEM((steps, states, SEGMENTS, LANES), F32),
            pltpu.VMEM((steps, SEGMENTS, lanes), F32),
        ]
        self.narrow_rows = jax.ShapeDtypeStruct((steps, chains, SEGMENTS, width), BF16)
        self.work = steps * chains * SEGMENTS * width * states

    def call(self, kernel, ops, args, in_specs, outs, out_specs, scratch=()):
        size = sum(math.prod(a.shape) * a.dtype.itemsize for a in (*args, *outs))
        return pl.pallas_call(
            kernel,
            grid=self.grid,
            in_specs=in_specs,
            out_specs=out_specs,
            out_shape=outs,
            scratch_shapes=list(scratch),
            compiler_params=pltpu.CompilerParams(vmem_limit_bytes=VMEM_LIMIT),
            cost_estimate=pl.CostEstimate(
                flops=ops * self.work, transcendentals=self.work, bytes_accessed=size // COVER
            ),
        )(*args)

    def ends(self, step, inputs, mix_in, rate):
        return self.call(
            ends_kernel, 5, (step, inputs, mix_in, rate),
            [self.rows_spec, self.rows_spec, self.mix_spec, self.rate_spec],
            [self.state, self.state, self.edge],
            [self.state_spec, self.state_spec, self.edge_spec],
        )

    def run(self, step, inputs, mix_in, mix_out, rate, decay, state, enter):
        return self.call(
            states_kernel, 7, (step, inputs, mix_in, mix_out, rate, decay, state, enter),
            [self.rows_spec, self.rows_spec, self.mix_spec, self.mix_spec, self.rate_spec,
             self.state_spec, self.state_spec, self.edge_spec],
            [self.rows, self.state],
            [self.rows_spec, self.state_spec],
        )

    def adjoint_ends(self, step, mix_out, grad, rate):
        return self.call(
            adjoint_ends_kernel, 5, (step, mix_out, grad, rate),
            [self.rows_spec, self.mix_spec, self.rows_spec, self.rate_spec],
            [self.state, self.state, self.edge],
            [self.state_spec, self.state_spec, self.edge_spec],
        )

    def adjoint(self, args):
        return self.call(
            adjoint_kernel, 20, args,
            [self.rows_spec, self.rows_spec, self.mix_spec, self.mix_spec, self.rows_spec,
             self.rate_spec, self.state_spec, self.state_spec, self.state_spec, self.edge_spec,
             self.skip_spec],
            [self.narrow_rows, self.rows, self.edge, self.sums, self.lane_sums],
            [self.rows_spec, self.rows_spec, self.edge_spec, self.sums_spec, self.lane_spec],
            self.scratch,
        )


def conv_back_kernel(
    proj_ref, weight_ref, grad_ref, input_ref, taps_ref, shift_ref,
    out_ref, sums_ref, head_ref, tail_ref, product_ref, conv_ref,
):
    steps, rows, lanes = grad_ref.shape
    count = taps_ref.shape[0]
    reach = count - 1
    taps = [taps_ref[at : at + 1] for at in range(count)]
    shift = shift_ref[...]
    product_ref[...] = jnp.dot(
        proj_ref[...], weight_ref[...], preferred_element_type=F32
    ).reshape(steps, rows, lanes)

    def slopes(at, sums):
        inputs = [input_ref[at + tap].astype(F32) for tap in range(count)]
        pre = shift + sum(tap * value for tap, value in zip(taps, inputs))
        share = 1.0 / (1.0 + jnp.exp(-pre))
        conv = (grad_ref[at] + product_ref[at]) * (share * (1.0 + pre * (1.0 - share)))
        conv_ref[at] = conv
        return (*(total + conv * value for total, value in zip(sums, inputs)), sums[-1] + conv)

    zero = jnp.zeros((rows, lanes), F32)
    sums = lax.fori_loop(0, steps, slopes, (zero,) * (count + 1), unroll=2)
    for at, total in enumerate(sums):
        sums_ref[at : at + 1] = jnp.sum(total, axis=0, keepdims=True)
    sums_ref[count + 1 :] = jnp.zeros((sums_ref.shape[0] - count - 1, lanes), F32)
    row = sublane_rows(lanes)
    for at in range(reach):
        head_ref[at] = conv_ref[at]
        for low in range(0, rows, SEGMENTS):
            rolled = pltpu.roll(conv_ref[at, low : low + SEGMENTS], SEGMENTS - 1, 0)
            conv_ref[steps + at, low : low + SEGMENTS] = jnp.where(
                row < SEGMENTS - 1, rolled, 0.0
            )

    def back(at):
        return sum(taps[tap] * conv_ref[at + reach - tap] for tap in range(count))

    def store(at, carry):
        out_ref[at] = back(at).astype(BF16)
        return carry

    lax.fori_loop(0, steps, store, 0, unroll=2)
    for at in range(reach):
        tail_ref[at] = back(steps - reach + at)


def conv_back(proj, weight, grad, inputs, taps, shift):
    steps, rows, width = grad.shape
    reach = taps.shape[0] - 1
    lanes = LANES * math.gcd(width // LANES, BLOCKS)

    def block(count, dtype=F32):
        spec = pl.BlockSpec((count, rows, lanes), lambda at: (0, 0, at))
        return spec, jax.ShapeDtypeStruct((count, rows, width), dtype)

    def columns(count):
        return pl.BlockSpec((count, lanes), lambda at: (0, at))

    outs = [
        block(steps, BF16),
        (columns(SEGMENTS), jax.ShapeDtypeStruct((SEGMENTS, width), F32)),
        block(reach),
        block(reach),
    ]
    return pl.pallas_call(
        conv_back_kernel,
        grid=(width // lanes,),
        in_specs=[
            pl.BlockSpec(proj.shape, lambda at: (0, 0)),
            columns(weight.shape[0]),
            block(steps)[0],
            block(steps + reach)[0],
            columns(reach + 1),
            columns(1),
        ],
        out_specs=[spec for spec, _ in outs],
        out_shape=[shape for _, shape in outs],
        scratch_shapes=[
            pltpu.VMEM((steps, rows, lanes), F32),
            pltpu.VMEM((steps + reach, rows, lanes), F32),
        ],
        compiler_params=pltpu.CompilerParams(vmem_limit_bytes=VMEM_LIMIT),
        cost_estimate=pl.CostEstimate(flops=1, transcendentals=0, bytes_accessed=1),
    )(proj, weight, grad, inputs, taps, shift)


def expert_kernel(
    kept, rows_ref, cotan_ref, router_ref, mask_ref, up_a, down_a, up_b, down_b, *refs
):
    out_ref, picked_ref, prob_ref, copy_ref, grad_ref, active_a, active_b, hidden_a, hidden_b = refs[kept:]
    rows = rows_ref[...]
    copy_ref[...] = rows
    logits = contract_cols(rows, router_ref[...])
    shifted = jnp.exp(logits - jnp.max(logits, axis=1, keepdims=True))
    prob = shifted / jnp.sum(shifted, axis=1, keepdims=True)
    gate = jnp.sum(prob * mask_ref[...], axis=1, keepdims=True)
    grad = (gate * cotan_ref[...].astype(F32)).astype(BF16)
    prob_ref[...] = prob
    grad_ref[...] = grad
    out, picked = None, None
    for up, down, active_ref, hidden_ref in (
        (up_a, down_a, active_a, hidden_a),
        (up_b, down_b, active_b, hidden_b),
    ):
        up, down = (value[...].reshape(-1, value.shape[2]) for value in (up, down))
        hidden = jnp.dot(rows, up, preferred_element_type=F32)
        share = 0.5 + 0.5 * lax.erf(hidden * math.sqrt(0.5))
        slope = share + hidden * (jnp.exp(-0.5 * hidden * hidden) * (1.0 / math.sqrt(2 * math.pi)))
        active = (hidden * share).astype(BF16)
        active_ref[...] = active
        hidden_grad = (jnp.dot(grad, down, preferred_element_type=F32) * slope).astype(BF16)
        hidden_ref[...] = hidden_grad
        out_part = contract_cols(active, down)
        picked_part = contract_cols(hidden_grad, up)
        out = out_part if out is None else out + out_part
        picked = picked_part if picked is None else picked + picked_part
    out_ref[...] = out
    picked_ref[...] = picked


def expert_call(rows, cotan, router_t, mask, blocks, far_up, far_down, part, parts, kept):
    count, width = rows.shape
    shard, hidden = far_up.shape[1:]
    block = math.gcd(count, 512)
    base = part * (count // block)

    def rows_of(columns, low=0):
        return pl.BlockSpec((block, columns), lambda at: (at + low, 0))

    def whole(array):
        return pl.BlockSpec(array.shape, lambda at: (0, 0), pipeline_mode=pl.Buffered(1))

    def layer(array, at):
        return pl.BlockSpec(
            (array.shape[0], shard, hidden), lambda step: (0, at, 0), pipeline_mode=pl.Buffered(1)
        )

    experts = router_t.shape[0]
    inputs = (rows, cotan, router_t, mask, blocks, blocks, far_up, far_down)
    columns = (width, width, hidden, hidden, hidden, hidden)
    return pl.pallas_call(
        partial(expert_kernel, len(kept)),
        grid=(count // block,),
        in_specs=[
            rows_of(width), rows_of(width), whole(router_t), whole(mask),
            layer(blocks, 0), layer(blocks, 1), layer(far_up, 0), layer(far_down, 0),
            *[pl.BlockSpec(memory_space=pl.ANY)] * len(kept),
        ],
        out_specs=[
            rows_of(width), rows_of(width), rows_of(experts), *(rows_of(one, base) for one in columns)
        ],
        out_shape=[
            *(jax.ShapeDtypeStruct((count, one), F32) for one in (width, width, experts)),
            *(jax.ShapeDtypeStruct((parts * count, one), BF16) for one in columns),
        ],
        input_output_aliases={len(inputs) + at: 3 + at for at in range(len(kept))},
        compiler_params=pltpu.CompilerParams(vmem_limit_bytes=EXPERT_VMEM),
        cost_estimate=pl.CostEstimate(
            flops=16 * count * width * hidden,
            transcendentals=4 * count * hidden,
            bytes_accessed=count * (14 * width + 8 * hidden) + 8 * width * hidden,
        ),
    )(*inputs, *kept)


def expert_exchange(value, experts):
    count = lax.axis_size("dp")
    groups = None
    if count != experts:
        groups = [
            [base + e for e in range(experts)] for base in range(0, count, experts)
        ]
    return lax.all_to_all(value, "dp", 0, 0, axis_index_groups=groups, tiled=True)


def by_ctx(first, second):
    lead = lax.axis_index("ctx") == 0
    return jnp.where(lead, first, second), jnp.where(lead, second, first)


def own_expert_blocks(up_shards, down_shards):
    experts, _, hidden = up_shards.shape
    count = lax.axis_size("dp")
    half = hidden // 2
    both = jnp.concatenate([up_shards, down_shards], axis=1)
    if lax.axis_size("ctx") == 2:
        both = by_ctx(both[:, :, :half], both[:, :, half:])[0]
    if count != experts:
        both = jnp.concatenate([both] * (count // experts), axis=0)
    return lax.all_to_all(both, "dp", 0, 0, tiled=True)


def other_hidden(both):
    rows = both.shape[1] // 2
    if lax.axis_size("ctx") == 2:
        return swapped(both[:, :rows], "ctx"), swapped(both[:, rows:], "ctx")
    half = both.shape[2] // 2
    return both[:, :rows, half:], both[:, rows:, half:]


def gather_kernel(count, number, parts, *refs):
    ins, outs = refs[:number], refs[number : 2 * number]
    send_sem, recv_sem, own_sem = refs[2 * number :]
    places = count // 2
    me = lax.axis_index("dp")
    place, side = lax.div(me, 2), lax.rem(me, 2)
    across = me + 1 - 2 * side
    barrier = pltpu.get_barrier_semaphore()
    late = [part for part, (_, _, _, early) in enumerate(parts) if not early]
    early = [part for part, (_, _, _, early) in enumerate(parts) if early]

    def greet(device):
        pl.semaphore_signal(
            barrier, inc=1, device_id={"dp": device}, device_id_type=pl.DeviceIdType.MESH
        )

    greet(across)
    for step in (-1, 1):
        there = place + step

        @pl.when((there >= 0) & (there < places))
        def greet_place(step=step):
            greet(me + 2 * step)

    neighbours = 1 + (place > 0).astype(jnp.int32) + (place < places - 1).astype(jnp.int32)
    pl.semaphore_wait(barrier, neighbours)

    def copy(part, slot, kind, device, own):
        array, low, rows, _ = parts[part]
        landing = outs[array].at[slot, pl.ds(low, rows)]
        return pltpu.make_async_remote_copy(
            src_ref=ins[array].at[pl.ds(low, rows)] if own else landing,
            dst_ref=landing,
            send_sem=send_sem.at[kind, part, slot],
            recv_sem=recv_sem.at[part, slot],
            device_id={"dp": device},
            device_id_type=pl.DeviceIdType.MESH,
        )

    def along(which, slot, steps, own, act):
        for step in steps:
            there = place + step

            @pl.when((there >= 0) & (there < places))
            def one_way(step=step):
                for part in which:
                    act(copy(part, slot, step + 1, me + 2 * step, own))

    def aside(which, slot, own, act):
        for part in which:
            act(copy(part, slot, 1, across, own))

    def arrived(which, slot):
        for part in which:
            copy(part, slot, 1, across, False).wait_recv()

    def start(one):
        one.start()

    def sent(one):
        one.wait_send()

    mine = [
        pltpu.make_async_copy(ins[array], outs[array].at[me], own_sem.at[array])
        for array in range(number)
    ]
    for one in mine:
        one.start()
    both = (-1, 1)
    aside(early, me, True, start)
    for part in late:
        along((part,), me, both, True, start)
        aside((part,), me, True, start)
    along(early, me, both, True, start)
    arrived(early, across)
    along(early, across, both, False, start)
    for far in range(1, places):
        for step in both:
            origin = place - step * far

            @pl.when((origin >= 0) & (origin < places))
            def forward(step=step, far=far):
                slot, other = me - 2 * step * far, across - 2 * step * far
                for part in late:
                    arrived((part,), slot)
                    along((part,), slot, (step,), False, start)
                    aside((part,), slot, False, start)
                arrived(early, slot)
                along(early, slot, (step,), False, start)
                arrived(early, other)
                along(early, other, (step,), False, start)

    for at in range(places):
        arrived(late, 2 * at + 1 - side)
    for one in mine:
        one.wait()
    aside(early + late, me, True, sent)
    along(early + late, me, both, True, sent)
    along(early, across, both, False, sent)
    for far in range(1, places):
        for step in both:
            origin = place - step * far

            @pl.when((origin >= 0) & (origin < places))
            def forwarded(step=step, far=far):
                slot, other = me - 2 * step * far, across - 2 * step * far
                aside(late, slot, False, sent)
                along(early + late, slot, (step,), False, sent)
                along(early, other, (step,), False, sent)


def gathered(*values):
    count = lax.axis_size("dp")
    number = len(values)
    parts = []
    for at, value in enumerate(values):
        rows = value.shape[0]
        step = rows // 3 if value.shape[1] > 1024 and rows % 24 == 0 else rows
        parts += [
            (at, low, step, at == number - 1 and 0 < low == rows - step)
            for low in range(0, rows, step)
        ]
    anywhere = pl.BlockSpec(memory_space=pl.ANY)
    size = sum(math.prod(value.shape) * 2 for value in values)
    return pl.pallas_call(
        partial(gather_kernel, count, number, parts),
        in_specs=[anywhere] * number,
        out_specs=[anywhere] * number,
        out_shape=[jax.ShapeDtypeStruct((count, *value.shape), value.dtype) for value in values],
        scratch_shapes=[
            pltpu.SemaphoreType.DMA((3, len(parts), count)),
            pltpu.SemaphoreType.DMA((len(parts), count)),
            pltpu.SemaphoreType.DMA((number,)),
        ],
        compiler_params=pltpu.CompilerParams(collective_id=0, has_side_effects=True),
        cost_estimate=pl.CostEstimate(
            flops=0, transcendentals=0, bytes_accessed=2 * count * size
        ),
    )(*values)


def other_joined(own, first_shard, second_shard):
    count = lax.axis_size("ctx")
    if count == 2:
        return by_ctx(own, swapped(own, "ctx"))
    del first_shard, second_shard
    every = lax.all_gather(own, "ctx")
    return every[0], every[1]


def expert_weight_products(rows, hidden_grads, grads, actives):
    pairs = ((rows, hidden_grads), (grads, actives))
    far = [contract_rows(left, rights[1]) for left, rights in pairs]
    if lax.axis_size("ctx") == 2:
        far = [value.astype(BF16) for value in far]
    return [contract_rows(left, rights[0]) for left, rights in pairs], far


def sent_far(value):
    return swapped(value, "ctx") if lax.axis_size("ctx") == 2 else value


def expert_weight_parts(near, far):
    count = lax.axis_size("dp")
    parts = []
    for own, other in zip(near, far):
        if lax.axis_size("ctx") == 2:
            part = own + other.astype(F32)
        else:
            part = lax.psum_scatter(
                jnp.concatenate([own, other], axis=1), "ctx", scatter_dimension=1, tiled=True
            )
        parts.append(part.astype(BF16).reshape(count, part.shape[0] // count, part.shape[1]))
    return jnp.concatenate(parts, axis=1)


def expert_weight_blocks(blocks, experts):
    count = lax.axis_size("dp")
    if count != experts:
        blocks = jnp.sum(
            blocks.reshape(count // experts, experts, *blocks.shape[1:]).astype(F32), axis=0
        ).astype(BF16)
    shard = blocks.shape[1] // 2
    return blocks[:, :shard], blocks[:, shard:]


def far_hidden(blocks):
    if lax.axis_size("ctx") == 2:
        return swapped(blocks, "ctx")
    return lax.all_gather(blocks, "ctx", axis=2, tiled=True)


def expert_weight_grad(blocks, far_blocks):
    if lax.axis_size("ctx") == 2:
        far_blocks = jnp.concatenate(by_ctx(blocks, far_blocks), axis=2)
    return far_blocks.astype(F32)


def pair_products(first, second):
    if lax.axis_size("ctx") != 2:
        return contract_rows(*first), contract_rows(*second).astype(BF16)
    lefts, rights = by_ctx(first[0], second[0]), by_ctx(first[1], second[1])
    return contract_rows(lefts[0], rights[0]), contract_rows(lefts[1], rights[1]).astype(BF16)


def product_part(near, far):
    count = lax.axis_size("dp")

    def blocks(value):
        return value.astype(BF16).reshape(count, value.shape[0] // count, value.shape[1])

    if lax.axis_size("ctx") != 2:
        return jnp.concatenate([blocks(near), blocks(far)], axis=1)
    return blocks(near + far.astype(F32))


def product_shards(blocks):
    sums = jnp.sum(blocks.astype(F32), axis=0)
    if lax.axis_size("ctx") == 2:
        return by_ctx(sums, swapped(sums, "ctx"))
    sums = lax.psum(sums, "ctx")
    rows = sums.shape[0] // 2
    return sums[:rows], sums[rows:]


def local(
    hidden_in,
    out_grad,
    norm1_gain,
    in_weight,
    conv_weight,
    conv_bias,
    xproj_weight,
    dt_weight,
    dt_bias,
    decay_log,
    skip_weight,
    out_weight,
    norm2_gain,
    router_weight,
    fc1_weight,
    fc2_weight,
    expert_ids,
    keep_mask,
):
    batches, seqs, length, model_width = hidden_in.shape
    chains = batches * seqs
    tokens = chains * length
    steps = length // SEGMENTS
    shard, _, inner = in_weight.shape
    taps = conv_weight.shape[0]
    low_rank = dt_weight.shape[0]
    states = decay_log.shape[0]
    experts = fc1_weight.shape[0]
    dp_count = lax.axis_size("dp")
    tp_count = lax.axis_size("tp")
    capacity = tokens // 4
    part_cap = capacity // tp_count // HALVES
    slots = experts * part_cap
    tp_index = lax.axis_index("tp")
    scan = Scan(steps, chains, states, inner)

    def to_rows(value):
        value = value.reshape(chains, SEGMENTS, steps, -1).transpose(2, 0, 1, 3)
        return value.reshape(tokens, -1)

    def from_rows(value):
        value = value.reshape(steps, chains, SEGMENTS, -1).transpose(1, 2, 0, 3)
        return value.reshape(batches, seqs, length, -1)

    pieces = [
        norm1_gain[None],
        conv_weight,
        conv_bias[None],
        dt_weight,
        dt_bias[None],
        decay_log,
        skip_weight[None],
        norm2_gain[None],
        router_weight.T,
        xproj_weight.T,
    ]
    bounds = [0]
    for piece in pieces:
        bounds.append(bounds[-1] + piece.shape[0])
    small = sum(
        jnp.pad(piece, ((low, bounds[-1] - high), (0, 0)))
        for piece, low, high in zip(pieces, bounds, bounds[1:])
    )
    kinds = small.shape[0]
    small_wide = jnp.pad(small.T, ((0, 0), (0, -kinds % LANES)))
    in_x, small_all, later = gathered(
        in_weight[:, 0], small_wide, by_ctx(out_weight.T, in_weight[:, 1])[0]
    )
    in_x = in_x.reshape(dp_count * shard, inner)
    later = later.reshape(dp_count * shard, inner)
    small_all = small_all.reshape(dp_count * shard, -1)[:, :kinds].T
    small_all, up_shards, down_shards = together(
        small_all, fc1_weight, fc2_weight.transpose(0, 2, 1)
    )
    pieces = [small_all[bounds[i] : bounds[i + 1]] for i in range(len(bounds) - 1)]
    gain_one_f = pieces[0].astype(F32)
    tap_weights = pieces[1].astype(F32)
    conv_shift = pieces[2].astype(F32)
    dt_proj = pieces[3]
    dt_shift = pieces[4].astype(F32)
    decay_rate = -jnp.exp(pieces[5].astype(F32))
    skip_row = pieces[6].astype(F32)
    gain_two_f = pieces[7].astype(F32)
    router_t = pieces[8]
    x_proj_t = pieces[9]
    rate_rows = jnp.broadcast_to((decay_rate * LOG2E)[:, None, :], (states, SEGMENTS, inner))
    expert_blocks = own_expert_blocks(up_shards, down_shards)

    values = to_rows(hidden_in).astype(F32)
    normalized_rows, inverse_one = rms_forward(values, gain_one_f)
    normed_bf = normalized_rows.astype(BF16)
    x_pre = jnp.dot(normed_bf, in_x, preferred_element_type=F32).astype(BF16)
    x_pre = x_pre.reshape(steps, chains, SEGMENTS, inner)
    tail = x_pre[steps - taps + 1 :]
    edge_in = passed_along(tail[:, :, SEGMENTS - 1 :], "ctx", 1)
    edge_in, later = together(edge_in, later)
    out_proj_t, in_z = other_joined(later, out_weight.T, in_weight[:, 1])
    halo = jnp.concatenate([edge_in, tail[:, :, : SEGMENTS - 1]], axis=2)
    extended_bf = jnp.concatenate([halo, x_pre], axis=0)
    extended = extended_bf.astype(F32)
    conv_pre = jnp.broadcast_to(conv_shift[0], x_pre.shape)
    for tap in range(taps):
        conv_pre = conv_pre + tap_weights[tap] * extended[tap : tap + steps]
    xconv_bf = jax.nn.silu(conv_pre).astype(BF16)
    xconv = xconv_bf.astype(F32)
    xconv_rows = xconv_bf.reshape(tokens, inner)
    projected = axis_sum(contract_cols(xconv_rows, x_proj_t), "tp")
    dt_low = projected[:, :low_rank].astype(BF16)

    def mixes(value):
        value = value.reshape(steps, chains, SEGMENTS, states).transpose(1, 0, 3, 2)
        return jnp.broadcast_to(value[..., None], (*value.shape, LANES))

    mix_in = mixes(projected[:, low_rank : low_rank + states])
    mix_out = mixes(projected[:, low_rank + states :])
    dt_pre = (jnp.dot(dt_low, dt_proj, preferred_element_type=F32) + dt_shift).reshape(x_pre.shape)
    step_size = jax.nn.softplus(dt_pre)
    seg_decay, seg_state, last_state = scan.ends(step_size, xconv, mix_in, rate_rows)
    later_ids, later_mask, later_grad, _ = together(expert_ids, keep_mask, out_grad, seg_state)
    route = to_rows(later_ids)[:, 0]
    keep = to_rows(later_mask)[:, 0].astype(F32)
    onehot_int = (route[:, None] == jnp.arange(experts, dtype=jnp.int32)[None, :]).astype(jnp.int32)
    rank = jnp.sum((jnp.cumsum(onehot_int, axis=0) - 1) * onehot_int, axis=1)
    places = []
    for half in range(HALVES):
        own = rank - (tp_index * HALVES + half) * part_cap
        token_slot = jnp.where((own >= 0) & (own < part_cap), route * part_cap + own, -1)
        places.append(
            (token_slot[None, :] == jnp.arange(slots, dtype=jnp.int32)[:, None]).astype(BF16)
        )

    def slotted(value, half):
        sent = jnp.dot(places[half], value, preferred_element_type=F32).astype(BF16)
        return sent.reshape(experts, part_cap, -1)

    def landed(values):
        total = sum(
            contract_rows(place, value.reshape(slots, -1)) for place, value in zip(places, values)
        )
        return axis_sum(total.astype(BF16), "tp").astype(F32)

    def halves_of(value):
        return [value[:, at : at + part_cap] for at in range(0, value.shape[1], part_cap)]

    cotan_bf = to_rows(later_grad)
    cotan = cotan_bf.astype(F32)
    kept_cotan = (cotan * keep[:, None]).astype(BF16)
    sent_cotan = jnp.concatenate([slotted(kept_cotan, half) for half in range(HALVES)], axis=1)
    entering = entering_pieces(seg_decay[:, :, SEGMENTS - 1], last_state, "ctx", False)
    entering, mix_out, expert_blocks, sent_cotan = together(
        entering, mix_out, expert_blocks, sent_cotan
    )
    slot_cotan = expert_exchange(sent_cotan, experts)
    far_up, far_down = other_hidden(expert_blocks)
    scan_out, seg_start = scan.run(
        step_size, xconv, mix_in, mix_out, rate_rows, seg_decay, seg_state, entering
    )
    z_gate = jnp.dot(normed_bf, in_z, preferred_element_type=F32).reshape(x_pre.shape)
    scanned = scan_out + skip_row[0] * xconv
    z_silu = jax.nn.silu(z_gate)
    gated_bf = (scanned * z_silu).astype(BF16).reshape(tokens, inner)
    gated_bf, far_up = together(gated_bf, far_up)
    mixer_part, slot_cotan = together(contract_cols(gated_bf, out_proj_t), slot_cotan)
    middle = values + axis_sum(mixer_part, "tp")

    normed_two, inverse_two = rms_forward(middle, gain_two_f)
    normed_two_bf = normed_two.astype(BF16)
    expert_mask = (
        jnp.arange(experts, dtype=jnp.int32) == lax.rem(lax.axis_index("dp"), experts)
    ).astype(F32)[None, :]
    kept = ()
    got_grads, slot_outs, router_grad_t = [], [], 0.0
    for half, half_cotan in enumerate(halves_of(slot_cotan)):
        own_rows = expert_exchange(slotted(normed_two_bf, half), experts)
        if not half:
            own_rows, far_down = together(own_rows, far_down)
        else:
            own_rows, kept = together(own_rows, kept)
        own_rows = own_rows.reshape(slots, model_width)
        half_cotan = half_cotan.reshape(slots, model_width)
        far_rows, far_cotan = swapped(own_rows, "tp"), swapped(half_cotan, "tp")
        call = partial(
            expert_call, router_t=router_t, mask=expert_mask, blocks=expert_blocks, far_up=far_up,
            far_down=far_down, parts=2 * HALVES,
        )
        far = call(far_rows, far_cotan, part=2 * half, kept=kept)
        near = call(own_rows, half_cotan, part=2 * half + 1, kept=far[3:])
        if half:
            near, got_grads = together(near, got_grads)
        kept = near[3:]
        slot_out = near[0] + swapped(far[0], "tp")
        picked_grad = near[1] + swapped(far[1], "tp")
        slot_prob = near[2]
        slot_gate = jnp.sum(slot_prob * expert_mask, axis=1, keepdims=True)
        gate_grad = jnp.sum(slot_out * half_cotan.astype(F32), axis=1, keepdims=True)
        logit_grad = gate_grad * slot_gate * (expert_mask - slot_prob)
        router_grad_t = router_grad_t + contract_rows(logit_grad, own_rows.astype(F32), HIGHEST)
        picked_grad = picked_grad + jnp.dot(
            logit_grad, router_t.astype(F32), precision=HIGHEST, preferred_element_type=F32
        )
        got_grads.append(
            expert_exchange(picked_grad.astype(BF16).reshape(experts, part_cap, -1), experts)
        )
        slot_outs.append(slot_out.astype(BF16).reshape(experts, part_cap, -1))
    router_grad_t = axis_sum(router_grad_t, "tp")
    all_rows, all_grads, active_a, active_b, hidden_a, hidden_b = kept
    near_parts, far_parts = expert_weight_products(
        all_rows, (hidden_a, hidden_b), all_grads, (active_a, active_b)
    )
    far_first = sent_far(far_parts[0])
    got_grads, near_parts, far_second, far_first, slot_outs, router_grad_t = together(
        got_grads, near_parts, far_parts[1], far_first, slot_outs, router_grad_t
    )
    far_parts = far_first, sent_far(far_second)
    normed_two_grad = landed(got_grads)
    got_out = expert_exchange(jnp.concatenate(slot_outs, axis=1), experts)
    middle_norm_grad, gain_two_grad = rms_backward(middle, inverse_two, gain_two_f, normed_two_grad)
    middle_grad = cotan + middle_norm_grad
    mixer_grad_bf = middle_grad.astype(BF16)
    gated_grad = jnp.dot(mixer_grad_bf, out_proj_t, preferred_element_type=F32).reshape(x_pre.shape)
    scan_grad = gated_grad * z_silu
    z_grad = jax.vjp(jax.nn.silu, z_gate)[1](gated_grad * scanned)[0]
    z_grad_bf = z_grad.astype(BF16).reshape(tokens, inner)
    near_product, far_product = pair_products((mixer_grad_bf, gated_bf), (normed_bf, z_grad_bf))
    back_decay, back_adjoint, first_adjoint = scan.adjoint_ends(
        step_size, mix_out, scan_grad, rate_rows
    )
    normed_part = contract_cols(z_grad_bf, in_z)
    far_parts, got_out, near_product, far_product, normed_part, _ = together(
        far_parts, got_out, near_product, far_product, normed_part, first_adjoint
    )
    weight_blocks = lax.all_to_all(
        expert_weight_parts(near_parts, far_parts), "dp", 0, 0, tiled=True
    )
    leaving = entering_pieces(back_decay[:, :, 0], first_adjoint, "ctx", True)
    leaving, near_product, far_product = together(leaving, near_product, far_product)
    far_product = sent_far(far_product)
    adjoint_args = (
        step_size, xconv, mix_in, mix_out, scan_grad, rate_rows, seg_start, back_decay, back_adjoint,
        leaving, skip_row,
    )
    pre_grad, xconv_grad, decay_sum, scan_sums, mix_grad = scan.adjoint(adjoint_args)
    pre_grad, far_product, weight_blocks = together(pre_grad, far_product, weight_blocks)
    weight_blocks = expert_weight_blocks(weight_blocks, experts)
    far_ups = far_hidden(weight_blocks[0])
    out_blocks = lax.all_to_all(product_part(near_product, far_product), "dp", 0, 0, tiled=True)
    decay_log_grad = jnp.sum(decay_sum, axis=0) * decay_rate
    dt_shift_grad, skip_grad = jnp.sum(scan_sums, axis=0)[:2]
    pre_grad = pre_grad.reshape(tokens, inner)
    dt_proj_grad = contract_rows(dt_low, pre_grad)
    dt_low_grad = contract_cols(pre_grad, dt_proj)
    mix_grad = mix_grad.reshape(tokens, LANES)[:, : 2 * states]
    proj_part = jnp.concatenate([dt_low_grad, mix_grad], axis=1)
    proj_grad_bf = axis_sum(proj_part, "tp").astype(BF16)
    x_proj_grad_t = contract_rows(proj_grad_bf, xconv_rows)
    flat = (chains * SEGMENTS, inner)
    x_grad_bf, conv_sums, head, last = conv_back(
        proj_grad_bf,
        x_proj_t,
        xconv_grad.reshape(steps, *flat),
        extended_bf.reshape(steps + taps - 1, *flat),
        tap_weights,
        conv_shift,
    )
    taps_grad, shift_grad = conv_sums[:taps], conv_sums[taps]
    edge_back = passed_along(
        head.reshape(taps - 1, chains, SEGMENTS, inner)[:, :, :1], "ctx", -1
    )
    edge_back, out_blocks, far_ups = together(edge_back, out_blocks, far_ups)
    reaching = jnp.stack(
        [
            sum(tap_weights[tap] * edge_back[at - tap] for tap in range(at + 1))
            for at in range(taps - 1)
        ]
    )
    reaching = jnp.pad(reaching, ((0, 0), (0, 0), (SEGMENTS - 1, 0), (0, 0)))
    last = (last + reaching.reshape(taps - 1, *flat)).astype(BF16)
    x_grad_bf = lax.dynamic_update_slice(x_grad_bf, last, (steps - taps + 1, 0, 0))
    x_grad_bf = x_grad_bf.reshape(tokens, inner)
    small_grads = jnp.concatenate(
        [
            taps_grad,
            shift_grad[None],
            dt_proj_grad,
            dt_shift_grad[None],
            decay_log_grad,
            skip_grad[None],
            gain_two_grad[None],
            router_grad_t,
            x_proj_grad_t,
        ],
        axis=0,
    )
    small_grads = small_grads.reshape(-1, dp_count, shard).transpose(1, 0, 2)
    small_size = small_grads.shape[1] * shard
    small_rows = small_grads.astype(BF16).reshape(dp_count, small_size)
    small_rows = jnp.pad(small_rows, ((0, 0), (0, -small_size % inner))).reshape(dp_count, -1, inner)
    x_grad_bf, small_rows, out_blocks = together(x_grad_bf, small_rows, out_blocks)
    normed_part = normed_part + contract_cols(x_grad_bf, in_x)
    normed_grad = axis_sum(normed_part, "tp")
    values_norm_grad, gain_one_grad = rms_backward(values, inverse_one, gain_one_f, normed_grad)
    input_grad = from_rows((middle_grad + values_norm_grad).astype(BF16))

    in_x_part = contract_rows(normed_bf, x_grad_bf).astype(BF16).reshape(dp_count, shard, inner)
    gain_row = gain_one_grad.reshape(dp_count, 1, shard)
    gain_high = gain_row.astype(BF16)
    gain_low = (gain_row - gain_high.astype(F32)).astype(BF16)
    gain_rows = jnp.concatenate([gain_high, gain_low], axis=1)
    gain_rows = jnp.pad(gain_rows, ((0, 0), (0, 6), (0, inner - shard)))
    in_x_part, out_blocks = together(in_x_part, out_blocks)
    out_proj_grad, in_z_grad = product_shards(out_blocks)
    in_x_blocks = lax.all_to_all(
        jnp.concatenate([in_x_part, gain_rows, small_rows], axis=1), "dp", 0, 0, tiled=True
    )
    out_proj_grad, in_z_grad, far_down_blocks = together(
        out_proj_grad, in_z_grad, weight_blocks[1]
    )
    far_downs, in_x_blocks = together(far_hidden(far_down_blocks), in_x_blocks)
    first_grad = expert_weight_grad(weight_blocks[0], far_ups)
    second_grad = expert_weight_grad(weight_blocks[1], far_downs)
    router_prob = jax.nn.softmax(contract_cols(normed_two_bf, router_t), axis=-1)
    gate_prob = jnp.sum(router_prob * onehot_int.astype(F32), axis=1) * keep
    result = from_rows((middle + gate_prob[:, None] * landed(halves_of(got_out))).astype(BF16))
    in_x_sums = jnp.sum(in_x_blocks.astype(F32), axis=0).astype(BF16)
    in_x_sums = narrow_sum(in_x_sums, "ctx")
    in_x_grad = in_x_sums[:shard]
    gain_one_grad = in_x_sums[shard : shard + 1, :shard] + in_x_sums[shard + 1 : shard + 2, :shard]
    small_grads = in_x_sums[shard + 8 :].reshape(-1)[:small_size].reshape(-1, shard)
    small_grads = jnp.concatenate([gain_one_grad, small_grads], axis=0)
    sums = [small_grads[bounds[i] : bounds[i + 1]] for i in range(len(bounds) - 1)]
    return (
        result,
        input_grad,
        sums[0][0],
        jnp.stack([in_x_grad, in_z_grad], axis=1),
        sums[1],
        sums[2][0],
        sums[9].T,
        sums[3],
        sums[4][0],
        sums[5],
        sums[6][0],
        out_proj_grad.T,
        sums[7][0],
        sums[8].T,
        first_grad,
        second_grad.transpose(0, 2, 1),
    )


def solution(mesh):
    weights = (
        P("dp"),
        P("dp", None, "tp"),
        P(None, ("tp", "dp")),
        P(("tp", "dp")),
        P(("tp", "dp"), None),
        P(None, ("tp", "dp")),
        P(("tp", "dp")),
        P(None, ("tp", "dp")),
        P(("tp", "dp")),
        P("tp", "dp"),
        P("dp"),
        P("dp", None),
        P(None, "dp", "tp"),
        P(None, "tp", "dp"),
    )
    rows = P(None, "dp", "ctx", None)
    return jax.shard_map(
        local,
        mesh=mesh,
        in_specs=(rows, rows, *weights, P(("dp", "ctx"), None), P(("dp", "ctx"))),
        out_specs=(rows, rows, *weights),
        check_vma=False,
    )
```

```python
from functools import partial
import math

import jax
import jax.numpy as jnp
from jax import lax
from jax.experimental import pallas as pl
from jax.experimental.pallas import tpu as pltpu
from jax.sharding import PartitionSpec as P

EPSILON = 1e-05
HIGHEST = lax.Precision.HIGHEST
SEGMENTS = 8
LANES = 128
VMEM_LIMIT = 56 * 1024 * 1024
EXPERT_VMEM = 56 * 1024 * 1024
LOG2E = math.log2(math.e)
GROUP_A = 4
GROUP_B = 4
GROUP_C = 8
UNROLL_A = 16
UNROLL_B = 16
UNROLL_C = 8
UNROLL_D = 4
UNROLL_E = 8
BLOCKS = 3
COVER = 100
HALVES = 1
BF16 = jnp.bfloat16
F32 = jnp.float32


def swapped(value, axis):
    return lax.ppermute(value, axis, [(0, 1), (1, 0)])


def passed_along(value, axis, steps):
    count = lax.axis_size(axis)
    leading, last = (max(0, -steps), min(count, count - steps))
    return lax.ppermute(value, axis, [(source, source + steps) for source in range(leading, last)])


def axis_sum(value, axis):
    if lax.axis_size(axis) == 2:
        return value + swapped(value, axis)
    return lax.psum(value, axis)


def together(*values):
    return lax.optimization_barrier(values)


def narrow_sum(value, axis):
    if lax.axis_size(axis) == 2:
        return value.astype(F32) + swapped(value, axis).astype(F32)
    return lax.psum(value.astype(F32), axis)


def entering_pieces(decay, value, axis, backward):
    count = lax.axis_size(axis)
    if count == 2:
        return passed_along(value, axis, -1 if backward else 1)
    mine = lax.axis_index(axis)
    decays = lax.all_gather(decay, axis)
    values = lax.all_gather(value, axis)
    running = jnp.zeros_like(value)
    for position in range(count - 1):
        at = count - 1 - position if backward else position
        longer = values[at] + decays[at] * running
        ahead = at > mine if backward else at < mine
        running = jnp.where(ahead, longer, running)
    return running


def contract_rows(left_side, right_side, precision=None):
    return lax.dot_general(
        left_side,
        right_side,
        (((0,), (0,)), ((), ())),
        precision=precision,
        preferred_element_type=F32,
    )


def contract_cols(left_side, right_side, precision=None):
    return lax.dot_general(
        left_side,
        right_side,
        (((1,), (1,)), ((), ())),
        precision=precision,
        preferred_element_type=F32,
    )


def rms_forward(values, gain_vec):
    inverse = lax.rsqrt(jnp.mean(values * values, axis=-1, keepdims=True) + EPSILON)
    return (values * inverse * gain_vec, inverse)


def rms_backward(values, inverse, gain_vec, grad_out):
    weighted = grad_out * gain_vec
    inner_mean = jnp.mean(values * weighted, axis=-1, keepdims=True)
    grad_values = inverse * weighted - values * inverse * inverse * inverse * inner_mean
    grad_gain = jnp.sum(grad_out * values * inverse, axis=0)
    return (grad_values, grad_gain)


def zeros_of(ref):
    return jnp.zeros(ref.shape[1:], F32)


def sublane_rows(lanes):
    return lax.broadcasted_iota(jnp.int32, (SEGMENTS, lanes), 0)


def widened(value, lanes):
    return jnp.concatenate([value] * (lanes // LANES), axis=1) if lanes > LANES else value


def narrowed(value):
    parts = [value[:, at : at + LANES] for at in range(0, value.shape[1], LANES)]
    return sum(parts[1:], parts[0])


def groups_of(states, size):
    size = math.gcd(states, size)
    return [range(first, first + size) for first in range(0, states, size)]


def joined_forward(decay, value, row):
    for reach in (1, 2, 4):
        inside = row >= reach
        value = value + jnp.where(inside, decay * pltpu.roll(value, reach, 0), 0.0)
        decay = jnp.where(inside, decay * pltpu.roll(decay, reach, 0), decay)
    return decay, value


def joined_backward(decay, value, row):
    for reach in (1, 2, 4):
        inside = row < SEGMENTS - reach
        value = value + jnp.where(inside, decay * pltpu.roll(value, SEGMENTS - reach, 0), 0.0)
        decay = jnp.where(inside, decay * pltpu.roll(decay, SEGMENTS - reach, 0), decay)
    return decay, value


def ends_kernel(step_ref, input_ref, mix_in_ref, rate_ref, decay_ref, state_ref, last_ref):
    steps, states, lanes = step_ref.shape[0], mix_in_ref.shape[1], step_ref.shape[2]
    zero = zeros_of(step_ref)
    row = sublane_rows(lanes)
    total = lax.fori_loop(0, steps, lambda at, total: total + step_ref[at], zero, unroll=UNROLL_E)
    for members in groups_of(states, GROUP_A):
        rates = [rate_ref[n] for n in members]

        def body(at, held):
            step = step_ref[at]
            driven = step * input_ref[at]
            return tuple(
                jnp.exp2(step * rate) * before + widened(mix_in_ref[at, n], lanes) * driven
                for n, rate, before in zip(members, rates, held)
            )

        held = lax.fori_loop(0, steps, body, (zero,) * len(members), unroll=UNROLL_A)
        for n, rate, end in zip(members, rates, held):
            decay, value = joined_forward(jnp.exp2(total * rate), end, row)
            decay_ref[n] = decay
            state_ref[n] = value
            last_ref[n : n + 1] = value[SEGMENTS - 1 :]


def states_kernel(
    step_ref, input_ref, mix_in_ref, mix_out_ref, rate_ref, decay_ref, state_ref, enter_ref,
    out_ref, start_ref,
):
    steps, states, lanes = step_ref.shape[0], mix_in_ref.shape[1], step_ref.shape[2]
    row = sublane_rows(lanes)
    for members in groups_of(states, GROUP_B):
        rates = [rate_ref[n] for n in members]
        held = []
        for n in members:
            first = jnp.broadcast_to(enter_ref[n : n + 1], (SEGMENTS, lanes))
            inner = pltpu.roll(state_ref[n], 1, 0) + pltpu.roll(decay_ref[n], 1, 0) * first
            start = jnp.where(row >= 1, inner, first)
            start_ref[n] = start
            held.append(start)

        def body(at, held):
            step = step_ref[at]
            driven = step * input_ref[at]
            held = tuple(
                jnp.exp2(step * rate) * before + widened(mix_in_ref[at, n], lanes) * driven
                for n, rate, before in zip(members, rates, held)
            )
            parts = [widened(mix_out_ref[at, n], lanes) * now for n, now in zip(members, held)]
            if members[0]:
                parts.append(out_ref[at])
            while len(parts) > 1:
                parts = [sum(parts[i + 1 : i + 2], parts[i]) for i in range(0, len(parts), 2)]
            out_ref[at] = parts[0]
            return held

        lax.fori_loop(0, steps, body, tuple(held), unroll=UNROLL_B)


def adjoint_ends_kernel(step_ref, mix_out_ref, grad_ref, rate_ref, decay_ref, adjoint_ref, first_ref):
    steps, states, lanes = step_ref.shape[0], mix_out_ref.shape[1], step_ref.shape[2]
    zero = zeros_of(step_ref)
    row = sublane_rows(lanes)
    total = lax.fori_loop(0, steps, lambda at, total: total + step_ref[at], zero, unroll=UNROLL_E)
    for members in groups_of(states, GROUP_A):
        rates = [rate_ref[n] for n in members]

        def body(back, incoming):
            at = steps - 1 - back
            step = step_ref[at]
            grad = grad_ref[at]
            return tuple(
                jnp.exp2(step * rate) * (widened(mix_out_ref[at, n], lanes) * grad + after)
                for n, rate, after in zip(members, rates, incoming)
            )

        incoming = lax.fori_loop(0, steps, body, (zero,) * len(members), unroll=UNROLL_A)
        for n, rate, end in zip(members, rates, incoming):
            decay, value = joined_backward(jnp.exp2(total * rate), end, row)
            decay_ref[n] = decay
            adjoint_ref[n] = value
            first_ref[n : n + 1] = value[:1]


def adjoint_kernel(
    step_ref, input_ref, mix_in_ref, mix_out_ref, grad_ref, rate_ref, start_ref, decay_ref, adjoint_ref,
    enter_ref, skip_ref,
    pre_out_ref, conv_ref, decay_sum_ref, sums_ref, mix_ref,
    states_ref, decays_ref, in_grad_ref, out_grad_ref, pre_ref,
):
    steps, states, lanes = step_ref.shape[0], mix_in_ref.shape[1], step_ref.shape[2]
    row = sublane_rows(lanes)
    zero = zeros_of(step_ref)

    @pl.when(pl.program_id(1) == 0)
    def clear():
        in_grad_ref[...] = jnp.zeros_like(in_grad_ref)
        out_grad_ref[...] = jnp.zeros_like(out_grad_ref)

    for members in groups_of(states, GROUP_C):
        first, group = members[0], len(members)
        rates = [rate_ref[n] for n in members]

        def ahead(at, held):
            step = step_ref[at]
            driven = step * input_ref[at]
            grad = grad_ref[at]
            after = []
            for i, n in enumerate(members):
                states_ref[at, i] = held[i]
                decay = jnp.exp2(step * rates[i])
                decays_ref[at, i] = decay
                now = decay * held[i] + widened(mix_in_ref[at, n], lanes) * driven
                out_grad_ref[at, n] += narrowed(grad * now)
                after.append(now)
            return tuple(after)

        lax.fori_loop(0, steps, ahead, tuple(start_ref[n] for n in members), unroll=UNROLL_C)

        incoming = []
        for n in members:
            final = jnp.broadcast_to(enter_ref[n : n + 1], (SEGMENTS, lanes))
            inner = (
                pltpu.roll(adjoint_ref[n], SEGMENTS - 1, 0)
                + pltpu.roll(decay_ref[n], SEGMENTS - 1, 0) * final
            )
            incoming.append(jnp.where(row < SEGMENTS - 1, inner, final))

        def body(back, carry):
            at = steps - 1 - back
            incoming, decay_sums = carry
            step = step_ref[at]
            grad = grad_ref[at]
            driven = step * input_ref[at]
            in_sum = conv_ref[at] if first else zero
            rate_sum = pre_ref[at] if first else zero
            following, sums = [], []
            for i, n in enumerate(members):
                adjoint = widened(mix_out_ref[at, n], lanes) * grad + incoming[i]
                onward = decays_ref[at, i] * adjoint
                decay_grad = onward * states_ref[at, i]
                in_sum = in_sum + adjoint * widened(mix_in_ref[at, n], lanes)
                rate_sum = rate_sum + decay_grad * rates[i]
                sums.append(decay_sums[i] + decay_grad * step)
                in_grad_ref[at, n] += narrowed(adjoint * driven)
                following.append(onward)
            conv_ref[at] = in_sum
            pre_ref[at] = rate_sum
            return tuple(following), tuple(sums)

        _, sums = lax.fori_loop(
            0, steps, body, (tuple(incoming), (zero,) * group), unroll=UNROLL_D
        )
        for i, n in enumerate(members):
            decay_sum_ref[n : n + 1] = jnp.sum(sums[i], axis=0, keepdims=True)

    skip = skip_ref[...]

    def close(at, carry):
        pre_sum, skip_sum = carry
        step, inputs, grad, in_sum = step_ref[at], input_ref[at], grad_ref[at], conv_ref[at]
        step_grad = pre_ref[at] * (1.0 / LOG2E) + in_sum * inputs
        pre = step_grad * (1.0 - jnp.exp2(step * -LOG2E))
        pre_out_ref[at] = pre.astype(BF16)
        conv_ref[at] = in_sum * step + skip * grad
        return pre_sum + pre, skip_sum + grad * inputs

    pre_sum, skip_sum = lax.fori_loop(0, steps, close, (zero, zero), unroll=UNROLL_E)
    sums_ref[0:1] = jnp.sum(pre_sum, axis=0, keepdims=True)
    sums_ref[1:2] = jnp.sum(skip_sum, axis=0, keepdims=True)
    sums_ref[2:] = jnp.zeros((SEGMENTS - 2, lanes), F32)

    @pl.when(pl.program_id(1) == pl.num_programs(1) - 1)
    def across_lanes():
        lane = lax.broadcasted_iota(jnp.int32, (SEGMENTS, LANES), 1)

        def one(at, carry):
            total = jnp.zeros((SEGMENTS, LANES), F32)
            for n in range(states):
                for base, ref in ((0, in_grad_ref), (states, out_grad_ref)):
                    value = jnp.sum(ref[at, n], axis=1, keepdims=True)
                    total = jnp.where(lane == base + n, value, total)
            mix_ref[at] = total
            return carry

        lax.fori_loop(0, steps, one, 0, unroll=UNROLL_E)


class Scan:
    def __init__(self, steps, chains, states, width):
        lanes = LANES * math.gcd(width // LANES, BLOCKS)
        self.grid = (chains, width // lanes)
        self.rows_spec = pl.BlockSpec(
            (steps, None, SEGMENTS, lanes), lambda chain, block: (0, chain, 0, block)
        )
        self.mix_spec = pl.BlockSpec(
            (None, steps, states, SEGMENTS, LANES), lambda chain, block: (chain, 0, 0, 0, 0)
        )
        self.rate_spec = pl.BlockSpec((states, SEGMENTS, lanes), lambda chain, block: (0, 0, block))
        self.state_spec = pl.BlockSpec(
            (None, states, SEGMENTS, lanes), lambda chain, block: (chain, 0, 0, block)
        )
        self.edge_spec = pl.BlockSpec((None, states, lanes), lambda chain, block: (chain, 0, block))
        self.rows = jax.ShapeDtypeStruct((steps, chains, SEGMENTS, width), F32)
        self.mix = jax.ShapeDtypeStruct((chains, steps, states, SEGMENTS, LANES), F32)
        self.state = jax.ShapeDtypeStruct((chains, states, SEGMENTS, width), F32)
        self.edge = jax.ShapeDtypeStruct((chains, states, width), F32)
        self.sums = jax.ShapeDtypeStruct((chains, SEGMENTS, width), F32)
        self.sums_spec = pl.BlockSpec((None, SEGMENTS, lanes), lambda chain, block: (chain, 0, block))
        self.lane_sums = jax.ShapeDtypeStruct((steps, chains, SEGMENTS, LANES), F32)
        self.lane_spec = pl.BlockSpec(
            (steps, None, SEGMENTS, LANES), lambda chain, block: (0, chain, 0, 0)
        )
        self.skip_spec = pl.BlockSpec((1, lanes), lambda chain, block: (0, block))
        self.scratch = [
            pltpu.VMEM((steps, math.gcd(states, GROUP_C), SEGMENTS, lanes), F32),
            pltpu.VMEM((steps, math.gcd(states, GROUP_C), SEGMENTS, lanes), F32),
            pltpu.VMEM((steps, states, SEGMENTS, LANES), F32),
            pltpu.VMEM((steps, states, SEGMENTS, LANES), F32),
            pltpu.VMEM((steps, SEGMENTS, lanes), F32),
        ]
        self.narrow_rows = jax.ShapeDtypeStruct((steps, chains, SEGMENTS, width), BF16)
        self.work = steps * chains * SEGMENTS * width * states

    def call(self, kernel, ops, args, in_specs, outs, out_specs, scratch=()):
        size = sum(math.prod(a.shape) * a.dtype.itemsize for a in (*args, *outs))
        return pl.pallas_call(
            kernel,
            grid=self.grid,
            in_specs=in_specs,
            out_specs=out_specs,
            out_shape=outs,
            scratch_shapes=list(scratch),
            compiler_params=pltpu.CompilerParams(vmem_limit_bytes=VMEM_LIMIT),
            cost_estimate=pl.CostEstimate(
                flops=ops * self.work, transcendentals=self.work, bytes_accessed=size // COVER
            ),
        )(*args)

    def ends(self, step, inputs, mix_in, rate):
        return self.call(
            ends_kernel, 5, (step, inputs, mix_in, rate),
            [self.rows_spec, self.rows_spec, self.mix_spec, self.rate_spec],
            [self.state, self.state, self.edge],
            [self.state_spec, self.state_spec, self.edge_spec],
        )

    def run(self, step, inputs, mix_in, mix_out, rate, decay, state, enter):
        return self.call(
            states_kernel, 7, (step, inputs, mix_in, mix_out, rate, decay, state, enter),
            [self.rows_spec, self.rows_spec, self.mix_spec, self.mix_spec, self.rate_spec,
             self.state_spec, self.state_spec, self.edge_spec],
            [self.rows, self.state],
            [self.rows_spec, self.state_spec],
        )

    def adjoint_ends(self, step, mix_out, grad, rate):
        return self.call(
            adjoint_ends_kernel, 5, (step, mix_out, grad, rate),
            [self.rows_spec, self.mix_spec, self.rows_spec, self.rate_spec],
            [self.state, self.state, self.edge],
            [self.state_spec, self.state_spec, self.edge_spec],
        )

    def adjoint(self, args):
        return self.call(
            adjoint_kernel, 20, args,
            [self.rows_spec, self.rows_spec, self.mix_spec, self.mix_spec, self.rows_spec,
             self.rate_spec, self.state_spec, self.state_spec, self.state_spec, self.edge_spec,
             self.skip_spec],
            [self.narrow_rows, self.rows, self.edge, self.sums, self.lane_sums],
            [self.rows_spec, self.rows_spec, self.edge_spec, self.sums_spec, self.lane_spec],
            self.scratch,
        )


def conv_back_kernel(
    proj_ref, weight_ref, grad_ref, input_ref, taps_ref, shift_ref,
    out_ref, sums_ref, head_ref, tail_ref, product_ref, conv_ref,
):
    steps, rows, lanes = grad_ref.shape
    count = taps_ref.shape[0]
    reach = count - 1
    taps = [taps_ref[at : at + 1] for at in range(count)]
    shift = shift_ref[...]
    product_ref[...] = jnp.dot(
        proj_ref[...], weight_ref[...], preferred_element_type=F32
    ).reshape(steps, rows, lanes)

    def slopes(at, sums):
        inputs = [input_ref[at + tap].astype(F32) for tap in range(count)]
        pre = shift + sum(tap * value for tap, value in zip(taps, inputs))
        share = 1.0 / (1.0 + jnp.exp(-pre))
        conv = (grad_ref[at] + product_ref[at]) * (share * (1.0 + pre * (1.0 - share)))
        conv_ref[at] = conv
        return (*(total + conv * value for total, value in zip(sums, inputs)), sums[-1] + conv)

    zero = jnp.zeros((rows, lanes), F32)
    sums = lax.fori_loop(0, steps, slopes, (zero,) * (count + 1), unroll=2)
    for at, total in enumerate(sums):
        sums_ref[at : at + 1] = jnp.sum(total, axis=0, keepdims=True)
    sums_ref[count + 1 :] = jnp.zeros((sums_ref.shape[0] - count - 1, lanes), F32)
    row = sublane_rows(lanes)
    for at in range(reach):
        head_ref[at] = conv_ref[at]
        for low in range(0, rows, SEGMENTS):
            rolled = pltpu.roll(conv_ref[at, low : low + SEGMENTS], SEGMENTS - 1, 0)
            conv_ref[steps + at, low : low + SEGMENTS] = jnp.where(
                row < SEGMENTS - 1, rolled, 0.0
            )

    def back(at):
        return sum(taps[tap] * conv_ref[at + reach - tap] for tap in range(count))

    def store(at, carry):
        out_ref[at] = back(at).astype(BF16)
        return carry

    lax.fori_loop(0, steps, store, 0, unroll=2)
    for at in range(reach):
        tail_ref[at] = back(steps - reach + at)


def conv_back(proj, weight, grad, inputs, taps, shift):
    steps, rows, width = grad.shape
    reach = taps.shape[0] - 1
    lanes = LANES * math.gcd(width // LANES, BLOCKS)

    def block(count, dtype=F32):
        spec = pl.BlockSpec((count, rows, lanes), lambda at: (0, 0, at))
        return spec, jax.ShapeDtypeStruct((count, rows, width), dtype)

    def columns(count):
        return pl.BlockSpec((count, lanes), lambda at: (0, at))

    outs = [
        block(steps, BF16),
        (columns(SEGMENTS), jax.ShapeDtypeStruct((SEGMENTS, width), F32)),
        block(reach),
        block(reach),
    ]
    return pl.pallas_call(
        conv_back_kernel,
        grid=(width // lanes,),
        in_specs=[
            pl.BlockSpec(proj.shape, lambda at: (0, 0)),
            columns(weight.shape[0]),
            block(steps)[0],
            block(steps + reach)[0],
            columns(reach + 1),
            columns(1),
        ],
        out_specs=[spec for spec, _ in outs],
        out_shape=[shape for _, shape in outs],
        scratch_shapes=[
            pltpu.VMEM((steps, rows, lanes), F32),
            pltpu.VMEM((steps + reach, rows, lanes), F32),
        ],
        compiler_params=pltpu.CompilerParams(vmem_limit_bytes=VMEM_LIMIT),
        cost_estimate=pl.CostEstimate(flops=1, transcendentals=0, bytes_accessed=1),
    )(proj, weight, grad, inputs, taps, shift)


def expert_kernel(
    kept, rows_ref, cotan_ref, router_ref, mask_ref, up_a, down_a, up_b, down_b, *refs
):
    out_ref, picked_ref, prob_ref, copy_ref, grad_ref, active_a, active_b, hidden_a, hidden_b = refs[kept:]
    rows = rows_ref[...]
    copy_ref[...] = rows
    logits = contract_cols(rows, router_ref[...])
    shifted = jnp.exp(logits - jnp.max(logits, axis=1, keepdims=True))
    prob = shifted / jnp.sum(shifted, axis=1, keepdims=True)
    gate = jnp.sum(prob * mask_ref[...], axis=1, keepdims=True)
    grad = (gate * cotan_ref[...].astype(F32)).astype(BF16)
    prob_ref[...] = prob
    grad_ref[...] = grad
    out, picked = None, None
    for up, down, active_ref, hidden_ref in (
        (up_a, down_a, active_a, hidden_a),
        (up_b, down_b, active_b, hidden_b),
    ):
        up, down = (value[...].reshape(-1, value.shape[2]) for value in (up, down))
        hidden = jnp.dot(rows, up, preferred_element_type=F32)
        share = 0.5 + 0.5 * lax.erf(hidden * math.sqrt(0.5))
        slope = share + hidden * (jnp.exp(-0.5 * hidden * hidden) * (1.0 / math.sqrt(2 * math.pi)))
        active = (hidden * share).astype(BF16)
        active_ref[...] = active
        hidden_grad = (jnp.dot(grad, down, preferred_element_type=F32) * slope).astype(BF16)
        hidden_ref[...] = hidden_grad
        out_part = contract_cols(active, down)
        picked_part = contract_cols(hidden_grad, up)
        out = out_part if out is None else out + out_part
        picked = picked_part if picked is None else picked + picked_part
    out_ref[...] = out
    picked_ref[...] = picked


def expert_call(rows, cotan, router_t, mask, blocks, far_up, far_down, part, parts, kept):
    count, width = rows.shape
    shard, hidden = far_up.shape[1:]
    block = math.gcd(count, 512)
    base = part * (count // block)

    def rows_of(columns, low=0):
        return pl.BlockSpec((block, columns), lambda at: (at + low, 0))

    def whole(array):
        return pl.BlockSpec(array.shape, lambda at: (0, 0), pipeline_mode=pl.Buffered(1))

    def layer(array, at):
        return pl.BlockSpec(
            (array.shape[0], shard, hidden), lambda step: (0, at, 0), pipeline_mode=pl.Buffered(1)
        )

    experts = router_t.shape[0]
    inputs = (rows, cotan, router_t, mask, blocks, blocks, far_up, far_down)
    columns = (width, width, hidden, hidden, hidden, hidden)
    return pl.pallas_call(
        partial(expert_kernel, len(kept)),
        grid=(count // block,),
        in_specs=[
            rows_of(width), rows_of(width), whole(router_t), whole(mask),
            layer(blocks, 0), layer(blocks, 1), layer(far_up, 0), layer(far_down, 0),
            *[pl.BlockSpec(memory_space=pl.ANY)] * len(kept),
        ],
        out_specs=[
            rows_of(width), rows_of(width), rows_of(experts), *(rows_of(one, base) for one in columns)
        ],
        out_shape=[
            *(jax.ShapeDtypeStruct((count, one), F32) for one in (width, width, experts)),
            *(jax.ShapeDtypeStruct((parts * count, one), BF16) for one in columns),
        ],
        input_output_aliases={len(inputs) + at: 3 + at for at in range(len(kept))},
        compiler_params=pltpu.CompilerParams(vmem_limit_bytes=EXPERT_VMEM),
        cost_estimate=pl.CostEstimate(
            flops=16 * count * width * hidden,
            transcendentals=4 * count * hidden,
            bytes_accessed=count * (14 * width + 8 * hidden) + 8 * width * hidden,
        ),
    )(*inputs, *kept)


def expert_exchange(value, experts):
    count = lax.axis_size("dp")
    groups = None
    if count != experts:
        groups = [
            [base + e for e in range(experts)] for base in range(0, count, experts)
        ]
    return lax.all_to_all(value, "dp", 0, 0, axis_index_groups=groups, tiled=True)


def by_ctx(first, second):
    lead = lax.axis_index("ctx") == 0
    return jnp.where(lead, first, second), jnp.where(lead, second, first)


def own_expert_blocks(up_shards, down_shards):
    experts, _, hidden = up_shards.shape
    count = lax.axis_size("dp")
    half = hidden // 2
    both = jnp.concatenate([up_shards, down_shards], axis=1)
    if lax.axis_size("ctx") == 2:
        both = by_ctx(both[:, :, :half], both[:, :, half:])[0]
    if count != experts:
        both = jnp.concatenate([both] * (count // experts), axis=0)
    return lax.all_to_all(both, "dp", 0, 0, tiled=True)


def other_hidden(both):
    rows = both.shape[1] // 2
    if lax.axis_size("ctx") == 2:
        return swapped(both[:, :rows], "ctx"), swapped(both[:, rows:], "ctx")
    half = both.shape[2] // 2
    return both[:, :rows, half:], both[:, rows:, half:]


def gather_kernel(count, number, parts, *refs):
    ins, outs = refs[:number], refs[number : 2 * number]
    send_sem, recv_sem, own_sem = refs[2 * number :]
    places = count // 2
    me = lax.axis_index("dp")
    place, side = lax.div(me, 2), lax.rem(me, 2)
    across = me + 1 - 2 * side
    barrier = pltpu.get_barrier_semaphore()
    late = [part for part, (_, _, _, early) in enumerate(parts) if not early]
    early = [part for part, (_, _, _, early) in enumerate(parts) if early]

    def greet(device):
        pl.semaphore_signal(
            barrier, inc=1, device_id={"dp": device}, device_id_type=pl.DeviceIdType.MESH
        )

    greet(across)
    for step in (-1, 1):
        there = place + step

        @pl.when((there >= 0) & (there < places))
        def greet_place(step=step):
            greet(me + 2 * step)

    neighbours = 1 + (place > 0).astype(jnp.int32) + (place < places - 1).astype(jnp.int32)
    pl.semaphore_wait(barrier, neighbours)

    def copy(part, slot, kind, device, own):
        array, low, rows, _ = parts[part]
        landing = outs[array].at[slot, pl.ds(low, rows)]
        return pltpu.make_async_remote_copy(
            src_ref=ins[array].at[pl.ds(low, rows)] if own else landing,
            dst_ref=landing,
            send_sem=send_sem.at[kind, part, slot],
            recv_sem=recv_sem.at[part, slot],
            device_id={"dp": device},
            device_id_type=pl.DeviceIdType.MESH,
        )

    def along(which, slot, steps, own, act):
        for step in steps:
            there = place + step

            @pl.when((there >= 0) & (there < places))
            def one_way(step=step):
                for part in which:
                    act(copy(part, slot, step + 1, me + 2 * step, own))

    def aside(which, slot, own, act):
        for part in which:
            act(copy(part, slot, 1, across, own))

    def arrived(which, slot):
        for part in which:
            copy(part, slot, 1, across, False).wait_recv()

    def start(one):
        one.start()

    def sent(one):
        one.wait_send()

    mine = [
        pltpu.make_async_copy(ins[array], outs[array].at[me], own_sem.at[array])
        for array in range(number)
    ]
    for one in mine:
        one.start()
    both = (-1, 1)
    aside(early, me, True, start)
    for part in late:
        along((part,), me, both, True, start)
        aside((part,), me, True, start)
    along(early, me, both, True, start)
    arrived(early, across)
    along(early, across, both, False, start)
    for far in range(1, places):
        for step in both:
            origin = place - step * far

            @pl.when((origin >= 0) & (origin < places))
            def forward(step=step, far=far):
                slot, other = me - 2 * step * far, across - 2 * step * far
                for part in late:
                    arrived((part,), slot)
                    along((part,), slot, (step,), False, start)
                    aside((part,), slot, False, start)
                arrived(early, slot)
                along(early, slot, (step,), False, start)
                arrived(early, other)
                along(early, other, (step,), False, start)

    for at in range(places):
        arrived(late, 2 * at + 1 - side)
    for one in mine:
        one.wait()
    aside(early + late, me, True, sent)
    along(early + late, me, both, True, sent)
    along(early, across, both, False, sent)
    for far in range(1, places):
        for step in both:
            origin = place - step * far

            @pl.when((origin >= 0) & (origin < places))
            def forwarded(step=step, far=far):
                slot, other = me - 2 * step * far, across - 2 * step * far
                aside(late, slot, False, sent)
                along(early + late, slot, (step,), False, sent)
                along(early, other, (step,), False, sent)


def gathered(*values):
    count = lax.axis_size("dp")
    number = len(values)
    parts = []
    for at, value in enumerate(values):
        rows = value.shape[0]
        step = rows // 3 if value.shape[1] > 1024 and rows % 24 == 0 else rows
        parts += [
            (at, low, step, at == number - 1 and 0 < low == rows - step)
            for low in range(0, rows, step)
        ]
    anywhere = pl.BlockSpec(memory_space=pl.ANY)
    size = sum(math.prod(value.shape) * 2 for value in values)
    return pl.pallas_call(
        partial(gather_kernel, count, number, parts),
        in_specs=[anywhere] * number,
        out_specs=[anywhere] * number,
        out_shape=[jax.ShapeDtypeStruct((count, *value.shape), value.dtype) for value in values],
        scratch_shapes=[
            pltpu.SemaphoreType.DMA((3, len(parts), count)),
            pltpu.SemaphoreType.DMA((len(parts), count)),
            pltpu.SemaphoreType.DMA((number,)),
        ],
        compiler_params=pltpu.CompilerParams(collective_id=0, has_side_effects=True),
        cost_estimate=pl.CostEstimate(
            flops=0, transcendentals=0, bytes_accessed=2 * count * size
        ),
    )(*values)


def other_joined(own, first_shard, second_shard):
    count = lax.axis_size("ctx")
    if count == 2:
        return by_ctx(own, swapped(own, "ctx"))
    del first_shard, second_shard
    every = lax.all_gather(own, "ctx")
    return every[0], every[1]


def expert_weight_products(rows, hidden_grads, grads, actives):
    pairs = ((rows, hidden_grads), (grads, actives))
    far = [contract_rows(left, rights[1]) for left, rights in pairs]
    if lax.axis_size("ctx") == 2:
        far = [value.astype(BF16) for value in far]
    return [contract_rows(left, rights[0]) for left, rights in pairs], far


def sent_far(value):
    return swapped(value, "ctx") if lax.axis_size("ctx") == 2 else value


def expert_weight_parts(near, far):
    count = lax.axis_size("dp")
    parts = []
    for own, other in zip(near, far):
        if lax.axis_size("ctx") == 2:
            part = own + other.astype(F32)
        else:
            part = lax.psum_scatter(
                jnp.concatenate([own, other], axis=1), "ctx", scatter_dimension=1, tiled=True
            )
        parts.append(part.astype(BF16).reshape(count, part.shape[0] // count, part.shape[1]))
    return jnp.concatenate(parts, axis=1)


def expert_weight_blocks(blocks, experts):
    count = lax.axis_size("dp")
    if count != experts:
        blocks = jnp.sum(
            blocks.reshape(count // experts, experts, *blocks.shape[1:]).astype(F32), axis=0
        ).astype(BF16)
    shard = blocks.shape[1] // 2
    return blocks[:, :shard], blocks[:, shard:]


def far_hidden(blocks):
    if lax.axis_size("ctx") == 2:
        return swapped(blocks, "ctx")
    return lax.all_gather(blocks, "ctx", axis=2, tiled=True)


def expert_weight_grad(blocks, far_blocks):
    if lax.axis_size("ctx") == 2:
        far_blocks = jnp.concatenate(by_ctx(blocks, far_blocks), axis=2)
    return far_blocks.astype(F32)


def pair_products(first, second):
    if lax.axis_size("ctx") != 2:
        return contract_rows(*first), contract_rows(*second).astype(BF16)
    lefts, rights = by_ctx(first[0], second[0]), by_ctx(first[1], second[1])
    return contract_rows(lefts[0], rights[0]), contract_rows(lefts[1], rights[1]).astype(BF16)


def product_part(near, far):
    count = lax.axis_size("dp")

    def blocks(value):
        return value.astype(BF16).reshape(count, value.shape[0] // count, value.shape[1])

    if lax.axis_size("ctx") != 2:
        return jnp.concatenate([blocks(near), blocks(far)], axis=1)
    return blocks(near + far.astype(F32))


def product_shards(blocks):
    sums = jnp.sum(blocks.astype(F32), axis=0)
    if lax.axis_size("ctx") == 2:
        return by_ctx(sums, swapped(sums, "ctx"))
    sums = lax.psum(sums, "ctx")
    rows = sums.shape[0] // 2
    return sums[:rows], sums[rows:]


def local(
    hidden_in,
    out_grad,
    norm1_gain,
    in_weight,
    conv_weight,
    conv_bias,
    xproj_weight,
    dt_weight,
    dt_bias,
    decay_log,
    skip_weight,
    out_weight,
    norm2_gain,
    router_weight,
    fc1_weight,
    fc2_weight,
    expert_ids,
    keep_mask,
):
    batches, seqs, length, model_width = hidden_in.shape
    chains = batches * seqs
    tokens = chains * length
    steps = length // SEGMENTS
    shard, _, inner = in_weight.shape
    taps = conv_weight.shape[0]
    low_rank = dt_weight.shape[0]
    states = decay_log.shape[0]
    experts = fc1_weight.shape[0]
    dp_count = lax.axis_size("dp")
    tp_count = lax.axis_size("tp")
    capacity = tokens // 4
    part_cap = capacity // tp_count // HALVES
    slots = experts * part_cap
    tp_index = lax.axis_index("tp")
    scan = Scan(steps, chains, states, inner)

    def to_rows(value):
        value = value.reshape(chains, SEGMENTS, steps, -1).transpose(2, 0, 1, 3)
        return value.reshape(tokens, -1)

    def from_rows(value):
        value = value.reshape(steps, chains, SEGMENTS, -1).transpose(1, 2, 0, 3)
        return value.reshape(batches, seqs, length, -1)

    pieces = [
        norm1_gain[None],
        conv_weight,
        conv_bias[None],
        dt_weight,
        dt_bias[None],
        decay_log,
        skip_weight[None],
        norm2_gain[None],
        router_weight.T,
        xproj_weight.T,
    ]
    bounds = [0]
    for piece in pieces:
        bounds.append(bounds[-1] + piece.shape[0])
    small = sum(
        jnp.pad(piece, ((low, bounds[-1] - high), (0, 0)))
        for piece, low, high in zip(pieces, bounds, bounds[1:])
    )
    kinds = small.shape[0]
    small_wide = jnp.pad(small.T, ((0, 0), (0, -kinds % LANES)))
    in_x, small_all, later = gathered(
        in_weight[:, 0], small_wide, by_ctx(out_weight.T, in_weight[:, 1])[0]
    )
    in_x = in_x.reshape(dp_count * shard, inner)
    later = later.reshape(dp_count * shard, inner)
    small_all = small_all.reshape(dp_count * shard, -1)[:, :kinds].T
    small_all, up_shards, down_shards = together(
        small_all, fc1_weight, fc2_weight.transpose(0, 2, 1)
    )
    pieces = [small_all[bounds[i] : bounds[i + 1]] for i in range(len(bounds) - 1)]
    gain_one_f = pieces[0].astype(F32)
    tap_weights = pieces[1].astype(F32)
    conv_shift = pieces[2].astype(F32)
    dt_proj = pieces[3]
    dt_shift = pieces[4].astype(F32)
    decay_rate = -jnp.exp(pieces[5].astype(F32))
    skip_row = pieces[6].astype(F32)
    gain_two_f = pieces[7].astype(F32)
    router_t = pieces[8]
    x_proj_t = pieces[9]
    rate_rows = jnp.broadcast_to((decay_rate * LOG2E)[:, None, :], (states, SEGMENTS, inner))
    expert_blocks = own_expert_blocks(up_shards, down_shards)

    values = lax.optimization_barrier(to_rows(hidden_in)).astype(F32)
    normalized_rows, inverse_one = rms_forward(values, gain_one_f)
    normed_bf = normalized_rows.astype(BF16)
    x_pre = jnp.dot(normed_bf, in_x, preferred_element_type=F32).astype(BF16)
    x_pre = x_pre.reshape(steps, chains, SEGMENTS, inner)
    tail = x_pre[steps - taps + 1 :]
    edge_in = passed_along(tail[:, :, SEGMENTS - 1 :], "ctx", 1)
    edge_in, later = together(edge_in, later)
    out_proj_t, in_z = other_joined(later, out_weight.T, in_weight[:, 1])
    halo = jnp.concatenate([edge_in, tail[:, :, : SEGMENTS - 1]], axis=2)
    extended_bf = jnp.concatenate([halo, x_pre], axis=0)
    extended = extended_bf.astype(F32)
    conv_pre = jnp.broadcast_to(conv_shift[0], x_pre.shape)
    for tap in range(taps):
        conv_pre = conv_pre + tap_weights[tap] * extended[tap : tap + steps]
    xconv_bf = jax.nn.silu(conv_pre).astype(BF16)
    xconv = xconv_bf.astype(F32)
    xconv_rows = xconv_bf.reshape(tokens, inner)
    projected = axis_sum(contract_cols(xconv_rows, x_proj_t), "tp")
    dt_low = projected[:, :low_rank].astype(BF16)

    def mixes(value):
        value = value.reshape(steps, chains, SEGMENTS, states).transpose(1, 0, 3, 2)
        return jnp.broadcast_to(value[..., None], (*value.shape, LANES))

    mix_in = mixes(projected[:, low_rank : low_rank + states])
    mix_out = mixes(projected[:, low_rank + states :])
    dt_pre = (jnp.dot(dt_low, dt_proj, preferred_element_type=F32) + dt_shift).reshape(x_pre.shape)
    step_size = jax.nn.softplus(dt_pre)
    seg_decay, seg_state, last_state = scan.ends(step_size, xconv, mix_in, rate_rows)
    later_ids, later_mask, later_grad, _ = together(expert_ids, keep_mask, out_grad, seg_state)
    route = to_rows(later_ids)[:, 0]
    keep = to_rows(later_mask)[:, 0].astype(F32)
    onehot_int = (route[:, None] == jnp.arange(experts, dtype=jnp.int32)[None, :]).astype(jnp.int32)
    rank = jnp.sum((jnp.cumsum(onehot_int, axis=0) - 1) * onehot_int, axis=1)
    places = []
    for half in range(HALVES):
        own = rank - (tp_index * HALVES + half) * part_cap
        token_slot = jnp.where((own >= 0) & (own < part_cap), route * part_cap + own, -1)
        places.append(
            (token_slot[None, :] == jnp.arange(slots, dtype=jnp.int32)[:, None]).astype(BF16)
        )

    def slotted(value, half):
        sent = jnp.dot(places[half], value, preferred_element_type=F32).astype(BF16)
        return sent.reshape(experts, part_cap, -1)

    def landed(values):
        total = sum(
            contract_rows(place, value.reshape(slots, -1)) for place, value in zip(places, values)
        )
        return axis_sum(total.astype(BF16), "tp").astype(F32)

    def halves_of(value):
        return [value[:, at : at + part_cap] for at in range(0, value.shape[1], part_cap)]

    cotan_bf = to_rows(later_grad)
    cotan = cotan_bf.astype(F32)
    kept_cotan = (cotan * keep[:, None]).astype(BF16)
    sent_cotan = jnp.concatenate([slotted(kept_cotan, half) for half in range(HALVES)], axis=1)
    entering = entering_pieces(seg_decay[:, :, SEGMENTS - 1], last_state, "ctx", False)
    entering, mix_out, expert_blocks, sent_cotan = together(
        entering, mix_out, expert_blocks, sent_cotan
    )
    slot_cotan = expert_exchange(sent_cotan, experts)
    far_up, far_down = other_hidden(expert_blocks)
    scan_out, seg_start = scan.run(
        step_size, xconv, mix_in, mix_out, rate_rows, seg_decay, seg_state, entering
    )
    z_gate = jnp.dot(normed_bf, in_z, preferred_element_type=F32).reshape(x_pre.shape)
    scanned = scan_out + skip_row[0] * xconv
    z_silu = jax.nn.silu(z_gate)
    gated_bf = (scanned * z_silu).astype(BF16).reshape(tokens, inner)
    gated_bf, far_up = together(gated_bf, far_up)
    mixer_part, slot_cotan = together(contract_cols(gated_bf, out_proj_t), slot_cotan)
    middle = values + axis_sum(mixer_part, "tp")

    normed_two, inverse_two = rms_forward(middle, gain_two_f)
    normed_two_bf = normed_two.astype(BF16)
    expert_mask = (
        jnp.arange(experts, dtype=jnp.int32) == lax.rem(lax.axis_index("dp"), experts)
    ).astype(F32)[None, :]
    kept = ()
    got_grads, slot_outs, router_grad_t = [], [], 0.0
    for half, half_cotan in enumerate(halves_of(slot_cotan)):
        own_rows = expert_exchange(slotted(normed_two_bf, half), experts)
        if not half:
            own_rows, far_down = together(own_rows, far_down)
        else:
            own_rows, kept = together(own_rows, kept)
        own_rows = own_rows.reshape(slots, model_width)
        half_cotan = half_cotan.reshape(slots, model_width)
        far_rows, far_cotan = swapped(own_rows, "tp"), swapped(half_cotan, "tp")
        call = partial(
            expert_call, router_t=router_t, mask=expert_mask, blocks=expert_blocks, far_up=far_up,
            far_down=far_down, parts=2 * HALVES,
        )
        far = call(far_rows, far_cotan, part=2 * half, kept=kept)
        near = call(own_rows, half_cotan, part=2 * half + 1, kept=far[3:])
        if half:
            near, got_grads = together(near, got_grads)
        kept = near[3:]
        slot_out = near[0] + swapped(far[0], "tp")
        picked_grad = near[1] + swapped(far[1], "tp")
        slot_prob = near[2]
        slot_gate = jnp.sum(slot_prob * expert_mask, axis=1, keepdims=True)
        gate_grad = jnp.sum(slot_out * half_cotan.astype(F32), axis=1, keepdims=True)
        logit_grad = gate_grad * slot_gate * (expert_mask - slot_prob)
        router_grad_t = router_grad_t + contract_rows(logit_grad, own_rows.astype(F32), HIGHEST)
        picked_grad = picked_grad + jnp.dot(
            logit_grad, router_t.astype(F32), precision=HIGHEST, preferred_element_type=F32
        )
        got_grads.append(
            expert_exchange(picked_grad.astype(BF16).reshape(experts, part_cap, -1), experts)
        )
        slot_outs.append(slot_out.astype(BF16).reshape(experts, part_cap, -1))
    router_grad_t = axis_sum(router_grad_t, "tp")
    all_rows, all_grads, active_a, active_b, hidden_a, hidden_b = kept
    near_parts, far_parts = expert_weight_products(
        all_rows, (hidden_a, hidden_b), all_grads, (active_a, active_b)
    )
    far_first = sent_far(far_parts[0])
    got_grads, near_parts, far_second, far_first, slot_outs, router_grad_t = together(
        got_grads, near_parts, far_parts[1], far_first, slot_outs, router_grad_t
    )
    far_parts = far_first, sent_far(far_second)
    normed_two_grad = landed(got_grads)
    got_out = expert_exchange(jnp.concatenate(slot_outs, axis=1), experts)
    middle_norm_grad, gain_two_grad = rms_backward(middle, inverse_two, gain_two_f, normed_two_grad)
    middle_grad = cotan + middle_norm_grad
    mixer_grad_bf = middle_grad.astype(BF16)
    gated_grad = jnp.dot(mixer_grad_bf, out_proj_t, preferred_element_type=F32).reshape(x_pre.shape)
    scan_grad = gated_grad * z_silu
    z_grad = jax.vjp(jax.nn.silu, z_gate)[1](gated_grad * scanned)[0]
    z_grad_bf = z_grad.astype(BF16).reshape(tokens, inner)
    near_product, far_product = pair_products((mixer_grad_bf, gated_bf), (normed_bf, z_grad_bf))
    back_decay, back_adjoint, first_adjoint = scan.adjoint_ends(
        step_size, mix_out, scan_grad, rate_rows
    )
    normed_part = contract_cols(z_grad_bf, in_z)
    far_parts, got_out, near_product, far_product, _ = together(
        far_parts, got_out, near_product, far_product, first_adjoint
    )
    weight_blocks = lax.all_to_all(
        expert_weight_parts(near_parts, far_parts), "dp", 0, 0, tiled=True
    )
    leaving = entering_pieces(back_decay[:, :, 0], first_adjoint, "ctx", True)
    leaving, near_product, far_product, normed_part = together(
        leaving, near_product, far_product, normed_part
    )
    far_product = sent_far(far_product)
    adjoint_args = (
        step_size, xconv, mix_in, mix_out, scan_grad, rate_rows, seg_start, back_decay, back_adjoint,
        leaving, skip_row,
    )
    pre_grad, xconv_grad, decay_sum, scan_sums, mix_grad = scan.adjoint(adjoint_args)
    pre_grad, far_product, weight_blocks = together(pre_grad, far_product, weight_blocks)
    weight_blocks = expert_weight_blocks(weight_blocks, experts)
    far_ups = far_hidden(weight_blocks[0])
    out_blocks = lax.all_to_all(product_part(near_product, far_product), "dp", 0, 0, tiled=True)
    decay_log_grad = jnp.sum(decay_sum, axis=0) * decay_rate
    dt_shift_grad, skip_grad = jnp.sum(scan_sums, axis=0)[:2]
    pre_grad = pre_grad.reshape(tokens, inner)
    dt_proj_grad = contract_rows(dt_low, pre_grad)
    dt_low_grad = contract_cols(pre_grad, dt_proj)
    mix_grad = mix_grad.reshape(tokens, LANES)[:, : 2 * states]
    proj_part = jnp.concatenate([dt_low_grad, mix_grad], axis=1)
    proj_grad_bf = axis_sum(proj_part, "tp").astype(BF16)
    x_proj_grad_t = contract_rows(proj_grad_bf, xconv_rows)
    flat = (chains * SEGMENTS, inner)
    x_grad_bf, conv_sums, head, last = conv_back(
        proj_grad_bf,
        x_proj_t,
        xconv_grad.reshape(steps, *flat),
        extended_bf.reshape(steps + taps - 1, *flat),
        tap_weights,
        conv_shift,
    )
    taps_grad, shift_grad = conv_sums[:taps], conv_sums[taps]
    edge_back = passed_along(
        head.reshape(taps - 1, chains, SEGMENTS, inner)[:, :, :1], "ctx", -1
    )
    edge_back, out_blocks, far_ups = together(edge_back, out_blocks, far_ups)
    reaching = jnp.stack(
        [
            sum(tap_weights[tap] * edge_back[at - tap] for tap in range(at + 1))
            for at in range(taps - 1)
        ]
    )
    reaching = jnp.pad(reaching, ((0, 0), (0, 0), (SEGMENTS - 1, 0), (0, 0)))
    last = (last + reaching.reshape(taps - 1, *flat)).astype(BF16)
    x_grad_bf = lax.dynamic_update_slice(x_grad_bf, last, (steps - taps + 1, 0, 0))
    x_grad_bf = x_grad_bf.reshape(tokens, inner)
    small_grads = jnp.concatenate(
        [
            taps_grad,
            shift_grad[None],
            dt_proj_grad,
            dt_shift_grad[None],
            decay_log_grad,
            skip_grad[None],
            gain_two_grad[None],
            router_grad_t,
            x_proj_grad_t,
        ],
        axis=0,
    )
    small_grads = small_grads.reshape(-1, dp_count, shard).transpose(1, 0, 2)
    small_size = small_grads.shape[1] * shard
    small_rows = small_grads.astype(BF16).reshape(dp_count, small_size)
    small_rows = jnp.pad(small_rows, ((0, 0), (0, -small_size % inner))).reshape(dp_count, -1, inner)
    x_grad_bf, small_rows, out_blocks = together(x_grad_bf, small_rows, out_blocks)
    normed_part = normed_part + contract_cols(x_grad_bf, in_x)
    normed_grad = axis_sum(normed_part, "tp")
    values_norm_grad, gain_one_grad = rms_backward(values, inverse_one, gain_one_f, normed_grad)
    input_grad = from_rows((middle_grad + values_norm_grad).astype(BF16))

    in_x_part = contract_rows(normed_bf, x_grad_bf).astype(BF16).reshape(dp_count, shard, inner)
    gain_row = gain_one_grad.reshape(dp_count, 1, shard)
    gain_high = gain_row.astype(BF16)
    gain_low = (gain_row - gain_high.astype(F32)).astype(BF16)
    gain_row = jnp.concatenate([gain_high, gain_low], axis=2)
    gain_row = jnp.pad(gain_row, ((0, 0), (0, 0), (0, inner - 2 * shard)))
    in_x_part, out_blocks = together(in_x_part, out_blocks)
    out_proj_grad, in_z_grad = product_shards(out_blocks)
    in_x_blocks = lax.all_to_all(
        jnp.concatenate([in_x_part, small_rows, gain_row], axis=1), "dp", 0, 0, tiled=True
    )
    out_proj_grad, in_z_grad, far_down_blocks = together(
        out_proj_grad, in_z_grad, weight_blocks[1]
    )
    far_downs, in_x_blocks = together(far_hidden(far_down_blocks), in_x_blocks)
    first_grad = expert_weight_grad(weight_blocks[0], far_ups)
    second_grad = expert_weight_grad(weight_blocks[1], far_downs)
    router_prob = jax.nn.softmax(contract_cols(normed_two_bf, router_t), axis=-1)
    gate_prob = jnp.sum(router_prob * onehot_int.astype(F32), axis=1) * keep
    result = from_rows((middle + gate_prob[:, None] * landed(halves_of(got_out))).astype(BF16))
    in_x_sums = jnp.sum(in_x_blocks.astype(F32), axis=0).astype(BF16)
    in_x_sums = narrow_sum(in_x_sums, "ctx")
    in_x_grad = in_x_sums[:shard]
    gain_one_grad = in_x_sums[-1:, :shard] + in_x_sums[-1:, shard : 2 * shard]
    small_grads = in_x_sums[shard:-1].reshape(-1)[:small_size].reshape(-1, shard)
    small_grads = jnp.concatenate([gain_one_grad, small_grads], axis=0)
    sums = [small_grads[bounds[i] : bounds[i + 1]] for i in range(len(bounds) - 1)]
    return (
        result,
        input_grad,
        sums[0][0],
        jnp.stack([in_x_grad, in_z_grad], axis=1),
        sums[1],
        sums[2][0],
        sums[9].T,
        sums[3],
        sums[4][0],
        sums[5],
        sums[6][0],
        out_proj_grad.T,
        sums[7][0],
        sums[8].T,
        first_grad,
        second_grad.transpose(0, 2, 1),
    )


def solution(mesh):
    weights = (
        P("dp"),
        P("dp", None, "tp"),
        P(None, ("tp", "dp")),
        P(("tp", "dp")),
        P(("tp", "dp"), None),
        P(None, ("tp", "dp")),
        P(("tp", "dp")),
        P(None, ("tp", "dp")),
        P(("tp", "dp")),
        P("tp", "dp"),
        P("dp"),
        P("dp", None),
        P(None, "dp", "tp"),
        P(None, "tp", "dp"),
    )
    rows = P(None, "dp", "ctx", None)
    return jax.shard_map(
        local,
        mesh=mesh,
        in_specs=(rows, rows, *weights, P(("dp", "ctx"), None), P(("dp", "ctx"))),
        out_specs=(rows, rows, *weights),
        check_vma=False,
    )
```

```python
from functools import partial
import math

import jax
import jax.numpy as jnp
from jax import lax
from jax.experimental import pallas as pl
from jax.experimental.pallas import tpu as pltpu
from jax.sharding import PartitionSpec as P

EPSILON = 1e-05
HIGHEST = lax.Precision.HIGHEST
SEGMENTS = 8
LANES = 128
VMEM_LIMIT = 56 * 1024 * 1024
EXPERT_VMEM = 56 * 1024 * 1024
LOG2E = math.log2(math.e)
GROUP_A = 4
GROUP_B = 4
GROUP_C = 8
UNROLL_A = 16
UNROLL_B = 16
UNROLL_C = 8
UNROLL_D = 4
UNROLL_E = 8
BLOCKS = 3
COVER = 100
HALVES = 1
BF16 = jnp.bfloat16
F32 = jnp.float32


def swapped(value, axis):
    return lax.ppermute(value, axis, [(0, 1), (1, 0)])


def passed_along(value, axis, steps):
    count = lax.axis_size(axis)
    leading, last = (max(0, -steps), min(count, count - steps))
    return lax.ppermute(value, axis, [(source, source + steps) for source in range(leading, last)])


def axis_sum(value, axis):
    if lax.axis_size(axis) == 2:
        return value + swapped(value, axis)
    return lax.psum(value, axis)


def together(*values):
    return lax.optimization_barrier(values)


def narrow_sum(value, axis):
    if lax.axis_size(axis) == 2:
        return value.astype(F32) + swapped(value, axis).astype(F32)
    return lax.psum(value.astype(F32), axis)


def entering_pieces(decay, value, axis, backward):
    count = lax.axis_size(axis)
    if count == 2:
        return passed_along(value, axis, -1 if backward else 1)
    mine = lax.axis_index(axis)
    decays = lax.all_gather(decay, axis)
    values = lax.all_gather(value, axis)
    running = jnp.zeros_like(value)
    for position in range(count - 1):
        at = count - 1 - position if backward else position
        longer = values[at] + decays[at] * running
        ahead = at > mine if backward else at < mine
        running = jnp.where(ahead, longer, running)
    return running


def contract_rows(left_side, right_side, precision=None):
    return lax.dot_general(
        left_side,
        right_side,
        (((0,), (0,)), ((), ())),
        precision=precision,
        preferred_element_type=F32,
    )


def contract_cols(left_side, right_side, precision=None):
    return lax.dot_general(
        left_side,
        right_side,
        (((1,), (1,)), ((), ())),
        precision=precision,
        preferred_element_type=F32,
    )


def rms_forward(values, gain_vec):
    inverse = lax.rsqrt(jnp.mean(values * values, axis=-1, keepdims=True) + EPSILON)
    return (values * inverse * gain_vec, inverse)


def rms_backward(values, inverse, gain_vec, grad_out):
    weighted = grad_out * gain_vec
    inner_mean = jnp.mean(values * weighted, axis=-1, keepdims=True)
    grad_values = inverse * weighted - values * inverse * inverse * inverse * inner_mean
    grad_gain = jnp.sum(grad_out * values * inverse, axis=0)
    return (grad_values, grad_gain)


def zeros_of(ref):
    return jnp.zeros(ref.shape[1:], F32)


def sublane_rows(lanes):
    return lax.broadcasted_iota(jnp.int32, (SEGMENTS, lanes), 0)


def widened(value, lanes):
    return jnp.concatenate([value] * (lanes // LANES), axis=1) if lanes > LANES else value


def narrowed(value):
    parts = [value[:, at : at + LANES] for at in range(0, value.shape[1], LANES)]
    return sum(parts[1:], parts[0])


def groups_of(states, size):
    size = math.gcd(states, size)
    return [range(first, first + size) for first in range(0, states, size)]


def joined_forward(decay, value, row):
    for reach in (1, 2, 4):
        inside = row >= reach
        value = value + jnp.where(inside, decay * pltpu.roll(value, reach, 0), 0.0)
        decay = jnp.where(inside, decay * pltpu.roll(decay, reach, 0), decay)
    return decay, value


def joined_backward(decay, value, row):
    for reach in (1, 2, 4):
        inside = row < SEGMENTS - reach
        value = value + jnp.where(inside, decay * pltpu.roll(value, SEGMENTS - reach, 0), 0.0)
        decay = jnp.where(inside, decay * pltpu.roll(decay, SEGMENTS - reach, 0), decay)
    return decay, value


def ends_kernel(step_ref, input_ref, mix_in_ref, rate_ref, decay_ref, state_ref, last_ref):
    steps, states, lanes = step_ref.shape[0], mix_in_ref.shape[1], step_ref.shape[2]
    zero = zeros_of(step_ref)
    row = sublane_rows(lanes)
    total = lax.fori_loop(0, steps, lambda at, total: total + step_ref[at], zero, unroll=UNROLL_E)
    for members in groups_of(states, GROUP_A):
        rates = [rate_ref[n] for n in members]

        def body(at, held):
            step = step_ref[at]
            driven = step * input_ref[at]
            return tuple(
                jnp.exp2(step * rate) * before + widened(mix_in_ref[at, n], lanes) * driven
                for n, rate, before in zip(members, rates, held)
            )

        held = lax.fori_loop(0, steps, body, (zero,) * len(members), unroll=UNROLL_A)
        for n, rate, end in zip(members, rates, held):
            decay, value = joined_forward(jnp.exp2(total * rate), end, row)
            decay_ref[n] = decay
            state_ref[n] = value
            last_ref[n : n + 1] = value[SEGMENTS - 1 :]


def states_kernel(
    step_ref, input_ref, mix_in_ref, mix_out_ref, rate_ref, decay_ref, state_ref, enter_ref,
    out_ref, start_ref,
):
    steps, states, lanes = step_ref.shape[0], mix_in_ref.shape[1], step_ref.shape[2]
    row = sublane_rows(lanes)
    for members in groups_of(states, GROUP_B):
        rates = [rate_ref[n] for n in members]
        held = []
        for n in members:
            first = jnp.broadcast_to(enter_ref[n : n + 1], (SEGMENTS, lanes))
            inner = pltpu.roll(state_ref[n], 1, 0) + pltpu.roll(decay_ref[n], 1, 0) * first
            start = jnp.where(row >= 1, inner, first)
            start_ref[n] = start
            held.append(start)

        def body(at, held):
            step = step_ref[at]
            driven = step * input_ref[at]
            held = tuple(
                jnp.exp2(step * rate) * before + widened(mix_in_ref[at, n], lanes) * driven
                for n, rate, before in zip(members, rates, held)
            )
            parts = [widened(mix_out_ref[at, n], lanes) * now for n, now in zip(members, held)]
            if members[0]:
                parts.append(out_ref[at])
            while len(parts) > 1:
                parts = [sum(parts[i + 1 : i + 2], parts[i]) for i in range(0, len(parts), 2)]
            out_ref[at] = parts[0]
            return held

        lax.fori_loop(0, steps, body, tuple(held), unroll=UNROLL_B)


def adjoint_ends_kernel(step_ref, mix_out_ref, grad_ref, rate_ref, decay_ref, adjoint_ref, first_ref):
    steps, states, lanes = step_ref.shape[0], mix_out_ref.shape[1], step_ref.shape[2]
    zero = zeros_of(step_ref)
    row = sublane_rows(lanes)
    total = lax.fori_loop(0, steps, lambda at, total: total + step_ref[at], zero, unroll=UNROLL_E)
    for members in groups_of(states, GROUP_A):
        rates = [rate_ref[n] for n in members]

        def body(back, incoming):
            at = steps - 1 - back
            step = step_ref[at]
            grad = grad_ref[at]
            return tuple(
                jnp.exp2(step * rate) * (widened(mix_out_ref[at, n], lanes) * grad + after)
                for n, rate, after in zip(members, rates, incoming)
            )

        incoming = lax.fori_loop(0, steps, body, (zero,) * len(members), unroll=UNROLL_A)
        for n, rate, end in zip(members, rates, incoming):
            decay, value = joined_backward(jnp.exp2(total * rate), end, row)
            decay_ref[n] = decay
            adjoint_ref[n] = value
            first_ref[n : n + 1] = value[:1]


def adjoint_kernel(
    step_ref, input_ref, mix_in_ref, mix_out_ref, grad_ref, rate_ref, start_ref, decay_ref, adjoint_ref,
    enter_ref, skip_ref,
    pre_out_ref, conv_ref, decay_sum_ref, sums_ref, mix_ref,
    states_ref, decays_ref, in_grad_ref, out_grad_ref, pre_ref,
):
    steps, states, lanes = step_ref.shape[0], mix_in_ref.shape[1], step_ref.shape[2]
    row = sublane_rows(lanes)
    zero = zeros_of(step_ref)

    @pl.when(pl.program_id(1) == 0)
    def clear():
        in_grad_ref[...] = jnp.zeros_like(in_grad_ref)
        out_grad_ref[...] = jnp.zeros_like(out_grad_ref)

    for members in groups_of(states, GROUP_C):
        first, group = members[0], len(members)
        rates = [rate_ref[n] for n in members]

        def ahead(at, held):
            step = step_ref[at]
            driven = step * input_ref[at]
            grad = grad_ref[at]
            after = []
            for i, n in enumerate(members):
                states_ref[at, i] = held[i]
                decay = jnp.exp2(step * rates[i])
                decays_ref[at, i] = decay
                now = decay * held[i] + widened(mix_in_ref[at, n], lanes) * driven
                out_grad_ref[at, n] += narrowed(grad * now)
                after.append(now)
            return tuple(after)

        lax.fori_loop(0, steps, ahead, tuple(start_ref[n] for n in members), unroll=UNROLL_C)

        incoming = []
        for n in members:
            final = jnp.broadcast_to(enter_ref[n : n + 1], (SEGMENTS, lanes))
            inner = (
                pltpu.roll(adjoint_ref[n], SEGMENTS - 1, 0)
                + pltpu.roll(decay_ref[n], SEGMENTS - 1, 0) * final
            )
            incoming.append(jnp.where(row < SEGMENTS - 1, inner, final))

        def body(back, carry):
            at = steps - 1 - back
            incoming, decay_sums = carry
            step = step_ref[at]
            grad = grad_ref[at]
            driven = step * input_ref[at]
            in_sum = conv_ref[at] if first else zero
            rate_sum = pre_ref[at] if first else zero
            following, sums = [], []
            for i, n in enumerate(members):
                adjoint = widened(mix_out_ref[at, n], lanes) * grad + incoming[i]
                onward = decays_ref[at, i] * adjoint
                decay_grad = onward * states_ref[at, i]
                in_sum = in_sum + adjoint * widened(mix_in_ref[at, n], lanes)
                rate_sum = rate_sum + decay_grad * rates[i]
                sums.append(decay_sums[i] + decay_grad * step)
                in_grad_ref[at, n] += narrowed(adjoint * driven)
                following.append(onward)
            conv_ref[at] = in_sum
            pre_ref[at] = rate_sum
            return tuple(following), tuple(sums)

        _, sums = lax.fori_loop(
            0, steps, body, (tuple(incoming), (zero,) * group), unroll=UNROLL_D
        )
        for i, n in enumerate(members):
            decay_sum_ref[n : n + 1] = jnp.sum(sums[i], axis=0, keepdims=True)

    skip = skip_ref[...]

    def close(at, carry):
        pre_sum, skip_sum = carry
        step, inputs, grad, in_sum = step_ref[at], input_ref[at], grad_ref[at], conv_ref[at]
        step_grad = pre_ref[at] * (1.0 / LOG2E) + in_sum * inputs
        pre = step_grad * (1.0 - jnp.exp2(step * -LOG2E))
        pre_out_ref[at] = pre.astype(BF16)
        conv_ref[at] = in_sum * step + skip * grad
        return pre_sum + pre, skip_sum + grad * inputs

    pre_sum, skip_sum = lax.fori_loop(0, steps, close, (zero, zero), unroll=UNROLL_E)
    sums_ref[0:1] = jnp.sum(pre_sum, axis=0, keepdims=True)
    sums_ref[1:2] = jnp.sum(skip_sum, axis=0, keepdims=True)
    sums_ref[2:] = jnp.zeros((SEGMENTS - 2, lanes), F32)

    @pl.when(pl.program_id(1) == pl.num_programs(1) - 1)
    def across_lanes():
        lane = lax.broadcasted_iota(jnp.int32, (SEGMENTS, LANES), 1)

        def one(at, carry):
            total = jnp.zeros((SEGMENTS, LANES), F32)
            for n in range(states):
                for base, ref in ((0, in_grad_ref), (states, out_grad_ref)):
                    value = jnp.sum(ref[at, n], axis=1, keepdims=True)
                    total = jnp.where(lane == base + n, value, total)
            mix_ref[at] = total
            return carry

        lax.fori_loop(0, steps, one, 0, unroll=UNROLL_E)


class Scan:
    def __init__(self, steps, chains, states, width):
        lanes = LANES * math.gcd(width // LANES, BLOCKS)
        self.grid = (chains, width // lanes)
        self.rows_spec = pl.BlockSpec(
            (steps, None, SEGMENTS, lanes), lambda chain, block: (0, chain, 0, block)
        )
        self.mix_spec = pl.BlockSpec(
            (None, steps, states, SEGMENTS, LANES), lambda chain, block: (chain, 0, 0, 0, 0)
        )
        self.rate_spec = pl.BlockSpec((states, SEGMENTS, lanes), lambda chain, block: (0, 0, block))
        self.state_spec = pl.BlockSpec(
            (None, states, SEGMENTS, lanes), lambda chain, block: (chain, 0, 0, block)
        )
        self.edge_spec = pl.BlockSpec((None, states, lanes), lambda chain, block: (chain, 0, block))
        self.rows = jax.ShapeDtypeStruct((steps, chains, SEGMENTS, width), F32)
        self.mix = jax.ShapeDtypeStruct((chains, steps, states, SEGMENTS, LANES), F32)
        self.state = jax.ShapeDtypeStruct((chains, states, SEGMENTS, width), F32)
        self.edge = jax.ShapeDtypeStruct((chains, states, width), F32)
        self.sums = jax.ShapeDtypeStruct((chains, SEGMENTS, width), F32)
        self.sums_spec = pl.BlockSpec((None, SEGMENTS, lanes), lambda chain, block: (chain, 0, block))
        self.lane_sums = jax.ShapeDtypeStruct((steps, chains, SEGMENTS, LANES), F32)
        self.lane_spec = pl.BlockSpec(
            (steps, None, SEGMENTS, LANES), lambda chain, block: (0, chain, 0, 0)
        )
        self.skip_spec = pl.BlockSpec((1, lanes), lambda chain, block: (0, block))
        self.scratch = [
            pltpu.VMEM((steps, math.gcd(states, GROUP_C), SEGMENTS, lanes), F32),
            pltpu.VMEM((steps, math.gcd(states, GROUP_C), SEGMENTS, lanes), F32),
            pltpu.VMEM((steps, states, SEGMENTS, LANES), F32),
            pltpu.VMEM((steps, states, SEGMENTS, LANES), F32),
            pltpu.VMEM((steps, SEGMENTS, lanes), F32),
        ]
        self.narrow_rows = jax.ShapeDtypeStruct((steps, chains, SEGMENTS, width), BF16)
        self.work = steps * chains * SEGMENTS * width * states

    def call(self, kernel, ops, args, in_specs, outs, out_specs, scratch=()):
        size = sum(math.prod(a.shape) * a.dtype.itemsize for a in (*args, *outs))
        return pl.pallas_call(
            kernel,
            grid=self.grid,
            in_specs=in_specs,
            out_specs=out_specs,
            out_shape=outs,
            scratch_shapes=list(scratch),
            compiler_params=pltpu.CompilerParams(vmem_limit_bytes=VMEM_LIMIT),
            cost_estimate=pl.CostEstimate(
                flops=ops * self.work, transcendentals=self.work, bytes_accessed=size // COVER
            ),
        )(*args)

    def ends(self, step, inputs, mix_in, rate):
        return self.call(
            ends_kernel, 5, (step, inputs, mix_in, rate),
            [self.rows_spec, self.rows_spec, self.mix_spec, self.rate_spec],
            [self.state, self.state, self.edge],
            [self.state_spec, self.state_spec, self.edge_spec],
        )

    def run(self, step, inputs, mix_in, mix_out, rate, decay, state, enter):
        return self.call(
            states_kernel, 7, (step, inputs, mix_in, mix_out, rate, decay, state, enter),
            [self.rows_spec, self.rows_spec, self.mix_spec, self.mix_spec, self.rate_spec,
             self.state_spec, self.state_spec, self.edge_spec],
            [self.rows, self.state],
            [self.rows_spec, self.state_spec],
        )

    def adjoint_ends(self, step, mix_out, grad, rate):
        return self.call(
            adjoint_ends_kernel, 5, (step, mix_out, grad, rate),
            [self.rows_spec, self.mix_spec, self.rows_spec, self.rate_spec],
            [self.state, self.state, self.edge],
            [self.state_spec, self.state_spec, self.edge_spec],
        )

    def adjoint(self, args):
        return self.call(
            adjoint_kernel, 20, args,
            [self.rows_spec, self.rows_spec, self.mix_spec, self.mix_spec, self.rows_spec,
             self.rate_spec, self.state_spec, self.state_spec, self.state_spec, self.edge_spec,
             self.skip_spec],
            [self.narrow_rows, self.rows, self.edge, self.sums, self.lane_sums],
            [self.rows_spec, self.rows_spec, self.edge_spec, self.sums_spec, self.lane_spec],
            self.scratch,
        )


def conv_back_kernel(
    proj_ref, weight_ref, grad_ref, input_ref, taps_ref, shift_ref,
    out_ref, sums_ref, head_ref, tail_ref, product_ref, conv_ref,
):
    steps, rows, lanes = grad_ref.shape
    count = taps_ref.shape[0]
    reach = count - 1
    taps = [taps_ref[at : at + 1] for at in range(count)]
    shift = shift_ref[...]
    product_ref[...] = jnp.dot(
        proj_ref[...], weight_ref[...], preferred_element_type=F32
    ).reshape(steps, rows, lanes)

    def slopes(at, sums):
        inputs = [input_ref[at + tap].astype(F32) for tap in range(count)]
        pre = shift + sum(tap * value for tap, value in zip(taps, inputs))
        share = 1.0 / (1.0 + jnp.exp(-pre))
        conv = (grad_ref[at] + product_ref[at]) * (share * (1.0 + pre * (1.0 - share)))
        conv_ref[at] = conv
        return (*(total + conv * value for total, value in zip(sums, inputs)), sums[-1] + conv)

    zero = jnp.zeros((rows, lanes), F32)
    sums = lax.fori_loop(0, steps, slopes, (zero,) * (count + 1), unroll=2)
    for at, total in enumerate(sums):
        sums_ref[at : at + 1] = jnp.sum(total, axis=0, keepdims=True)
    sums_ref[count + 1 :] = jnp.zeros((sums_ref.shape[0] - count - 1, lanes), F32)
    row = sublane_rows(lanes)
    for at in range(reach):
        head_ref[at] = conv_ref[at]
        for low in range(0, rows, SEGMENTS):
            rolled = pltpu.roll(conv_ref[at, low : low + SEGMENTS], SEGMENTS - 1, 0)
            conv_ref[steps + at, low : low + SEGMENTS] = jnp.where(
                row < SEGMENTS - 1, rolled, 0.0
            )

    def back(at):
        return sum(taps[tap] * conv_ref[at + reach - tap] for tap in range(count))

    def store(at, carry):
        out_ref[at] = back(at).astype(BF16)
        return carry

    lax.fori_loop(0, steps, store, 0, unroll=2)
    for at in range(reach):
        tail_ref[at] = back(steps - reach + at)


def conv_back(proj, weight, grad, inputs, taps, shift):
    steps, rows, width = grad.shape
    reach = taps.shape[0] - 1
    lanes = LANES * math.gcd(width // LANES, BLOCKS)

    def block(count, dtype=F32):
        spec = pl.BlockSpec((count, rows, lanes), lambda at: (0, 0, at))
        return spec, jax.ShapeDtypeStruct((count, rows, width), dtype)

    def columns(count):
        return pl.BlockSpec((count, lanes), lambda at: (0, at))

    outs = [
        block(steps, BF16),
        (columns(SEGMENTS), jax.ShapeDtypeStruct((SEGMENTS, width), F32)),
        block(reach),
        block(reach),
    ]
    return pl.pallas_call(
        conv_back_kernel,
        grid=(width // lanes,),
        in_specs=[
            pl.BlockSpec(proj.shape, lambda at: (0, 0)),
            columns(weight.shape[0]),
            block(steps)[0],
            block(steps + reach)[0],
            columns(reach + 1),
            columns(1),
        ],
        out_specs=[spec for spec, _ in outs],
        out_shape=[shape for _, shape in outs],
        scratch_shapes=[
            pltpu.VMEM((steps, rows, lanes), F32),
            pltpu.VMEM((steps + reach, rows, lanes), F32),
        ],
        compiler_params=pltpu.CompilerParams(vmem_limit_bytes=VMEM_LIMIT),
        cost_estimate=pl.CostEstimate(flops=1, transcendentals=0, bytes_accessed=1),
    )(proj, weight, grad, inputs, taps, shift)


def expert_kernel(
    kept, rows_ref, cotan_ref, router_ref, mask_ref, up_a, down_a, up_b, down_b, *refs
):
    out_ref, picked_ref, prob_ref, copy_ref, grad_ref, active_a, active_b, hidden_a, hidden_b = refs[kept:]
    rows = rows_ref[...]
    copy_ref[...] = rows
    logits = contract_cols(rows, router_ref[...])
    shifted = jnp.exp(logits - jnp.max(logits, axis=1, keepdims=True))
    prob = shifted / jnp.sum(shifted, axis=1, keepdims=True)
    gate = jnp.sum(prob * mask_ref[...], axis=1, keepdims=True)
    grad = (gate * cotan_ref[...].astype(F32)).astype(BF16)
    prob_ref[...] = prob
    grad_ref[...] = grad
    out, picked = None, None
    for up, down, active_ref, hidden_ref in (
        (up_a, down_a, active_a, hidden_a),
        (up_b, down_b, active_b, hidden_b),
    ):
        up, down = (value[...].reshape(-1, value.shape[2]) for value in (up, down))
        hidden = jnp.dot(rows, up, preferred_element_type=F32)
        share = 0.5 + 0.5 * lax.erf(hidden * math.sqrt(0.5))
        slope = share + hidden * (jnp.exp(-0.5 * hidden * hidden) * (1.0 / math.sqrt(2 * math.pi)))
        active = (hidden * share).astype(BF16)
        active_ref[...] = active
        hidden_grad = (jnp.dot(grad, down, preferred_element_type=F32) * slope).astype(BF16)
        hidden_ref[...] = hidden_grad
        out_part = contract_cols(active, down)
        picked_part = contract_cols(hidden_grad, up)
        out = out_part if out is None else out + out_part
        picked = picked_part if picked is None else picked + picked_part
    out_ref[...] = out
    picked_ref[...] = picked


def expert_call(rows, cotan, router_t, mask, blocks, far_up, far_down, part, parts, kept):
    count, width = rows.shape
    shard, hidden = far_up.shape[1:]
    block = math.gcd(count, 512)
    base = part * (count // block)

    def rows_of(columns, low=0):
        return pl.BlockSpec((block, columns), lambda at: (at + low, 0))

    def whole(array):
        return pl.BlockSpec(array.shape, lambda at: (0, 0), pipeline_mode=pl.Buffered(1))

    def layer(array, at):
        return pl.BlockSpec(
            (array.shape[0], shard, hidden), lambda step: (0, at, 0), pipeline_mode=pl.Buffered(1)
        )

    experts = router_t.shape[0]
    inputs = (rows, cotan, router_t, mask, blocks, blocks, far_up, far_down)
    columns = (width, width, hidden, hidden, hidden, hidden)
    return pl.pallas_call(
        partial(expert_kernel, len(kept)),
        grid=(count // block,),
        in_specs=[
            rows_of(width), rows_of(width), whole(router_t), whole(mask),
            layer(blocks, 0), layer(blocks, 1), layer(far_up, 0), layer(far_down, 0),
            *[pl.BlockSpec(memory_space=pl.ANY)] * len(kept),
        ],
        out_specs=[
            rows_of(width), rows_of(width), rows_of(experts), *(rows_of(one, base) for one in columns)
        ],
        out_shape=[
            *(jax.ShapeDtypeStruct((count, one), F32) for one in (width, width, experts)),
            *(jax.ShapeDtypeStruct((parts * count, one), BF16) for one in columns),
        ],
        input_output_aliases={len(inputs) + at: 3 + at for at in range(len(kept))},
        compiler_params=pltpu.CompilerParams(vmem_limit_bytes=EXPERT_VMEM),
        cost_estimate=pl.CostEstimate(
            flops=16 * count * width * hidden,
            transcendentals=4 * count * hidden,
            bytes_accessed=count * (14 * width + 8 * hidden) + 8 * width * hidden,
        ),
    )(*inputs, *kept)


def expert_exchange(value, experts):
    count = lax.axis_size("dp")
    groups = None
    if count != experts:
        groups = [
            [base + e for e in range(experts)] for base in range(0, count, experts)
        ]
    return lax.all_to_all(value, "dp", 0, 0, axis_index_groups=groups, tiled=True)


def by_ctx(first, second):
    lead = lax.axis_index("ctx") == 0
    return jnp.where(lead, first, second), jnp.where(lead, second, first)


def own_expert_blocks(up_shards, down_shards):
    experts, _, hidden = up_shards.shape
    count = lax.axis_size("dp")
    half = hidden // 2
    both = jnp.concatenate([up_shards, down_shards], axis=1)
    if lax.axis_size("ctx") == 2:
        both = by_ctx(both[:, :, :half], both[:, :, half:])[0]
    if count != experts:
        both = jnp.concatenate([both] * (count // experts), axis=0)
    return lax.all_to_all(both, "dp", 0, 0, tiled=True)


def other_hidden(both, layer):
    rows = both.shape[1] // 2
    both = both[:, layer * rows : (layer + 1) * rows]
    if lax.axis_size("ctx") == 2:
        return swapped(both, "ctx")
    return both[:, :, both.shape[2] // 2 :]


def gather_kernel(count, number, parts, *refs):
    ins, outs = refs[:number], refs[number : 2 * number]
    send_sem, recv_sem, own_sem = refs[2 * number :]
    places = count // 2
    me = lax.axis_index("dp")
    place, side = lax.div(me, 2), lax.rem(me, 2)
    across = me + 1 - 2 * side
    barrier = pltpu.get_barrier_semaphore()
    late = [part for part, (_, _, _, early) in enumerate(parts) if not early]
    early = [part for part, (_, _, _, early) in enumerate(parts) if early]

    def greet(device):
        pl.semaphore_signal(
            barrier, inc=1, device_id={"dp": device}, device_id_type=pl.DeviceIdType.MESH
        )

    greet(across)
    for step in (-1, 1):
        there = place + step

        @pl.when((there >= 0) & (there < places))
        def greet_place(step=step):
            greet(me + 2 * step)

    neighbours = 1 + (place > 0).astype(jnp.int32) + (place < places - 1).astype(jnp.int32)
    pl.semaphore_wait(barrier, neighbours)

    def copy(part, slot, kind, device, own):
        array, low, rows, _ = parts[part]
        landing = outs[array].at[slot, pl.ds(low, rows)]
        return pltpu.make_async_remote_copy(
            src_ref=ins[array].at[pl.ds(low, rows)] if own else landing,
            dst_ref=landing,
            send_sem=send_sem.at[kind, part, slot],
            recv_sem=recv_sem.at[part, slot],
            device_id={"dp": device},
            device_id_type=pl.DeviceIdType.MESH,
        )

    def along(which, slot, steps, own, act):
        for step in steps:
            there = place + step

            @pl.when((there >= 0) & (there < places))
            def one_way(step=step):
                for part in which:
                    act(copy(part, slot, step + 1, me + 2 * step, own))

    def aside(which, slot, own, act):
        for part in which:
            act(copy(part, slot, 1, across, own))

    def arrived(which, slot):
        for part in which:
            copy(part, slot, 1, across, False).wait_recv()

    def start(one):
        one.start()

    def sent(one):
        one.wait_send()

    mine = [
        pltpu.make_async_copy(ins[array], outs[array].at[me], own_sem.at[array])
        for array in range(number)
    ]
    for one in mine:
        one.start()
    both = (-1, 1)
    aside(early, me, True, start)
    for part in late:
        along((part,), me, both, True, start)
        aside((part,), me, True, start)
    along(early, me, both, True, start)
    arrived(early, across)
    along(early, across, both, False, start)
    for far in range(1, places):
        for step in both:
            origin = place - step * far

            @pl.when((origin >= 0) & (origin < places))
            def forward(step=step, far=far):
                slot, other = me - 2 * step * far, across - 2 * step * far
                for part in late:
                    arrived((part,), slot)
                    along((part,), slot, (step,), False, start)
                    aside((part,), slot, False, start)
                arrived(early, slot)
                along(early, slot, (step,), False, start)
                arrived(early, other)
                along(early, other, (step,), False, start)

    for at in range(places):
        arrived(late, 2 * at + 1 - side)
    for one in mine:
        one.wait()
    aside(early + late, me, True, sent)
    along(early + late, me, both, True, sent)
    along(early, across, both, False, sent)
    for far in range(1, places):
        for step in both:
            origin = place - step * far

            @pl.when((origin >= 0) & (origin < places))
            def forwarded(step=step, far=far):
                slot, other = me - 2 * step * far, across - 2 * step * far
                aside(late, slot, False, sent)
                along(early + late, slot, (step,), False, sent)
                along(early, other, (step,), False, sent)


def gathered(*values):
    count = lax.axis_size("dp")
    number = len(values)
    parts = []
    for at, value in enumerate(values):
        rows = value.shape[0]
        step = rows // 3 if value.shape[1] > 1024 and rows % 24 == 0 else rows
        parts += [
            (at, low, step, at == number - 1 and 0 < low == rows - step)
            for low in range(0, rows, step)
        ]
    anywhere = pl.BlockSpec(memory_space=pl.ANY)
    size = sum(math.prod(value.shape) * 2 for value in values)
    return pl.pallas_call(
        partial(gather_kernel, count, number, parts),
        in_specs=[anywhere] * number,
        out_specs=[anywhere] * number,
        out_shape=[jax.ShapeDtypeStruct((count, *value.shape), value.dtype) for value in values],
        scratch_shapes=[
            pltpu.SemaphoreType.DMA((3, len(parts), count)),
            pltpu.SemaphoreType.DMA((len(parts), count)),
            pltpu.SemaphoreType.DMA((number,)),
        ],
        compiler_params=pltpu.CompilerParams(collective_id=0, has_side_effects=True),
        cost_estimate=pl.CostEstimate(
            flops=0, transcendentals=0, bytes_accessed=2 * count * size
        ),
    )(*values)


def other_joined(own, first_shard, second_shard):
    count = lax.axis_size("ctx")
    if count == 2:
        return by_ctx(own, swapped(own, "ctx"))
    del first_shard, second_shard
    every = lax.all_gather(own, "ctx")
    return every[0], every[1]


def expert_weight_products(rows, hidden_grads, grads, actives):
    pairs = ((rows, hidden_grads), (grads, actives))
    far = [contract_rows(left, rights[1]) for left, rights in pairs]
    if lax.axis_size("ctx") == 2:
        far = [value.astype(BF16) for value in far]
    return [contract_rows(left, rights[0]) for left, rights in pairs], far


def sent_far(value):
    return swapped(value, "ctx") if lax.axis_size("ctx") == 2 else value


def expert_weight_parts(near, far):
    count = lax.axis_size("dp")
    parts = []
    for own, other in zip(near, far):
        if lax.axis_size("ctx") == 2:
            part = own + other.astype(F32)
        else:
            part = lax.psum_scatter(
                jnp.concatenate([own, other], axis=1), "ctx", scatter_dimension=1, tiled=True
            )
        parts.append(part.astype(BF16).reshape(count, part.shape[0] // count, part.shape[1]))
    return jnp.concatenate(parts, axis=1)


def expert_weight_blocks(blocks, experts):
    count = lax.axis_size("dp")
    if count != experts:
        blocks = jnp.sum(
            blocks.reshape(count // experts, experts, *blocks.shape[1:]).astype(F32), axis=0
        ).astype(BF16)
    return blocks


def far_hidden(blocks):
    if lax.axis_size("ctx") == 2:
        return swapped(blocks, "ctx")
    return lax.all_gather(blocks, "ctx", axis=2, tiled=True)


def expert_weight_grad(blocks, far_blocks):
    if lax.axis_size("ctx") == 2:
        far_blocks = jnp.concatenate(by_ctx(blocks, far_blocks), axis=2)
    return far_blocks.astype(F32)


def pair_products(first, second):
    if lax.axis_size("ctx") != 2:
        return contract_rows(*first), contract_rows(*second).astype(BF16)
    lefts, rights = by_ctx(first[0], second[0]), by_ctx(first[1], second[1])
    return contract_rows(lefts[0], rights[0]), contract_rows(lefts[1], rights[1]).astype(BF16)


def product_part(near, far):
    count = lax.axis_size("dp")

    def blocks(value):
        return value.astype(BF16).reshape(count, value.shape[0] // count, value.shape[1])

    if lax.axis_size("ctx") != 2:
        return jnp.concatenate([blocks(near), blocks(far)], axis=1)
    return blocks(near + far.astype(F32))


def product_shards(blocks):
    sums = jnp.sum(blocks.astype(F32), axis=0)
    if lax.axis_size("ctx") == 2:
        return by_ctx(sums, swapped(sums, "ctx"))
    sums = lax.psum(sums, "ctx")
    rows = sums.shape[0] // 2
    return sums[:rows], sums[rows:]


def local(
    hidden_in,
    out_grad,
    norm1_gain,
    in_weight,
    conv_weight,
    conv_bias,
    xproj_weight,
    dt_weight,
    dt_bias,
    decay_log,
    skip_weight,
    out_weight,
    norm2_gain,
    router_weight,
    fc1_weight,
    fc2_weight,
    expert_ids,
    keep_mask,
):
    batches, seqs, length, model_width = hidden_in.shape
    chains = batches * seqs
    tokens = chains * length
    steps = length // SEGMENTS
    shard, _, inner = in_weight.shape
    taps = conv_weight.shape[0]
    low_rank = dt_weight.shape[0]
    states = decay_log.shape[0]
    experts = fc1_weight.shape[0]
    dp_count = lax.axis_size("dp")
    tp_count = lax.axis_size("tp")
    capacity = tokens // 4
    part_cap = capacity // tp_count // HALVES
    slots = experts * part_cap
    tp_index = lax.axis_index("tp")
    scan = Scan(steps, chains, states, inner)

    def to_rows(value):
        value = value.reshape(chains, SEGMENTS, steps, -1).transpose(2, 0, 1, 3)
        return value.reshape(tokens, -1)

    def from_rows(value):
        value = value.reshape(steps, chains, SEGMENTS, -1).transpose(1, 2, 0, 3)
        return value.reshape(batches, seqs, length, -1)

    pieces = [
        norm1_gain[None],
        conv_weight,
        conv_bias[None],
        dt_weight,
        dt_bias[None],
        decay_log,
        skip_weight[None],
        norm2_gain[None],
        router_weight.T,
        xproj_weight.T,
    ]
    bounds = [0]
    for piece in pieces:
        bounds.append(bounds[-1] + piece.shape[0])
    small = sum(
        jnp.pad(piece, ((low, bounds[-1] - high), (0, 0)))
        for piece, low, high in zip(pieces, bounds, bounds[1:])
    )
    kinds = small.shape[0]
    small_wide = jnp.pad(small.T, ((0, 0), (0, -kinds % LANES)))
    in_x, small_all, later = gathered(
        in_weight[:, 0], small_wide, by_ctx(out_weight.T, in_weight[:, 1])[0]
    )
    in_x = in_x.reshape(dp_count * shard, inner)
    later = later.reshape(dp_count * shard, inner)
    small_all = small_all.reshape(dp_count * shard, -1)[:, :kinds].T
    small_all, up_shards, down_shards = together(
        small_all, fc1_weight, fc2_weight.transpose(0, 2, 1)
    )
    pieces = [small_all[bounds[i] : bounds[i + 1]] for i in range(len(bounds) - 1)]
    gain_one_f = pieces[0].astype(F32)
    tap_weights = pieces[1].astype(F32)
    conv_shift = pieces[2].astype(F32)
    dt_proj = pieces[3]
    dt_shift = pieces[4].astype(F32)
    decay_rate = -jnp.exp(pieces[5].astype(F32))
    skip_row = pieces[6].astype(F32)
    gain_two_f = pieces[7].astype(F32)
    router_t = pieces[8]
    x_proj_t = pieces[9]
    rate_rows = jnp.broadcast_to((decay_rate * LOG2E)[:, None, :], (states, SEGMENTS, inner))
    expert_blocks = own_expert_blocks(up_shards, down_shards)

    values = lax.optimization_barrier(to_rows(hidden_in)).astype(F32)
    normalized_rows, inverse_one = rms_forward(values, gain_one_f)
    normed_bf = normalized_rows.astype(BF16)
    x_pre = jnp.dot(normed_bf, in_x, preferred_element_type=F32).astype(BF16)
    x_pre = x_pre.reshape(steps, chains, SEGMENTS, inner)
    tail = x_pre[steps - taps + 1 :]
    edge_in = passed_along(tail[:, :, SEGMENTS - 1 :], "ctx", 1)
    edge_in, later = together(edge_in, later)
    out_proj_t, in_z = other_joined(later, out_weight.T, in_weight[:, 1])
    halo = jnp.concatenate([edge_in, tail[:, :, : SEGMENTS - 1]], axis=2)
    extended_bf = jnp.concatenate([halo, x_pre], axis=0)
    extended = extended_bf.astype(F32)
    conv_pre = jnp.broadcast_to(conv_shift[0], x_pre.shape)
    for tap in range(taps):
        conv_pre = conv_pre + tap_weights[tap] * extended[tap : tap + steps]
    xconv_bf = jax.nn.silu(conv_pre).astype(BF16)
    xconv = xconv_bf.astype(F32)
    xconv_rows = xconv_bf.reshape(tokens, inner)
    projected = axis_sum(contract_cols(xconv_rows, x_proj_t), "tp")
    dt_low = projected[:, :low_rank].astype(BF16)

    def mixes(value):
        value = value.reshape(steps, chains, SEGMENTS, states).transpose(1, 0, 3, 2)
        return jnp.broadcast_to(value[..., None], (*value.shape, LANES))

    mix_in = mixes(projected[:, low_rank : low_rank + states])
    mix_out = mixes(projected[:, low_rank + states :])
    dt_pre = (jnp.dot(dt_low, dt_proj, preferred_element_type=F32) + dt_shift).reshape(x_pre.shape)
    step_size = jax.nn.softplus(dt_pre)
    seg_decay, seg_state, last_state = scan.ends(step_size, xconv, mix_in, rate_rows)
    later_ids, later_mask, later_grad, mix_out, _ = together(
        expert_ids, keep_mask, out_grad, mix_out, seg_state
    )
    route = to_rows(later_ids)[:, 0]
    keep = to_rows(later_mask)[:, 0].astype(F32)
    onehot_int = (route[:, None] == jnp.arange(experts, dtype=jnp.int32)[None, :]).astype(jnp.int32)
    rank = jnp.sum((jnp.cumsum(onehot_int, axis=0) - 1) * onehot_int, axis=1)
    places = []
    for half in range(HALVES):
        own = rank - (tp_index * HALVES + half) * part_cap
        token_slot = jnp.where((own >= 0) & (own < part_cap), route * part_cap + own, -1)
        places.append(
            (token_slot[None, :] == jnp.arange(slots, dtype=jnp.int32)[:, None]).astype(BF16)
        )

    def slotted(value, half):
        sent = jnp.dot(places[half], value, preferred_element_type=F32).astype(BF16)
        return sent.reshape(experts, part_cap, -1)

    def landed(values):
        total = sum(
            contract_rows(place, value.reshape(slots, -1)) for place, value in zip(places, values)
        )
        return axis_sum(total.astype(BF16), "tp").astype(F32)

    def halves_of(value):
        return [value[:, at : at + part_cap] for at in range(0, value.shape[1], part_cap)]

    cotan_bf = to_rows(later_grad)
    cotan = cotan_bf.astype(F32)
    kept_cotan = (cotan * keep[:, None]).astype(BF16)
    sent_cotan = jnp.concatenate([slotted(kept_cotan, half) for half in range(HALVES)], axis=1)
    entering = entering_pieces(seg_decay[:, :, SEGMENTS - 1], last_state, "ctx", False)
    entering, mix_out, expert_blocks, sent_cotan = together(
        entering, mix_out, expert_blocks, sent_cotan
    )
    slot_cotan = expert_exchange(sent_cotan, experts)
    far_up = other_hidden(expert_blocks, 0)
    scan_out, seg_start = scan.run(
        step_size, xconv, mix_in, mix_out, rate_rows, seg_decay, seg_state, entering
    )
    z_gate = jnp.dot(normed_bf, in_z, preferred_element_type=F32).reshape(x_pre.shape)
    scanned = scan_out + skip_row[0] * xconv
    z_silu = jax.nn.silu(z_gate)
    gated_bf = (scanned * z_silu).astype(BF16).reshape(tokens, inner)
    gated_bf, far_up = together(gated_bf, far_up)
    mixer_part, slot_cotan = together(contract_cols(gated_bf, out_proj_t), slot_cotan)
    middle = values + axis_sum(mixer_part, "tp")

    normed_two, inverse_two = rms_forward(middle, gain_two_f)
    normed_two_bf = normed_two.astype(BF16)
    expert_mask = (
        jnp.arange(experts, dtype=jnp.int32) == lax.rem(lax.axis_index("dp"), experts)
    ).astype(F32)[None, :]
    kept = ()
    got_grads, slot_outs, router_grad_t = [], [], 0.0
    for half, half_cotan in enumerate(halves_of(slot_cotan)):
        sent_rows = slotted(normed_two_bf, half)
        if not half:
            sent_rows, expert_blocks = together(sent_rows, expert_blocks)
            far_down = other_hidden(expert_blocks, 1)
        own_rows = expert_exchange(sent_rows, experts)
        if not half:
            own_rows, far_down = together(own_rows, far_down)
        else:
            own_rows, kept = together(own_rows, kept)
        own_rows = own_rows.reshape(slots, model_width)
        half_cotan = half_cotan.reshape(slots, model_width)
        far_rows, far_cotan = swapped(own_rows, "tp"), swapped(half_cotan, "tp")
        call = partial(
            expert_call, router_t=router_t, mask=expert_mask, blocks=expert_blocks, far_up=far_up,
            far_down=far_down, parts=2 * HALVES,
        )
        far = call(far_rows, far_cotan, part=2 * half, kept=kept)
        near = call(own_rows, half_cotan, part=2 * half + 1, kept=far[3:])
        if half:
            near, got_grads = together(near, got_grads)
        kept = near[3:]
        slot_out = near[0] + swapped(far[0], "tp")
        picked_grad = near[1] + swapped(far[1], "tp")
        slot_prob = near[2]
        slot_gate = jnp.sum(slot_prob * expert_mask, axis=1, keepdims=True)
        gate_grad = jnp.sum(slot_out * half_cotan.astype(F32), axis=1, keepdims=True)
        logit_grad = gate_grad * slot_gate * (expert_mask - slot_prob)
        router_grad_t = router_grad_t + contract_rows(logit_grad, own_rows.astype(F32), HIGHEST)
        picked_grad = picked_grad + jnp.dot(
            logit_grad, router_t.astype(F32), precision=HIGHEST, preferred_element_type=F32
        )
        got_grads.append(
            expert_exchange(picked_grad.astype(BF16).reshape(experts, part_cap, -1), experts)
        )
        slot_outs.append(slot_out.astype(BF16).reshape(experts, part_cap, -1))
    router_grad_t = axis_sum(router_grad_t, "tp")
    all_rows, all_grads, active_a, active_b, hidden_a, hidden_b = kept
    near_parts, far_parts = expert_weight_products(
        all_rows, (hidden_a, hidden_b), all_grads, (active_a, active_b)
    )
    far_first = sent_far(far_parts[0])
    (
        got_grads, near_parts, far_second, far_first, slot_outs, router_grad_t, extended_bf, xconv_t
    ) = together(
        got_grads, near_parts, far_parts[1], far_first, slot_outs, router_grad_t, extended_bf,
        xconv_rows.T,
    )
    far_parts = far_first, sent_far(far_second)
    normed_two_grad = landed(got_grads)
    got_out = expert_exchange(jnp.concatenate(slot_outs, axis=1), experts)
    middle_norm_grad, gain_two_grad = rms_backward(middle, inverse_two, gain_two_f, normed_two_grad)
    middle_grad = cotan + middle_norm_grad
    mixer_grad_bf = middle_grad.astype(BF16)
    gated_grad = jnp.dot(mixer_grad_bf, out_proj_t, preferred_element_type=F32).reshape(x_pre.shape)
    scan_grad = gated_grad * z_silu
    z_grad = jax.vjp(jax.nn.silu, z_gate)[1](gated_grad * scanned)[0]
    z_grad_bf = z_grad.astype(BF16).reshape(tokens, inner)
    near_product, far_product = pair_products((mixer_grad_bf, gated_bf), (normed_bf, z_grad_bf))
    back_decay, back_adjoint, first_adjoint = scan.adjoint_ends(
        step_size, mix_out, scan_grad, rate_rows
    )
    normed_part = contract_cols(z_grad_bf, in_z)
    far_parts, got_out, near_product, far_product, _ = together(
        far_parts, got_out, near_product, far_product, first_adjoint
    )
    weight_blocks = lax.all_to_all(
        expert_weight_parts(near_parts, far_parts), "dp", 0, 0, tiled=True
    )
    leaving = entering_pieces(back_decay[:, :, 0], first_adjoint, "ctx", True)
    leaving, near_product, far_product, normed_part = together(
        leaving, near_product, far_product, normed_part
    )
    far_product = sent_far(far_product)
    adjoint_args = (
        step_size, xconv, mix_in, mix_out, scan_grad, rate_rows, seg_start, back_decay, back_adjoint,
        leaving, skip_row,
    )
    pre_grad, xconv_grad, decay_sum, scan_sums, mix_grad = scan.adjoint(adjoint_args)
    pre_grad, far_product, weight_blocks = together(pre_grad, far_product, weight_blocks)
    weight_blocks = expert_weight_blocks(weight_blocks, experts)
    far_ups = far_hidden(weight_blocks[:, :shard])
    out_blocks = lax.all_to_all(product_part(near_product, far_product), "dp", 0, 0, tiled=True)
    decay_log_grad = jnp.sum(decay_sum, axis=0) * decay_rate
    dt_shift_grad, skip_grad = jnp.sum(scan_sums, axis=0)[:2]
    pre_grad = pre_grad.reshape(tokens, inner)
    dt_proj_grad = contract_rows(dt_low, pre_grad)
    dt_low_grad = contract_cols(pre_grad, dt_proj)
    mix_grad = mix_grad.reshape(tokens, LANES)[:, : 2 * states]
    proj_part = jnp.concatenate([dt_low_grad, mix_grad], axis=1)
    proj_grad_bf = axis_sum(proj_part, "tp").astype(BF16)
    x_proj_grad_t = lax.dot_general(
        proj_grad_bf, xconv_t, (((0,), (1,)), ((), ())), preferred_element_type=F32
    )
    flat = (chains * SEGMENTS, inner)
    x_grad_bf, conv_sums, head, last = conv_back(
        proj_grad_bf,
        x_proj_t,
        xconv_grad.reshape(steps, *flat),
        extended_bf.reshape(steps + taps - 1, *flat),
        tap_weights,
        conv_shift,
    )
    taps_grad, shift_grad = conv_sums[:taps], conv_sums[taps]
    edge_back = passed_along(
        head.reshape(taps - 1, chains, SEGMENTS, inner)[:, :, :1], "ctx", -1
    )
    edge_back, out_blocks, far_ups, weight_blocks = together(
        edge_back, out_blocks, far_ups, weight_blocks
    )
    reaching = jnp.stack(
        [
            sum(tap_weights[tap] * edge_back[at - tap] for tap in range(at + 1))
            for at in range(taps - 1)
        ]
    )
    reaching = jnp.pad(reaching, ((0, 0), (0, 0), (SEGMENTS - 1, 0), (0, 0)))
    last = (last + reaching.reshape(taps - 1, *flat)).astype(BF16)
    x_grad_bf = lax.dynamic_update_slice(x_grad_bf, last, (steps - taps + 1, 0, 0))
    x_grad_bf = x_grad_bf.reshape(tokens, inner)
    small_grads = jnp.concatenate(
        [
            taps_grad,
            shift_grad[None],
            dt_proj_grad,
            dt_shift_grad[None],
            decay_log_grad,
            skip_grad[None],
            gain_two_grad[None],
            router_grad_t,
            x_proj_grad_t,
        ],
        axis=0,
    )
    small_grads = small_grads.reshape(-1, dp_count, shard).transpose(1, 0, 2)
    small_size = small_grads.shape[1] * shard
    small_rows = small_grads.astype(BF16).reshape(dp_count, small_size)
    small_rows = jnp.pad(small_rows, ((0, 0), (0, -small_size % inner))).reshape(dp_count, -1, inner)
    x_grad_bf, small_rows, out_blocks = together(x_grad_bf, small_rows, out_blocks)
    normed_part = normed_part + contract_cols(x_grad_bf, in_x)
    normed_grad = axis_sum(normed_part, "tp")
    values_norm_grad, gain_one_grad = rms_backward(values, inverse_one, gain_one_f, normed_grad)
    input_grad = from_rows((middle_grad + values_norm_grad).astype(BF16))

    in_x_part = contract_rows(normed_bf, x_grad_bf).astype(BF16).reshape(dp_count, shard, inner)
    gain_row = gain_one_grad.reshape(dp_count, 1, shard)
    gain_high = gain_row.astype(BF16)
    gain_low = (gain_row - gain_high.astype(F32)).astype(BF16)
    gain_row = jnp.concatenate([gain_high, gain_low], axis=2)
    gain_row = jnp.pad(gain_row, ((0, 0), (0, 0), (0, inner - 2 * shard)))
    in_x_part, out_blocks = together(in_x_part, out_blocks)
    out_proj_grad, in_z_grad = product_shards(out_blocks)
    in_x_blocks = lax.all_to_all(
        jnp.concatenate([in_x_part, small_rows, gain_row], axis=1), "dp", 0, 0, tiled=True
    )
    out_proj_grad, in_z_grad, far_down_blocks = together(
        out_proj_grad, in_z_grad, weight_blocks[:, shard:]
    )
    far_downs, in_x_blocks = together(far_hidden(far_down_blocks), in_x_blocks)
    first_grad = expert_weight_grad(weight_blocks[:, :shard], far_ups)
    second_grad = expert_weight_grad(far_down_blocks, far_downs)
    router_prob = jax.nn.softmax(contract_cols(normed_two_bf, router_t), axis=-1)
    gate_prob = jnp.sum(router_prob * onehot_int.astype(F32), axis=1) * keep
    result = from_rows((middle + gate_prob[:, None] * landed(halves_of(got_out))).astype(BF16))
    in_x_sums = jnp.sum(in_x_blocks.astype(F32), axis=0).astype(BF16)
    in_x_sums = narrow_sum(in_x_sums, "ctx")
    in_x_grad = in_x_sums[:shard]
    gain_one_grad = in_x_sums[-1:, :shard] + in_x_sums[-1:, shard : 2 * shard]
    small_grads = in_x_sums[shard:-1].reshape(-1)[:small_size].reshape(-1, shard)
    small_grads = jnp.concatenate([gain_one_grad, small_grads], axis=0)
    sums = [small_grads[bounds[i] : bounds[i + 1]] for i in range(len(bounds) - 1)]
    return (
        result,
        input_grad,
        sums[0][0],
        jnp.stack([in_x_grad, in_z_grad], axis=1),
        sums[1],
        sums[2][0],
        sums[9].T,
        sums[3],
        sums[4][0],
        sums[5],
        sums[6][0],
        out_proj_grad.T,
        sums[7][0],
        sums[8].T,
        first_grad,
        second_grad.transpose(0, 2, 1),
    )


def solution(mesh):
    weights = (
        P("dp"),
        P("dp", None, "tp"),
        P(None, ("tp", "dp")),
        P(("tp", "dp")),
        P(("tp", "dp"), None),
        P(None, ("tp", "dp")),
        P(("tp", "dp")),
        P(None, ("tp", "dp")),
        P(("tp", "dp")),
        P("tp", "dp"),
        P("dp"),
        P("dp", None),
        P(None, "dp", "tp"),
        P(None, "tp", "dp"),
    )
    rows = P(None, "dp", "ctx", None)
    return jax.shard_map(
        local,
        mesh=mesh,
        in_specs=(rows, rows, *weights, P(("dp", "ctx"), None), P(("dp", "ctx"))),
        out_specs=(rows, rows, *weights),
        check_vma=False,
    )
```

```python
from functools import partial
import math

import jax
import jax.numpy as jnp
from jax import lax
from jax.experimental import pallas as pl
from jax.experimental.pallas import tpu as pltpu
from jax.sharding import PartitionSpec as P

EPSILON = 1e-05
HIGHEST = lax.Precision.HIGHEST
SEGMENTS = 8
LANES = 128
VMEM_LIMIT = 56 * 1024 * 1024
EXPERT_VMEM = 56 * 1024 * 1024
LOG2E = math.log2(math.e)
GROUP_A = 4
GROUP_B = 4
GROUP_C = 8
UNROLL_A = 16
UNROLL_B = 16
UNROLL_C = 8
UNROLL_D = 4
UNROLL_E = 8
BLOCKS = 3
COVER = 100
HALVES = 1
BF16 = jnp.bfloat16
F32 = jnp.float32


def swapped(value, axis):
    return lax.ppermute(value, axis, [(0, 1), (1, 0)])


def passed_along(value, axis, steps):
    count = lax.axis_size(axis)
    leading, last = (max(0, -steps), min(count, count - steps))
    return lax.ppermute(value, axis, [(source, source + steps) for source in range(leading, last)])


def axis_sum(value, axis):
    if lax.axis_size(axis) == 2:
        return value + swapped(value, axis)
    return lax.psum(value, axis)


def together(*values):
    return lax.optimization_barrier(values)


def narrow_sum(value, axis):
    if lax.axis_size(axis) == 2:
        return value.astype(F32) + swapped(value, axis).astype(F32)
    return lax.psum(value.astype(F32), axis)


def entering_pieces(decay, value, axis, backward):
    count = lax.axis_size(axis)
    if count == 2:
        return passed_along(value, axis, -1 if backward else 1)
    mine = lax.axis_index(axis)
    decays = lax.all_gather(decay, axis)
    values = lax.all_gather(value, axis)
    running = jnp.zeros_like(value)
    for position in range(count - 1):
        at = count - 1 - position if backward else position
        longer = values[at] + decays[at] * running
        ahead = at > mine if backward else at < mine
        running = jnp.where(ahead, longer, running)
    return running


def contract_rows(left_side, right_side, precision=None):
    return lax.dot_general(
        left_side,
        right_side,
        (((0,), (0,)), ((), ())),
        precision=precision,
        preferred_element_type=F32,
    )


def contract_cols(left_side, right_side, precision=None):
    return lax.dot_general(
        left_side,
        right_side,
        (((1,), (1,)), ((), ())),
        precision=precision,
        preferred_element_type=F32,
    )


def rms_forward(values, gain_vec):
    inverse = lax.rsqrt(jnp.mean(values * values, axis=-1, keepdims=True) + EPSILON)
    return (values * inverse * gain_vec, inverse)


def rms_backward(values, inverse, gain_vec, grad_out):
    weighted = grad_out * gain_vec
    inner_mean = jnp.mean(values * weighted, axis=-1, keepdims=True)
    grad_values = inverse * weighted - values * inverse * inverse * inverse * inner_mean
    grad_gain = jnp.sum(grad_out * values * inverse, axis=0)
    return (grad_values, grad_gain)


def zeros_of(ref):
    return jnp.zeros(ref.shape[1:], F32)


def sublane_rows(lanes):
    return lax.broadcasted_iota(jnp.int32, (SEGMENTS, lanes), 0)


def widened(value, lanes):
    return jnp.concatenate([value] * (lanes // LANES), axis=1) if lanes > LANES else value


def narrowed(value):
    parts = [value[:, at : at + LANES] for at in range(0, value.shape[1], LANES)]
    return sum(parts[1:], parts[0])


def groups_of(states, size):
    size = math.gcd(states, size)
    return [range(first, first + size) for first in range(0, states, size)]


def joined_forward(decay, value, row):
    for reach in (1, 2, 4):
        inside = row >= reach
        value = value + jnp.where(inside, decay * pltpu.roll(value, reach, 0), 0.0)
        decay = jnp.where(inside, decay * pltpu.roll(decay, reach, 0), decay)
    return decay, value


def joined_backward(decay, value, row):
    for reach in (1, 2, 4):
        inside = row < SEGMENTS - reach
        value = value + jnp.where(inside, decay * pltpu.roll(value, SEGMENTS - reach, 0), 0.0)
        decay = jnp.where(inside, decay * pltpu.roll(decay, SEGMENTS - reach, 0), decay)
    return decay, value


def ends_kernel(step_ref, input_ref, mix_in_ref, rate_ref, decay_ref, state_ref, last_ref):
    steps, states, lanes = step_ref.shape[0], mix_in_ref.shape[1], step_ref.shape[2]
    zero = zeros_of(step_ref)
    row = sublane_rows(lanes)
    total = lax.fori_loop(0, steps, lambda at, total: total + step_ref[at], zero, unroll=UNROLL_E)
    for members in groups_of(states, GROUP_A):
        rates = [rate_ref[n] for n in members]

        def body(at, held):
            step = step_ref[at]
            driven = step * input_ref[at]
            return tuple(
                jnp.exp2(step * rate) * before + widened(mix_in_ref[at, n], lanes) * driven
                for n, rate, before in zip(members, rates, held)
            )

        held = lax.fori_loop(0, steps, body, (zero,) * len(members), unroll=UNROLL_A)
        for n, rate, end in zip(members, rates, held):
            decay, value = joined_forward(jnp.exp2(total * rate), end, row)
            decay_ref[n] = decay
            state_ref[n] = value
            last_ref[n : n + 1] = value[SEGMENTS - 1 :]


def states_kernel(
    step_ref, input_ref, mix_in_ref, mix_out_ref, rate_ref, decay_ref, state_ref, enter_ref,
    out_ref, start_ref,
):
    steps, states, lanes = step_ref.shape[0], mix_in_ref.shape[1], step_ref.shape[2]
    row = sublane_rows(lanes)
    for members in groups_of(states, GROUP_B):
        rates = [rate_ref[n] for n in members]
        held = []
        for n in members:
            first = jnp.broadcast_to(enter_ref[n : n + 1], (SEGMENTS, lanes))
            inner = pltpu.roll(state_ref[n], 1, 0) + pltpu.roll(decay_ref[n], 1, 0) * first
            start = jnp.where(row >= 1, inner, first)
            start_ref[n] = start
            held.append(start)

        def body(at, held):
            step = step_ref[at]
            driven = step * input_ref[at]
            held = tuple(
                jnp.exp2(step * rate) * before + widened(mix_in_ref[at, n], lanes) * driven
                for n, rate, before in zip(members, rates, held)
            )
            parts = [widened(mix_out_ref[at, n], lanes) * now for n, now in zip(members, held)]
            if members[0]:
                parts.append(out_ref[at])
            while len(parts) > 1:
                parts = [sum(parts[i + 1 : i + 2], parts[i]) for i in range(0, len(parts), 2)]
            out_ref[at] = parts[0]
            return held

        lax.fori_loop(0, steps, body, tuple(held), unroll=UNROLL_B)


def adjoint_ends_kernel(step_ref, mix_out_ref, grad_ref, rate_ref, decay_ref, adjoint_ref, first_ref):
    steps, states, lanes = step_ref.shape[0], mix_out_ref.shape[1], step_ref.shape[2]
    zero = zeros_of(step_ref)
    row = sublane_rows(lanes)
    total = lax.fori_loop(0, steps, lambda at, total: total + step_ref[at], zero, unroll=UNROLL_E)
    for members in groups_of(states, GROUP_A):
        rates = [rate_ref[n] for n in members]

        def body(back, incoming):
            at = steps - 1 - back
            step = step_ref[at]
            grad = grad_ref[at]
            return tuple(
                jnp.exp2(step * rate) * (widened(mix_out_ref[at, n], lanes) * grad + after)
                for n, rate, after in zip(members, rates, incoming)
            )

        incoming = lax.fori_loop(0, steps, body, (zero,) * len(members), unroll=UNROLL_A)
        for n, rate, end in zip(members, rates, incoming):
            decay, value = joined_backward(jnp.exp2(total * rate), end, row)
            decay_ref[n] = decay
            adjoint_ref[n] = value
            first_ref[n : n + 1] = value[:1]


def adjoint_kernel(
    step_ref, input_ref, mix_in_ref, mix_out_ref, grad_ref, rate_ref, start_ref, decay_ref, adjoint_ref,
    enter_ref, skip_ref,
    pre_out_ref, conv_ref, decay_sum_ref, sums_ref, mix_ref,
    states_ref, decays_ref, in_grad_ref, out_grad_ref, pre_ref,
):
    steps, states, lanes = step_ref.shape[0], mix_in_ref.shape[1], step_ref.shape[2]
    row = sublane_rows(lanes)
    zero = zeros_of(step_ref)

    @pl.when(pl.program_id(1) == 0)
    def clear():
        in_grad_ref[...] = jnp.zeros_like(in_grad_ref)
        out_grad_ref[...] = jnp.zeros_like(out_grad_ref)

    for members in groups_of(states, GROUP_C):
        first, group = members[0], len(members)
        rates = [rate_ref[n] for n in members]

        def ahead(at, held):
            step = step_ref[at]
            driven = step * input_ref[at]
            grad = grad_ref[at]
            after = []
            for i, n in enumerate(members):
                states_ref[at, i] = held[i]
                decay = jnp.exp2(step * rates[i])
                decays_ref[at, i] = decay
                now = decay * held[i] + widened(mix_in_ref[at, n], lanes) * driven
                out_grad_ref[at, n] += narrowed(grad * now)
                after.append(now)
            return tuple(after)

        lax.fori_loop(0, steps, ahead, tuple(start_ref[n] for n in members), unroll=UNROLL_C)

        incoming = []
        for n in members:
            final = jnp.broadcast_to(enter_ref[n : n + 1], (SEGMENTS, lanes))
            inner = (
                pltpu.roll(adjoint_ref[n], SEGMENTS - 1, 0)
                + pltpu.roll(decay_ref[n], SEGMENTS - 1, 0) * final
            )
            incoming.append(jnp.where(row < SEGMENTS - 1, inner, final))

        def body(back, carry):
            at = steps - 1 - back
            incoming, decay_sums = carry
            step = step_ref[at]
            grad = grad_ref[at]
            driven = step * input_ref[at]
            in_sum = conv_ref[at] if first else zero
            rate_sum = pre_ref[at] if first else zero
            following, sums = [], []
            for i, n in enumerate(members):
                adjoint = widened(mix_out_ref[at, n], lanes) * grad + incoming[i]
                onward = decays_ref[at, i] * adjoint
                decay_grad = onward * states_ref[at, i]
                in_sum = in_sum + adjoint * widened(mix_in_ref[at, n], lanes)
                rate_sum = rate_sum + decay_grad * rates[i]
                sums.append(decay_sums[i] + decay_grad * step)
                in_grad_ref[at, n] += narrowed(adjoint * driven)
                following.append(onward)
            conv_ref[at] = in_sum
            pre_ref[at] = rate_sum
            return tuple(following), tuple(sums)

        _, sums = lax.fori_loop(
            0, steps, body, (tuple(incoming), (zero,) * group), unroll=UNROLL_D
        )
        for i, n in enumerate(members):
            decay_sum_ref[n : n + 1] = jnp.sum(sums[i], axis=0, keepdims=True)

    skip = skip_ref[...]

    def close(at, carry):
        pre_sum, skip_sum = carry
        step, inputs, grad, in_sum = step_ref[at], input_ref[at], grad_ref[at], conv_ref[at]
        step_grad = pre_ref[at] * (1.0 / LOG2E) + in_sum * inputs
        pre = step_grad * (1.0 - jnp.exp2(step * -LOG2E))
        pre_out_ref[at] = pre.astype(BF16)
        conv_ref[at] = in_sum * step + skip * grad
        return pre_sum + pre, skip_sum + grad * inputs

    pre_sum, skip_sum = lax.fori_loop(0, steps, close, (zero, zero), unroll=UNROLL_E)
    sums_ref[0:1] = jnp.sum(pre_sum, axis=0, keepdims=True)
    sums_ref[1:2] = jnp.sum(skip_sum, axis=0, keepdims=True)
    sums_ref[2:] = jnp.zeros((SEGMENTS - 2, lanes), F32)

    @pl.when(pl.program_id(1) == pl.num_programs(1) - 1)
    def across_lanes():
        lane = lax.broadcasted_iota(jnp.int32, (SEGMENTS, LANES), 1)

        def one(at, carry):
            total = jnp.zeros((SEGMENTS, LANES), F32)
            for n in range(states):
                for base, ref in ((0, in_grad_ref), (states, out_grad_ref)):
                    value = jnp.sum(ref[at, n], axis=1, keepdims=True)
                    total = jnp.where(lane == base + n, value, total)
            mix_ref[at] = total
            return carry

        lax.fori_loop(0, steps, one, 0, unroll=UNROLL_E)


class Scan:
    def __init__(self, steps, chains, states, width):
        lanes = LANES * math.gcd(width // LANES, BLOCKS)
        self.grid = (chains, width // lanes)
        self.rows_spec = pl.BlockSpec(
            (steps, None, SEGMENTS, lanes), lambda chain, block: (0, chain, 0, block)
        )
        self.mix_spec = pl.BlockSpec(
            (None, steps, states, SEGMENTS, LANES), lambda chain, block: (chain, 0, 0, 0, 0)
        )
        self.rate_spec = pl.BlockSpec((states, SEGMENTS, lanes), lambda chain, block: (0, 0, block))
        self.state_spec = pl.BlockSpec(
            (None, states, SEGMENTS, lanes), lambda chain, block: (chain, 0, 0, block)
        )
        self.edge_spec = pl.BlockSpec((None, states, lanes), lambda chain, block: (chain, 0, block))
        self.rows = jax.ShapeDtypeStruct((steps, chains, SEGMENTS, width), F32)
        self.mix = jax.ShapeDtypeStruct((chains, steps, states, SEGMENTS, LANES), F32)
        self.state = jax.ShapeDtypeStruct((chains, states, SEGMENTS, width), F32)
        self.edge = jax.ShapeDtypeStruct((chains, states, width), F32)
        self.sums = jax.ShapeDtypeStruct((chains, SEGMENTS, width), F32)
        self.sums_spec = pl.BlockSpec((None, SEGMENTS, lanes), lambda chain, block: (chain, 0, block))
        self.lane_sums = jax.ShapeDtypeStruct((steps, chains, SEGMENTS, LANES), F32)
        self.lane_spec = pl.BlockSpec(
            (steps, None, SEGMENTS, LANES), lambda chain, block: (0, chain, 0, 0)
        )
        self.skip_spec = pl.BlockSpec((1, lanes), lambda chain, block: (0, block))
        self.scratch = [
            pltpu.VMEM((steps, math.gcd(states, GROUP_C), SEGMENTS, lanes), F32),
            pltpu.VMEM((steps, math.gcd(states, GROUP_C), SEGMENTS, lanes), F32),
            pltpu.VMEM((steps, states, SEGMENTS, LANES), F32),
            pltpu.VMEM((steps, states, SEGMENTS, LANES), F32),
            pltpu.VMEM((steps, SEGMENTS, lanes), F32),
        ]
        self.narrow_rows = jax.ShapeDtypeStruct((steps, chains, SEGMENTS, width), BF16)
        self.work = steps * chains * SEGMENTS * width * states

    def call(self, kernel, ops, args, in_specs, outs, out_specs, scratch=()):
        size = sum(math.prod(a.shape) * a.dtype.itemsize for a in (*args, *outs))
        return pl.pallas_call(
            kernel,
            grid=self.grid,
            in_specs=in_specs,
            out_specs=out_specs,
            out_shape=outs,
            scratch_shapes=list(scratch),
            compiler_params=pltpu.CompilerParams(vmem_limit_bytes=VMEM_LIMIT),
            cost_estimate=pl.CostEstimate(
                flops=ops * self.work, transcendentals=self.work, bytes_accessed=size // COVER
            ),
        )(*args)

    def ends(self, step, inputs, mix_in, rate):
        return self.call(
            ends_kernel, 5, (step, inputs, mix_in, rate),
            [self.rows_spec, self.rows_spec, self.mix_spec, self.rate_spec],
            [self.state, self.state, self.edge],
            [self.state_spec, self.state_spec, self.edge_spec],
        )

    def run(self, step, inputs, mix_in, mix_out, rate, decay, state, enter):
        return self.call(
            states_kernel, 7, (step, inputs, mix_in, mix_out, rate, decay, state, enter),
            [self.rows_spec, self.rows_spec, self.mix_spec, self.mix_spec, self.rate_spec,
             self.state_spec, self.state_spec, self.edge_spec],
            [self.rows, self.state],
            [self.rows_spec, self.state_spec],
        )

    def adjoint_ends(self, step, mix_out, grad, rate):
        return self.call(
            adjoint_ends_kernel, 5, (step, mix_out, grad, rate),
            [self.rows_spec, self.mix_spec, self.rows_spec, self.rate_spec],
            [self.state, self.state, self.edge],
            [self.state_spec, self.state_spec, self.edge_spec],
        )

    def adjoint(self, args):
        return self.call(
            adjoint_kernel, 20, args,
            [self.rows_spec, self.rows_spec, self.mix_spec, self.mix_spec, self.rows_spec,
             self.rate_spec, self.state_spec, self.state_spec, self.state_spec, self.edge_spec,
             self.skip_spec],
            [self.narrow_rows, self.rows, self.edge, self.sums, self.lane_sums],
            [self.rows_spec, self.rows_spec, self.edge_spec, self.sums_spec, self.lane_spec],
            self.scratch,
        )


def conv_back_kernel(
    proj_ref, weight_ref, grad_ref, input_ref, taps_ref, shift_ref,
    out_ref, sums_ref, head_ref, tail_ref, product_ref, conv_ref,
):
    steps, rows, lanes = grad_ref.shape
    count = taps_ref.shape[0]
    reach = count - 1
    taps = [taps_ref[at : at + 1] for at in range(count)]
    shift = shift_ref[...]
    product_ref[...] = jnp.dot(
        proj_ref[...], weight_ref[...], preferred_element_type=F32
    ).reshape(steps, rows, lanes)

    def slopes(at, sums):
        inputs = [input_ref[at + tap].astype(F32) for tap in range(count)]
        pre = shift + sum(tap * value for tap, value in zip(taps, inputs))
        share = 1.0 / (1.0 + jnp.exp(-pre))
        conv = (grad_ref[at] + product_ref[at]) * (share * (1.0 + pre * (1.0 - share)))
        conv_ref[at] = conv
        return (*(total + conv * value for total, value in zip(sums, inputs)), sums[-1] + conv)

    zero = jnp.zeros((rows, lanes), F32)
    sums = lax.fori_loop(0, steps, slopes, (zero,) * (count + 1), unroll=2)
    for at, total in enumerate(sums):
        sums_ref[at : at + 1] = jnp.sum(total, axis=0, keepdims=True)
    sums_ref[count + 1 :] = jnp.zeros((sums_ref.shape[0] - count - 1, lanes), F32)
    row = sublane_rows(lanes)
    for at in range(reach):
        head_ref[at] = conv_ref[at]
        for low in range(0, rows, SEGMENTS):
            rolled = pltpu.roll(conv_ref[at, low : low + SEGMENTS], SEGMENTS - 1, 0)
            conv_ref[steps + at, low : low + SEGMENTS] = jnp.where(
                row < SEGMENTS - 1, rolled, 0.0
            )

    def back(at):
        return sum(taps[tap] * conv_ref[at + reach - tap] for tap in range(count))

    def store(at, carry):
        out_ref[at] = back(at).astype(BF16)
        return carry

    lax.fori_loop(0, steps, store, 0, unroll=2)
    for at in range(reach):
        tail_ref[at] = back(steps - reach + at)


def conv_back(proj, weight, grad, inputs, taps, shift):
    steps, rows, width = grad.shape
    reach = taps.shape[0] - 1
    lanes = LANES * math.gcd(width // LANES, BLOCKS)

    def block(count, dtype=F32):
        spec = pl.BlockSpec((count, rows, lanes), lambda at: (0, 0, at))
        return spec, jax.ShapeDtypeStruct((count, rows, width), dtype)

    def columns(count):
        return pl.BlockSpec((count, lanes), lambda at: (0, at))

    outs = [
        block(steps, BF16),
        (columns(SEGMENTS), jax.ShapeDtypeStruct((SEGMENTS, width), F32)),
        block(reach),
        block(reach),
    ]
    return pl.pallas_call(
        conv_back_kernel,
        grid=(width // lanes,),
        in_specs=[
            pl.BlockSpec(proj.shape, lambda at: (0, 0)),
            columns(weight.shape[0]),
            block(steps)[0],
            block(steps + reach)[0],
            columns(reach + 1),
            columns(1),
        ],
        out_specs=[spec for spec, _ in outs],
        out_shape=[shape for _, shape in outs],
        scratch_shapes=[
            pltpu.VMEM((steps, rows, lanes), F32),
            pltpu.VMEM((steps + reach, rows, lanes), F32),
        ],
        compiler_params=pltpu.CompilerParams(vmem_limit_bytes=VMEM_LIMIT),
        cost_estimate=pl.CostEstimate(flops=1, transcendentals=0, bytes_accessed=1),
    )(proj, weight, grad, inputs, taps, shift)


def expert_kernel(
    kept, rows_ref, cotan_ref, router_ref, mask_ref, up_a, down_a, up_b, down_b, *refs
):
    out_ref, picked_ref, prob_ref, copy_ref, grad_ref, active_a, active_b, hidden_a, hidden_b = refs[kept:]
    rows = rows_ref[...]
    copy_ref[...] = rows
    logits = contract_cols(rows, router_ref[...])
    shifted = jnp.exp(logits - jnp.max(logits, axis=1, keepdims=True))
    prob = shifted / jnp.sum(shifted, axis=1, keepdims=True)
    gate = jnp.sum(prob * mask_ref[...], axis=1, keepdims=True)
    grad = (gate * cotan_ref[...].astype(F32)).astype(BF16)
    prob_ref[...] = prob
    grad_ref[...] = grad
    out, picked = None, None
    for up, down, active_ref, hidden_ref in (
        (up_a, down_a, active_a, hidden_a),
        (up_b, down_b, active_b, hidden_b),
    ):
        up, down = (value[...].reshape(-1, value.shape[2]) for value in (up, down))
        hidden = jnp.dot(rows, up, preferred_element_type=F32)
        share = 0.5 + 0.5 * lax.erf(hidden * math.sqrt(0.5))
        slope = share + hidden * (jnp.exp(-0.5 * hidden * hidden) * (1.0 / math.sqrt(2 * math.pi)))
        active = (hidden * share).astype(BF16)
        active_ref[...] = active
        hidden_grad = (jnp.dot(grad, down, preferred_element_type=F32) * slope).astype(BF16)
        hidden_ref[...] = hidden_grad
        out_part = contract_cols(active, down)
        picked_part = contract_cols(hidden_grad, up)
        out = out_part if out is None else out + out_part
        picked = picked_part if picked is None else picked + picked_part
    out_ref[...] = out
    picked_ref[...] = picked


def expert_call(rows, cotan, router_t, mask, blocks, far_up, far_down, part, parts, kept):
    count, width = rows.shape
    shard, hidden = far_up.shape[1:]
    block = math.gcd(count, 512)
    base = part * (count // block)

    def rows_of(columns, low=0):
        return pl.BlockSpec((block, columns), lambda at: (at + low, 0))

    def whole(array):
        return pl.BlockSpec(array.shape, lambda at: (0, 0), pipeline_mode=pl.Buffered(1))

    def layer(array, at):
        return pl.BlockSpec(
            (array.shape[0], shard, hidden), lambda step: (0, at, 0), pipeline_mode=pl.Buffered(1)
        )

    experts = router_t.shape[0]
    inputs = (rows, cotan, router_t, mask, blocks, blocks, far_up, far_down)
    columns = (width, width, hidden, hidden, hidden, hidden)
    return pl.pallas_call(
        partial(expert_kernel, len(kept)),
        grid=(count // block,),
        in_specs=[
            rows_of(width), rows_of(width), whole(router_t), whole(mask),
            layer(blocks, 0), layer(blocks, 1), layer(far_up, 0), layer(far_down, 0),
            *[pl.BlockSpec(memory_space=pl.ANY)] * len(kept),
        ],
        out_specs=[
            rows_of(width), rows_of(width), rows_of(experts), *(rows_of(one, base) for one in columns)
        ],
        out_shape=[
            *(jax.ShapeDtypeStruct((count, one), F32) for one in (width, width, experts)),
            *(jax.ShapeDtypeStruct((parts * count, one), BF16) for one in columns),
        ],
        input_output_aliases={len(inputs) + at: 3 + at for at in range(len(kept))},
        compiler_params=pltpu.CompilerParams(vmem_limit_bytes=EXPERT_VMEM),
        cost_estimate=pl.CostEstimate(
            flops=16 * count * width * hidden,
            transcendentals=4 * count * hidden,
            bytes_accessed=count * (14 * width + 8 * hidden) + 8 * width * hidden,
        ),
    )(*inputs, *kept)


def expert_exchange(value, experts):
    count = lax.axis_size("dp")
    groups = None
    if count != experts:
        groups = [
            [base + e for e in range(experts)] for base in range(0, count, experts)
        ]
    return lax.all_to_all(value, "dp", 0, 0, axis_index_groups=groups, tiled=True)


def by_ctx(first, second):
    lead = lax.axis_index("ctx") == 0
    return jnp.where(lead, first, second), jnp.where(lead, second, first)


def own_expert_blocks(up_shards, down_shards):
    experts, _, hidden = up_shards.shape
    count = lax.axis_size("dp")
    half = hidden // 2
    both = jnp.concatenate([up_shards, down_shards], axis=1)
    if lax.axis_size("ctx") == 2:
        both = by_ctx(both[:, :, :half], both[:, :, half:])[0]
    if count != experts:
        both = jnp.concatenate([both] * (count // experts), axis=0)
    return lax.all_to_all(both, "dp", 0, 0, tiled=True)


def other_hidden(both, layer):
    rows = both.shape[1] // 2
    both = both[:, layer * rows : (layer + 1) * rows]
    if lax.axis_size("ctx") == 2:
        return swapped(both, "ctx")
    return both[:, :, both.shape[2] // 2 :]


def gather_kernel(count, number, parts, *refs):
    ins, outs = refs[:number], refs[number : 2 * number]
    send_sem, recv_sem, own_sem = refs[2 * number :]
    places = count // 2
    me = lax.axis_index("dp")
    place, side = lax.div(me, 2), lax.rem(me, 2)
    across = me + 1 - 2 * side
    barrier = pltpu.get_barrier_semaphore()
    late = [part for part, (_, _, _, early) in enumerate(parts) if not early]
    early = [part for part, (_, _, _, early) in enumerate(parts) if early]

    def greet(device):
        pl.semaphore_signal(
            barrier, inc=1, device_id={"dp": device}, device_id_type=pl.DeviceIdType.MESH
        )

    greet(across)
    for step in (-1, 1):
        there = place + step

        @pl.when((there >= 0) & (there < places))
        def greet_place(step=step):
            greet(me + 2 * step)

    neighbours = 1 + (place > 0).astype(jnp.int32) + (place < places - 1).astype(jnp.int32)
    pl.semaphore_wait(barrier, neighbours)

    def copy(part, slot, kind, device, own):
        array, low, rows, _ = parts[part]
        landing = outs[array].at[slot, pl.ds(low, rows)]
        return pltpu.make_async_remote_copy(
            src_ref=ins[array].at[pl.ds(low, rows)] if own else landing,
            dst_ref=landing,
            send_sem=send_sem.at[kind, part, slot],
            recv_sem=recv_sem.at[part, slot],
            device_id={"dp": device},
            device_id_type=pl.DeviceIdType.MESH,
        )

    def along(which, slot, steps, own, act):
        for step in steps:
            there = place + step

            @pl.when((there >= 0) & (there < places))
            def one_way(step=step):
                for part in which:
                    act(copy(part, slot, step + 1, me + 2 * step, own))

    def aside(which, slot, own, act):
        for part in which:
            act(copy(part, slot, 1, across, own))

    def arrived(which, slot):
        for part in which:
            copy(part, slot, 1, across, False).wait_recv()

    def start(one):
        one.start()

    def sent(one):
        one.wait_send()

    mine = [
        pltpu.make_async_copy(ins[array], outs[array].at[me], own_sem.at[array])
        for array in range(number)
    ]
    for one in mine:
        one.start()
    both = (-1, 1)
    aside(early, me, True, start)
    for part in late:
        along((part,), me, both, True, start)
        aside((part,), me, True, start)
    along(early, me, both, True, start)
    arrived(early, across)
    along(early, across, both, False, start)
    for far in range(1, places):
        for step in both:
            origin = place - step * far

            @pl.when((origin >= 0) & (origin < places))
            def forward(step=step, far=far):
                slot, other = me - 2 * step * far, across - 2 * step * far
                for part in late:
                    arrived((part,), slot)
                    along((part,), slot, (step,), False, start)
                    aside((part,), slot, False, start)
                arrived(early, slot)
                along(early, slot, (step,), False, start)
                arrived(early, other)
                along(early, other, (step,), False, start)

    for at in range(places):
        arrived(late, 2 * at + 1 - side)
    for one in mine:
        one.wait()
    aside(early + late, me, True, sent)
    along(early + late, me, both, True, sent)
    along(early, across, both, False, sent)
    for far in range(1, places):
        for step in both:
            origin = place - step * far

            @pl.when((origin >= 0) & (origin < places))
            def forwarded(step=step, far=far):
                slot, other = me - 2 * step * far, across - 2 * step * far
                aside(late, slot, False, sent)
                along(early + late, slot, (step,), False, sent)
                along(early, other, (step,), False, sent)


def gathered(*values):
    count = lax.axis_size("dp")
    number = len(values)
    parts = []
    for at, value in enumerate(values):
        rows = value.shape[0]
        step = rows // 3 if value.shape[1] > 1024 and rows % 24 == 0 else rows
        parts += [
            (at, low, step, at == number - 1 and 0 < low == rows - step)
            for low in range(0, rows, step)
        ]
    anywhere = pl.BlockSpec(memory_space=pl.ANY)
    size = sum(math.prod(value.shape) * 2 for value in values)
    return pl.pallas_call(
        partial(gather_kernel, count, number, parts),
        in_specs=[anywhere] * number,
        out_specs=[anywhere] * number,
        out_shape=[jax.ShapeDtypeStruct((count, *value.shape), value.dtype) for value in values],
        scratch_shapes=[
            pltpu.SemaphoreType.DMA((3, len(parts), count)),
            pltpu.SemaphoreType.DMA((len(parts), count)),
            pltpu.SemaphoreType.DMA((number,)),
        ],
        compiler_params=pltpu.CompilerParams(collective_id=0, has_side_effects=True),
        cost_estimate=pl.CostEstimate(
            flops=0, transcendentals=0, bytes_accessed=2 * count * size
        ),
    )(*values)


def other_joined(own, first_shard, second_shard):
    count = lax.axis_size("ctx")
    if count == 2:
        return by_ctx(own, swapped(own, "ctx"))
    del first_shard, second_shard
    every = lax.all_gather(own, "ctx")
    return every[0], every[1]


def expert_weight_products(rows, hidden_grads, grads, actives):
    pairs = ((rows, hidden_grads), (grads, actives))
    far = [contract_rows(left, rights[1]) for left, rights in pairs]
    if lax.axis_size("ctx") == 2:
        far = [value.astype(BF16) for value in far]
    return [contract_rows(left, rights[0]) for left, rights in pairs], far


def sent_far(value):
    return swapped(value, "ctx") if lax.axis_size("ctx") == 2 else value


def expert_weight_parts(near, far):
    count = lax.axis_size("dp")
    parts = []
    for own, other in zip(near, far):
        if lax.axis_size("ctx") == 2:
            part = own + other.astype(F32)
        else:
            part = lax.psum_scatter(
                jnp.concatenate([own, other], axis=1), "ctx", scatter_dimension=1, tiled=True
            )
        parts.append(part.astype(BF16).reshape(count, part.shape[0] // count, part.shape[1]))
    return jnp.concatenate(parts, axis=1)


def expert_weight_blocks(blocks, experts):
    count = lax.axis_size("dp")
    if count != experts:
        blocks = jnp.sum(
            blocks.reshape(count // experts, experts, *blocks.shape[1:]).astype(F32), axis=0
        ).astype(BF16)
    return blocks


def far_hidden(blocks):
    if lax.axis_size("ctx") == 2:
        return swapped(blocks, "ctx")
    return lax.all_gather(blocks, "ctx", axis=2, tiled=True)


def expert_weight_grad(blocks, far_blocks):
    if lax.axis_size("ctx") == 2:
        far_blocks = jnp.concatenate(by_ctx(blocks, far_blocks), axis=2)
    return far_blocks.astype(F32)


def pair_products(first, second):
    if lax.axis_size("ctx") != 2:
        return contract_rows(*first), contract_rows(*second).astype(BF16)
    lefts, rights = by_ctx(first[0], second[0]), by_ctx(first[1], second[1])
    return contract_rows(lefts[0], rights[0]), contract_rows(lefts[1], rights[1]).astype(BF16)


def product_part(near, far):
    count = lax.axis_size("dp")

    def blocks(value):
        return value.astype(BF16).reshape(count, value.shape[0] // count, value.shape[1])

    if lax.axis_size("ctx") != 2:
        return jnp.concatenate([blocks(near), blocks(far)], axis=1)
    return blocks(near + far.astype(F32))


def product_shards(blocks):
    sums = jnp.sum(blocks.astype(F32), axis=0)
    if lax.axis_size("ctx") == 2:
        return by_ctx(sums, swapped(sums, "ctx"))
    sums = lax.psum(sums, "ctx")
    rows = sums.shape[0] // 2
    return sums[:rows], sums[rows:]


def local(
    hidden_in,
    out_grad,
    norm1_gain,
    in_weight,
    conv_weight,
    conv_bias,
    xproj_weight,
    dt_weight,
    dt_bias,
    decay_log,
    skip_weight,
    out_weight,
    norm2_gain,
    router_weight,
    fc1_weight,
    fc2_weight,
    expert_ids,
    keep_mask,
):
    batches, seqs, length, model_width = hidden_in.shape
    chains = batches * seqs
    tokens = chains * length
    steps = length // SEGMENTS
    shard, _, inner = in_weight.shape
    taps = conv_weight.shape[0]
    low_rank = dt_weight.shape[0]
    states = decay_log.shape[0]
    experts = fc1_weight.shape[0]
    dp_count = lax.axis_size("dp")
    tp_count = lax.axis_size("tp")
    capacity = tokens // 4
    part_cap = capacity // tp_count // HALVES
    slots = experts * part_cap
    tp_index = lax.axis_index("tp")
    scan = Scan(steps, chains, states, inner)

    def to_rows(value):
        value = value.reshape(chains, SEGMENTS, steps, -1).transpose(2, 0, 1, 3)
        return value.reshape(tokens, -1)

    def from_rows(value):
        value = value.reshape(steps, chains, SEGMENTS, -1).transpose(1, 2, 0, 3)
        return value.reshape(batches, seqs, length, -1)

    pieces = [
        norm1_gain[None],
        conv_weight,
        conv_bias[None],
        dt_weight,
        dt_bias[None],
        decay_log,
        skip_weight[None],
        norm2_gain[None],
        router_weight.T,
        xproj_weight.T,
    ]
    bounds = [0]
    for piece in pieces:
        bounds.append(bounds[-1] + piece.shape[0])
    small = sum(
        jnp.pad(piece, ((low, bounds[-1] - high), (0, 0)))
        for piece, low, high in zip(pieces, bounds, bounds[1:])
    )
    kinds = small.shape[0]
    small_wide = jnp.pad(small.T, ((0, 0), (0, -kinds % LANES)))
    in_x, small_all, later = gathered(
        in_weight[:, 0], small_wide, by_ctx(out_weight.T, in_weight[:, 1])[0]
    )
    in_x = in_x.reshape(dp_count * shard, inner)
    later = later.reshape(dp_count * shard, inner)
    small_all = small_all.reshape(dp_count * shard, -1)[:, :kinds].T
    small_all, up_shards, down_shards = together(
        small_all, fc1_weight, fc2_weight.transpose(0, 2, 1)
    )
    pieces = [small_all[bounds[i] : bounds[i + 1]] for i in range(len(bounds) - 1)]
    gain_one_f = pieces[0].astype(F32)
    tap_weights = pieces[1].astype(F32)
    conv_shift = pieces[2].astype(F32)
    dt_proj = pieces[3]
    dt_shift = pieces[4].astype(F32)
    decay_rate = -jnp.exp(pieces[5].astype(F32))
    skip_row = pieces[6].astype(F32)
    gain_two_f = pieces[7].astype(F32)
    router_t = pieces[8]
    x_proj_t = pieces[9]
    rate_rows = jnp.broadcast_to((decay_rate * LOG2E)[:, None, :], (states, SEGMENTS, inner))
    expert_blocks = own_expert_blocks(up_shards, down_shards)

    values = lax.optimization_barrier(to_rows(hidden_in)).astype(F32)
    normalized_rows, inverse_one = rms_forward(values, gain_one_f)
    normed_bf = normalized_rows.astype(BF16)
    x_pre = jnp.dot(normed_bf, in_x, preferred_element_type=F32).astype(BF16)
    x_pre = x_pre.reshape(steps, chains, SEGMENTS, inner)
    tail = x_pre[steps - taps + 1 :]
    edge_in = passed_along(tail[:, :, SEGMENTS - 1 :], "ctx", 1)
    edge_in, later = together(edge_in, later)
    out_proj_t, in_z = other_joined(later, out_weight.T, in_weight[:, 1])
    halo = jnp.concatenate([edge_in, tail[:, :, : SEGMENTS - 1]], axis=2)
    extended_bf = jnp.concatenate([halo, x_pre], axis=0)
    extended = extended_bf.astype(F32)
    conv_pre = jnp.broadcast_to(conv_shift[0], x_pre.shape)
    for tap in range(taps):
        conv_pre = conv_pre + tap_weights[tap] * extended[tap : tap + steps]
    xconv_bf = jax.nn.silu(conv_pre).astype(BF16)
    xconv = xconv_bf.astype(F32)
    xconv_rows = xconv_bf.reshape(tokens, inner)
    projected = axis_sum(contract_cols(xconv_rows, x_proj_t), "tp")
    dt_low = projected[:, :low_rank].astype(BF16)

    def mixes(value):
        value = value.reshape(steps, chains, SEGMENTS, states).transpose(1, 0, 3, 2)
        return jnp.broadcast_to(value[..., None], (*value.shape, LANES))

    mix_in = mixes(projected[:, low_rank : low_rank + states])
    mix_out = mixes(projected[:, low_rank + states :])
    dt_pre = (jnp.dot(dt_low, dt_proj, preferred_element_type=F32) + dt_shift).reshape(x_pre.shape)
    step_size = jax.nn.softplus(dt_pre)
    seg_decay, seg_state, last_state = scan.ends(step_size, xconv, mix_in, rate_rows)
    later_ids, later_mask, later_grad, mix_out, _ = together(
        expert_ids, keep_mask, out_grad, mix_out, seg_state
    )
    route = to_rows(later_ids)[:, 0]
    keep = to_rows(later_mask)[:, 0].astype(F32)
    onehot_int = (route[:, None] == jnp.arange(experts, dtype=jnp.int32)[None, :]).astype(jnp.int32)
    rank = jnp.sum((jnp.cumsum(onehot_int, axis=0) - 1) * onehot_int, axis=1)
    places = []
    for half in range(HALVES):
        own = rank - (tp_index * HALVES + half) * part_cap
        token_slot = jnp.where((own >= 0) & (own < part_cap), route * part_cap + own, -1)
        places.append(
            (token_slot[None, :] == jnp.arange(slots, dtype=jnp.int32)[:, None]).astype(BF16)
        )

    def slotted(value, half):
        sent = jnp.dot(places[half], value, preferred_element_type=F32).astype(BF16)
        return sent.reshape(experts, part_cap, -1)

    def landed(values):
        total = sum(
            contract_rows(place, value.reshape(slots, -1)) for place, value in zip(places, values)
        )
        return axis_sum(total.astype(BF16), "tp").astype(F32)

    def halves_of(value):
        return [value[:, at : at + part_cap] for at in range(0, value.shape[1], part_cap)]

    cotan_bf = to_rows(later_grad)
    cotan = cotan_bf.astype(F32)
    kept_cotan = (cotan * keep[:, None]).astype(BF16)
    sent_cotan = jnp.concatenate([slotted(kept_cotan, half) for half in range(HALVES)], axis=1)
    entering = entering_pieces(seg_decay[:, :, SEGMENTS - 1], last_state, "ctx", False)
    entering, mix_out, expert_blocks, sent_cotan = together(
        entering, mix_out, expert_blocks, sent_cotan
    )
    slot_cotan = expert_exchange(sent_cotan, experts)
    far_up = other_hidden(expert_blocks, 0)
    scan_out, seg_start = scan.run(
        step_size, xconv, mix_in, mix_out, rate_rows, seg_decay, seg_state, entering
    )
    z_gate = jnp.dot(normed_bf, in_z, preferred_element_type=F32).reshape(x_pre.shape)
    scanned = scan_out + skip_row[0] * xconv
    z_silu = jax.nn.silu(z_gate)
    gated_bf = (scanned * z_silu).astype(BF16).reshape(tokens, inner)
    gated_bf, far_up = together(gated_bf, far_up)
    mixer_part, slot_cotan = together(contract_cols(gated_bf, out_proj_t), slot_cotan)
    middle = values + axis_sum(mixer_part, "tp")

    normed_two, inverse_two = rms_forward(middle, gain_two_f)
    normed_two_bf = normed_two.astype(BF16)
    expert_mask = (
        jnp.arange(experts, dtype=jnp.int32) == lax.rem(lax.axis_index("dp"), experts)
    ).astype(F32)[None, :]
    kept = ()
    got_grads, slot_outs, router_grad_t = [], [], 0.0
    for half, half_cotan in enumerate(halves_of(slot_cotan)):
        sent_rows = slotted(normed_two_bf, half)
        if not half:
            sent_rows, expert_blocks = together(sent_rows, expert_blocks)
            far_down = other_hidden(expert_blocks, 1)
        own_rows = expert_exchange(sent_rows, experts)
        if not half:
            own_rows, far_down = together(own_rows, far_down)
        else:
            own_rows, kept = together(own_rows, kept)
        own_rows = own_rows.reshape(slots, model_width)
        half_cotan = half_cotan.reshape(slots, model_width)
        far_rows, far_cotan = swapped(own_rows, "tp"), swapped(half_cotan, "tp")
        call = partial(
            expert_call, router_t=router_t, mask=expert_mask, blocks=expert_blocks, far_up=far_up,
            far_down=far_down, parts=2 * HALVES,
        )
        far = call(far_rows, far_cotan, part=2 * half, kept=kept)
        near = call(own_rows, half_cotan, part=2 * half + 1, kept=far[3:])
        if half:
            near, got_grads = together(near, got_grads)
        kept = near[3:]
        slot_out = near[0] + swapped(far[0], "tp")
        picked_grad = near[1] + swapped(far[1], "tp")
        slot_prob = near[2]
        slot_gate = jnp.sum(slot_prob * expert_mask, axis=1, keepdims=True)
        gate_grad = jnp.sum(slot_out * half_cotan.astype(F32), axis=1, keepdims=True)
        logit_grad = gate_grad * slot_gate * (expert_mask - slot_prob)
        router_grad_t = router_grad_t + contract_rows(logit_grad, own_rows.astype(F32), HIGHEST)
        picked_grad = picked_grad + jnp.dot(
            logit_grad, router_t.astype(F32), precision=HIGHEST, preferred_element_type=F32
        )
        got_grads.append(
            expert_exchange(picked_grad.astype(BF16).reshape(experts, part_cap, -1), experts)
        )
        slot_outs.append(slot_out.astype(BF16).reshape(experts, part_cap, -1))
    router_grad_t = axis_sum(router_grad_t, "tp")
    all_rows, all_grads, active_a, active_b, hidden_a, hidden_b = kept
    near_parts, far_parts = expert_weight_products(
        all_rows, (hidden_a, hidden_b), all_grads, (active_a, active_b)
    )
    far_first = sent_far(far_parts[0])
    (
        got_grads, near_parts, far_second, far_first, slot_outs, router_grad_t, extended_bf, xconv_t
    ) = together(
        got_grads, near_parts, far_parts[1], far_first, slot_outs, router_grad_t, extended_bf,
        xconv_rows.T,
    )
    far_parts = far_first, sent_far(far_second)
    normed_two_grad = landed(got_grads)
    got_out = expert_exchange(jnp.concatenate(slot_outs, axis=1), experts)
    middle_norm_grad, gain_two_grad = rms_backward(middle, inverse_two, gain_two_f, normed_two_grad)
    middle_grad = cotan + middle_norm_grad
    mixer_grad_bf = middle_grad.astype(BF16)
    gated_grad = jnp.dot(mixer_grad_bf, out_proj_t, preferred_element_type=F32).reshape(x_pre.shape)
    scan_grad = gated_grad * z_silu
    z_grad = jax.vjp(jax.nn.silu, z_gate)[1](gated_grad * scanned)[0]
    z_grad_bf = z_grad.astype(BF16).reshape(tokens, inner)
    near_product, far_product = pair_products((mixer_grad_bf, gated_bf), (normed_bf, z_grad_bf))
    back_decay, back_adjoint, first_adjoint = scan.adjoint_ends(
        step_size, mix_out, scan_grad, rate_rows
    )
    normed_part = contract_cols(z_grad_bf, in_z)
    far_parts, got_out, near_product, far_product, _ = together(
        far_parts, got_out, near_product, far_product, first_adjoint
    )
    weight_blocks = lax.all_to_all(
        expert_weight_parts(near_parts, far_parts), "dp", 0, 0, tiled=True
    )
    leaving = entering_pieces(back_decay[:, :, 0], first_adjoint, "ctx", True)
    leaving, near_product, far_product, normed_part = together(
        leaving, near_product, far_product, normed_part
    )
    far_product = sent_far(far_product)
    adjoint_args = (
        step_size, xconv, mix_in, mix_out, scan_grad, rate_rows, seg_start, back_decay, back_adjoint,
        leaving, skip_row,
    )
    pre_grad, xconv_grad, decay_sum, scan_sums, mix_grad = scan.adjoint(adjoint_args)
    pre_grad, far_product, weight_blocks = together(pre_grad, far_product, weight_blocks)
    weight_blocks = expert_weight_blocks(weight_blocks, experts)
    far_ups = far_hidden(weight_blocks[:, :shard])
    out_blocks = lax.all_to_all(product_part(near_product, far_product), "dp", 0, 0, tiled=True)
    decay_log_grad = jnp.sum(decay_sum, axis=0) * decay_rate
    dt_shift_grad, skip_grad = jnp.sum(scan_sums, axis=0)[:2]
    pre_grad = pre_grad.reshape(tokens, inner)
    dt_proj_grad = contract_rows(dt_low, pre_grad)
    dt_low_grad = contract_cols(pre_grad, dt_proj)
    mix_grad = mix_grad.reshape(tokens, LANES)[:, : 2 * states]
    proj_part = jnp.concatenate([dt_low_grad, mix_grad], axis=1)
    proj_grad_bf = axis_sum(proj_part, "tp").astype(BF16)
    x_proj_grad_t = lax.dot_general(
        proj_grad_bf, xconv_t, (((0,), (1,)), ((), ())), preferred_element_type=F32
    )
    flat = (chains * SEGMENTS, inner)
    x_grad_bf, conv_sums, head, last = conv_back(
        proj_grad_bf,
        x_proj_t,
        xconv_grad.reshape(steps, *flat),
        extended_bf.reshape(steps + taps - 1, *flat),
        tap_weights,
        conv_shift,
    )
    taps_grad, shift_grad = conv_sums[:taps], conv_sums[taps]
    edge_back = passed_along(
        head.reshape(taps - 1, chains, SEGMENTS, inner)[:, :, :1], "ctx", -1
    )
    edge_back, out_blocks, far_ups, weight_blocks = together(
        edge_back, out_blocks, far_ups, weight_blocks
    )
    reaching = jnp.stack(
        [
            sum(tap_weights[tap] * edge_back[at - tap] for tap in range(at + 1))
            for at in range(taps - 1)
        ]
    )
    reaching = jnp.pad(reaching, ((0, 0), (0, 0), (SEGMENTS - 1, 0), (0, 0)))
    last = (last + reaching.reshape(taps - 1, *flat)).astype(BF16)
    x_grad_bf = lax.dynamic_update_slice(x_grad_bf, last, (steps - taps + 1, 0, 0))
    x_grad_bf = x_grad_bf.reshape(tokens, inner)
    small_grads = jnp.concatenate(
        [
            taps_grad,
            shift_grad[None],
            dt_proj_grad,
            dt_shift_grad[None],
            decay_log_grad,
            skip_grad[None],
            gain_two_grad[None],
            router_grad_t,
            x_proj_grad_t,
        ],
        axis=0,
    )
    small_grads = small_grads.reshape(-1, dp_count, shard).transpose(1, 0, 2)
    small_size = small_grads.shape[1] * shard
    small_rows = small_grads.astype(BF16).reshape(dp_count, small_size)
    small_rows = jnp.pad(small_rows, ((0, 0), (0, -small_size % inner))).reshape(dp_count, -1, inner)
    x_grad_bf, small_rows, out_blocks = together(x_grad_bf, small_rows, out_blocks)
    normed_part = normed_part + contract_cols(x_grad_bf, in_x)
    normed_grad = axis_sum(normed_part, "tp")
    values_norm_grad, gain_one_grad = rms_backward(values, inverse_one, gain_one_f, normed_grad)
    input_grad = from_rows((middle_grad + values_norm_grad).astype(BF16))

    in_x_part = contract_rows(normed_bf, x_grad_bf).astype(BF16).reshape(dp_count, shard, inner)
    gain_row = gain_one_grad.reshape(dp_count, 1, shard)
    gain_high = gain_row.astype(BF16)
    gain_low = (gain_row - gain_high.astype(F32)).astype(BF16)
    gain_row = jnp.concatenate([gain_high, gain_low], axis=2)
    gain_row = jnp.pad(gain_row, ((0, 0), (0, 0), (0, inner - 2 * shard)))
    in_x_part, out_blocks = together(in_x_part, out_blocks)
    out_proj_grad, in_z_grad = product_shards(out_blocks)
    in_x_part, got_out, normed_two_bf = together(
        jnp.concatenate([in_x_part, small_rows, gain_row], axis=1), got_out, normed_two_bf
    )
    in_x_blocks = lax.all_to_all(in_x_part, "dp", 0, 0, tiled=True)
    out_proj_grad, in_z_grad, far_down_blocks = together(
        out_proj_grad, in_z_grad, weight_blocks[:, shard:]
    )
    far_downs, in_x_blocks = together(far_hidden(far_down_blocks), in_x_blocks)
    first_grad = expert_weight_grad(weight_blocks[:, :shard], far_ups)
    second_grad = expert_weight_grad(far_down_blocks, far_downs)
    router_prob = jax.nn.softmax(contract_cols(normed_two_bf, router_t), axis=-1)
    gate_prob = jnp.sum(router_prob * onehot_int.astype(F32), axis=1) * keep
    result = from_rows((middle + gate_prob[:, None] * landed(halves_of(got_out))).astype(BF16))
    in_x_sums = jnp.sum(in_x_blocks.astype(F32), axis=0).astype(BF16)
    in_x_sums = narrow_sum(in_x_sums, "ctx")
    in_x_grad = in_x_sums[:shard]
    gain_one_grad = in_x_sums[-1:, :shard] + in_x_sums[-1:, shard : 2 * shard]
    small_grads = in_x_sums[shard:-1].reshape(-1)[:small_size].reshape(-1, shard)
    small_grads = jnp.concatenate([gain_one_grad, small_grads], axis=0)
    sums = [small_grads[bounds[i] : bounds[i + 1]] for i in range(len(bounds) - 1)]
    return (
        result,
        input_grad,
        sums[0][0],
        jnp.stack([in_x_grad, in_z_grad], axis=1),
        sums[1],
        sums[2][0],
        sums[9].T,
        sums[3],
        sums[4][0],
        sums[5],
        sums[6][0],
        out_proj_grad.T,
        sums[7][0],
        sums[8].T,
        first_grad,
        second_grad.transpose(0, 2, 1),
    )


def solution(mesh):
    weights = (
        P("dp"),
        P("dp", None, "tp"),
        P(None, ("tp", "dp")),
        P(("tp", "dp")),
        P(("tp", "dp"), None),
        P(None, ("tp", "dp")),
        P(("tp", "dp")),
        P(None, ("tp", "dp")),
        P(("tp", "dp")),
        P("tp", "dp"),
        P("dp"),
        P("dp", None),
        P(None, "dp", "tp"),
        P(None, "tp", "dp"),
    )
    rows = P(None, "dp", "ctx", None)
    return jax.shard_map(
        local,
        mesh=mesh,
        in_specs=(rows, rows, *weights, P(("dp", "ctx"), None), P(("dp", "ctx"))),
        out_specs=(rows, rows, *weights),
        check_vma=False,
    )
```
